32 devices in a mesh: tx: 8 (over z, y), ty: 4 (over x, core).
Axes of the slice: x: 2, y: 2, z: 4, core: 2. Of those that a mesh axis runs over, the one named last changes fastest.
Arguments:
- concentration: float32 [64, 64, 256], P('tx', 'ty'), may hold values from -6 to 6
- source: float32 [64, 64, 256], P('tx', 'ty'), may hold values from -4 to 4
- material: int32 [64, 64, 256], P('tx', 'ty'), may hold values from 0 to 7
Outputs:
- updated: float32 [64, 64, 256], P('tx', 'ty')
The draws below stay inside these ranges and needn't reach their ends.
All inputs are finite; a program needn't handle non-finite values.
Results may differ from the reference program's by a relative error of at most 0.00017.
Values sent between devices are 32-bit elements; how exact they have to be, the bound alone decides.
No kernel may reach another device: no remote copies, remote signals or barrier semaphores. Data moves between devices by JAX's collectives and lax.ppermute only.
A program may use at most 128 MiB of HBM per device.

```python
import jax
import jax.numpy as jnp

NX = 64
NY = 64
NZ = 256


def draw_source(key, part):
    return jnp.clip(jax.random.normal(key, (NX, NY, NZ), jnp.float32), -4.0, 4.0)


def with_ends(values, stream_key, smallest, top_value):
    place = [jax.random.randint(jax.random.fold_in(stream_key, axis), (), 0, length) for axis, length in enumerate(values.shape)]
    widest = values.shape.index(max(values.shape))
    next_to = place[:widest] + [(place[widest] + 1) % values.shape[widest]] + place[widest + 1:]
    return values.at[tuple(place)].set(smallest).at[tuple(next_to)].set(top_value)


def block_scale(key, shape, pieces, least, top_value):
    def one(position, parts):
        heights = jax.random.uniform(jax.random.fold_in(jax.random.fold_in(key, 6), position), (parts,), jnp.float32, least / len(pieces), top_value / len(pieces))
        return jnp.repeat(jnp.exp(heights), shape[position] // parts).reshape((-1,) + (1,) * (len(shape) - position - 1))

    factor_of = one(*pieces[0])
    for cut in pieces[1:]:
        factor_of = factor_of * one(*cut)
    return factor_of


def scatter_about(own_key, shape, width, reach, cuts=(), kind=jnp.bfloat16):
    values = jax.random.normal(own_key, shape, jnp.float32) * width
    if len(cuts) > 0:
        values = block_scale(own_key, shape, cuts, -0.22, 0.18) * values
    return jnp.clip(values, min=-reach, max=reach).astype(kind)


def setup_inputs(seed: int = 0) -> dict:
    seeds = jax.random.split(jax.random.key(seed), 4)
    return {
        "concentration": scatter_about(seeds[0], (NX, NY, NZ), 1.0, 6.0, ((0, 8), (1, 4)), jnp.float32),
        "source": draw_source(jax.random.fold_in(seeds[3], 71), 0),
        "material": with_ends(jax.random.randint(seeds[2], (NX, NY, NZ), 0, 8), jax.random.fold_in(seeds[2], 1), 0, 7).astype(jnp.int32),
    }


mass_rate = 0.001
relax_weight = 0.8
diffusivities = (0.15, 0.3, 0.5, 0.8, 1.2, 2.0, 3.2, 5.0)

def lookup(material):
    result = jnp.zeros(material.shape, jnp.float32)
    for slot_id, coeff_value in enumerate(diffusivities):
        result = jnp.where(material == slot_id, jnp.float32(coeff_value), result)
    return result

def couplings(kappa_pad, scales):
    scale_x, scale_y, scale_z = scales
    centre = kappa_pad[1:-1, 1:-1]
    return [0.5 * scale_x * (centre + kappa_pad[2:, 1:-1]), 0.5 * scale_x * (centre + kappa_pad[:-2, 1:-1]), 0.5 * scale_y * (centre + kappa_pad[1:-1, 2:]), 0.5 * scale_y * (centre + kappa_pad[1:-1, :-2]), 0.5 * scale_z * (centre + jnp.roll(centre, -1, axis=2)), 0.5 * scale_z * (centre + jnp.roll(centre, 1, axis=2))]

def diagonal_of(coupled):
    summed = mass_rate + coupled[0]
    for coupled_term in coupled[1:]:
        summed = summed + coupled_term
    return summed

def operate(field_pad, coupled, diagonal):
    centre = field_pad[1:-1, 1:-1]
    beside_all = (field_pad[2:, 1:-1], field_pad[:-2, 1:-1], field_pad[1:-1, 2:], field_pad[1:-1, :-2], jnp.roll(centre, -1, axis=2), jnp.roll(centre, 1, axis=2))
    off_sum = coupled[0] * beside_all[0]
    for number in range(1, 6):
        off_sum = off_sum + coupled[number] * beside_all[number]
    return diagonal * centre - off_sum

def sweep(field_pad, forcing, coupled, diagonal):
    centre = field_pad[1:-1, 1:-1]
    return centre + relax_weight * (forcing - operate(field_pad, coupled, diagonal)) / diagonal

def restrict(cells, ratios=(2, 2, 2)):
    size_x, size_y, size_z = cells.shape
    ratio_x, ratio_y, ratio_z = ratios
    grouped = cells.reshape(size_x // ratio_x, ratio_x, size_y // ratio_y, ratio_y, size_z // ratio_z, ratio_z)
    return jnp.sum(grouped, axis=(1, 3, 5)) * (1.0 / (ratio_x * ratio_y * ratio_z))

def prolong(coarse, ratios=(2, 2, 2)):
    return jnp.repeat(jnp.repeat(jnp.repeat(coarse, ratios[0], 0), ratios[1], 1), ratios[2], 2)

def wrap_pad(cells):
    return jnp.pad(cells, ((1, 1), (1, 1), (0, 0)), mode='wrap')

def scales_of(spacing):
    return tuple((1.0 / (step_size * step_size) for step_size in spacing))

def next_ratios(shape):
    return tuple((2 if extent % 2 == 0 else 1 for extent in shape))

def exact_solve(forcing, coupled, diagonal):
    shape = forcing.shape
    cells = forcing.size
    basis = jnp.eye(cells, dtype=forcing.dtype).reshape((cells,) + shape)
    matrix = jax.vmap(lambda unit: operate(wrap_pad(unit), coupled, diagonal).reshape(cells))(basis)
    return jnp.linalg.solve(matrix, forcing.reshape(cells)).reshape(shape)

def coarse_solve(forcing, kappa, spacing):
    coupled = couplings(wrap_pad(kappa), scales_of(spacing))
    diagonal = diagonal_of(coupled)
    ratios = next_ratios(forcing.shape)
    if forcing.size <= 64 or ratios == (1, 1, 1):
        return exact_solve(forcing, coupled, diagonal)
    current = relax_weight * forcing / diagonal
    current = sweep(wrap_pad(current), forcing, coupled, diagonal)
    residual = forcing - operate(wrap_pad(current), coupled, diagonal)
    wider = tuple((step_size * ratio for step_size, ratio in zip(spacing, ratios)))
    correction = coarse_solve(restrict(residual, ratios), restrict(kappa, ratios), wider)
    current = current + prolong(correction, ratios)
    for repeat in range(2):
        current = sweep(wrap_pad(current), forcing, coupled, diagonal)
    return current

def reference(concentration, source, material):
    kappas = [lookup(material)]
    for depth_level in range(3):
        kappas.append(restrict(kappas[-1]))
    operators = []
    for depth_level in range(3):
        coupled = couplings(wrap_pad(kappas[depth_level]), (0.25 ** depth_level,) * 3)
        operators.append((coupled, diagonal_of(coupled)))

    def vcycle(depth_level, initial, forcing):
        if depth_level == 3:
            return coarse_solve(forcing, kappas[3], (8.0, 8.0, 8.0))
        coupled, diagonal = operators[depth_level]
        if initial is None:
            current = relax_weight * forcing / diagonal
        else:
            current = sweep(wrap_pad(initial), forcing, coupled, diagonal)
        current = sweep(wrap_pad(current), forcing, coupled, diagonal)
        residual = forcing - operate(wrap_pad(current), coupled, diagonal)
        correction = vcycle(depth_level + 1, None, restrict(residual))
        current = current + prolong(correction)
        for repeat in range(2):
            current = sweep(wrap_pad(current), forcing, coupled, diagonal)
        return current
    forcing_top = mass_rate * concentration + source
    return vcycle(0, concentration, forcing_top)
```

```python
import functools

import jax
import jax.numpy as jnp
from jax import lax
from jax.experimental import pallas as pl
from jax.experimental.pallas import tpu as pltpu
from jax.sharding import PartitionSpec as P

mass_rate = 0.001
relax_weight = 0.8
diffusivities = (0.15, 0.3, 0.5, 0.8, 1.2, 2.0, 3.2, 5.0)
RIM = 4
LANES = 128
F32 = jnp.float32
BF16 = jnp.bfloat16


def with_halo(cells, sides, width):
    for axis, dim in sides:
        count = lax.axis_size(axis)
        head = lax.slice_in_dim(cells, 0, width, axis=dim)
        tail = lax.slice_in_dim(cells, cells.shape[dim] - width, cells.shape[dim], axis=dim)
        cells = jnp.concatenate(
            [
                lax.ppermute(tail, axis, [(i, (i + 1) % count) for i in range(count)]),
                cells,
                lax.ppermute(head, axis, [((i + 1) % count, i) for i in range(count)]),
            ],
            axis=dim,
        )
    return cells


def lookup(material):
    result = jnp.zeros(material.shape, F32)
    for slot_id, coeff_value in enumerate(diffusivities):
        result = jnp.where(material == slot_id, F32(coeff_value), result)
    return result


def iota(shape, dim):
    return lax.broadcasted_iota(jnp.int32, shape, dim)


def div(a, b):
    return lax.div(a, jnp.full_like(a, b))


def mod(a, b):
    return lax.rem(a, jnp.full_like(a, b))


def ones_where(mask):
    return jnp.where(mask, F32(1.0), F32(0.0)).astype(BF16)


def three_terms(x):
    high = x.astype(BF16)
    rest = x - high.astype(F32)
    middle = rest.astype(BF16)
    low = (rest - middle.astype(F32)).astype(BF16)
    return high, middle, low


def times_right(x, selector):
    parts = [jnp.dot(part, selector, preferred_element_type=F32) for part in three_terms(x)]
    return parts[0] + (parts[1] + parts[2])


def times_left(selector, x):
    parts = [jnp.dot(selector, part, preferred_element_type=F32) for part in three_terms(x)]
    return parts[0] + (parts[1] + parts[2])


def back(v, axis):
    return pltpu.roll(v, 1, axis)


def ahead(v, axis):
    return pltpu.roll(v, v.shape[axis] - 1, axis)


def halve_lanes(fine, coarse, start=0):
    shape = (fine, coarse)
    return ones_where(div(iota(shape, 0), 2) + start == iota(shape, 1))


def plane_setup(kappa, cx, cy, cz, weight, diag, scale, first, last):
    half = 0.5 * scale
    for x in range(first - 1, last):
        cx[x] = half * (kappa[x] + kappa[x + 1])
    for x in range(first, last):
        k = kappa[x]
        y_part = half * (k + ahead(k, 0))
        z_part = half * (k + ahead(k, 1))
        cy[x] = y_part
        cz[x] = z_part
        d = mass_rate + cx[x] + cx[x - 1] + y_part + back(y_part, 0) + z_part + back(z_part, 1)
        weight[x] = relax_weight / d
        if diag is not None:
            diag[x] = d


def neighbours(v, cx, cy, cz, x):
    here = v[x]
    y_part = cy[x]
    z_part = cz[x]
    total = cx[x] * v[x + 1] + cx[x - 1] * v[x - 1]
    total = total + (y_part * ahead(here, 0) + back(y_part * here, 0))
    return total + (z_part * ahead(here, 1) + back(z_part * here, 1))


def plane_sweep(v, out, forcing, cx, cy, cz, weight, first, last):
    for x in range(first, last):
        out[x] = (1.0 - relax_weight) * v[x] + weight[x] * (forcing[x] + neighbours(v, cx, cy, cz, x))


def fine_down(window, v_out, cx, cy, cz, weight, level_one, once, diag, paired, k_one, d_one):
    planes, rows, size_z = v_out.shape
    conc, forcing, kappa = window.at[0], window.at[1], window.at[2]
    plane_setup(kappa, cx, cy, cz, weight, diag, 1.0, 1, planes - 1)
    plane_sweep(conc, once, forcing, cx, cy, cz, weight, 1, planes - 1)
    plane_sweep(once, v_out, forcing, cx, cy, cz, weight, 2, planes - 2)
    half_z = size_z // 2
    chunks = size_z // LANES
    to_half = [halve_lanes(LANES, half_z, chunk * LANES // 2) for chunk in range(chunks)]
    tile_x, tile_y = planes - 2 * RIM, rows - 2 * RIM
    half_y = tile_y // 2

    def put(pair, total):
        for chunk in range(chunks):
            paired[chunk, pair, 0:rows] = total[:, chunk * LANES : (chunk + 1) * LANES]

    def narrowed(pairs, start, count):
        result = None
        for chunk in range(chunks):
            stacked = [
                paired[chunk, pair, pl.ds(start, count, stride=2)]
                + paired[chunk, pair, pl.ds(start + 1, count, stride=2)]
                for pair in range(pairs)
            ]
            part = times_right(jnp.concatenate(stacked, 0), to_half[chunk])
            result = part if result is None else result + part
        return 0.125 * result

    for pair in range(tile_x // 2):
        total = None
        for x in (RIM + 2 * pair, RIM + 2 * pair + 1):
            part = forcing[x] + neighbours(v_out, cx, cy, cz, x) - diag[x] * v_out[x]
            total = part if total is None else total + part
        put(pair, total)
    forcing_one = narrowed(tile_x // 2, RIM, half_y)
    wide = paired.shape[2] // 2
    if 2 * wide > rows:
        for chunk in range(chunks):
            for pair in range(planes // 2):
                paired[chunk, pair, rows:] = jnp.ones((2 * wide - rows, LANES), F32)
    for pair in range(planes // 2):
        put(pair, kappa[2 * pair] + kappa[2 * pair + 1])
    coarse = narrowed(planes // 2, 0, wide)
    for pair in range(planes // 2):
        k_one[pair] = coarse[pair * wide : (pair + 1) * wide]
    rim = RIM // 2
    half = 0.5 * 0.25
    for x in range(tile_x // 2):
        k = k_one[x + rim]
        y_part = half * (k + ahead(k, 0))
        z_part = half * (k + ahead(k, 1))
        d = mass_rate + half * (k + k_one[x + rim + 1]) + half * (k + k_one[x + rim - 1])
        d = d + y_part + back(y_part, 0) + z_part + back(z_part, 1)
        d_one[x] = d
        f = forcing_one[x * half_y : (x + 1) * half_y]
        level_one[0, x] = f
        level_one[1, x] = relax_weight * f / d_one[x, pl.ds(rim, half_y)]
        level_one[2, x] = k_one[x + rim, pl.ds(rim, half_y)]


def middle_down(window, v_out, cx, cy, cz, weight, block, diag, paired):
    planes, rows, size_z = v_out.shape
    forcing, start, kappa = window.at[0], window.at[1], window.at[2]
    plane_setup(kappa, cx, cy, cz, weight, diag, 0.25, 1, planes - 1)
    plane_sweep(start, v_out, forcing, cx, cy, cz, weight, 1, planes - 1)
    half_x, half_y = (planes - 2 * RIM) // 2, (rows - 2 * RIM) // 2
    pieces = ([], [])
    for pair in range(half_x):
        total = None
        for x in (RIM + 2 * pair, RIM + 2 * pair + 1):
            part = forcing[x] + neighbours(v_out, cx, cy, cz, x) - diag[x] * v_out[x]
            total = part if total is None else total + part
        paired[0, pair] = total
        paired[1, pair] = kappa[RIM + 2 * pair] + kappa[RIM + 2 * pair + 1]
    for which in range(2):
        for pair in range(half_x):
            pieces[which].append(
                paired[which, pair, pl.ds(RIM, half_y, stride=2)]
                + paired[which, pair, pl.ds(RIM + 1, half_y, stride=2)]
            )
    half_z = size_z // 2
    forced = times_right(jnp.concatenate(pieces[0], 0), halve_lanes(size_z, 2 * half_z))
    spread = times_right(jnp.concatenate(pieces[1], 0), halve_lanes(size_z, 2 * half_z, half_z))
    block[...] = 0.125 * (forced + spread)


class Grid:
    def __init__(self, sizes, scales):
        self.sizes = sizes
        self.scales = scales
        self.rows_y = max(8, sizes[1])
        self.rows = sizes[0] * self.rows_y
        self.lanes = max(LANES, sizes[2])
        self.ratios = tuple(2 if extent % 2 == 0 else 1 for extent in sizes)
        assert self.rows_y % sizes[1] == 0 and self.lanes % sizes[2] == 0
        self.cells = sizes[0] * sizes[1] * sizes[2]
        self.exact = self.cells <= 64 or self.ratios == (1, 1, 1)

    def coarser(self):
        sizes = tuple(extent // ratio for extent, ratio in zip(self.sizes, self.ratios))
        scales = tuple(s / (ratio * ratio) for s, ratio in zip(self.scales, self.ratios))
        return Grid(sizes, scales)


def flat(v):
    return v.reshape(v.shape[0] * v.shape[1], v.shape[2])


def cube(v, grid):
    return v.reshape(grid.sizes[0], grid.rows_y, grid.lanes)


def next_plane(v):
    return v if v.shape[0] == 1 else jnp.concatenate([v[1:], v[:1]], 0)


def last_plane(v):
    return v if v.shape[0] == 1 else jnp.concatenate([v[-1:], v[:-1]], 0)


def restrict_whole(v, grid, below):
    shape = (below.rows, grid.rows)
    out_row, in_row = iota(shape, 0), iota(shape, 1)
    in_x, in_y = div(in_row, grid.rows_y), mod(in_row, grid.rows_y)
    out_x, out_y = div(out_row, below.rows_y), mod(mod(out_row, below.rows_y), below.sizes[1])
    left = ones_where(
        (div(in_x, grid.ratios[0]) == out_x)
        & (in_y < grid.sizes[1])
        & (div(in_y, grid.ratios[1]) == out_y)
    )
    shape = (grid.lanes, below.lanes)
    in_z, out_z = iota(shape, 0), mod(iota(shape, 1), below.sizes[2])
    right = ones_where((in_z < grid.sizes[2]) & (div(in_z, grid.ratios[2]) == out_z))
    count = grid.ratios[0] * grid.ratios[1] * grid.ratios[2]
    return cube((1.0 / count) * times_right(times_left(left, flat(v)), right), below)


def prolong_whole(v, below, grid):
    shape = (grid.rows, below.rows)
    out_row, in_row = iota(shape, 0), iota(shape, 1)
    out_x, out_y = div(out_row, grid.rows_y), mod(mod(out_row, grid.rows_y), grid.sizes[1])
    target = div(out_x, grid.ratios[0]) * below.rows_y + div(out_y, grid.ratios[1])
    left = ones_where(target == in_row)
    shape = (below.lanes, grid.lanes)
    right = ones_where(iota(shape, 0) == div(mod(iota(shape, 1), grid.sizes[2]), grid.ratios[2]))
    return cube(times_left(left, times_right(flat(v), right)), grid)


def whole_operator(kappa, grid):
    half_x, half_y, half_z = (0.5 * s for s in grid.scales)
    cx = half_x * (kappa + next_plane(kappa))
    cy = half_y * (kappa + ahead(kappa, 1))
    cz = half_z * (kappa + ahead(kappa, 2))
    diag = mass_rate + cx + last_plane(cx) + cy + back(cy, 1) + cz + back(cz, 2)
    return cx, cy, cz, diag, relax_weight / diag


def whole_neighbours(v, operator):
    cx, cy, cz = operator[:3]
    total = cx * next_plane(v) + last_plane(cx * v)
    total = total + (cy * ahead(v, 1) + back(cy * v, 1))
    return total + (cz * ahead(v, 2) + back(cz * v, 2))


def whole_sweep(v, forcing, operator):
    return (1.0 - relax_weight) * v + operator[4] * (forcing + whole_neighbours(v, operator))


def solve_exactly(forcing, kappa, grid):
    size_x, size_y, size_z = grid.sizes
    cells = grid.cells
    padded = -(-cells // 8) * 8
    assert cells < LANES and grid.lanes == LANES
    shape = (grid.rows, LANES)
    row, lane = iota(shape, 0), iota(shape, 1)
    owner = div(lane, size_z)
    picked = (lane < cells) & (
        div(owner, size_y) * grid.rows_y + mod(owner, size_y) == row
    )

    def as_row(v):
        return jnp.sum(jnp.where(picked, flat(v), 0.0), axis=0, keepdims=True)

    shape = (padded, LANES)
    i, j = iota(shape, 0), iota(shape, 1)
    eye = i == j

    def as_column(row_vector):
        return jnp.sum(jnp.where(eye, row_vector, 0.0), axis=1, keepdims=True)

    k_row, f_row = as_row(kappa), as_row(forcing)
    k_column, f_column = as_column(k_row), as_column(f_row)

    def places(n):
        return div(n, size_y * size_z), mod(div(n, size_z), size_y), mod(n, size_z)

    at_i, at_j = places(i), places(j)
    factor = jnp.zeros(shape, F32)
    for d in range(3):
        same = [at_i[other] == at_j[other] for other in range(3) if other != d]
        for step in (1, grid.sizes[d] - 1):
            hit = mod(at_i[d] + step, grid.sizes[d]) == at_j[d]
            factor = factor + jnp.where(hit & same[0] & same[1], F32(0.5 * grid.scales[d]), 0.0)
    inside = (i < cells) & (j < cells)
    coupled = jnp.where(inside, factor * (k_column + k_row), 0.0)
    diag = mass_rate + jnp.sum(coupled, axis=1, keepdims=True)
    matrix = jnp.where(eye, diag - coupled, -coupled)
    matrix = jnp.where(j == cells, f_column, matrix)
    for step in range(cells):
        pivot_row = matrix[step : step + 1] / matrix[step : step + 1, step : step + 1]
        column = matrix[:, step : step + 1]
        matrix = jnp.where(i == step, pivot_row, matrix - column * pivot_row)
    solved = matrix[:, cells : cells + 1]
    spread = jnp.where(mod(i, size_z) == mod(j, size_z), solved, 0.0)
    shape = (grid.rows, padded)
    row, cell = iota(shape, 0), iota(shape, 1)
    place = div(row, grid.rows_y) * size_y + mod(mod(row, grid.rows_y), size_y)
    return cube(times_left(ones_where(div(cell, size_z) == place), spread), grid)


def solve_whole(forcing, kappa, grid):
    if grid.exact:
        return solve_exactly(forcing, kappa, grid)
    operator = whole_operator(kappa, grid)
    v = operator[4] * forcing
    v = whole_sweep(v, forcing, operator)
    residual = forcing + whole_neighbours(v, operator) - operator[3] * v
    below = grid.coarser()
    correction = solve_whole(
        restrict_whole(residual, grid, below), restrict_whole(kappa, grid, below), below
    )
    v = v + prolong_whole(correction, below, grid)
    for repeat in range(2):
        v = whole_sweep(v, forcing, operator)
    return v


def coarse_up(
    sizes, gathered, window_one, v_one, cx1, cy1, cz1, w1, window, v_zero, cx, cy, cz, weight, out,
    one_a, one_b, zero_a, zero_b
):
    grid = Grid(sizes, (0.0625, 0.0625, 0.0625))
    size_z2 = sizes[2]
    both = gathered[...]
    lane = iota(both.shape, 1)
    turned = pltpu.roll(both, size_z2, 1)
    forcing = jnp.where(lane < size_z2, both, turned)
    kappa = jnp.where(lane < size_z2, turned, both)
    solved = flat(solve_whole(cube(forcing, grid), cube(kappa, grid), grid))

    planes1, rows1, size_z1 = v_one.shape
    tile_x1, tile_y1 = planes1 - 2 * RIM, rows1 - 2 * RIM
    whole_x1, whole_y1 = 2 * sizes[0], 2 * sizes[1]
    start_x = lax.axis_index("tx") * tile_x1 + (whole_x1 - RIM)
    start_y = lax.axis_index("ty") * tile_y1 + (whole_y1 - RIM)
    row = iota((planes1 * rows1, 1), 0)
    at_x = mod(div(row, rows1) + start_x, whole_x1)
    at_y = mod(mod(row, rows1) + start_y, whole_y1)
    target = div(at_x, 2) * grid.rows_y + div(at_y, 2)
    left = ones_where(iota((planes1 * rows1, grid.rows), 1) == target)
    shape = (grid.lanes, size_z1)
    right = ones_where(iota(shape, 0) == div(iota(shape, 1), 2))
    raised = times_right(times_left(left, solved), right)
    for x in range(1, planes1 - 1):
        one_a[x] = v_one[x] + raised[x * rows1 : (x + 1) * rows1]
    forcing1 = window_one.at[0]
    plane_sweep(one_a, one_b, forcing1, cx1, cy1, cz1, w1, 2, planes1 - 2)
    plane_sweep(one_b, one_a, forcing1, cx1, cy1, cz1, w1, 3, planes1 - 3)

    planes, rows, size_z = v_zero.shape
    first, last = RIM - 1, planes1 - RIM + 1
    stacked = jnp.concatenate([one_a[x] for x in range(first, last)], 0)
    count = last - first
    shape = (count * rows, count * rows1)
    out_row, in_row = iota((count * rows, 1), 0), iota(shape, 1)
    target = div(out_row, rows) * rows1 + div(mod(out_row, rows) + RIM, 2)
    left = ones_where(in_row == target)
    shape = (size_z1, size_z)
    right = ones_where(iota(shape, 0) == div(iota(shape, 1), 2))
    raised = times_right(times_left(left, stacked), right)
    for x in range(2, planes - 2):
        at = (x + RIM) // 2 - first
        zero_a[x] = v_zero[x] + raised[at * rows : (at + 1) * rows]
    forcing0 = window.at[1]
    plane_sweep(zero_a, zero_b, forcing0, cx, cy, cz, weight, 3, planes - 3)
    plane_sweep(zero_b, zero_a, forcing0, cx, cy, cz, weight, RIM, planes - RIM)
    for x in range(planes - 2 * RIM):
        out[x] = zero_a[x + RIM, pl.ds(RIM, rows - 2 * RIM)]


VM = pl.BlockSpec(memory_space=pltpu.VMEM)


def call(kernel, operands, outputs, scratch, name):
    return pl.pallas_call(
        kernel,
        in_specs=[VM] * len(operands),
        out_specs=[VM] * len(outputs),
        out_shape=[jax.ShapeDtypeStruct(shape, F32) for shape in outputs],
        scratch_shapes=[pltpu.VMEM(shape, F32) for shape in scratch],
        compiler_params=pltpu.CompilerParams(vmem_limit_bytes=48 * 1024 * 1024),
        name=name,
    )(*operands)


def shards(concentration, source, material):
    sides = (("tx", 1), ("ty", 2))
    forcing = mass_rate * concentration + source
    window = with_halo(jnp.stack([concentration, forcing, lookup(material)]), sides[::-1], RIM)
    zero = window.shape[1:]
    tile_x, tile_y, size_z = concentration.shape
    one_tile = (tile_x // 2, tile_y // 2, size_z // 2)
    wide = -(-zero[1] // 16) * 16
    v_zero, cx, cy, cz, weight, level_one = call(
        fine_down,
        (window,),
        (zero,) * 5 + ((3,) + one_tile,),
        (
            zero,
            zero,
            (size_z // LANES, zero[0] // 2, wide, LANES),
            (zero[0] // 2, wide // 2, size_z // 2),
            (zero[0] // 2, wide // 2, size_z // 2),
        ),
        "fine_down",
    )
    window_one = with_halo(level_one, sides[::-1], RIM)
    one = window_one.shape[1:]
    rows_two = one_tile[0] * one_tile[1] // 4
    v_one, cx1, cy1, cz1, w1, block = call(
        middle_down,
        (window_one,),
        (one,) * 5 + ((rows_two, one_tile[2]),),
        (one, (2, one_tile[0] // 2) + one[1:]),
        "middle_down",
    )
    count_x, count_y = lax.axis_size("tx"), lax.axis_size("ty")
    everyone = count_x * count_y
    blocks = jnp.broadcast_to(block[None], (everyone,) + block.shape)
    blocks = lax.all_to_all(blocks, ("tx", "ty"), 0, 0)
    half_x, half_y = one_tile[0] // 2, one_tile[1] // 2
    gathered = blocks.reshape(count_x, count_y, half_x, half_y, one_tile[2])
    gathered = gathered.transpose(0, 2, 1, 3, 4).reshape(-1, one_tile[2])
    sizes = (count_x * half_x, count_y * half_y, size_z // 4)
    (updated,) = call(
        functools.partial(coarse_up, sizes),
        (gathered, window_one, v_one, cx1, cy1, cz1, w1, window, v_zero, cx, cy, cz, weight),
        (concentration.shape,),
        (one, one, zero, zero),
        "coarse_up",
    )
    return updated


def solution(mesh):
    placed = (P("tx", "ty", None), P("tx", "ty", None), P("tx", "ty", None))
    return jax.shard_map(
        shards, mesh=mesh, in_specs=placed, out_specs=P("tx", "ty", None), check_vma=False
    )
```

```python
import functools

import jax
import jax.numpy as jnp
from jax import lax
from jax.experimental import pallas as pl
from jax.experimental.pallas import tpu as pltpu
from jax.sharding import PartitionSpec as P

mass_rate = 0.001
relax_weight = 0.8
diffusivities = (0.15, 0.3, 0.5, 0.8, 1.2, 2.0, 3.2, 5.0)
LANES = 128
ROWS = 8
RX = 3
RY = 4
R1 = 4
RC = 2
F32 = jnp.float32
BF16 = jnp.bfloat16


def lookup(material):
    result = jnp.zeros(material.shape, F32)
    for slot_id, coeff_value in enumerate(diffusivities):
        result = jnp.where(material == slot_id, F32(coeff_value), result)
    return result


class Planes:
    def __init__(self, first, planes):
        self.first = first
        self.planes = planes

    def __getitem__(self, x):
        ref, index = self.planes[x - self.first]
        return ref[index]


def iota(shape, dim):
    return lax.broadcasted_iota(jnp.int32, shape, dim)


def div(a, b):
    return lax.div(a, jnp.full_like(a, b))


def mod(a, b):
    return lax.rem(a, jnp.full_like(a, b))


def ones_where(mask):
    return jnp.where(mask, F32(1.0), F32(0.0)).astype(BF16)


def three_terms(x):
    high = x.astype(BF16)
    rest = x - high.astype(F32)
    middle = rest.astype(BF16)
    low = (rest - middle.astype(F32)).astype(BF16)
    return high, middle, low


def times_right(x, selector):
    parts = [jnp.dot(part, selector, preferred_element_type=F32) for part in three_terms(x)]
    return parts[0] + (parts[1] + parts[2])


def times_left(selector, x):
    parts = [jnp.dot(selector, part, preferred_element_type=F32) for part in three_terms(x)]
    return parts[0] + (parts[1] + parts[2])


def back(v, axis, step=1):
    return pltpu.roll(v, step, axis)


def ahead(v, axis, step=1):
    return pltpu.roll(v, v.shape[axis] - step, axis)


def halve_lanes(fine, coarse, start=0):
    shape = (fine, coarse)
    return ones_where(div(iota(shape, 0), 2) + start == iota(shape, 1))


def plane_setup(kappa, cx, cy, cz, weight, diag, scale, first, last):
    half = 0.5 * scale
    for x in range(first - 1, last):
        cx[x] = half * (kappa[x] + kappa[x + 1])
    for x in range(first, last):
        k = kappa[x]
        y_part = half * (k + ahead(k, 0))
        z_part = half * (k + ahead(k, 1))
        cy[x] = y_part
        cz[x] = z_part
        d = mass_rate + cx[x] + cx[x - 1] + y_part + back(y_part, 0) + z_part + back(z_part, 1)
        weight[x] = relax_weight / d
        if diag is not None:
            diag[x] = d


def in_plane(here, cy, cz, x):
    y_part = cy[x]
    z_part = cz[x]
    total = y_part * ahead(here, 0) + back(y_part * here, 0)
    return total + (z_part * ahead(here, 1) + back(z_part * here, 1))


def neighbours(v, cx, cy, cz, x):
    return (cx[x] * v[x + 1] + cx[x - 1] * v[x - 1]) + in_plane(v[x], cy, cz, x)


def plane_sweep(v, out, forcing, cx, cy, cz, weight, first, last):
    for x in range(first, last):
        out[x] = (1.0 - relax_weight) * v[x] + weight[x] * (forcing[x] + neighbours(v, cx, cy, cz, x))


def edges(conc, source, material, to_low, to_high):
    tile_x, tile_y, size_z = conc.shape
    for to, low in ((to_low, True), (to_high, False)):
        for x in range(tile_x):
            rows = slice(0, 4) if low else slice(tile_y - 4, tile_y)
            near = slice(0, 3) if low else slice(1, 4)
            pair = slice(0, 2) if low else slice(2, 4)
            c = conc[x, rows]
            f = mass_rate * c + source[x, rows]
            k = lookup(material[x, rows])
            to[x, 0:3] = c[near]
            to[x, 3:5] = f[pair]
            to[x, 5:8] = k[near]
            to[tile_x, x : x + 1] = k[3:4] if low else k[0:1]


def sides(conc, source, material, from_low, from_high, window, to_low, to_high):
    tile_x, tile_y, size_z = conc.shape
    top = RY + tile_y
    for x in range(tile_x):
        c = conc[x]
        window[0, x, RY:top] = c
        window[1, x, RY:top] = mass_rate * c + source[x]
        window[2, x, RY:top] = lookup(material[x])
        window[0, x, 0:1] = jnp.zeros((1, size_z), F32)
        window[0, x, 1:4] = from_low[x, 0:3]
        window[0, x, top : top + 3] = from_high[x, 0:3]
        window[0, x, top + 3 :] = jnp.zeros((1, size_z), F32)
        window[1, x, 0:2] = jnp.zeros((2, size_z), F32)
        window[1, x, 2:4] = from_low[x, 3:5]
        window[1, x, top : top + 2] = from_high[x, 3:5]
        window[1, x, top + 2 :] = jnp.zeros((2, size_z), F32)
        window[2, x, 0:1] = from_low[tile_x, x : x + 1]
        window[2, x, 1:4] = from_low[x, 5:8]
        window[2, x, top : top + 3] = from_high[x, 5:8]
        window[2, x, top + 3 :] = from_high[tile_x, x : x + 1]
    for to, plane in ((to_low, lambda l: l - 1), (to_high, lambda l: tile_x - l)):
        for at, (which, layer) in enumerate(BASE_PLANES):
            to[at] = window[which, plane(layer), RY:top]
        at = 0
        for which, layer, reach in EXTRA_ROWS:
            to[len(BASE_PLANES), at : at + reach] = window[which, plane(layer), RY - reach : RY]
            at += reach
            to[len(BASE_PLANES), at : at + reach] = window[which, plane(layer), top : top + reach]
            at += reach


BASE_PLANES = (
    (0, 1), (0, 2), (0, 3), (1, 1), (1, 2), (2, 1), (2, 2), (2, 3), (2, 4),
)
EXTRA_ROWS = ((0, 1, 2), (0, 2, 1), (1, 1, 1), (2, 1, 2), (2, 2, 2))


def fine_down(
    window, from_low, from_high,
    v_out, forcing_out, cx, cy, cz, weight, level_one, block, to_low, to_high,
    conc_rim, forcing_rim, kappa_rim, once, diag, paired,
    k_one, f_one, u_one, v_one, cx1, cy1, cz1, w1, d1, paired_one, packed,
):
    _, tile_x, rows, size_z = window.shape
    tile_y = rows - 2 * RY
    top = RY + tile_y
    planes = tile_x + 2 * RX
    rims = (conc_rim, forcing_rim, kappa_rim)
    depths = (3, 2, 4)
    for which, rim in enumerate(rims):
        fill = jnp.full((rows, size_z), 1.0 if which == 2 else 0.0, F32)
        for x in range(2 * depths[which]):
            rim[x] = fill

    def place(which, layer, low):
        return depths[which] - layer if low else depths[which] + layer - 1

    for message, low in ((from_low, True), (from_high, False)):
        for at, (which, layer) in enumerate(BASE_PLANES):
            rims[which][place(which, layer, low), RY:top] = message[at]
        at = 0
        for which, layer, reach in EXTRA_ROWS:
            rim, x = rims[which], place(which, layer, low)
            rim[x, RY - reach : RY] = message[len(BASE_PLANES), at : at + reach]
            at += reach
            rim[x, top : top + reach] = message[len(BASE_PLANES), at : at + reach]
            at += reach

    def stacked(which):
        depth = depths[which]
        whole = [(rims[which], x) for x in range(depth)]
        whole += [(window.at[which], x) for x in range(tile_x)]
        whole += [(rims[which], depth + x) for x in range(depth)]
        return Planes(RX - depth, whole)

    conc, forcing, kappa = stacked(0), stacked(1), stacked(2)
    plane_setup(kappa, cx, cy, cz, weight, diag, 1.0, 1, planes - 1)
    plane_sweep(conc, once, forcing, cx, cy, cz, weight, 1, planes - 1)
    plane_sweep(once, v_out, forcing, cx, cy, cz, weight, 2, planes - 2)
    for x in range(RX - 1, planes - RX + 1):
        forcing_out[x] = forcing[x]
    chunks = size_z // LANES
    size_z1 = size_z // 2
    to_half = [halve_lanes(LANES, size_z1, chunk * LANES // 2) for chunk in range(chunks)]
    tile_x1, tile_y1 = tile_x // 2, tile_y // 2

    def put(pair, total):
        for chunk in range(chunks):
            paired[chunk, pair, 0:rows] = total[:, chunk * LANES : (chunk + 1) * LANES]

    def narrowed(pairs, start, count):
        result = None
        for chunk in range(chunks):
            stack = [
                paired[chunk, pair, pl.ds(start, count, stride=2)]
                + paired[chunk, pair, pl.ds(start + 1, count, stride=2)]
                for pair in range(pairs)
            ]
            part = times_right(jnp.concatenate(stack, 0), to_half[chunk])
            result = part if result is None else result + part
        return 0.125 * result

    wide = paired.shape[2] // 2
    planes1 = tile_x1 + 2 * RC
    if 2 * wide > rows:
        for chunk in range(chunks):
            for pair in range(planes1):
                paired[chunk, pair, rows:] = jnp.ones((2 * wide - rows, LANES), F32)
    for pair in range(planes1):
        x = RX - 2 * RC + 2 * pair
        put(pair, kappa[x] + kappa[x + 1])
    coarse = narrowed(planes1, 0, wide)
    for pair in range(planes1):
        k_one[pair] = coarse[pair * wide : (pair + 1) * wide]
    plane_setup(k_one, cx1, cy1, cz1, w1, d1, 0.25, 1, planes1 - 1)

    for pair in range(tile_x1):
        total = None
        for x in (RX + 2 * pair, RX + 2 * pair + 1):
            part = forcing[x] + neighbours(v_out, cx, cy, cz, x) - diag[x] * v_out[x]
            total = part if total is None else total + part
        put(pair, total)
    forcing_one = narrowed(tile_x1, RY, tile_y1)

    low, high = RC, RC + tile_y1
    nothing = jnp.zeros((wide, size_z1), F32)
    for x in range(planes1):
        f_one[x] = nothing
        if x in (0, planes1 - 1):
            v_one[x] = nothing
    for x in (0, 1, planes1 - 2, planes1 - 1):
        u_one[x] = nothing
    for x in range(tile_x1):
        f = forcing_one[x * tile_y1 : (x + 1) * tile_y1]
        f_one[x + RC, low:high] = f
        u_one[x + RC] = w1[x + RC] * f_one[x + RC]
        level_one[0, x] = f
        level_one[1, x] = u_one[x + RC, low:high]
        level_one[2, x] = k_one[x + RC, low:high]
    plane_sweep(u_one, v_one, f_one, cx1, cy1, cz1, w1, 1, planes1 - 1)
    half_x, half_y = tile_x1 // 2, tile_y1 // 2
    pairs1 = planes1 // 2
    for pair in range(pairs1):
        total = None
        for x in (2 * pair, 2 * pair + 1):
            if x == 0:
                part = cx1[0] * v_one[1]
            elif x == planes1 - 1:
                part = cx1[x - 1] * v_one[x - 1]
            else:
                part = f_one[x] + neighbours(v_one, cx1, cy1, cz1, x) - d1[x] * v_one[x]
            total = part if total is None else total + part
        paired_one[pair] = total
    for pair in range(half_x):
        x = RC + 2 * pair
        paired_one[pairs1 + pair] = k_one[x] + k_one[x + 1]
    used = half_y + RC
    spare = ROWS - used
    for pair in range(pairs1):
        packed[pair] = (
            paired_one[pair, pl.ds(0, ROWS, stride=2)] + paired_one[pair, pl.ds(1, ROWS, stride=2)]
        )
    per_plane = half_y // spare
    for pair in range(half_x):
        spread = (
            paired_one[pairs1 + pair, pl.ds(RC, half_y, stride=2)]
            + paired_one[pairs1 + pair, pl.ds(RC + 1, half_y, stride=2)]
        )
        for share in range(per_plane):
            packed[pair * per_plane + share, used:] = spread[share * spare : (share + 1) * spare]
    half_pairs = pairs1 // 2
    result = times_right(
        jnp.concatenate([packed[p] for p in range(half_pairs)], 0), halve_lanes(size_z1, size_z1)
    ) + times_right(
        jnp.concatenate([packed[half_pairs + p] for p in range(half_pairs)], 0),
        halve_lanes(size_z1, size_z1, size_z1 // 2),
    )
    for p in range(half_pairs):
        block[p] = 0.125 * result[p * ROWS : (p + 1) * ROWS]

    for to, rows1, row0 in (
        (to_low, slice(0, R1), RY + 1),
        (to_high, slice(tile_y1 - R1, tile_y1), top - 2),
    ):
        for which in range(3):
            for x in range(tile_x1):
                flat_row = which * tile_x1 * R1 + x * R1
                to[flat_row // ROWS, flat_row % ROWS : flat_row % ROWS + R1] = level_one[
                    which, x, rows1
                ]
        start = 3 * tile_x1 * R1 // ROWS
        for x in range(tile_x):
            row = v_out[RX + x, row0 : row0 + 1]
            for chunk in range(chunks):
                to[start + chunk, x : x + 1] = row[:, chunk * LANES : (chunk + 1) * LANES]


def middle(level_one, v_zero, block, from_low, from_high, window, to_low, to_high, blocks):
    _, tile_x1, tile_y1, size_z1 = level_one.shape
    planes, rows, size_z = v_zero.shape
    top1 = R1 + tile_y1
    for which in range(3):
        for x in range(tile_x1):
            flat_row = which * tile_x1 * R1 + x * R1
            at, sub = flat_row // ROWS, flat_row % ROWS
            window[which, x, R1:top1] = level_one[which, x]
            window[which, x, 0:R1] = from_low[at, sub : sub + R1]
            window[which, x, top1:] = from_high[at, sub : sub + R1]
            to_low[which * tile_x1 + x] = window[which, x]
            to_high[which * tile_x1 + x] = window[which, x]
    chunks = size_z // LANES
    top = rows - RY
    for to, second, first in ((to_low, RX + 1, RX), (to_high, planes - RX - 2, planes - RX - 1)):
        at = 3 * tile_x1
        corner = [v_zero[first, RY - 1 : RY], v_zero[first, top : top + 1]]
        for chunk in range(chunks):
            lanes = slice(chunk * LANES, (chunk + 1) * LANES)
            to[at + chunk] = v_zero[second, RY:top, lanes]
        to[at + chunks] = jnp.zeros(to.shape[1:], F32)
        for chunk in range(chunks):
            lanes = slice(chunk * LANES, (chunk + 1) * LANES)
            for n in range(2):
                to[at + chunks, 2 * chunk + n : 2 * chunk + n + 1] = corner[n][:, lanes]
    for device in range(blocks.shape[0]):
        blocks[device] = block[...]


class Grid:
    def __init__(self, sizes, strides, scales, rows, lanes):
        self.sizes = sizes
        self.strides = strides
        self.scales = scales
        self.rows = rows
        self.lanes = lanes
        self.ratios = tuple(2 if extent % 2 == 0 else 1 for extent in sizes)
        self.cells = sizes[0] * sizes[1] * sizes[2]
        self.exact = self.cells <= 64 or self.ratios == (1, 1, 1)

    def coarser(self):
        sizes = tuple(extent // ratio for extent, ratio in zip(self.sizes, self.ratios))
        scales = tuple(s / (ratio * ratio) for s, ratio in zip(self.scales, self.ratios))
        strides = tuple(s * ratio for s, ratio in zip(self.strides, self.ratios[1:]))
        return Grid(sizes, strides, scales, self.rows, self.lanes)


def next_plane(v):
    return v if v.shape[0] == 1 else jnp.concatenate([v[1:], v[:1]], 0)


def last_plane(v):
    return v if v.shape[0] == 1 else jnp.concatenate([v[-1:], v[:-1]], 0)


def restrict_whole(v, grid):
    if grid.ratios[0] == 2:
        v = jnp.concatenate(
            [v[2 * x : 2 * x + 1] + v[2 * x + 1 : 2 * x + 2] for x in range(grid.sizes[0] // 2)], 0
        )
    for axis in (1, 2):
        if grid.ratios[axis] == 2:
            step = grid.strides[axis - 1]
            even = mod(div(iota(v.shape, axis), step), 2) == 0
            v = v + jnp.where(even, ahead(v, axis, step), back(v, axis, step))
    return (1.0 / (grid.ratios[0] * grid.ratios[1] * grid.ratios[2])) * v


def prolong_whole(v, grid):
    if grid.ratios[0] == 1:
        return v
    return jnp.concatenate([v[x // 2 : x // 2 + 1] for x in range(grid.sizes[0])], 0)


def whole_operator(kappa, grid):
    half_x, half_y, half_z = (0.5 * s for s in grid.scales)
    step_y, step_z = grid.strides
    cx = half_x * (kappa + next_plane(kappa))
    cy = half_y * (kappa + ahead(kappa, 1, step_y))
    cz = half_z * (kappa + ahead(kappa, 2, step_z))
    diag = mass_rate + cx + last_plane(cx)
    diag = diag + (cy + back(cy, 1, step_y)) + (cz + back(cz, 2, step_z))
    return cx, cy, cz, diag, relax_weight / diag


def whole_neighbours(v, operator, grid):
    cx, cy, cz = operator[:3]
    step_y, step_z = grid.strides
    total = cx * next_plane(v) + last_plane(cx * v)
    total = total + (cy * ahead(v, 1, step_y) + back(cy * v, 1, step_y))
    return total + (cz * ahead(v, 2, step_z) + back(cz * v, 2, step_z))


def whole_sweep(v, forcing, operator, grid):
    return (1.0 - relax_weight) * v + operator[4] * (forcing + whole_neighbours(v, operator, grid))


class ExactSolve:
    def __init__(self, kappa, grid):
        size_x, size_y, size_z = grid.sizes
        self.grid = grid
        self.across = across = size_x * size_y
        step_y, step_z = grid.strides
        self.period = period = size_z * step_z
        cells = grid.cells
        padded = -(-cells // ROWS) * ROWS
        assert across <= step_z and 2 * period <= grid.lanes
        shape = (padded, grid.lanes)
        i, j = iota(shape, 0), iota(shape, 1)
        self.i, self.j = i, j

        def places_of_row(n):
            return div(mod(n, across), size_y), mod(n, size_y), div(n, across)

        def places_of_lane(n):
            n = mod(n, period)
            sub = mod(n, step_z)
            return div(sub, size_y), mod(sub, size_y), div(n, step_z)

        at_i, at_j = places_of_row(i), places_of_lane(j)
        at_i = (at_i[0], mod(mod(i, across), size_y), at_i[2])
        live = (mod(j, step_z) < across) & (i < cells)
        same = (at_i[0] == at_j[0]) & (at_i[1] == at_j[1]) & (at_i[2] == at_j[2]) & live
        left = j < period
        factor = jnp.zeros(shape, F32)
        for d in range(3):
            equal = [at_i[other] == at_j[other] for other in range(3) if other != d]
            for step in (1, grid.sizes[d] - 1):
                hit = mod(at_i[d] + step, grid.sizes[d]) == at_j[d]
                factor = factor + jnp.where(
                    hit & equal[0] & equal[1], F32(0.5 * grid.scales[d]), F32(0.0)
                )
        k_row = self.as_row(kappa)
        k_column = jnp.sum(jnp.where(same & left, k_row, 0.0), axis=1, keepdims=True)
        coupled = jnp.where(live & left, factor * (k_column + k_row), 0.0)
        diag = mass_rate + jnp.sum(coupled, axis=1, keepdims=True)
        matrix = jnp.where(same & left, diag - coupled, -coupled)
        matrix = jnp.where(left, matrix, jnp.where(same, F32(1.0), F32(0.0)))
        for n in range(cells):
            lane = (n // across) * step_z + n % across
            pivot_row = matrix[n : n + 1] / matrix[n : n + 1, lane : lane + 1]
            column = matrix[:, lane : lane + 1]
            matrix = jnp.where(i == n, pivot_row, matrix - column * pivot_row)
        self.inverse = jnp.where((j >= period) & (j < 2 * period) & live, matrix, 0.0)

    def as_row(self, v):
        grid = self.grid
        size_x, size_y, _ = grid.sizes
        step_y, step_z = grid.strides
        sub = mod(iota((1, grid.lanes), 1), step_z)
        result = jnp.zeros((1, grid.lanes), F32)
        for x in range(size_x):
            for y in range(size_y):
                row = v[x, y * step_y : y * step_y + 1]
                result = jnp.where(sub == x * size_y + y, row, result)
        return result

    def solve(self, forcing):
        grid = self.grid
        size_x, size_y, size_z = grid.sizes
        step_y, step_z = grid.strides
        solved = jnp.sum(self.inverse * self.as_row(forcing), axis=1, keepdims=True)
        at_z = div(mod(self.j, self.period), step_z)
        spread = jnp.where(div(self.i, self.across) == at_z, solved, 0.0)
        planes = []
        for x in range(size_x):
            rows = []
            for y in range(size_y):
                mine = mod(self.i, self.across) == x * size_y + y
                row = jnp.sum(jnp.where(mine, spread, 0.0), axis=0, keepdims=True)
                rows.append(jnp.broadcast_to(row, (step_y, grid.lanes)))
            planes.append(jnp.concatenate(rows, 0)[None])
        return jnp.concatenate(planes, 0)


def prepare_whole(kappa, grid):
    levels = []
    while not grid.exact:
        levels.append((grid, whole_operator(kappa, grid)))
        kappa = restrict_whole(kappa, grid)
        grid = grid.coarser()
    return levels, ExactSolve(kappa, grid)


def solve_whole(forcing, levels, exact):
    if not levels:
        return exact.solve(forcing)
    grid, operator = levels[0]
    v = operator[4] * forcing
    v = whole_sweep(v, forcing, operator, grid)
    residual = forcing + whole_neighbours(v, operator, grid) - operator[3] * v
    v = v + prolong_whole(solve_whole(restrict_whole(residual, grid), levels[1:], exact), grid)
    for repeat in range(2):
        v = whole_sweep(v, forcing, operator, grid)
    return v


def assemble(blocks, count_x, count_y, half_x, half_y, size_z2):
    rows = count_y * half_y
    groups = rows // ROWS
    planes = count_x * half_x
    assert rows % ROWS == 0
    used = half_y + RC
    spare = ROWS - used
    per_plane = half_y // spare
    sub = iota((ROWS, LANES), 0)
    lane = iota((ROWS, LANES), 1)
    nothing = jnp.zeros((ROWS, LANES), F32)
    forcing = [[nothing] * groups for x in range(planes)]
    kappa = [[nothing] * groups for x in range(planes)]
    half_pairs = blocks.shape[1]
    ring = RC // 2
    for tx in range(count_x):
        for ty in range(count_y):
            for p in range(2 * half_pairs):
                piece = blocks[tx * count_y + ty, p % half_pairs]
                turned = pltpu.roll(piece, size_z2, 1)
                piece = jnp.where((lane < size_z2) == (p < half_pairs), piece, turned)
                x = (tx * half_x - ring + p) % planes
                start = (ty * half_y - ring) % rows
                moved = pltpu.roll(piece, start % ROWS, 0) if start % ROWS else piece
                group, offset = start // ROWS, start % ROWS
                mine = (sub >= offset) & (sub < offset + used)
                forcing[x][group] = forcing[x][group] + jnp.where(mine, moved, 0.0)
                if offset + used > ROWS:
                    group = (group + 1) % groups
                    mine = sub < offset + used - ROWS
                    forcing[x][group] = forcing[x][group] + jnp.where(mine, moved, 0.0)
                if p // per_plane < half_x:
                    x = tx * half_x + p // per_plane
                    start = ty * half_y + (p % per_plane) * spare
                    shift = (start - used) % ROWS
                    moved = pltpu.roll(piece, shift, 0) if shift else piece
                    group, offset = start // ROWS, start % ROWS
                    mine = (sub >= offset) & (sub < offset + spare)
                    kappa[x][group] = jnp.where(mine, moved, kappa[x][group])

    def joined(parts):
        return jnp.concatenate([jnp.concatenate(groups, 0)[None] for groups in parts], 0)

    return joined(forcing), joined(kappa)


def coarse_up(
    counts, blocks, window_one, one_low, one_high, row_low, row_high,
    v_zero, forcing0, cx, cy, cz, weight, out,
    rim_one, v_one, cx1, cy1, cz1, w1, one_a, one_b, zero_a, zero_b,
):
    count_x, count_y = counts
    _, tile_x1, rows1, size_z1 = window_one.shape
    tile_y1 = rows1 - 2 * R1
    half_x, half_y, size_z2 = tile_x1 // 2, tile_y1 // 2, size_z1 // 2
    sizes = (count_x * half_x, count_y * half_y, size_z2)
    forcing2, kappa2 = assemble(blocks, count_x, count_y, half_x, half_y, size_z2)
    grid = Grid(sizes, (1, 1), (0.0625, 0.0625, 0.0625), sizes[1], LANES)
    levels, exact = prepare_whole(kappa2, grid)

    planes1 = tile_x1 + 2 * R1

    def stacked(which):
        whole = [(one_low, which * tile_x1 + x) for x in range(tile_x1)]
        whole += [(window_one.at[which], x) for x in range(tile_x1)]
        whole += [(one_high, which * tile_x1 + x) for x in range(tile_x1)]
        return Planes(R1 - tile_x1, whole)

    assert tile_x1 >= R1
    forcing1, start1, kappa1 = stacked(0), stacked(1), stacked(2)
    plane_setup(kappa1, cx1, cy1, cz1, w1, None, 0.25, 1, planes1 - 1)
    plane_sweep(start1, v_one, forcing1, cx1, cy1, cz1, w1, 1, planes1 - 1)

    solved = solve_whole(forcing2, levels, exact)
    solved = solved.reshape(sizes[0] * sizes[1], LANES)

    whole_x1, whole_y1 = 2 * sizes[0], 2 * sizes[1]
    start_x = lax.axis_index("tx") * tile_x1 + (whole_x1 - R1)
    start_y = lax.axis_index("ty") * tile_y1 + (whole_y1 - R1)
    row = iota((planes1 * rows1, 1), 0)
    at_x = mod(div(row, rows1) + start_x, whole_x1)
    at_y = mod(mod(row, rows1) + start_y, whole_y1)
    target = div(at_x, 2) * sizes[1] + div(at_y, 2)
    left = ones_where(iota((planes1 * rows1, sizes[0] * sizes[1]), 1) == target)
    shape = (LANES, size_z1)
    right = ones_where(iota(shape, 0) == div(iota(shape, 1), 2))
    raised = times_right(times_left(left, solved), right)
    for x in range(1, planes1 - 1):
        one_a[x] = v_one[x] + raised[x * rows1 : (x + 1) * rows1]
    plane_sweep(one_a, one_b, forcing1, cx1, cy1, cz1, w1, 2, planes1 - 2)
    plane_sweep(one_b, one_a, forcing1, cx1, cy1, cz1, w1, 3, planes1 - 3)

    planes, rows, size_z = v_zero.shape
    first, last = R1 - 1, planes1 - R1 + 1
    stack = jnp.concatenate([one_a[x] for x in range(first, last)], 0)
    count = last - first
    shape = (count * rows, count * rows1)
    out_row, in_row = iota((count * rows, 1), 0), iota(shape, 1)
    target = div(out_row, rows) * rows1 + div(mod(out_row, rows) + (2 * R1 - RY), 2)
    left = ones_where(in_row == target)
    shape = (size_z1, size_z)
    right = ones_where(iota(shape, 0) == div(iota(shape, 1), 2))
    raised = times_right(times_left(left, stack), right)
    chunks = size_z // LANES
    top = rows - RY
    for x in range(RX - 1, planes - RX + 1):
        zero_b[x] = v_zero[x]
    for rim_x in (RX - 2, planes - RX + 1):
        zero_b[rim_x] = jnp.zeros((rows, size_z), F32)
    for x in range(planes - 2 * RX):
        at = 3 * tile_x1 * R1 // ROWS
        for chunk in range(chunks):
            lanes = slice(chunk * LANES, (chunk + 1) * LANES)
            zero_b[RX + x, RY - 2 : RY - 1, lanes] = row_low[at + chunk, x : x + 1]
            zero_b[RX + x, top + 1 : top + 2, lanes] = row_high[at + chunk, x : x + 1]
    for message, second, nearest in (
        (one_low, RX - 2, RX - 1), (one_high, planes - RX + 1, planes - RX)
    ):
        at = 3 * tile_x1
        for chunk in range(chunks):
            lanes = slice(chunk * LANES, (chunk + 1) * LANES)
            zero_b[second, RY:top, lanes] = message[at + chunk]
            for n, r in enumerate((RY - 1, top)):
                zero_b[nearest, r : r + 1, lanes] = message[
                    at + chunks, 2 * chunk + n : 2 * chunk + n + 1
                ]
    for x in range(RX - 2, planes - RX + 2):
        at = (x - RX + 2 * R1) // 2 - first
        zero_a[x] = zero_b[x] + raised[at * rows : (at + 1) * rows]
    plane_sweep(zero_a, zero_b, forcing0, cx, cy, cz, weight, RX - 1, planes - RX + 1)
    plane_sweep(zero_b, zero_a, forcing0, cx, cy, cz, weight, RX, planes - RX)
    for x in range(planes - 2 * RX):
        out[x] = zero_a[x + RX, RY:top]


VM = pl.BlockSpec(memory_space=pltpu.VMEM)


def call(kernel, operands, outputs, scratch, name):
    return pl.pallas_call(
        kernel,
        in_specs=[VM] * len(operands),
        out_specs=[VM] * len(outputs),
        out_shape=[jax.ShapeDtypeStruct(shape, F32) for shape in outputs],
        scratch_shapes=[pltpu.VMEM(shape, F32) for shape in scratch],
        compiler_params=pltpu.CompilerParams(vmem_limit_bytes=48 * 1024 * 1024),
        name=name,
    )(*operands)


def exchange(to_low, to_high, axis):
    count = lax.axis_size(axis)
    from_low = lax.ppermute(to_high, axis, [(i, (i + 1) % count) for i in range(count)])
    from_high = lax.ppermute(to_low, axis, [((i + 1) % count, i) for i in range(count)])
    return from_low, from_high


def shards(concentration, source, material):
    inputs = (concentration, source, material)
    tile_x, tile_y, size_z = concentration.shape
    chunks = size_z // LANES
    count_x, count_y = lax.axis_size("tx"), lax.axis_size("ty")
    rows = tile_y + 2 * RY
    message = (tile_x + 1, ROWS, size_z)
    to_low, to_high = call(edges, inputs, (message, message), (), "edges")
    from_low, from_high = exchange(to_low, to_high, "ty")
    message = (len(BASE_PLANES) + 1, tile_y, size_z)
    window, to_low, to_high = call(
        sides,
        inputs + (from_low, from_high),
        ((3, tile_x, rows, size_z), message, message),
        (),
        "sides",
    )
    from_low, from_high = exchange(to_low, to_high, "tx")

    zero = (tile_x + 2 * RX, rows, size_z)
    one_tile = (tile_x // 2, tile_y // 2, size_z // 2)
    wide = -(-rows // (2 * ROWS)) * ROWS
    small = (one_tile[0] + 2 * RC, wide, one_tile[2])
    pairs1 = small[0] // 2
    block_shape = (pairs1 // 2, ROWS, LANES)
    message = (3 * one_tile[0] * R1 // ROWS + chunks, ROWS, LANES)
    assert one_tile[2] == LANES and tile_x <= ROWS and one_tile[1] // 2 + RC < ROWS
    v_zero, forcing0, cx, cy, cz, weight, level_one, block, to_low, to_high = call(
        fine_down,
        (window, from_low, from_high),
        (zero,) * 6 + ((3,) + one_tile, block_shape, message, message),
        (
            (6, rows, size_z),
            (4, rows, size_z),
            (8, rows, size_z),
            zero,
            zero,
            (chunks, max(small[0], tile_x), 2 * wide, LANES),
        )
        + (small,) * 9
        + ((pairs1 + one_tile[0] // 2, wide, one_tile[2]), (pairs1, ROWS, one_tile[2])),
        "fine_down",
    )
    row_low, row_high = exchange(to_low, to_high, "ty")
    rows1 = one_tile[1] + 2 * R1
    message = (3 * one_tile[0] + chunks + 1, rows1, LANES)
    everyone = count_x * count_y
    window_one, to_low, to_high, blocks = call(
        middle,
        (level_one, v_zero, block, row_low, row_high),
        ((3, one_tile[0], rows1, one_tile[2]), message, message, (everyone,) + block_shape),
        (),
        "middle",
    )
    one_low, one_high = exchange(to_low, to_high, "tx")
    blocks = lax.all_to_all(blocks, ("tx", "ty"), 0, 0)
    one = (one_tile[0] + 2 * R1, rows1, one_tile[2])
    (updated,) = call(
        functools.partial(coarse_up, (count_x, count_y)),
        (blocks, window_one, one_low, one_high, row_low, row_high)
        + (v_zero, forcing0, cx, cy, cz, weight),
        (concentration.shape,),
        (one,) * 8 + (zero, zero),
        "coarse_up",
    )
    return updated


def solution(mesh):
    placed = (P("tx", "ty", None), P("tx", "ty", None), P("tx", "ty", None))
    return jax.shard_map(
        shards, mesh=mesh, in_specs=placed, out_specs=P("tx", "ty", None), check_vma=False
    )
```

```python
import functools

import jax
import jax.numpy as jnp
from jax import lax
from jax.experimental import pallas as pl
from jax.experimental.pallas import tpu as pltpu
from jax.sharding import PartitionSpec as P


mass_rate = 0.001
relax_weight = 0.8
diffusivities = (0.15, 0.3, 0.5, 0.8, 1.2, 2.0, 3.2, 5.0)
LANES = 128
ROWS = 8
RX = 3
RY = 4
R1 = 4
RC = 2
F32 = jnp.float32
BF16 = jnp.bfloat16


def lookup(material):
    result = jnp.zeros(material.shape, F32)
    for slot_id, coeff_value in enumerate(diffusivities):
        result = jnp.where(material == slot_id, F32(coeff_value), result)
    return result


class Planes:
    def __init__(self, first, planes):
        self.first = first
        self.planes = planes

    def __getitem__(self, x):
        ref, index = self.planes[x - self.first]
        return ref[index]


def iota(shape, dim):
    return lax.broadcasted_iota(jnp.int32, shape, dim)


def div(a, b):
    return lax.div(a, jnp.full_like(a, b))


def mod(a, b):
    return lax.rem(a, jnp.full_like(a, b))


def ones_where(mask):
    return jnp.where(mask, F32(1.0), F32(0.0)).astype(BF16)


def three_terms(x):
    high = x.astype(BF16)
    rest = x - high.astype(F32)
    middle = rest.astype(BF16)
    low = (rest - middle.astype(F32)).astype(BF16)
    return high, middle, low


def times_right(x, selector):
    parts = [jnp.dot(part, selector, preferred_element_type=F32) for part in three_terms(x)]
    return parts[0] + (parts[1] + parts[2])


def times_left(selector, x):
    parts = [jnp.dot(selector, part, preferred_element_type=F32) for part in three_terms(x)]
    return parts[0] + (parts[1] + parts[2])


def back(v, axis, step=1):
    return pltpu.roll(v, step, axis)


def ahead(v, axis, step=1):
    return pltpu.roll(v, v.shape[axis] - step, axis)


def halve_lanes(fine, coarse, start=0):
    shape = (fine, coarse)
    return ones_where(div(iota(shape, 0), 2) + start == iota(shape, 1))


def plane_setup(kappa, cx, cy, cz, weight, diag, scale, first, last):
    half = 0.5 * scale
    for x in range(first - 1, last):
        cx[x] = half * (kappa[x] + kappa[x + 1])
    for x in range(first, last):
        k = kappa[x]
        y_part = half * (k + ahead(k, 0))
        z_part = half * (k + ahead(k, 1))
        cy[x] = y_part
        cz[x] = z_part
        d = mass_rate + cx[x] + cx[x - 1] + y_part + back(y_part, 0) + z_part + back(z_part, 1)
        weight[x] = relax_weight / d
        if diag is not None:
            diag[x] = d


def in_plane(here, cy, cz, x):
    y_part = cy[x]
    z_part = cz[x]
    total = y_part * ahead(here, 0) + back(y_part * here, 0)
    return total + (z_part * ahead(here, 1) + back(z_part * here, 1))


def neighbours(v, cx, cy, cz, x):
    return (cx[x] * v[x + 1] + cx[x - 1] * v[x - 1]) + in_plane(v[x], cy, cz, x)


def plane_sweep(v, out, forcing, cx, cy, cz, weight, first, last):
    for x in range(first, last):
        out[x] = (1.0 - relax_weight) * v[x] + weight[x] * (forcing[x] + neighbours(v, cx, cy, cz, x))


def edges(conc_in, source_in, material_in, conc, source, material, to_low, to_high, arrived):
    copies = [
        pltpu.make_async_copy(whence, whither, arrived.at[n])
        for n, (whence, whither) in enumerate(
            ((conc_in, conc), (source_in, source), (material_in, material))
        )
    ]
    for copy in copies:
        copy.start()
    for copy in copies:
        copy.wait()
    tile_x, tile_y, _ = conc.shape
    for to, low in ((to_low, True), (to_high, False)):
        for x in range(tile_x):
            rows = slice(0, 4) if low else slice(tile_y - 4, tile_y)
            near = slice(0, 3) if low else slice(1, 4)
            pair = slice(0, 2) if low else slice(2, 4)
            c = conc[x, rows]
            f = mass_rate * c + source[x, rows]
            k = lookup(material[x, rows])
            to[x, 0:3] = c[near]
            to[x, 3:5] = f[pair]
            to[x, 5:8] = k[near]
            to[tile_x, x : x + 1] = k[3:4] if low else k[0:1]


def sides(conc, source, material, from_low, from_high, window, to_low, to_high):
    tile_x, tile_y, size_z = conc.shape
    top = RY + tile_y
    for x in range(tile_x):
        c = conc[x]
        window[0, x, RY:top] = c
        window[1, x, RY:top] = mass_rate * c + source[x]
        window[2, x, RY:top] = lookup(material[x])
        window[0, x, 0:1] = jnp.zeros((1, size_z), F32)
        window[0, x, 1:4] = from_low[x, 0:3]
        window[0, x, top : top + 3] = from_high[x, 0:3]
        window[0, x, top + 3 :] = jnp.zeros((1, size_z), F32)
        window[1, x, 0:2] = jnp.zeros((2, size_z), F32)
        window[1, x, 2:4] = from_low[x, 3:5]
        window[1, x, top : top + 2] = from_high[x, 3:5]
        window[1, x, top + 2 :] = jnp.zeros((2, size_z), F32)
        window[2, x, 0:1] = from_low[tile_x, x : x + 1]
        window[2, x, 1:4] = from_low[x, 5:8]
        window[2, x, top : top + 3] = from_high[x, 5:8]
        window[2, x, top + 3 :] = from_high[tile_x, x : x + 1]
    for to, plane in ((to_low, lambda l: l - 1), (to_high, lambda l: tile_x - l)):
        for at, (which, layer) in enumerate(BASE_PLANES):
            to[at] = window[which, plane(layer), RY:top]
        at = 0
        for which, layer, reach in EXTRA_ROWS:
            to[len(BASE_PLANES), at : at + reach] = window[which, plane(layer), RY - reach : RY]
            at += reach
            to[len(BASE_PLANES), at : at + reach] = window[which, plane(layer), top : top + reach]
            at += reach


BASE_PLANES = (
    (0, 1), (0, 2), (0, 3), (1, 1), (1, 2), (2, 1), (2, 2), (2, 3), (2, 4),
)
EXTRA_ROWS = ((0, 1, 2), (0, 2, 1), (1, 1, 1), (2, 1, 2), (2, 2, 2))


def shrink(window, blocks, paired, paired_one):
    _, tile_x, rows, size_z = window.shape
    tile_x1, tile_y1, size_z1 = tile_x // 2, (rows - 2 * RY) // 2, size_z // 2
    k_one = None
    for chunk in range(size_z // LANES):
        lanes = slice(chunk * LANES, (chunk + 1) * LANES)
        for pair in range(tile_x1):
            paired[pair] = window[2, 2 * pair, :, lanes] + window[2, 2 * pair + 1, :, lanes]
        stack = [
            paired[pair, pl.ds(RY, tile_y1, stride=2)] + paired[pair, pl.ds(RY + 1, tile_y1, stride=2)]
            for pair in range(tile_x1)
        ]
        part = times_right(
            jnp.concatenate(stack, 0), halve_lanes(LANES, size_z1, chunk * LANES // 2)
        )
        k_one = part if k_one is None else k_one + part
    pieces = []
    for pair in range(tile_x1 // 2):
        at = 2 * pair * tile_y1
        paired_one[...] = k_one[at : at + tile_y1] + k_one[at + tile_y1 : at + 2 * tile_y1]
        pieces.append(
            paired_one[pl.ds(0, tile_y1 // 2, stride=2)] + paired_one[pl.ds(1, tile_y1 // 2, stride=2)]
        )
    shape = (size_z1, LANES)
    twice = ones_where(div(iota(shape, 0), 2) == mod(iota(shape, 1), size_z1 // 2))
    block = (0.125 * 0.125) * times_right(jnp.concatenate(pieces, 0), twice)
    for device in range(blocks.shape[0]):
        blocks[device] = block


def fine_down(
    window, from_low, from_high,
    v_out, forcing_out, cx, cy, cz, weight, level_one, blocks, to_low, to_high,
    conc_rim, forcing_rim, kappa_rim, once, diag, paired,
    k_one, f_one, u_one, v_one, cx1, cy1, cz1, w1, d1, paired_one, packed,
):
    _, tile_x, rows, size_z = window.shape
    tile_y = rows - 2 * RY
    top = RY + tile_y
    planes = tile_x + 2 * RX
    rims = (conc_rim, forcing_rim, kappa_rim)
    depths = (3, 2, 4)
    for which, rim in enumerate(rims):
        fill = jnp.full((rows, size_z), 1.0 if which == 2 else 0.0, F32)
        for x in range(2 * depths[which]):
            rim[x] = fill

    def place(which, layer, low):
        return depths[which] - layer if low else depths[which] + layer - 1

    for message, low in ((from_low, True), (from_high, False)):
        for at, (which, layer) in enumerate(BASE_PLANES):
            rims[which][place(which, layer, low), RY:top] = message[at]
        at = 0
        for which, layer, reach in EXTRA_ROWS:
            rim, x = rims[which], place(which, layer, low)
            rim[x, RY - reach : RY] = message[len(BASE_PLANES), at : at + reach]
            at += reach
            rim[x, top : top + reach] = message[len(BASE_PLANES), at : at + reach]
            at += reach

    def stacked(which):
        depth = depths[which]
        whole = [(rims[which], x) for x in range(depth)]
        whole += [(window.at[which], x) for x in range(tile_x)]
        whole += [(rims[which], depth + x) for x in range(depth)]
        return Planes(RX - depth, whole)

    conc, forcing, kappa = stacked(0), stacked(1), stacked(2)
    plane_setup(kappa, cx, cy, cz, weight, diag, 1.0, 1, planes - 1)
    plane_sweep(conc, once, forcing, cx, cy, cz, weight, 1, planes - 1)
    plane_sweep(once, v_out, forcing, cx, cy, cz, weight, 2, planes - 2)
    for x in range(RX - 1, planes - RX + 1):
        forcing_out[x] = forcing[x]
    chunks = size_z // LANES
    size_z1 = size_z // 2
    to_half = [halve_lanes(LANES, size_z1, chunk * LANES // 2) for chunk in range(chunks)]
    tile_x1, tile_y1 = tile_x // 2, tile_y // 2

    def put(pair, total):
        for chunk in range(chunks):
            paired[chunk, pair, 0:rows] = total[:, chunk * LANES : (chunk + 1) * LANES]

    def narrowed(pairs, start, count):
        result = None
        for chunk in range(chunks):
            stack = [
                paired[chunk, pair, pl.ds(start, count, stride=2)]
                + paired[chunk, pair, pl.ds(start + 1, count, stride=2)]
                for pair in range(pairs)
            ]
            part = times_right(jnp.concatenate(stack, 0), to_half[chunk])
            result = part if result is None else result + part
        return 0.125 * result

    wide = paired.shape[2] // 2
    planes1 = tile_x1 + 2 * RC
    if 2 * wide > rows:
        for chunk in range(chunks):
            for pair in range(planes1):
                paired[chunk, pair, rows:] = jnp.ones((2 * wide - rows, LANES), F32)
    for pair in range(planes1):
        x = RX - 2 * RC + 2 * pair
        put(pair, kappa[x] + kappa[x + 1])
    coarse = narrowed(planes1, 0, wide)
    for pair in range(planes1):
        k_one[pair] = coarse[pair * wide : (pair + 1) * wide]
    plane_setup(k_one, cx1, cy1, cz1, w1, d1, 0.25, 1, planes1 - 1)

    for pair in range(tile_x1):
        total = None
        for x in (RX + 2 * pair, RX + 2 * pair + 1):
            part = forcing[x] + neighbours(v_out, cx, cy, cz, x) - diag[x] * v_out[x]
            total = part if total is None else total + part
        put(pair, total)
    forcing_one = narrowed(tile_x1, RY, tile_y1)

    low, high = RC, RC + tile_y1
    nothing = jnp.zeros((wide, size_z1), F32)
    for x in range(planes1):
        f_one[x] = nothing
        if x in (0, planes1 - 1):
            v_one[x] = nothing
    for x in (0, 1, planes1 - 2, planes1 - 1):
        u_one[x] = nothing
    for x in range(tile_x1):
        f = forcing_one[x * tile_y1 : (x + 1) * tile_y1]
        f_one[x + RC, low:high] = f
        u_one[x + RC] = w1[x + RC] * f_one[x + RC]
        level_one[0, x] = f
        level_one[1, x] = u_one[x + RC, low:high]
        level_one[2, x] = k_one[x + RC, low:high]
    plane_sweep(u_one, v_one, f_one, cx1, cy1, cz1, w1, 1, planes1 - 1)
    pairs1 = planes1 // 2
    for pair in range(pairs1):
        total = None
        for x in (2 * pair, 2 * pair + 1):
            if x == 0:
                part = cx1[0] * v_one[1]
            elif x == planes1 - 1:
                part = cx1[x - 1] * v_one[x - 1]
            else:
                part = f_one[x] + neighbours(v_one, cx1, cy1, cz1, x) - d1[x] * v_one[x]
            total = part if total is None else total + part
        paired_one[pair] = total
    for pair in range(pairs1):
        packed[pair] = (
            paired_one[pair, pl.ds(0, ROWS, stride=2)] + paired_one[pair, pl.ds(1, ROWS, stride=2)]
        )
    half_pairs = pairs1 // 2
    result = times_right(
        jnp.concatenate([packed[p] for p in range(half_pairs)], 0), halve_lanes(size_z1, size_z1)
    ) + times_right(
        jnp.concatenate([packed[half_pairs + p] for p in range(half_pairs)], 0),
        halve_lanes(size_z1, size_z1, size_z1 // 2),
    )
    for p in range(half_pairs):
        block = 0.125 * result[p * ROWS : (p + 1) * ROWS]
        for device in range(blocks.shape[0]):
            blocks[device, p] = block

    for to, rows1, row0 in (
        (to_low, slice(0, R1), RY + 1),
        (to_high, slice(tile_y1 - R1, tile_y1), top - 2),
    ):
        for which in range(3):
            for x in range(tile_x1):
                flat_row = which * tile_x1 * R1 + x * R1
                to[flat_row // ROWS, flat_row % ROWS : flat_row % ROWS + R1] = level_one[
                    which, x, rows1
                ]
        start = 3 * tile_x1 * R1 // ROWS
        for x in range(tile_x):
            row = v_out[RX + x, row0 : row0 + 1]
            for chunk in range(chunks):
                to[start + chunk, x : x + 1] = row[:, chunk * LANES : (chunk + 1) * LANES]


def reach_of(layer):
    return R1 + 1 - layer


def middle(level_one, v_zero, from_low, from_high, window, to_low, to_high):
    _, tile_x1, tile_y1, _ = level_one.shape
    planes, rows, size_z = v_zero.shape
    top1 = R1 + tile_y1
    for which in range(3):
        for x in range(tile_x1):
            flat_row = which * tile_x1 * R1 + x * R1
            at, sub = flat_row // ROWS, flat_row % ROWS
            window[which, x, R1:top1] = level_one[which, x]
            window[which, x, 0:R1] = from_low[at, sub : sub + R1]
            window[which, x, top1:] = from_high[at, sub : sub + R1]
    chunks = size_z // LANES
    top = rows - RY
    for to, low in ((to_low, True), (to_high, False)):
        at = 0
        for which in (0, 2):
            for layer in range(1, R1 + 1):
                x = layer - 1 if low else tile_x1 - layer
                outer = 1 if which == 0 and layer == R1 else which
                to[at] = window[outer, x, R1:top1]
                at += 1
        loose = at * ROWS
        for which in (0, 2):
            for layer in range(1, R1 + 1):
                x = layer - 1 if low else tile_x1 - layer
                outer = 1 if which == 0 else which
                for distance in range(1, reach_of(layer) + 1):
                    source = outer if distance == reach_of(layer) else which
                    for row in (R1 - distance, top1 + distance - 1):
                        to[loose // ROWS, loose % ROWS : loose % ROWS + 1] = window[
                            source, x, row : row + 1
                        ]
                        loose += 1
        second, first = (RX + 1, RX) if low else (planes - RX - 2, planes - RX - 1)
        for row in (RY - 1, top):
            for chunk in range(chunks):
                lanes = slice(chunk * LANES, (chunk + 1) * LANES)
                to[loose // ROWS, loose % ROWS : loose % ROWS + 1] = v_zero[first, row : row + 1, lanes]
                loose += 1
        at = -(-loose // ROWS)
        for chunk in range(chunks):
            lanes = slice(chunk * LANES, (chunk + 1) * LANES)
            for half in range((top - RY) // ROWS):
                to[at] = v_zero[second, RY + half * ROWS : RY + (half + 1) * ROWS, lanes]
                at += 1


def middle_tiles(tile_y, chunks):
    loose = 2 * sum(2 * reach_of(layer) for layer in range(1, R1 + 1)) + 2 * chunks
    return 2 * R1 + -(-loose // ROWS) + chunks * tile_y // ROWS


class Grid:
    def __init__(self, sizes, strides, scales, rows, lanes):
        self.sizes = sizes
        self.strides = strides
        self.scales = scales
        self.rows = rows
        self.lanes = lanes
        self.ratios = tuple(2 if extent % 2 == 0 else 1 for extent in sizes)
        self.cells = sizes[0] * sizes[1] * sizes[2]
        self.exact = self.cells <= 64 or self.ratios == (1, 1, 1)

    def coarser(self):
        sizes = tuple(extent // ratio for extent, ratio in zip(self.sizes, self.ratios))
        scales = tuple(s / (ratio * ratio) for s, ratio in zip(self.scales, self.ratios))
        strides = tuple(s * ratio for s, ratio in zip(self.strides, self.ratios[1:]))
        return Grid(sizes, strides, scales, self.rows, self.lanes)


def next_plane(v):
    return v if v.shape[0] == 1 else jnp.concatenate([v[1:], v[:1]], 0)


def last_plane(v):
    return v if v.shape[0] == 1 else jnp.concatenate([v[-1:], v[:-1]], 0)


def restrict_whole(v, grid):
    if grid.ratios[0] == 2:
        v = jnp.concatenate(
            [v[2 * x : 2 * x + 1] + v[2 * x + 1 : 2 * x + 2] for x in range(grid.sizes[0] // 2)], 0
        )
    for axis in (1, 2):
        if grid.ratios[axis] == 2:
            step = grid.strides[axis - 1]
            even = mod(div(iota(v.shape, axis), step), 2) == 0
            v = v + jnp.where(even, ahead(v, axis, step), back(v, axis, step))
    return (1.0 / (grid.ratios[0] * grid.ratios[1] * grid.ratios[2])) * v


def prolong_whole(v, grid):
    if grid.ratios[0] == 1:
        return v
    return jnp.concatenate([v[x // 2 : x // 2 + 1] for x in range(grid.sizes[0])], 0)


def whole_operator(kappa, grid):
    half_x, half_y, half_z = (0.5 * s for s in grid.scales)
    step_y, step_z = grid.strides
    cx = half_x * (kappa + next_plane(kappa))
    cy = half_y * (kappa + ahead(kappa, 1, step_y))
    cz = half_z * (kappa + ahead(kappa, 2, step_z))
    diag = mass_rate + cx + last_plane(cx)
    diag = diag + (cy + back(cy, 1, step_y)) + (cz + back(cz, 2, step_z))
    return cx, cy, cz, diag, relax_weight / diag


def whole_neighbours(v, operator, grid):
    cx, cy, cz = operator[:3]
    step_y, step_z = grid.strides
    total = cx * next_plane(v) + last_plane(cx * v)
    total = total + (cy * ahead(v, 1, step_y) + back(cy * v, 1, step_y))
    return total + (cz * ahead(v, 2, step_z) + back(cz * v, 2, step_z))


def whole_sweep(v, forcing, operator, grid):
    return (1.0 - relax_weight) * v + operator[4] * (forcing + whole_neighbours(v, operator, grid))


class ExactSolve:
    def __init__(self, grid, kappa=None, inverse=None):
        size_x, size_y, size_z = grid.sizes
        self.grid = grid
        self.across = across = size_x * size_y
        _, step_z = grid.strides
        self.period = period = size_z * step_z
        cells = grid.cells
        padded = -(-cells // ROWS) * ROWS
        assert across <= step_z and 2 * period <= grid.lanes
        shape = (padded, grid.lanes)
        i, j = iota(shape, 0), iota(shape, 1)
        self.i, self.j = i, j
        if kappa is None:
            self.inverse = inverse
            return

        def places_of_row(n):
            sub = mod(n, across)
            return div(sub, size_y), mod(sub, size_y), div(n, across)

        def places_of_lane(n):
            n = mod(n, period)
            sub = mod(n, step_z)
            return div(sub, size_y), mod(sub, size_y), div(n, step_z)

        at_i, at_j = places_of_row(i), places_of_lane(j)
        live = (mod(j, step_z) < across) & (i < cells)
        same = (at_i[0] == at_j[0]) & (at_i[1] == at_j[1]) & (at_i[2] == at_j[2]) & live
        left = j < period
        factor = jnp.zeros(shape, F32)
        for d in range(3):
            equal = [at_i[other] == at_j[other] for other in range(3) if other != d]
            for step in (1, grid.sizes[d] - 1):
                hit = mod(at_i[d] + step, grid.sizes[d]) == at_j[d]
                factor = factor + jnp.where(
                    hit & equal[0] & equal[1], F32(0.5 * grid.scales[d]), F32(0.0)
                )
        k_row = self.as_row(kappa)
        k_column = jnp.sum(jnp.where(same & left, k_row, 0.0), axis=1, keepdims=True)
        coupled = jnp.where(live & left, factor * (k_column + k_row), 0.0)
        diag = mass_rate + jnp.sum(coupled, axis=1, keepdims=True)
        matrix = jnp.where(same & left, diag - coupled, -coupled)
        matrix = jnp.where(left, matrix, jnp.where(same, F32(1.0), F32(0.0)))
        for n in range(cells):
            lane = (n // across) * step_z + n % across
            pivot_row = matrix[n : n + 1] / matrix[n : n + 1, lane : lane + 1]
            column = matrix[:, lane : lane + 1]
            matrix = jnp.where(i == n, pivot_row, matrix - column * pivot_row)
        self.inverse = jnp.where((j >= period) & (j < 2 * period) & live, matrix, 0.0)

    def as_row(self, v):
        grid = self.grid
        size_x, size_y, _ = grid.sizes
        step_y, step_z = grid.strides
        sub = mod(iota((1, grid.lanes), 1), step_z)
        result = jnp.zeros((1, grid.lanes), F32)
        for x in range(size_x):
            for y in range(size_y):
                row = v[x, y * step_y : y * step_y + 1]
                result = jnp.where(sub == x * size_y + y, row, result)
        return result

    def solve(self, forcing):
        grid = self.grid
        size_x, size_y, _ = grid.sizes
        step_y, step_z = grid.strides
        solved = jnp.sum(self.inverse * self.as_row(forcing), axis=1, keepdims=True)
        at_z = div(mod(self.j, self.period), step_z)
        spread = jnp.where(div(self.i, self.across) == at_z, solved, 0.0)
        planes = []
        for x in range(size_x):
            rows = []
            for y in range(size_y):
                mine = mod(self.i, self.across) == x * size_y + y
                row = jnp.sum(jnp.where(mine, spread, 0.0), axis=0, keepdims=True)
                rows.append(jnp.broadcast_to(row, (step_y, grid.lanes)))
            planes.append(jnp.concatenate(rows, 0)[None])
        return jnp.concatenate(planes, 0)


def levels_of(counts, tile_sizes):
    sizes = tuple(count * extent for count, extent in zip(counts, tile_sizes)) + tile_sizes[2:]
    grid = Grid(sizes, (1, 1), (0.0625, 0.0625, 0.0625), sizes[1], LANES)
    grids = [grid]
    while not grid.exact:
        grid = grid.coarser()
        grids.append(grid)
    return grids


class Operator:
    def __init__(self, ref):
        self.ref = ref

    def __getitem__(self, part):
        if isinstance(part, slice):
            return [self.ref[p] for p in range(*part.indices(5))]
        return self.ref[part]


def prepare(counts, grids, blocks, _, *outputs):
    count_x, count_y = counts
    planes, rows, _ = grids[0].sizes
    half_x, half_y = planes // count_x, rows // count_y
    assert half_x * half_y == ROWS and ROWS % half_y == 0
    sub = iota((ROWS, LANES), 0)
    kappa = [[jnp.ones((ROWS, LANES), F32)] * (rows // ROWS) for _ in range(planes)]
    for tx in range(count_x):
        for ty in range(count_y):
            piece = blocks[tx * count_y + ty]
            for p in range(half_x):
                x, start = tx * half_x + p, ty * half_y
                group, offset = start // ROWS, start % ROWS
                shift = (offset - p * half_y) % ROWS
                moved = pltpu.roll(piece, shift, 0) if shift else piece
                mine = (sub >= offset) & (sub < offset + half_y)
                kappa[x][group] = jnp.where(mine, moved, kappa[x][group])
    kappa = jnp.concatenate([jnp.concatenate(groups, 0)[None] for groups in kappa], 0)
    kappas = [kappa]
    for grid in grids[:-1]:
        kappas.append(restrict_whole(kappas[-1], grid))
    outputs[-1][...] = ExactSolve(grids[-1], kappas[-1]).inverse
    for number, grid in enumerate(grids[:-1]):
        for part, value in enumerate(whole_operator(kappas[number], grid)):
            outputs[number][part] = value


def solve_whole(forcing, levels, exact):
    if not levels:
        return exact.solve(forcing)
    grid, operator = levels[0]
    v = operator[4] * forcing
    v = whole_sweep(v, forcing, operator, grid)
    residual = forcing + whole_neighbours(v, operator, grid) - operator[3] * v
    v = v + prolong_whole(solve_whole(restrict_whole(residual, grid), levels[1:], exact), grid)
    for _ in range(2):
        v = whole_sweep(v, forcing, operator, grid)
    return v


def assemble(blocks, count_x, count_y, half_x, half_y, size_z2):
    rows = count_y * half_y
    groups = rows // ROWS
    planes = count_x * half_x
    assert rows % ROWS == 0
    used = half_y + RC
    sub = iota((ROWS, LANES), 0)
    lane = iota((ROWS, LANES), 1)
    nothing = jnp.zeros((ROWS, LANES), F32)
    forcing = [[nothing] * groups for _ in range(planes)]
    half_pairs = blocks.shape[1]
    ring = RC // 2
    for tx in range(count_x):
        for ty in range(count_y):
            for p in range(half_pairs):
                piece = blocks[tx * count_y + ty, p]
                start = (ty * half_y - ring) % rows
                group, offset = start // ROWS, start % ROWS
                piece = pltpu.roll(piece, offset, 0) if offset else piece
                turned = pltpu.roll(piece, size_z2, 1)
                for half in range(2):
                    moved = jnp.where((lane < size_z2) == (half == 0), piece, turned)
                    x = (tx * half_x - ring + half * half_pairs + p) % planes
                    at = group
                    mine = (sub >= offset) & (sub < offset + used)
                    forcing[x][at] = forcing[x][at] + jnp.where(mine, moved, 0.0)
                    if offset + used > ROWS:
                        at = (group + 1) % groups
                        mine = sub < offset + used - ROWS
                        forcing[x][at] = forcing[x][at] + jnp.where(mine, moved, 0.0)
    return jnp.concatenate([jnp.concatenate(groups, 0)[None] for groups in forcing], 0)


def coarse_up(
    counts, grids, blocks, window_one, one_low, one_high, row_low, row_high,
    v_zero, forcing0, cx, cy, cz, weight, *rest,
):
    prepared, rest = rest[: len(grids)], rest[len(grids) :]
    (
        out, mixed_low, mixed_high, kappa_low, kappa_high, first_low, first_high,
        v_one, cx1, cy1, cz1, w1, one_a, one_b, zero_a, zero_b,
    ) = rest
    count_x, count_y = counts
    _, tile_x1, rows1, size_z1 = window_one.shape
    tile_y1 = rows1 - 2 * R1
    top1 = R1 + tile_y1
    half_x, half_y, size_z2 = tile_x1 // 2, tile_y1 // 2, size_z1 // 2
    sizes = grids[0].sizes
    forcing2 = assemble(blocks, count_x, count_y, half_x, half_y, size_z2)
    levels = [
        (grid, Operator(prepared[number])) for number, grid in enumerate(grids[:-1])
    ]
    exact = ExactSolve(grids[-1], inverse=prepared[-1][...])

    planes1 = tile_x1 + 2 * R1
    for message, mixed, kappa_rim, low in (
        (one_low, mixed_low, kappa_low, True), (one_high, mixed_high, kappa_high, False)
    ):
        at, loose = 0, 2 * R1 * ROWS
        for rim, fill in ((mixed, 0.0), (kappa_rim, 1.0)):
            for layer in range(1, R1 + 1):
                x = R1 - layer if low else layer - 1
                rim[x] = jnp.full((rows1, size_z1), fill, F32)
                rim[x, R1:top1] = message[at]
                at += 1
                for distance in range(1, reach_of(layer) + 1):
                    for row in (R1 - distance, top1 + distance - 1):
                        rim[x, row : row + 1] = message[
                            loose // ROWS, loose % ROWS : loose % ROWS + 1
                        ]
                        loose += 1

    def stacked(low, which, high):
        whole = [(low, x) for x in range(R1)]
        whole += [(window_one.at[which], x) for x in range(tile_x1)]
        whole += [(high, x) for x in range(R1)]
        return Planes(0, whole)

    forcing1 = stacked(mixed_low, 0, mixed_high)
    kappa1 = stacked(kappa_low, 2, kappa_high)
    plane_setup(kappa1, cx1, cy1, cz1, w1, None, 0.25, 1, planes1 - 1)
    row = iota((rows1, size_z1), 0)
    for mixed, rim, low in ((mixed_low, first_low, True), (mixed_high, first_high, False)):
        for layer in range(1, R1 + 1):
            x = R1 - layer if low else layer - 1
            if layer == R1:
                rim[x] = mixed[x]
            else:
                reach = reach_of(layer) - 1
                inside = (row >= R1 - reach) & (row < top1 + reach)
                at = x if low else R1 + tile_x1 + x
                rim[x] = jnp.where(inside, w1[at] * mixed[x], mixed[x])
    start1 = stacked(first_low, 1, first_high)
    plane_sweep(start1, v_one, forcing1, cx1, cy1, cz1, w1, 1, planes1 - 1)

    solved = solve_whole(forcing2, levels, exact)
    solved = solved.reshape(sizes[0] * sizes[1], LANES)

    whole_x1, whole_y1 = 2 * sizes[0], 2 * sizes[1]
    start_x = lax.axis_index("tx") * tile_x1 + (whole_x1 - R1)
    start_y = lax.axis_index("ty") * tile_y1 + (whole_y1 - R1)
    row = iota((planes1 * rows1, 1), 0)
    at_x = mod(div(row, rows1) + start_x, whole_x1)
    at_y = mod(mod(row, rows1) + start_y, whole_y1)
    target = div(at_x, 2) * sizes[1] + div(at_y, 2)
    left = ones_where(iota((planes1 * rows1, sizes[0] * sizes[1]), 1) == target)
    shape = (LANES, size_z1)
    right = ones_where(iota(shape, 0) == div(iota(shape, 1), 2))
    raised = times_right(times_left(left, solved), right)
    for x in range(1, planes1 - 1):
        one_a[x] = v_one[x] + raised[x * rows1 : (x + 1) * rows1]
    plane_sweep(one_a, one_b, forcing1, cx1, cy1, cz1, w1, 2, planes1 - 2)
    plane_sweep(one_b, one_a, forcing1, cx1, cy1, cz1, w1, 3, planes1 - 3)

    planes, rows, size_z = v_zero.shape
    first, last = R1 - 1, planes1 - R1 + 1
    stack = jnp.concatenate([one_a[x] for x in range(first, last)], 0)
    count = last - first
    shape = (count * rows, count * rows1)
    out_row, in_row = iota((count * rows, 1), 0), iota(shape, 1)
    target = div(out_row, rows) * rows1 + div(mod(out_row, rows) + (2 * R1 - RY), 2)
    left = ones_where(in_row == target)
    shape = (size_z1, size_z)
    right = ones_where(iota(shape, 0) == div(iota(shape, 1), 2))
    raised = times_right(times_left(left, stack), right)
    chunks = size_z // LANES
    top = rows - RY
    for x in range(RX - 1, planes - RX + 1):
        zero_b[x] = v_zero[x]
    for rim_x in (RX - 2, planes - RX + 1):
        zero_b[rim_x] = jnp.zeros((rows, size_z), F32)
    for x in range(planes - 2 * RX):
        at = 3 * tile_x1 * R1 // ROWS
        for chunk in range(chunks):
            lanes = slice(chunk * LANES, (chunk + 1) * LANES)
            zero_b[RX + x, RY - 2 : RY - 1, lanes] = row_low[at + chunk, x : x + 1]
            zero_b[RX + x, top + 1 : top + 2, lanes] = row_high[at + chunk, x : x + 1]
    for message, second, nearest in (
        (one_low, RX - 2, RX - 1), (one_high, planes - RX + 1, planes - RX)
    ):
        loose = 2 * R1 * ROWS + 2 * sum(2 * reach_of(layer) for layer in range(1, R1 + 1))
        for r in (RY - 1, top):
            for chunk in range(chunks):
                lanes = slice(chunk * LANES, (chunk + 1) * LANES)
                zero_b[nearest, r : r + 1, lanes] = message[
                    loose // ROWS, loose % ROWS : loose % ROWS + 1
                ]
                loose += 1
        at = -(-loose // ROWS)
        for chunk in range(chunks):
            lanes = slice(chunk * LANES, (chunk + 1) * LANES)
            for half in range((top - RY) // ROWS):
                zero_b[second, RY + half * ROWS : RY + (half + 1) * ROWS, lanes] = message[at]
                at += 1
    for x in range(RX - 2, planes - RX + 2):
        at = (x - RX + 2 * R1) // 2 - first
        zero_a[x] = zero_b[x] + raised[at * rows : (at + 1) * rows]
    plane_sweep(zero_a, zero_b, forcing0, cx, cy, cz, weight, RX - 1, planes - RX + 1)
    plane_sweep(zero_b, zero_a, forcing0, cx, cy, cz, weight, RX, planes - RX)
    for x in range(planes - 2 * RX):
        out[x] = zero_a[x + RX, RY:top]


VM = pl.BlockSpec(memory_space=pltpu.VMEM)
IN_PLACE = pl.BlockSpec(memory_space=pltpu.HBM)


def call(kernel, operands, outputs, scratch, spec=VM):
    def typed(output):
        return output if isinstance(output, jax.ShapeDtypeStruct) else jax.ShapeDtypeStruct(output, F32)

    return pl.pallas_call(
        kernel,
        in_specs=[spec] * len(operands),
        out_specs=[VM] * len(outputs),
        out_shape=[typed(output) for output in outputs],
        scratch_shapes=[pltpu.VMEM(s, F32) if isinstance(s, tuple) else s for s in scratch],
        compiler_params=pltpu.CompilerParams(vmem_limit_bytes=24 * 1024 * 1024),
    )(*operands)


def exchange(to_low, to_high, axis):
    count = lax.axis_size(axis)
    from_low = lax.ppermute(to_high, axis, [(i, (i + 1) % count) for i in range(count)])
    from_high = lax.ppermute(to_low, axis, [((i + 1) % count, i) for i in range(count)])
    return from_low, from_high


def to_everyone(blocks):
    return lax.all_to_all(blocks, ("tx", "ty"), 0, 0)


def cycle(concentration, source, material):
    tile_x, tile_y, size_z = concentration.shape
    chunks = size_z // LANES
    counts = lax.axis_size("tx"), lax.axis_size("ty")
    everyone = counts[0] * counts[1]
    rows = tile_y + 2 * RY
    message = (tile_x + 1, ROWS, size_z)
    *inputs, to_low, to_high = call(
        edges,
        (concentration, source, material),
        tuple(jax.ShapeDtypeStruct(v.shape, v.dtype) for v in (concentration, source, material))
        + (message, message),
        (pltpu.SemaphoreType.DMA((3,)),),
        IN_PLACE,
    )
    from_low, from_high = exchange(to_low, to_high, "ty")
    message = (len(BASE_PLANES) + 1, tile_y, size_z)
    window, to_low, to_high = call(
        sides, (*inputs, from_low, from_high), ((3, tile_x, rows, size_z), message, message), ()
    )
    from_low, from_high = exchange(to_low, to_high, "tx")

    zero = (tile_x + 2 * RX, rows, size_z)
    one_tile = (tile_x // 2, tile_y // 2, size_z // 2)
    two_tile = tuple(extent // 2 for extent in one_tile)
    grids = levels_of(counts, two_tile)
    (kappa_blocks,) = call(
        shrink,
        (window,),
        ((everyone, two_tile[0] * two_tile[1], LANES),),
        ((one_tile[0], rows, LANES), one_tile[1:]),
    )
    kappa_blocks = to_everyone(kappa_blocks)

    wide = -(-rows // (2 * ROWS)) * ROWS
    small = (one_tile[0] + 2 * RC, wide, one_tile[2])
    pairs1 = small[0] // 2
    message = (3 * one_tile[0] * R1 // ROWS + chunks, ROWS, LANES)
    assert one_tile[2] == LANES and tile_x <= ROWS and one_tile[1] == ROWS
    v_zero, forcing0, cx, cy, cz, weight, level_one, blocks, to_low, to_high = call(
        fine_down,
        (window, from_low, from_high),
        (zero,) * 6
        + ((3,) + one_tile, (everyone, pairs1 // 2, ROWS, LANES), message, message),
        (
            (6, rows, size_z),
            (4, rows, size_z),
            (8, rows, size_z),
            zero,
            zero,
            (chunks, max(small[0], tile_x), 2 * wide, LANES),
        )
        + (small,) * 9
        + ((pairs1, wide, one_tile[2]), (pairs1, ROWS, one_tile[2])),
    )
    row_low, row_high = exchange(to_low, to_high, "ty")
    blocks = to_everyone(blocks)
    rows1 = one_tile[1] + 2 * R1
    message = (middle_tiles(tile_y, chunks), ROWS, LANES)
    window_one, to_low, to_high = call(
        middle,
        (level_one, v_zero, row_low, row_high),
        ((3, one_tile[0], rows1, one_tile[2]), message, message),
        (),
    )
    one_low, one_high = exchange(to_low, to_high, "tx")
    lattice = grids[0].sizes[1], LANES
    prepared = call(
        functools.partial(prepare, counts, grids),
        (kappa_blocks, window_one),
        tuple((5, grid.sizes[0]) + lattice for grid in grids[:-1])
        + ((-(-grids[-1].cells // ROWS) * ROWS, LANES),),
        (),
    )
    one = (one_tile[0] + 2 * R1, rows1, one_tile[2])
    rim = (R1,) + one[1:]
    (updated,) = call(
        functools.partial(coarse_up, counts, grids),
        (blocks, window_one, one_low, one_high, row_low, row_high)
        + (v_zero, forcing0, cx, cy, cz, weight, *prepared),
        (concentration.shape,),
        (rim,) * 6 + (one,) * 7 + (zero, zero),
    )
    return updated


def solution(mesh):
    placed = (P("tx", "ty", None), P("tx", "ty", None), P("tx", "ty", None))
    return jax.shard_map(
        cycle, mesh=mesh, in_specs=placed, out_specs=P("tx", "ty", None), check_vma=False
    )
```

```python
import functools

import jax
import jax.numpy as jnp
from jax import lax
from jax.experimental import pallas as pl
from jax.experimental.pallas import tpu as pltpu
from jax.sharding import PartitionSpec as P


mass_rate = 0.001
relax_weight = 0.8
diffusivities = (0.15, 0.3, 0.5, 0.8, 1.2, 2.0, 3.2, 5.0)
LANES = 128
ROWS = 8
RX = 3
RY = 4
R1 = 4
RC = 2
F32 = jnp.float32
BF16 = jnp.bfloat16


def lookup(material):
    result = jnp.zeros(material.shape, F32)
    for slot_id, coeff_value in enumerate(diffusivities):
        result = jnp.where(material == slot_id, F32(coeff_value), result)
    return result


class Planes:
    def __init__(self, first, planes):
        self.first = first
        self.planes = planes

    def __getitem__(self, x):
        ref, index = self.planes[x - self.first]
        return ref[index]

    def __setitem__(self, x, value):
        ref, index = self.planes[x - self.first]
        ref[index] = value


def kept(ref, first, before=None, after=None):
    planes = [(ref, x) for x in range(ref.shape[0])]
    if before is not None:
        planes = [before] + planes
        first -= 1
    if after is not None:
        planes = planes + [after]
    return Planes(first, planes)


def iota(shape, dim):
    return lax.broadcasted_iota(jnp.int32, shape, dim)


def div(a, b):
    return lax.div(a, jnp.full_like(a, b))


def mod(a, b):
    return lax.rem(a, jnp.full_like(a, b))


def ones_where(mask):
    return jnp.where(mask, F32(1.0), F32(0.0)).astype(BF16)


def three_terms(x):
    high = x.astype(BF16)
    rest = x - high.astype(F32)
    middle = rest.astype(BF16)
    low = (rest - middle.astype(F32)).astype(BF16)
    return high, middle, low


def times_right(x, selector):
    parts = [jnp.dot(part, selector, preferred_element_type=F32) for part in three_terms(x)]
    return parts[0] + (parts[1] + parts[2])


def times_left(selector, x):
    parts = [jnp.dot(selector, part, preferred_element_type=F32) for part in three_terms(x)]
    return parts[0] + (parts[1] + parts[2])


def back(v, axis, step=1):
    return pltpu.roll(v, step, axis)


def ahead(v, axis, step=1):
    return pltpu.roll(v, v.shape[axis] - step, axis)


def halve_lanes(fine, coarse, start=0):
    shape = (fine, coarse)
    return ones_where(div(iota(shape, 0), 2) + start == iota(shape, 1))


def plane_setup(kappa, cx, cy, cz, weight, diag, scale, first, last):
    half = 0.5 * scale
    for x in range(first - 1, last):
        cx[x] = half * (kappa[x] + kappa[x + 1])
    for x in range(first, last):
        k = kappa[x]
        y_part = half * (k + ahead(k, 0))
        z_part = half * (k + ahead(k, 1))
        cy[x] = y_part
        cz[x] = z_part
        d = mass_rate + cx[x] + cx[x - 1] + y_part + back(y_part, 0) + z_part + back(z_part, 1)
        weight[x] = relax_weight / d
        if diag is not None:
            diag[x] = d


def in_plane(here, cy, cz, x):
    y_part = cy[x]
    z_part = cz[x]
    total = y_part * ahead(here, 0) + back(y_part * here, 0)
    return total + (z_part * ahead(here, 1) + back(z_part * here, 1))


def neighbours(v, cx, cy, cz, x):
    return (cx[x] * v[x + 1] + cx[x - 1] * v[x - 1]) + in_plane(v[x], cy, cz, x)


def plane_sweep(v, out, forcing, cx, cy, cz, weight, first, last):
    for x in range(first, last):
        out[x] = (1.0 - relax_weight) * v[x] + weight[x] * (forcing[x] + neighbours(v, cx, cy, cz, x))


def edges(conc_in, source_in, material_in, conc, source, material, to_low, to_high, arrived):
    copies = [
        pltpu.make_async_copy(whence, whither, arrived.at[n])
        for n, (whence, whither) in enumerate(
            ((conc_in, conc), (source_in, source), (material_in, material))
        )
    ]
    for copy in copies:
        copy.start()
    for copy in copies:
        copy.wait()
    tile_x, tile_y, _ = conc.shape
    for to, low in ((to_low, True), (to_high, False)):
        for x in range(tile_x):
            rows = slice(0, 4) if low else slice(tile_y - 4, tile_y)
            near = slice(0, 3) if low else slice(1, 4)
            pair = slice(0, 2) if low else slice(2, 4)
            c = conc[x, rows]
            f = mass_rate * c + source[x, rows]
            k = lookup(material[x, rows])
            to[x, 0:3] = c[near]
            to[x, 3:5] = f[pair]
            to[x, 5:8] = k[near]
            to[tile_x, x : x + 1] = k[3:4] if low else k[0:1]


def sides(conc, source, material, from_low, from_high, window, to_low, to_high):
    tile_x, tile_y, size_z = conc.shape
    top = RY + tile_y
    for x in range(tile_x):
        c = conc[x]
        window[0, x, RY:top] = c
        window[1, x, RY:top] = mass_rate * c + source[x]
        window[2, x, RY:top] = lookup(material[x])
        window[0, x, 0:1] = jnp.zeros((1, size_z), F32)
        window[0, x, 1:4] = from_low[x, 0:3]
        window[0, x, top : top + 3] = from_high[x, 0:3]
        window[0, x, top + 3 :] = jnp.zeros((1, size_z), F32)
        window[1, x, 0:2] = jnp.zeros((2, size_z), F32)
        window[1, x, 2:4] = from_low[x, 3:5]
        window[1, x, top : top + 2] = from_high[x, 3:5]
        window[1, x, top + 2 :] = jnp.zeros((2, size_z), F32)
        window[2, x, 0:1] = from_low[tile_x, x : x + 1]
        window[2, x, 1:4] = from_low[x, 5:8]
        window[2, x, top : top + 3] = from_high[x, 5:8]
        window[2, x, top + 3 :] = from_high[tile_x, x : x + 1]
    for to, plane in ((to_low, lambda l: l - 1), (to_high, lambda l: tile_x - l)):
        for at, (which, layer) in enumerate(BASE_PLANES):
            to[at] = window[which, plane(layer), RY:top]
        at = 0
        for which, layer, reach in EXTRA_ROWS:
            to[len(BASE_PLANES), at : at + reach] = window[which, plane(layer), RY - reach : RY]
            at += reach
            to[len(BASE_PLANES), at : at + reach] = window[which, plane(layer), top : top + reach]
            at += reach


BASE_PLANES = (
    (0, 1), (0, 2), (0, 3), (1, 1), (1, 2), (2, 1), (2, 2), (2, 3), (2, 4),
)
EXTRA_ROWS = ((0, 1, 2), (0, 2, 1), (1, 1, 1), (2, 1, 2), (2, 2, 2))


def shrink(window, blocks, paired, paired_one):
    _, tile_x, rows, size_z = window.shape
    tile_x1, tile_y1, size_z1 = tile_x // 2, (rows - 2 * RY) // 2, size_z // 2
    k_one = None
    for chunk in range(size_z // LANES):
        lanes = slice(chunk * LANES, (chunk + 1) * LANES)
        for pair in range(tile_x1):
            paired[pair] = window[2, 2 * pair, :, lanes] + window[2, 2 * pair + 1, :, lanes]
        stack = [
            paired[pair, pl.ds(RY, tile_y1, stride=2)] + paired[pair, pl.ds(RY + 1, tile_y1, stride=2)]
            for pair in range(tile_x1)
        ]
        part = times_right(
            jnp.concatenate(stack, 0), halve_lanes(LANES, size_z1, chunk * LANES // 2)
        )
        k_one = part if k_one is None else k_one + part
    assert tile_x1 // 2 * (size_z1 // 2) <= LANES
    block = None
    for pair in range(tile_x1 // 2):
        at = 2 * pair * tile_y1
        paired_one[...] = k_one[at : at + tile_y1] + k_one[at + tile_y1 : at + 2 * tile_y1]
        piece = (
            paired_one[pl.ds(0, tile_y1 // 2, stride=2)] + paired_one[pl.ds(1, tile_y1 // 2, stride=2)]
        )
        part = times_right(piece, halve_lanes(size_z1, LANES, pair * size_z1 // 2))
        block = part if block is None else block + part
    block = (0.125 * 0.125) * block
    for device in range(blocks.shape[0]):
        blocks[device] = block


def fine_down(
    window, from_low, from_high,
    v_zero, forcing_out, cx, cy, cz, weight, level_one, blocks, to_low, to_high,
    conc_rim, forcing_rim, kappa_rim, once, diag, paired, outer,
    k_one, f_one, u_one, v_one, cx1, cy1, cz1, w1, d1, paired_one, packed,
):
    _, tile_x, rows, size_z = window.shape
    tile_y = rows - 2 * RY
    top = RY + tile_y
    planes = tile_x + 2 * RX
    rims = (conc_rim, forcing_rim, kappa_rim)
    depths = (3, 2, 4)
    for which, rim in enumerate(rims):
        fill = jnp.full((rows, size_z), 1.0 if which == 2 else 0.0, F32)
        for x in range(2 * depths[which]):
            rim[x] = fill

    def place(which, layer, low):
        return depths[which] - layer if low else depths[which] + layer - 1

    for message, low in ((from_low, True), (from_high, False)):
        for at, (which, layer) in enumerate(BASE_PLANES):
            rims[which][place(which, layer, low), RY:top] = message[at]
        at = 0
        for which, layer, reach in EXTRA_ROWS:
            rim, x = rims[which], place(which, layer, low)
            rim[x, RY - reach : RY] = message[len(BASE_PLANES), at : at + reach]
            at += reach
            rim[x, top : top + reach] = message[len(BASE_PLANES), at : at + reach]
            at += reach

    def stacked(which):
        depth = depths[which]
        whole = [(rims[which], x) for x in range(depth)]
        whole += [(window.at[which], x) for x in range(tile_x)]
        whole += [(rims[which], depth + x) for x in range(depth)]
        return Planes(RX - depth, whole)

    conc, forcing, kappa = stacked(0), stacked(1), stacked(2)
    cx = kept(cx, RX - 2, (outer, 0), (outer, 1))
    cy = kept(cy, RX - 1, (outer, 2), (outer, 3))
    cz = kept(cz, RX - 1, (outer, 4), (outer, 5))
    weight = kept(weight, RX - 1, (outer, 6), (outer, 7))
    v_out = kept(v_zero, RX - 1)
    plane_setup(kappa, cx, cy, cz, weight, diag, 1.0, 1, planes - 1)
    plane_sweep(conc, once, forcing, cx, cy, cz, weight, 1, planes - 1)
    plane_sweep(once, v_out, forcing, cx, cy, cz, weight, 2, planes - 2)
    for x in range(RX - 1, planes - RX + 1):
        forcing_out[x - RX + 1] = forcing[x]
    chunks = size_z // LANES
    size_z1 = size_z // 2
    to_half = [halve_lanes(LANES, size_z1, chunk * LANES // 2) for chunk in range(chunks)]
    tile_x1, tile_y1 = tile_x // 2, tile_y // 2

    def put(pair, total):
        for chunk in range(chunks):
            paired[chunk, pair, 0:rows] = total[:, chunk * LANES : (chunk + 1) * LANES]

    def narrowed(pairs, start, count):
        result = None
        for chunk in range(chunks):
            stack = [
                paired[chunk, pair, pl.ds(start, count, stride=2)]
                + paired[chunk, pair, pl.ds(start + 1, count, stride=2)]
                for pair in range(pairs)
            ]
            part = times_right(jnp.concatenate(stack, 0), to_half[chunk])
            result = part if result is None else result + part
        return 0.125 * result

    wide = paired.shape[2] // 2
    planes1 = tile_x1 + 2 * RC
    if 2 * wide > rows:
        for chunk in range(chunks):
            for pair in range(planes1):
                paired[chunk, pair, rows:] = jnp.ones((2 * wide - rows, LANES), F32)
    for pair in range(planes1):
        x = RX - 2 * RC + 2 * pair
        put(pair, kappa[x] + kappa[x + 1])
    coarse = narrowed(planes1, 0, wide)
    for pair in range(planes1):
        k_one[pair] = coarse[pair * wide : (pair + 1) * wide]
    plane_setup(k_one, cx1, cy1, cz1, w1, d1, 0.25, 1, planes1 - 1)

    for pair in range(tile_x1):
        total = None
        for x in (RX + 2 * pair, RX + 2 * pair + 1):
            part = forcing[x] + neighbours(v_out, cx, cy, cz, x) - diag[x] * v_out[x]
            total = part if total is None else total + part
        put(pair, total)
    forcing_one = narrowed(tile_x1, RY, tile_y1)

    low, high = RC, RC + tile_y1
    nothing = jnp.zeros((wide, size_z1), F32)
    for x in range(planes1):
        f_one[x] = nothing
        if x in (0, planes1 - 1):
            v_one[x] = nothing
    for x in (0, 1, planes1 - 2, planes1 - 1):
        u_one[x] = nothing
    for x in range(tile_x1):
        f = forcing_one[x * tile_y1 : (x + 1) * tile_y1]
        f_one[x + RC, low:high] = f
        u_one[x + RC] = w1[x + RC] * f_one[x + RC]
        level_one[0, x] = f
        level_one[1, x] = u_one[x + RC, low:high]
        level_one[2, x] = k_one[x + RC, low:high]
    plane_sweep(u_one, v_one, f_one, cx1, cy1, cz1, w1, 1, planes1 - 1)
    pairs1 = planes1 // 2
    for pair in range(pairs1):
        total = None
        for x in (2 * pair, 2 * pair + 1):
            if x == 0:
                part = cx1[0] * v_one[1]
            elif x == planes1 - 1:
                part = cx1[x - 1] * v_one[x - 1]
            else:
                part = f_one[x] + neighbours(v_one, cx1, cy1, cz1, x) - d1[x] * v_one[x]
            total = part if total is None else total + part
        paired_one[pair] = total
    for pair in range(pairs1):
        packed[pair] = (
            paired_one[pair, pl.ds(0, ROWS, stride=2)] + paired_one[pair, pl.ds(1, ROWS, stride=2)]
        )
    half_pairs = pairs1 // 2
    result = times_right(
        jnp.concatenate([packed[p] for p in range(half_pairs)], 0), halve_lanes(size_z1, size_z1)
    ) + times_right(
        jnp.concatenate([packed[half_pairs + p] for p in range(half_pairs)], 0),
        halve_lanes(size_z1, size_z1, size_z1 // 2),
    )
    for p in range(half_pairs):
        block = 0.125 * result[p * ROWS : (p + 1) * ROWS]
        for device in range(blocks.shape[0]):
            blocks[device, p] = block

    for to, rows1, row0 in (
        (to_low, slice(0, R1), RY + 1),
        (to_high, slice(tile_y1 - R1, tile_y1), top - 2),
    ):
        for which in range(3):
            for x in range(tile_x1):
                flat_row = which * tile_x1 * R1 + x * R1
                to[flat_row // ROWS, flat_row % ROWS : flat_row % ROWS + R1] = level_one[
                    which, x, rows1
                ]
        start = 3 * tile_x1 * R1 // ROWS
        for x in range(tile_x):
            row = v_zero[x + 1, row0 : row0 + 1]
            for chunk in range(chunks):
                to[start + chunk, x : x + 1] = row[:, chunk * LANES : (chunk + 1) * LANES]


def reach_of(layer):
    return R1 + 1 - layer


def middle(level_one, v_zero, from_low, from_high, window, to_low, to_high):
    _, tile_x1, tile_y1, _ = level_one.shape
    planes, rows, size_z = v_zero.shape
    top1 = R1 + tile_y1
    for which in range(3):
        for x in range(tile_x1):
            flat_row = which * tile_x1 * R1 + x * R1
            at, sub = flat_row // ROWS, flat_row % ROWS
            window[which, x, R1:top1] = level_one[which, x]
            window[which, x, 0:R1] = from_low[at, sub : sub + R1]
            window[which, x, top1:] = from_high[at, sub : sub + R1]
    chunks = size_z // LANES
    top = rows - RY
    for to, low in ((to_low, True), (to_high, False)):
        at = 0
        for which in (0, 2):
            for layer in range(1, R1 + 1):
                x = layer - 1 if low else tile_x1 - layer
                outer = 1 if which == 0 and layer == R1 else which
                to[at] = window[outer, x, R1:top1]
                at += 1
        loose = at * ROWS
        for which in (0, 2):
            for layer in range(1, R1 + 1):
                x = layer - 1 if low else tile_x1 - layer
                outer = 1 if which == 0 else which
                for distance in range(1, reach_of(layer) + 1):
                    source = outer if distance == reach_of(layer) else which
                    for row in (R1 - distance, top1 + distance - 1):
                        to[loose // ROWS, loose % ROWS : loose % ROWS + 1] = window[
                            source, x, row : row + 1
                        ]
                        loose += 1
        second, first = (2, 1) if low else (planes - 3, planes - 2)
        for row in (RY - 1, top):
            for chunk in range(chunks):
                lanes = slice(chunk * LANES, (chunk + 1) * LANES)
                to[loose // ROWS, loose % ROWS : loose % ROWS + 1] = v_zero[first, row : row + 1, lanes]
                loose += 1
        at = -(-loose // ROWS)
        for chunk in range(chunks):
            lanes = slice(chunk * LANES, (chunk + 1) * LANES)
            for half in range((top - RY) // ROWS):
                to[at] = v_zero[second, RY + half * ROWS : RY + (half + 1) * ROWS, lanes]
                at += 1


def middle_tiles(tile_y, chunks):
    loose = 2 * sum(2 * reach_of(layer) for layer in range(1, R1 + 1)) + 2 * chunks
    return 2 * R1 + -(-loose // ROWS) + chunks * tile_y // ROWS


class Grid:
    def __init__(self, sizes, strides, scales, rows, lanes):
        self.sizes = sizes
        self.strides = strides
        self.scales = scales
        self.rows = rows
        self.lanes = lanes
        self.ratios = tuple(2 if extent % 2 == 0 else 1 for extent in sizes)
        self.cells = sizes[0] * sizes[1] * sizes[2]
        self.exact = self.cells <= 64 or self.ratios == (1, 1, 1)

    def coarser(self):
        sizes = tuple(extent // ratio for extent, ratio in zip(self.sizes, self.ratios))
        scales = tuple(s / (ratio * ratio) for s, ratio in zip(self.scales, self.ratios))
        strides = tuple(s * ratio for s, ratio in zip(self.strides, self.ratios[1:]))
        return Grid(sizes, strides, scales, self.rows, self.lanes)


def next_plane(v):
    return v if v.shape[0] == 1 else jnp.concatenate([v[1:], v[:1]], 0)


def last_plane(v):
    return v if v.shape[0] == 1 else jnp.concatenate([v[-1:], v[:-1]], 0)


def restrict_whole(v, grid):
    if grid.ratios[0] == 2:
        v = jnp.concatenate(
            [v[2 * x : 2 * x + 1] + v[2 * x + 1 : 2 * x + 2] for x in range(grid.sizes[0] // 2)], 0
        )
    for axis in (1, 2):
        if grid.ratios[axis] == 2:
            step = grid.strides[axis - 1]
            even = mod(div(iota(v.shape, axis), step), 2) == 0
            v = v + jnp.where(even, ahead(v, axis, step), back(v, axis, step))
    return (1.0 / (grid.ratios[0] * grid.ratios[1] * grid.ratios[2])) * v


def prolong_whole(v, grid):
    if grid.ratios[0] == 1:
        return v
    return jnp.concatenate([v[x // 2 : x // 2 + 1] for x in range(grid.sizes[0])], 0)


def whole_operator(kappa, grid):
    half_x, half_y, half_z = (0.5 * s for s in grid.scales)
    step_y, step_z = grid.strides
    cx = half_x * (kappa + next_plane(kappa))
    cy = half_y * (kappa + ahead(kappa, 1, step_y))
    cz = half_z * (kappa + ahead(kappa, 2, step_z))
    diag = mass_rate + cx + last_plane(cx)
    diag = diag + (cy + back(cy, 1, step_y)) + (cz + back(cz, 2, step_z))
    return cx, cy, cz, diag, relax_weight / diag


def whole_neighbours(v, operator, grid):
    cx, cy, cz = operator[:3]
    step_y, step_z = grid.strides
    total = cx * next_plane(v) + last_plane(cx * v)
    total = total + (cy * ahead(v, 1, step_y) + back(cy * v, 1, step_y))
    return total + (cz * ahead(v, 2, step_z) + back(cz * v, 2, step_z))


def whole_sweep(v, forcing, operator, grid):
    return (1.0 - relax_weight) * v + operator[4] * (forcing + whole_neighbours(v, operator, grid))


class ExactSolve:
    def __init__(self, grid, kappa=None, inverse=None):
        size_x, size_y, size_z = grid.sizes
        self.grid = grid
        self.across = across = size_x * size_y
        _, step_z = grid.strides
        self.period = period = size_z * step_z
        cells = grid.cells
        padded = -(-cells // ROWS) * ROWS
        assert across <= step_z and 2 * period <= grid.lanes
        shape = (padded, grid.lanes)
        i, j = iota(shape, 0), iota(shape, 1)
        self.i, self.j = i, j
        if kappa is None:
            self.inverse = inverse
            return

        def places_of_row(n):
            sub = mod(n, across)
            return div(sub, size_y), mod(sub, size_y), div(n, across)

        def places_of_lane(n):
            n = mod(n, period)
            sub = mod(n, step_z)
            return div(sub, size_y), mod(sub, size_y), div(n, step_z)

        at_i, at_j = places_of_row(i), places_of_lane(j)
        live = (mod(j, step_z) < across) & (i < cells)
        same = (at_i[0] == at_j[0]) & (at_i[1] == at_j[1]) & (at_i[2] == at_j[2]) & live
        left = j < period
        factor = jnp.zeros(shape, F32)
        for d in range(3):
            equal = [at_i[other] == at_j[other] for other in range(3) if other != d]
            for step in (1, grid.sizes[d] - 1):
                hit = mod(at_i[d] + step, grid.sizes[d]) == at_j[d]
                factor = factor + jnp.where(
                    hit & equal[0] & equal[1], F32(0.5 * grid.scales[d]), F32(0.0)
                )
        k_row = self.as_row(kappa)
        k_column = jnp.sum(jnp.where(same & left, k_row, 0.0), axis=1, keepdims=True)
        coupled = jnp.where(live & left, factor * (k_column + k_row), 0.0)
        diag = mass_rate + jnp.sum(coupled, axis=1, keepdims=True)
        matrix = jnp.where(same & left, diag - coupled, -coupled)
        matrix = jnp.where(left, matrix, jnp.where(same, F32(1.0), F32(0.0)))
        for n in range(cells):
            lane = (n // across) * step_z + n % across
            pivot_row = matrix[n : n + 1] / matrix[n : n + 1, lane : lane + 1]
            column = matrix[:, lane : lane + 1]
            matrix = jnp.where(i == n, pivot_row, matrix - column * pivot_row)
        self.inverse = jnp.where((j >= period) & (j < 2 * period) & live, matrix, 0.0)

    def as_row(self, v):
        grid = self.grid
        size_x, size_y, _ = grid.sizes
        step_y, step_z = grid.strides
        sub = mod(iota((1, grid.lanes), 1), step_z)
        result = jnp.zeros((1, grid.lanes), F32)
        for x in range(size_x):
            for y in range(size_y):
                row = v[x, y * step_y : y * step_y + 1]
                result = jnp.where(sub == x * size_y + y, row, result)
        return result

    def solve(self, forcing):
        grid = self.grid
        size_x, size_y, _ = grid.sizes
        step_y, step_z = grid.strides
        solved = jnp.sum(self.inverse * self.as_row(forcing), axis=1, keepdims=True)
        at_z = div(mod(self.j, self.period), step_z)
        spread = jnp.where(div(self.i, self.across) == at_z, solved, 0.0)
        planes = []
        for x in range(size_x):
            rows = []
            for y in range(size_y):
                mine = mod(self.i, self.across) == x * size_y + y
                row = jnp.sum(jnp.where(mine, spread, 0.0), axis=0, keepdims=True)
                rows.append(jnp.broadcast_to(row, (step_y, grid.lanes)))
            planes.append(jnp.concatenate(rows, 0)[None])
        return jnp.concatenate(planes, 0)


def levels_of(counts, tile_sizes):
    sizes = tuple(count * extent for count, extent in zip(counts, tile_sizes)) + tile_sizes[2:]
    grid = Grid(sizes, (1, 1), (0.0625, 0.0625, 0.0625), sizes[1], LANES)
    grids = [grid]
    while not grid.exact:
        grid = grid.coarser()
        grids.append(grid)
    return grids


class Operator:
    def __init__(self, ref):
        self.ref = ref

    def __getitem__(self, part):
        if isinstance(part, slice):
            return [self.ref[p] for p in range(*part.indices(5))]
        return self.ref[part]


def prepare(counts, grids, blocks, _, *outputs):
    count_x, count_y = counts
    planes, rows, _ = grids[0].sizes
    half_x, half_y = planes // count_x, rows // count_y
    size_z2 = grids[0].sizes[2]
    assert half_x * size_z2 == LANES and half_x == 2 and ROWS % half_y == 0
    share = ROWS // half_y
    kappa = [[None] * (rows // ROWS) for _ in range(planes)]
    lane = iota((ROWS, LANES), 1)
    for tx in range(count_x):
        for group in range(rows // ROWS):
            pieces = [blocks[tx * count_y + group * share + n] for n in range(share)]
            piece = jnp.concatenate(pieces, 0)
            turned = pltpu.roll(piece, size_z2, 1)
            for p in range(half_x):
                mine = (lane < size_z2) == (p == 0)
                kappa[tx * half_x + p][group] = jnp.where(mine, piece, turned)
    kappa = jnp.concatenate([jnp.concatenate(groups, 0)[None] for groups in kappa], 0)
    kappas = [kappa]
    for grid in grids[:-1]:
        kappas.append(restrict_whole(kappas[-1], grid))
    outputs[-1][...] = ExactSolve(grids[-1], kappas[-1]).inverse
    for number, grid in enumerate(grids[:-1]):
        for part, value in enumerate(whole_operator(kappas[number], grid)):
            outputs[number][part] = value


def solve_whole(forcing, levels, exact):
    if not levels:
        return exact.solve(forcing)
    grid, operator = levels[0]
    v = operator[4] * forcing
    v = whole_sweep(v, forcing, operator, grid)
    residual = forcing + whole_neighbours(v, operator, grid) - operator[3] * v
    v = v + prolong_whole(solve_whole(restrict_whole(residual, grid), levels[1:], exact), grid)
    for _ in range(2):
        v = whole_sweep(v, forcing, operator, grid)
    return v


def assemble(blocks, count_x, count_y, half_x, half_y, size_z2):
    rows = count_y * half_y
    groups = rows // ROWS
    planes = count_x * half_x
    assert rows % ROWS == 0
    used = half_y + RC
    sub = iota((ROWS, LANES), 0)
    lane = iota((ROWS, LANES), 1)
    nothing = jnp.zeros((ROWS, LANES), F32)
    forcing = [[nothing] * groups for _ in range(planes)]
    half_pairs = blocks.shape[1]
    ring = RC // 2
    for tx in range(count_x):
        for ty in range(count_y):
            for p in range(half_pairs):
                piece = blocks[tx * count_y + ty, p]
                start = (ty * half_y - ring) % rows
                group, offset = start // ROWS, start % ROWS
                piece = pltpu.roll(piece, offset, 0) if offset else piece
                turned = pltpu.roll(piece, size_z2, 1)
                for half in range(2):
                    moved = jnp.where((lane < size_z2) == (half == 0), piece, turned)
                    x = (tx * half_x - ring + half * half_pairs + p) % planes
                    at = group
                    mine = (sub >= offset) & (sub < offset + used)
                    forcing[x][at] = forcing[x][at] + jnp.where(mine, moved, 0.0)
                    if offset + used > ROWS:
                        at = (group + 1) % groups
                        mine = sub < offset + used - ROWS
                        forcing[x][at] = forcing[x][at] + jnp.where(mine, moved, 0.0)
    return jnp.concatenate([jnp.concatenate(groups, 0)[None] for groups in forcing], 0)


def coarse_up(
    counts, grids, blocks, window_one, one_low, one_high, row_low, row_high,
    v_zero, forcing0, cx, cy, cz, weight, *rest,
):
    prepared, rest = rest[: len(grids)], rest[len(grids) :]
    (
        out, mixed_low, mixed_high, kappa_low, kappa_high, first_low, first_high,
        v_one, cx1, cy1, cz1, w1, one_a, one_b, zero_a, zero_b,
    ) = rest
    count_x, count_y = counts
    _, tile_x1, rows1, size_z1 = window_one.shape
    tile_y1 = rows1 - 2 * R1
    top1 = R1 + tile_y1
    half_x, half_y, size_z2 = tile_x1 // 2, tile_y1 // 2, size_z1 // 2
    sizes = grids[0].sizes
    forcing2 = assemble(blocks, count_x, count_y, half_x, half_y, size_z2)
    levels = [
        (grid, Operator(prepared[number])) for number, grid in enumerate(grids[:-1])
    ]
    exact = ExactSolve(grids[-1], inverse=prepared[-1][...])

    planes1 = tile_x1 + 2 * R1
    for message, mixed, kappa_rim, low in (
        (one_low, mixed_low, kappa_low, True), (one_high, mixed_high, kappa_high, False)
    ):
        at, loose = 0, 2 * R1 * ROWS
        for rim, fill in ((mixed, 0.0), (kappa_rim, 1.0)):
            for layer in range(1, R1 + 1):
                x = R1 - layer if low else layer - 1
                rim[x] = jnp.full((rows1, size_z1), fill, F32)
                rim[x, R1:top1] = message[at]
                at += 1
                for distance in range(1, reach_of(layer) + 1):
                    for row in (R1 - distance, top1 + distance - 1):
                        rim[x, row : row + 1] = message[
                            loose // ROWS, loose % ROWS : loose % ROWS + 1
                        ]
                        loose += 1

    def stacked(low, which, high):
        whole = [(low, x) for x in range(R1)]
        whole += [(window_one.at[which], x) for x in range(tile_x1)]
        whole += [(high, x) for x in range(R1)]
        return Planes(0, whole)

    forcing1 = stacked(mixed_low, 0, mixed_high)
    kappa1 = stacked(kappa_low, 2, kappa_high)
    plane_setup(kappa1, cx1, cy1, cz1, w1, None, 0.25, 1, planes1 - 1)
    row = iota((rows1, size_z1), 0)
    for mixed, rim, low in ((mixed_low, first_low, True), (mixed_high, first_high, False)):
        for layer in range(1, R1 + 1):
            x = R1 - layer if low else layer - 1
            if layer == R1:
                rim[x] = mixed[x]
            else:
                reach = reach_of(layer) - 1
                inside = (row >= R1 - reach) & (row < top1 + reach)
                at = x if low else R1 + tile_x1 + x
                rim[x] = jnp.where(inside, w1[at] * mixed[x], mixed[x])
    start1 = stacked(first_low, 1, first_high)
    plane_sweep(start1, v_one, forcing1, cx1, cy1, cz1, w1, 1, planes1 - 1)

    solved = solve_whole(forcing2, levels, exact)
    solved = solved.reshape(sizes[0] * sizes[1], LANES)

    whole_x1, whole_y1 = 2 * sizes[0], 2 * sizes[1]
    start_x = lax.axis_index("tx") * tile_x1 + (whole_x1 - R1)
    start_y = lax.axis_index("ty") * tile_y1 + (whole_y1 - R1)
    row = iota((planes1 * rows1, 1), 0)
    at_x = mod(div(row, rows1) + start_x, whole_x1)
    at_y = mod(mod(row, rows1) + start_y, whole_y1)
    target = div(at_x, 2) * sizes[1] + div(at_y, 2)
    left = ones_where(iota((planes1 * rows1, sizes[0] * sizes[1]), 1) == target)
    shape = (LANES, size_z1)
    right = ones_where(iota(shape, 0) == div(iota(shape, 1), 2))
    raised = times_right(times_left(left, solved), right)
    for x in range(1, planes1 - 1):
        one_a[x] = v_one[x] + raised[x * rows1 : (x + 1) * rows1]
    plane_sweep(one_a, one_b, forcing1, cx1, cy1, cz1, w1, 2, planes1 - 2)
    plane_sweep(one_b, one_a, forcing1, cx1, cy1, cz1, w1, 3, planes1 - 3)

    planes, rows, size_z = zero_a.shape
    v_zero, forcing0 = kept(v_zero, RX - 1), kept(forcing0, RX - 1)
    cx, cy, cz, weight = kept(cx, RX - 2), kept(cy, RX - 1), kept(cz, RX - 1), kept(weight, RX - 1)
    first, last = R1 - 1, planes1 - R1 + 1
    stack = jnp.concatenate([one_a[x] for x in range(first, last)], 0)
    count = last - first
    shape = (count * rows, count * rows1)
    out_row, in_row = iota((count * rows, 1), 0), iota(shape, 1)
    target = div(out_row, rows) * rows1 + div(mod(out_row, rows) + (2 * R1 - RY), 2)
    left = ones_where(in_row == target)
    shape = (size_z1, size_z)
    right = ones_where(iota(shape, 0) == div(iota(shape, 1), 2))
    raised = times_right(times_left(left, stack), right)
    chunks = size_z // LANES
    top = rows - RY
    for x in range(RX - 1, planes - RX + 1):
        zero_b[x] = v_zero[x]
    for rim_x in (RX - 2, planes - RX + 1):
        zero_b[rim_x] = jnp.zeros((rows, size_z), F32)
    for x in range(planes - 2 * RX):
        at = 3 * tile_x1 * R1 // ROWS
        for chunk in range(chunks):
            lanes = slice(chunk * LANES, (chunk + 1) * LANES)
            zero_b[RX + x, RY - 2 : RY - 1, lanes] = row_low[at + chunk, x : x + 1]
            zero_b[RX + x, top + 1 : top + 2, lanes] = row_high[at + chunk, x : x + 1]
    for message, second, nearest in (
        (one_low, RX - 2, RX - 1), (one_high, planes - RX + 1, planes - RX)
    ):
        loose = 2 * R1 * ROWS + 2 * sum(2 * reach_of(layer) for layer in range(1, R1 + 1))
        for r in (RY - 1, top):
            for chunk in range(chunks):
                lanes = slice(chunk * LANES, (chunk + 1) * LANES)
                zero_b[nearest, r : r + 1, lanes] = message[
                    loose // ROWS, loose % ROWS : loose % ROWS + 1
                ]
                loose += 1
        at = -(-loose // ROWS)
        for chunk in range(chunks):
            lanes = slice(chunk * LANES, (chunk + 1) * LANES)
            for half in range((top - RY) // ROWS):
                zero_b[second, RY + half * ROWS : RY + (half + 1) * ROWS, lanes] = message[at]
                at += 1
    for x in range(RX - 2, planes - RX + 2):
        at = (x - RX + 2 * R1) // 2 - first
        zero_a[x] = zero_b[x] + raised[at * rows : (at + 1) * rows]
    plane_sweep(zero_a, zero_b, forcing0, cx, cy, cz, weight, RX - 1, planes - RX + 1)
    plane_sweep(zero_b, zero_a, forcing0, cx, cy, cz, weight, RX, planes - RX)
    for x in range(planes - 2 * RX):
        out[x] = zero_a[x + RX, RY:top]


VM = pl.BlockSpec(memory_space=pltpu.VMEM)
IN_PLACE = pl.BlockSpec(memory_space=pltpu.HBM)


def call(kernel, operands, outputs, scratch, spec=VM):
    def typed(output):
        return output if isinstance(output, jax.ShapeDtypeStruct) else jax.ShapeDtypeStruct(output, F32)

    return pl.pallas_call(
        kernel,
        in_specs=[spec] * len(operands),
        out_specs=[VM] * len(outputs),
        out_shape=[typed(output) for output in outputs],
        scratch_shapes=[pltpu.VMEM(s, F32) if isinstance(s, tuple) else s for s in scratch],
        compiler_params=pltpu.CompilerParams(vmem_limit_bytes=24 * 1024 * 1024),
    )(*operands)


def exchange(to_low, to_high, axis):
    count = lax.axis_size(axis)
    from_low = lax.ppermute(to_high, axis, [(i, (i + 1) % count) for i in range(count)])
    from_high = lax.ppermute(to_low, axis, [((i + 1) % count, i) for i in range(count)])
    return from_low, from_high


def to_everyone(blocks):
    return lax.all_to_all(blocks, ("tx", "ty"), 0, 0)


def cycle(concentration, source, material):
    tile_x, tile_y, size_z = concentration.shape
    chunks = size_z // LANES
    counts = lax.axis_size("tx"), lax.axis_size("ty")
    everyone = counts[0] * counts[1]
    rows = tile_y + 2 * RY
    message = (tile_x + 1, ROWS, size_z)
    *inputs, to_low, to_high = call(
        edges,
        tuple(
            pltpu.with_memory_space_constraint(v, pltpu.HBM)
            for v in (concentration, source, material)
        ),
        tuple(jax.ShapeDtypeStruct(v.shape, v.dtype) for v in (concentration, source, material))
        + (message, message),
        (pltpu.SemaphoreType.DMA((3,)),),
        IN_PLACE,
    )
    from_low, from_high = exchange(to_low, to_high, "ty")
    message = (len(BASE_PLANES) + 1, tile_y, size_z)
    window, to_low, to_high = call(
        sides, (*inputs, from_low, from_high), ((3, tile_x, rows, size_z), message, message), ()
    )
    from_low, from_high = exchange(to_low, to_high, "tx")

    zero = (tile_x + 2 * RX, rows, size_z)
    inner = (tile_x + 2, rows, size_z)
    one_tile = (tile_x // 2, tile_y // 2, size_z // 2)
    two_tile = tuple(extent // 2 for extent in one_tile)
    grids = levels_of(counts, two_tile)
    (kappa_blocks,) = call(
        shrink,
        (window,),
        ((everyone, two_tile[1], LANES),),
        ((one_tile[0], rows, LANES), one_tile[1:]),
    )
    kappa_blocks = to_everyone(kappa_blocks)

    wide = -(-rows // (2 * ROWS)) * ROWS
    small = (one_tile[0] + 2 * RC, wide, one_tile[2])
    pairs1 = small[0] // 2
    message = (3 * one_tile[0] * R1 // ROWS + chunks, ROWS, LANES)
    assert one_tile[2] == LANES and tile_x <= ROWS and one_tile[1] == ROWS
    v_zero, forcing0, cx, cy, cz, weight, level_one, blocks, to_low, to_high = call(
        fine_down,
        (window, from_low, from_high),
        (inner, inner, (tile_x + 3, rows, size_z), inner, inner, inner)
        + ((3,) + one_tile, (everyone, pairs1 // 2, ROWS, LANES), message, message),
        (
            (6, rows, size_z),
            (4, rows, size_z),
            (8, rows, size_z),
            zero,
            zero,
            (chunks, max(small[0], tile_x), 2 * wide, LANES),
            (8, rows, size_z),
        )
        + (small,) * 9
        + ((pairs1, wide, one_tile[2]), (pairs1, ROWS, one_tile[2])),
    )
    row_low, row_high = exchange(to_low, to_high, "ty")
    blocks = to_everyone(blocks)
    rows1 = one_tile[1] + 2 * R1
    message = (middle_tiles(tile_y, chunks), ROWS, LANES)
    window_one, to_low, to_high = call(
        middle,
        (level_one, v_zero, row_low, row_high),
        ((3, one_tile[0], rows1, one_tile[2]), message, message),
        (),
    )
    one_low, one_high = exchange(to_low, to_high, "tx")
    lattice = grids[0].sizes[1], LANES
    prepared = call(
        functools.partial(prepare, counts, grids),
        (kappa_blocks, window_one),
        tuple((5, grid.sizes[0]) + lattice for grid in grids[:-1])
        + ((-(-grids[-1].cells // ROWS) * ROWS, LANES),),
        (),
    )
    one = (one_tile[0] + 2 * R1, rows1, one_tile[2])
    rim = (R1,) + one[1:]
    (updated,) = call(
        functools.partial(coarse_up, counts, grids),
        (blocks, window_one, one_low, one_high, row_low, row_high)
        + (v_zero, forcing0, cx, cy, cz, weight, *prepared),
        (concentration.shape,),
        (rim,) * 6 + (one,) * 7 + (zero, zero),
    )
    return updated


def solution(mesh):
    placed = (P("tx", "ty", None), P("tx", "ty", None), P("tx", "ty", None))
    return jax.shard_map(
        cycle, mesh=mesh, in_specs=placed, out_specs=P("tx", "ty", None), check_vma=False
    )
```

```python
import functools

import jax
import jax.numpy as jnp
from jax import lax
from jax.experimental import pallas as pl
from jax.experimental.pallas import tpu as pltpu
from jax.sharding import PartitionSpec as P


mass_rate = 0.001
relax_weight = 0.8
diffusivities = (0.15, 0.3, 0.5, 0.8, 1.2, 2.0, 3.2, 5.0)
LANES = 128
ROWS = 8
SHORT = 4
RX = 3
RY = 4
R1 = 4
RC = 2
F32 = jnp.float32
BF16 = jnp.bfloat16


def lookup(material):
    result = jnp.zeros(material.shape, F32)
    for slot_id, coeff_value in enumerate(diffusivities):
        result = jnp.where(material == slot_id, F32(coeff_value), result)
    return result


class Planes:
    def __init__(self, first, planes):
        self.first = first
        self.planes = planes

    def __getitem__(self, x):
        ref, index = self.planes[x - self.first]
        return ref[index]

    def __setitem__(self, x, value):
        ref, index = self.planes[x - self.first]
        ref[index] = value


def kept(ref, first, before=None, after=None):
    planes = [(ref, x) for x in range(ref.shape[0])]
    if before is not None:
        planes = [before] + planes
        first -= 1
    if after is not None:
        planes = planes + [after]
    return Planes(first, planes)


def is_even(axis):
    return lax.rem(lax.axis_index(axis), 2) == 0


def on_sides(axis, near, far, body):
    @pl.when(is_even(axis))
    def _():
        body(far, near)

    @pl.when(jnp.logical_not(is_even(axis)))
    def _():
        body(near, far)


class Picked:
    def __init__(self, flag, when_true, when_false):
        self.flag = flag
        self.when_true = when_true
        self.when_false = when_false

    def __getitem__(self, index):
        first, second = self.when_true[index], self.when_false[index]
        flag = jnp.where(self.flag, jnp.int32(1), jnp.int32(0))
        return jnp.where(jnp.full(first.shape, flag) == 1, first, second)


def by_side(axis, near, far):
    even = is_even(axis)
    return Picked(even, far, near), Picked(even, near, far)


def iota(shape, dim):
    return lax.broadcasted_iota(jnp.int32, shape, dim)


def div(a, b):
    return lax.div(a, jnp.full_like(a, b))


def mod(a, b):
    return lax.rem(a, jnp.full_like(a, b))


def ones_where(mask):
    return jnp.where(mask, F32(1.0), F32(0.0)).astype(BF16)


def three_terms(x):
    high = x.astype(BF16)
    rest = x - high.astype(F32)
    middle = rest.astype(BF16)
    low = (rest - middle.astype(F32)).astype(BF16)
    return high, middle, low


def times_right(x, selector):
    parts = [jnp.dot(part, selector, preferred_element_type=F32) for part in three_terms(x)]
    return parts[0] + (parts[1] + parts[2])


def times_left(selector, x):
    parts = [jnp.dot(selector, part, preferred_element_type=F32) for part in three_terms(x)]
    return parts[0] + (parts[1] + parts[2])


def back(v, axis, step=1):
    return pltpu.roll(v, step, axis)


def ahead(v, axis, step=1):
    return pltpu.roll(v, v.shape[axis] - step, axis)


def halve_lanes(fine, coarse, start=0):
    shape = (fine, coarse)
    return ones_where(div(iota(shape, 0), 2) + start == iota(shape, 1))


def plane_setup(kappa, cx, cy, cz, weight, diag, scale, first, last):
    half = 0.5 * scale
    for x in range(first - 1, last):
        cx[x] = half * (kappa[x] + kappa[x + 1])
    for x in range(first, last):
        k = kappa[x]
        y_part = half * (k + ahead(k, 0))
        z_part = half * (k + ahead(k, 1))
        cy[x] = y_part
        cz[x] = z_part
        d = mass_rate + cx[x] + cx[x - 1] + y_part + back(y_part, 0) + z_part + back(z_part, 1)
        weight[x] = relax_weight / d
        if diag is not None:
            diag[x] = d


def in_plane(here, cy, cz, x):
    y_part = cy[x]
    z_part = cz[x]
    total = y_part * ahead(here, 0) + back(y_part * here, 0)
    return total + (z_part * ahead(here, 1) + back(z_part * here, 1))


def neighbours(v, cx, cy, cz, x):
    return (cx[x] * v[x + 1] + cx[x - 1] * v[x - 1]) + in_plane(v[x], cy, cz, x)


def plane_sweep(v, out, forcing, cx, cy, cz, weight, first, last):
    for x in range(first, last):
        out[x] = (1.0 - relax_weight) * v[x] + weight[x] * (forcing[x] + neighbours(v, cx, cy, cz, x))


def edges(conc_in, source_in, material_in, conc, source, material, near, far, arrived):
    copies = [
        pltpu.make_async_copy(whence, whither, arrived.at[n])
        for n, (whence, whither) in enumerate(
            ((conc_in, conc), (source_in, source), (material_in, material))
        )
    ]
    for copy in copies:
        copy.start()
    for copy in copies:
        copy.wait()
    tile_x, tile_y, _ = conc.shape

    def pack(to_low, to_high):
        for to, low in ((to_low, True), (to_high, False)):
            for x in range(tile_x):
                rows = slice(0, 4) if low else slice(tile_y - 4, tile_y)
                near = slice(0, 3) if low else slice(1, 4)
                pair = slice(0, 2) if low else slice(2, 4)
                c = conc[x, rows]
                f = mass_rate * c + source[x, rows]
                k = lookup(material[x, rows])
                to[x, 0:3] = c[near]
                to[x, 3:5] = f[pair]
                to[x, 5:8] = k[near]
                to[tile_x, x : x + 1] = k[3:4] if low else k[0:1]

    on_sides("ty", near, far, pack)


def sides(conc, source, material, from_near, from_far, window, near, far):
    from_low, from_high = by_side("ty", from_near, from_far)
    tile_x, tile_y, size_z = conc.shape
    top = RY + tile_y
    for x in range(tile_x):
        c = conc[x]
        window[0, x, RY:top] = c
        window[1, x, RY:top] = mass_rate * c + source[x]
        window[2, x, RY:top] = lookup(material[x])
        window[0, x, 0:1] = jnp.zeros((1, size_z), F32)
        window[0, x, 1:4] = from_low[x, 0:3]
        window[0, x, top : top + 3] = from_high[x, 0:3]
        window[0, x, top + 3 :] = jnp.zeros((1, size_z), F32)
        window[1, x, 0:2] = jnp.zeros((2, size_z), F32)
        window[1, x, 2:4] = from_low[x, 3:5]
        window[1, x, top : top + 2] = from_high[x, 3:5]
        window[1, x, top + 2 :] = jnp.zeros((2, size_z), F32)
        window[2, x, 0:1] = from_low[tile_x, x : x + 1]
        window[2, x, 1:4] = from_low[x, 5:8]
        window[2, x, top : top + 3] = from_high[x, 5:8]
        window[2, x, top + 3 :] = from_high[tile_x, x : x + 1]

    def pack(to_low, to_high):
        for to, plane in ((to_low, lambda l: l - 1), (to_high, lambda l: tile_x - l)):
            for at, (which, layer) in enumerate(BASE_PLANES):
                to[at] = window[which, plane(layer), RY:top]
            at = 0
            for which, layer, reach in EXTRA_ROWS:
                for start in (RY - reach, top):
                    to[len(BASE_PLANES), at : at + reach] = window[
                        which, plane(layer), start : start + reach
                    ]
                    at += reach

    on_sides("tx", near, far, pack)


BASE_PLANES = (
    (0, 1), (0, 2), (0, 3), (1, 1), (1, 2), (2, 1), (2, 2), (2, 3), (2, 4),
)
EXTRA_ROWS = ((0, 1, 2), (0, 2, 1), (1, 1, 1), (2, 1, 2), (2, 2, 2))


def shrink(window, blocks, paired, paired_one):
    _, tile_x, rows, size_z = window.shape
    tile_x1, tile_y1, size_z1 = tile_x // 2, (rows - 2 * RY) // 2, size_z // 2
    k_one = None
    for chunk in range(size_z // LANES):
        lanes = slice(chunk * LANES, (chunk + 1) * LANES)
        for pair in range(tile_x1):
            paired[pair] = window[2, 2 * pair, :, lanes] + window[2, 2 * pair + 1, :, lanes]
        stack = [
            paired[pair, pl.ds(RY, tile_y1, stride=2)] + paired[pair, pl.ds(RY + 1, tile_y1, stride=2)]
            for pair in range(tile_x1)
        ]
        part = times_right(
            jnp.concatenate(stack, 0), halve_lanes(LANES, size_z1, chunk * LANES // 2)
        )
        k_one = part if k_one is None else k_one + part
    assert tile_x1 // 2 * (size_z1 // 2) <= LANES
    block = None
    for pair in range(tile_x1 // 2):
        at = 2 * pair * tile_y1
        paired_one[...] = k_one[at : at + tile_y1] + k_one[at + tile_y1 : at + 2 * tile_y1]
        piece = (
            paired_one[pl.ds(0, tile_y1 // 2, stride=2)] + paired_one[pl.ds(1, tile_y1 // 2, stride=2)]
        )
        part = times_right(piece, halve_lanes(size_z1, LANES, pair * size_z1 // 2))
        block = part if block is None else block + part
    block = (0.125 * 0.125) * block
    for device in range(blocks.shape[0]):
        blocks[device] = block


def fine_down(
    window, from_near, from_far,
    v_zero, forcing_out, cx, cy, cz, weight, level_one, blocks, near, far,
    conc_rim, forcing_rim, kappa_rim, once, diag, paired, outer,
    k_one, f_one, u_one, v_one, cx1, cy1, cz1, w1, d1, paired_one, packed,
):
    from_low, from_high = by_side("tx", from_near, from_far)
    _, tile_x, rows, size_z = window.shape
    tile_y = rows - 2 * RY
    top = RY + tile_y
    planes = tile_x + 2 * RX
    rims = (conc_rim, forcing_rim, kappa_rim)
    depths = (3, 2, 4)
    for which, rim in enumerate(rims):
        fill = jnp.full((rows, size_z), 1.0 if which == 2 else 0.0, F32)
        for x in range(2 * depths[which]):
            rim[x] = fill

    def place(which, layer, low):
        return depths[which] - layer if low else depths[which] + layer - 1

    for message, low in ((from_low, True), (from_high, False)):
        for at, (which, layer) in enumerate(BASE_PLANES):
            rims[which][place(which, layer, low), RY:top] = message[at]
        at = 0
        for which, layer, reach in EXTRA_ROWS:
            rim, x = rims[which], place(which, layer, low)
            rim[x, RY - reach : RY] = message[len(BASE_PLANES), at : at + reach]
            at += reach
            rim[x, top : top + reach] = message[len(BASE_PLANES), at : at + reach]
            at += reach

    def stacked(which):
        depth = depths[which]
        whole = [(rims[which], x) for x in range(depth)]
        whole += [(window.at[which], x) for x in range(tile_x)]
        whole += [(rims[which], depth + x) for x in range(depth)]
        return Planes(RX - depth, whole)

    conc, forcing, kappa = stacked(0), stacked(1), stacked(2)
    cx = kept(cx, RX - 2, (outer, 0), (outer, 1))
    cy = kept(cy, RX - 1, (outer, 2), (outer, 3))
    cz = kept(cz, RX - 1, (outer, 4), (outer, 5))
    weight = kept(weight, RX - 1, (outer, 6), (outer, 7))
    v_out = kept(v_zero, RX - 1)
    plane_setup(kappa, cx, cy, cz, weight, diag, 1.0, 1, planes - 1)
    plane_sweep(conc, once, forcing, cx, cy, cz, weight, 1, planes - 1)
    plane_sweep(once, v_out, forcing, cx, cy, cz, weight, 2, planes - 2)
    for x in range(RX - 1, planes - RX + 1):
        forcing_out[x - RX + 1] = forcing[x]
    chunks = size_z // LANES
    size_z1 = size_z // 2
    to_half = [halve_lanes(LANES, size_z1, chunk * LANES // 2) for chunk in range(chunks)]
    tile_x1, tile_y1 = tile_x // 2, tile_y // 2

    def put(pair, total):
        for chunk in range(chunks):
            paired[chunk, pair, 0:rows] = total[:, chunk * LANES : (chunk + 1) * LANES]

    def narrowed(pairs, start, count):
        result = None
        for chunk in range(chunks):
            stack = [
                paired[chunk, pair, pl.ds(start, count, stride=2)]
                + paired[chunk, pair, pl.ds(start + 1, count, stride=2)]
                for pair in range(pairs)
            ]
            part = times_right(jnp.concatenate(stack, 0), to_half[chunk])
            result = part if result is None else result + part
        return 0.125 * result

    wide = paired.shape[2] // 2
    planes1 = tile_x1 + 2 * RC
    if 2 * wide > rows:
        for chunk in range(chunks):
            for pair in range(planes1):
                paired[chunk, pair, rows:] = jnp.ones((2 * wide - rows, LANES), F32)
    for pair in range(planes1):
        x = RX - 2 * RC + 2 * pair
        put(pair, kappa[x] + kappa[x + 1])
    coarse = narrowed(planes1, 0, wide)
    for pair in range(planes1):
        k_one[pair] = coarse[pair * wide : (pair + 1) * wide]
    plane_setup(k_one, cx1, cy1, cz1, w1, d1, 0.25, 1, planes1 - 1)

    for pair in range(tile_x1):
        total = None
        for x in (RX + 2 * pair, RX + 2 * pair + 1):
            part = forcing[x] + neighbours(v_out, cx, cy, cz, x) - diag[x] * v_out[x]
            total = part if total is None else total + part
        put(pair, total)
    forcing_one = narrowed(tile_x1, RY, tile_y1)

    low, high = RC, RC + tile_y1
    nothing = jnp.zeros((wide, size_z1), F32)
    for x in range(planes1):
        f_one[x] = nothing
        if x in (0, planes1 - 1):
            v_one[x] = nothing
    for x in (0, 1, planes1 - 2, planes1 - 1):
        u_one[x] = nothing
    for x in range(tile_x1):
        f = forcing_one[x * tile_y1 : (x + 1) * tile_y1]
        f_one[x + RC, low:high] = f
        u_one[x + RC] = w1[x + RC] * f_one[x + RC]
        level_one[0, x] = f
        level_one[1, x] = u_one[x + RC, low:high]
        level_one[2, x] = k_one[x + RC, low:high]
    plane_sweep(u_one, v_one, f_one, cx1, cy1, cz1, w1, 1, planes1 - 1)
    pairs1 = planes1 // 2
    for pair in range(pairs1):
        total = None
        for x in (2 * pair, 2 * pair + 1):
            if x == 0:
                part = cx1[0] * v_one[1]
            elif x == planes1 - 1:
                part = cx1[x - 1] * v_one[x - 1]
            else:
                part = f_one[x] + neighbours(v_one, cx1, cy1, cz1, x) - d1[x] * v_one[x]
            total = part if total is None else total + part
        paired_one[pair] = total
    for pair in range(pairs1):
        packed[pair] = (
            paired_one[pair, pl.ds(0, ROWS, stride=2)] + paired_one[pair, pl.ds(1, ROWS, stride=2)]
        )
    half_pairs = pairs1 // 2
    result = times_right(
        jnp.concatenate([packed[p] for p in range(half_pairs)], 0), halve_lanes(size_z1, size_z1)
    ) + times_right(
        jnp.concatenate([packed[half_pairs + p] for p in range(half_pairs)], 0),
        halve_lanes(size_z1, size_z1, size_z1 // 2),
    )
    used = tile_y1 // 2 + RC
    block = jnp.concatenate([result[p * ROWS : p * ROWS + used] for p in range(half_pairs)], 0)
    block = 0.125 * block
    for part in range(blocks.shape[1]):
        piece = block[part * SHORT : (part + 1) * SHORT]
        for device in range(blocks.shape[0]):
            blocks[device, part] = piece

    def pack(to_low, to_high):
        for to, rows1, row0 in (
            (to_low, slice(0, R1), RY + 1),
            (to_high, slice(tile_y1 - R1, tile_y1), top - 2),
        ):
            for which in range(3):
                for x in range(tile_x1):
                    flat_row = which * tile_x1 * R1 + x * R1
                    to[flat_row // ROWS, flat_row % ROWS : flat_row % ROWS + R1] = level_one[
                        which, x, rows1
                    ]
            start = 3 * tile_x1 * R1 // ROWS
            for x in range(tile_x):
                row = v_zero[x + 1, row0 : row0 + 1]
                for chunk in range(chunks):
                    to[start + chunk, x : x + 1] = row[:, chunk * LANES : (chunk + 1) * LANES]

    on_sides("ty", near, far, pack)


def reach_of(layer):
    return R1 + 1 - layer


def middle(level_one, v_zero, from_near, from_far, window, near, far):
    from_low, from_high = by_side("ty", from_near, from_far)
    _, tile_x1, tile_y1, _ = level_one.shape
    planes, rows, size_z = v_zero.shape
    top1 = R1 + tile_y1
    for which in range(3):
        for x in range(tile_x1):
            flat_row = which * tile_x1 * R1 + x * R1
            at, sub = flat_row // ROWS, flat_row % ROWS
            window[which, x, R1:top1] = level_one[which, x]
            window[which, x, 0:R1] = from_low[at, sub : sub + R1]
            window[which, x, top1:] = from_high[at, sub : sub + R1]
    chunks = size_z // LANES
    top = rows - RY

    def pack(to_low, to_high):
        for to, low in ((to_low, True), (to_high, False)):
            at = 0
            for which in (0, 2):
                for layer in range(1, R1 + 1):
                    x = layer - 1 if low else tile_x1 - layer
                    outer = 1 if which == 0 and layer == R1 else which
                    to[at] = window[outer, x, R1:top1]
                    at += 1
            loose = at * ROWS
            for which in (0, 2):
                for layer in range(1, R1 + 1):
                    x = layer - 1 if low else tile_x1 - layer
                    outer = 1 if which == 0 else which
                    for distance in range(1, reach_of(layer) + 1):
                        source = outer if distance == reach_of(layer) else which
                        for row in (R1 - distance, top1 + distance - 1):
                            to[loose // ROWS, loose % ROWS : loose % ROWS + 1] = window[
                                source, x, row : row + 1
                            ]
                            loose += 1
            second, first = (2, 1) if low else (planes - 3, planes - 2)
            for row in (RY - 1, top):
                for chunk in range(chunks):
                    lanes = slice(chunk * LANES, (chunk + 1) * LANES)
                    to[loose // ROWS, loose % ROWS : loose % ROWS + 1] = v_zero[first, row : row + 1, lanes]
                    loose += 1
            at = -(-loose // ROWS)
            for chunk in range(chunks):
                lanes = slice(chunk * LANES, (chunk + 1) * LANES)
                for half in range((top - RY) // ROWS):
                    to[at] = v_zero[second, RY + half * ROWS : RY + (half + 1) * ROWS, lanes]
                    at += 1

    on_sides("tx", near, far, pack)


def middle_tiles(tile_y, chunks):
    loose = 2 * sum(2 * reach_of(layer) for layer in range(1, R1 + 1)) + 2 * chunks
    return 2 * R1 + -(-loose // ROWS) + chunks * tile_y // ROWS


class Grid:
    def __init__(self, sizes, strides, scales, rows, lanes):
        self.sizes = sizes
        self.strides = strides
        self.scales = scales
        self.rows = rows
        self.lanes = lanes
        self.ratios = tuple(2 if extent % 2 == 0 else 1 for extent in sizes)
        self.cells = sizes[0] * sizes[1] * sizes[2]
        self.exact = self.cells <= 64 or self.ratios == (1, 1, 1)

    def coarser(self):
        sizes = tuple(extent // ratio for extent, ratio in zip(self.sizes, self.ratios))
        scales = tuple(s / (ratio * ratio) for s, ratio in zip(self.scales, self.ratios))
        strides = tuple(s * ratio for s, ratio in zip(self.strides, self.ratios[1:]))
        return Grid(sizes, strides, scales, self.rows, self.lanes)


def next_plane(v):
    return v if v.shape[0] == 1 else jnp.concatenate([v[1:], v[:1]], 0)


def last_plane(v):
    return v if v.shape[0] == 1 else jnp.concatenate([v[-1:], v[:-1]], 0)


def restrict_whole(v, grid):
    if grid.ratios[0] == 2:
        v = jnp.concatenate(
            [v[2 * x : 2 * x + 1] + v[2 * x + 1 : 2 * x + 2] for x in range(grid.sizes[0] // 2)], 0
        )
    for axis in (1, 2):
        if grid.ratios[axis] == 2:
            step = grid.strides[axis - 1]
            even = mod(div(iota(v.shape, axis), step), 2) == 0
            v = v + jnp.where(even, ahead(v, axis, step), back(v, axis, step))
    return (1.0 / (grid.ratios[0] * grid.ratios[1] * grid.ratios[2])) * v


def prolong_whole(v, grid):
    if grid.ratios[0] == 1:
        return v
    return jnp.concatenate([v[x // 2 : x // 2 + 1] for x in range(grid.sizes[0])], 0)


def whole_operator(kappa, grid):
    half_x, half_y, half_z = (0.5 * s for s in grid.scales)
    step_y, step_z = grid.strides
    cx = half_x * (kappa + next_plane(kappa))
    cy = half_y * (kappa + ahead(kappa, 1, step_y))
    cz = half_z * (kappa + ahead(kappa, 2, step_z))
    diag = mass_rate + cx + last_plane(cx)
    diag = diag + (cy + back(cy, 1, step_y)) + (cz + back(cz, 2, step_z))
    return cx, cy, cz, diag, relax_weight / diag


def whole_neighbours(v, operator, grid):
    cx, cy, cz = operator[:3]
    step_y, step_z = grid.strides
    total = cx * next_plane(v) + last_plane(cx * v)
    total = total + (cy * ahead(v, 1, step_y) + back(cy * v, 1, step_y))
    return total + (cz * ahead(v, 2, step_z) + back(cz * v, 2, step_z))


def whole_sweep(v, forcing, operator, grid):
    return (1.0 - relax_weight) * v + operator[4] * (forcing + whole_neighbours(v, operator, grid))


class ExactSolve:
    def __init__(self, grid, kappa=None, inverse=None):
        size_x, size_y, size_z = grid.sizes
        self.grid = grid
        self.across = across = size_x * size_y
        _, step_z = grid.strides
        self.period = period = size_z * step_z
        cells = grid.cells
        padded = -(-cells // ROWS) * ROWS
        assert across <= step_z and 2 * period <= grid.lanes
        shape = (padded, grid.lanes)
        i, j = iota(shape, 0), iota(shape, 1)
        self.i, self.j = i, j
        if kappa is None:
            self.inverse = inverse
            return

        def places_of_row(n):
            sub = mod(n, across)
            return div(sub, size_y), mod(sub, size_y), div(n, across)

        def places_of_lane(n):
            n = mod(n, period)
            sub = mod(n, step_z)
            return div(sub, size_y), mod(sub, size_y), div(n, step_z)

        at_i, at_j = places_of_row(i), places_of_lane(j)
        live = (mod(j, step_z) < across) & (i < cells)
        same = (at_i[0] == at_j[0]) & (at_i[1] == at_j[1]) & (at_i[2] == at_j[2]) & live
        left = j < period
        factor = jnp.zeros(shape, F32)
        for d in range(3):
            equal = [at_i[other] == at_j[other] for other in range(3) if other != d]
            for step in (1, grid.sizes[d] - 1):
                hit = mod(at_i[d] + step, grid.sizes[d]) == at_j[d]
                factor = factor + jnp.where(
                    hit & equal[0] & equal[1], F32(0.5 * grid.scales[d]), F32(0.0)
                )
        k_row = self.as_row(kappa)
        k_column = jnp.sum(jnp.where(same & left, k_row, 0.0), axis=1, keepdims=True)
        coupled = jnp.where(live & left, factor * (k_column + k_row), 0.0)
        diag = mass_rate + jnp.sum(coupled, axis=1, keepdims=True)
        matrix = jnp.where(same & left, diag - coupled, -coupled)
        matrix = jnp.where(left, matrix, jnp.where(same, F32(1.0), F32(0.0)))
        for n in range(cells):
            lane = (n // across) * step_z + n % across
            pivot_row = matrix[n : n + 1] / matrix[n : n + 1, lane : lane + 1]
            column = matrix[:, lane : lane + 1]
            matrix = jnp.where(i == n, pivot_row, matrix - column * pivot_row)
        self.inverse = jnp.where((j >= period) & (j < 2 * period) & live, matrix, 0.0)

    def as_row(self, v):
        grid = self.grid
        size_x, size_y, _ = grid.sizes
        step_y, step_z = grid.strides
        sub = mod(iota((1, grid.lanes), 1), step_z)
        result = jnp.zeros((1, grid.lanes), F32)
        for x in range(size_x):
            for y in range(size_y):
                row = v[x, y * step_y : y * step_y + 1]
                result = jnp.where(sub == x * size_y + y, row, result)
        return result

    def solve(self, forcing):
        grid = self.grid
        size_x, size_y, _ = grid.sizes
        step_y, step_z = grid.strides
        solved = jnp.sum(self.inverse * self.as_row(forcing), axis=1, keepdims=True)
        at_z = div(mod(self.j, self.period), step_z)
        spread = jnp.where(div(self.i, self.across) == at_z, solved, 0.0)
        planes = []
        for x in range(size_x):
            rows = []
            for y in range(size_y):
                mine = mod(self.i, self.across) == x * size_y + y
                row = jnp.sum(jnp.where(mine, spread, 0.0), axis=0, keepdims=True)
                rows.append(jnp.broadcast_to(row, (step_y, grid.lanes)))
            planes.append(jnp.concatenate(rows, 0)[None])
        return jnp.concatenate(planes, 0)


def levels_of(counts, tile_sizes):
    sizes = tuple(count * extent for count, extent in zip(counts, tile_sizes)) + tile_sizes[2:]
    grid = Grid(sizes, (1, 1), (0.0625, 0.0625, 0.0625), sizes[1], LANES)
    grids = [grid]
    while not grid.exact:
        grid = grid.coarser()
        grids.append(grid)
    return grids


class Operator:
    def __init__(self, ref):
        self.ref = ref

    def __getitem__(self, part):
        if isinstance(part, slice):
            return [self.ref[p] for p in range(*part.indices(5))]
        return self.ref[part]


def prepare(counts, grids, blocks, _, *outputs):
    count_x, count_y = counts
    planes, rows, _ = grids[0].sizes
    half_x, half_y = planes // count_x, rows // count_y
    size_z2 = grids[0].sizes[2]
    assert half_x * size_z2 == LANES and half_x == 2 and ROWS % half_y == 0
    share = ROWS // half_y
    kappa = [[None] * (rows // ROWS) for _ in range(planes)]
    lane = iota((ROWS, LANES), 1)
    for tx in range(count_x):
        for group in range(rows // ROWS):
            pieces = [blocks[tx * count_y + group * share + n] for n in range(share)]
            piece = jnp.concatenate(pieces, 0)
            turned = pltpu.roll(piece, size_z2, 1)
            for p in range(half_x):
                mine = (lane < size_z2) == (p == 0)
                kappa[tx * half_x + p][group] = jnp.where(mine, piece, turned)
    kappa = jnp.concatenate([jnp.concatenate(groups, 0)[None] for groups in kappa], 0)
    kappas = [kappa]
    for grid in grids[:-1]:
        kappas.append(restrict_whole(kappas[-1], grid))
    outputs[-1][...] = ExactSolve(grids[-1], kappas[-1]).inverse
    for number, grid in enumerate(grids[:-1]):
        for part, value in enumerate(whole_operator(kappas[number], grid)):
            outputs[number][part] = value


def solve_whole(forcing, levels, exact):
    if not levels:
        return exact.solve(forcing)
    grid, operator = levels[0]
    v = operator[4] * forcing
    v = whole_sweep(v, forcing, operator, grid)
    residual = forcing + whole_neighbours(v, operator, grid) - operator[3] * v
    v = v + prolong_whole(solve_whole(restrict_whole(residual, grid), levels[1:], exact), grid)
    for _ in range(2):
        v = whole_sweep(v, forcing, operator, grid)
    return v


def assemble(blocks, count_x, count_y, half_x, half_y, size_z2):
    rows = count_y * half_y
    groups = rows // ROWS
    planes = count_x * half_x
    assert rows % ROWS == 0
    used = half_y + RC
    sub = iota((ROWS, LANES), 0)
    lane = iota((ROWS, LANES), 1)
    nothing = jnp.zeros((ROWS, LANES), F32)
    forcing = [[nothing] * groups for _ in range(planes)]
    half_pairs = (half_x + RC) // 2
    ring = RC // 2
    for tx in range(count_x):
        for ty in range(count_y):
            for p in range(half_pairs):
                tile, base = p * used // SHORT, p * used % SHORT
                assert base + used <= 2 * SHORT == ROWS
                source = tx * count_y + ty
                piece = jnp.concatenate([blocks[source, tile], blocks[source, tile + 1]], 0)
                start = (ty * half_y - ring) % rows
                group, offset = start // ROWS, start % ROWS
                shift = (offset - base) % ROWS
                piece = pltpu.roll(piece, shift, 0) if shift else piece
                turned = pltpu.roll(piece, size_z2, 1)
                for half in range(2):
                    moved = jnp.where((lane < size_z2) == (half == 0), piece, turned)
                    x = (tx * half_x - ring + half * half_pairs + p) % planes
                    at = group
                    mine = (sub >= offset) & (sub < offset + used)
                    forcing[x][at] = forcing[x][at] + jnp.where(mine, moved, 0.0)
                    if offset + used > ROWS:
                        at = (group + 1) % groups
                        mine = sub < offset + used - ROWS
                        forcing[x][at] = forcing[x][at] + jnp.where(mine, moved, 0.0)
    return jnp.concatenate([jnp.concatenate(groups, 0)[None] for groups in forcing], 0)


def coarse_up(
    counts, grids, blocks, window_one, one_near, one_far, row_near, row_far,
    v_zero, forcing0, cx, cy, cz, weight, *rest,
):
    prepared, rest = rest[: len(grids)], rest[len(grids) :]
    (
        out, mixed_low, mixed_high, kappa_low, kappa_high, first_low, first_high,
        v_one, cx1, cy1, cz1, w1, one_a, one_b, zero_a, zero_b,
    ) = rest
    count_x, count_y = counts
    one_low, one_high = by_side("tx", one_near, one_far)
    row_low, row_high = by_side("ty", row_near, row_far)
    _, tile_x1, rows1, size_z1 = window_one.shape
    tile_y1 = rows1 - 2 * R1
    top1 = R1 + tile_y1
    half_x, half_y, size_z2 = tile_x1 // 2, tile_y1 // 2, size_z1 // 2
    sizes = grids[0].sizes
    forcing2 = assemble(blocks, count_x, count_y, half_x, half_y, size_z2)
    levels = [
        (grid, Operator(prepared[number])) for number, grid in enumerate(grids[:-1])
    ]
    exact = ExactSolve(grids[-1], inverse=prepared[-1][...])

    planes1 = tile_x1 + 2 * R1
    for message, mixed, kappa_rim, low in (
        (one_low, mixed_low, kappa_low, True), (one_high, mixed_high, kappa_high, False)
    ):
        at, loose = 0, 2 * R1 * ROWS
        for rim, fill in ((mixed, 0.0), (kappa_rim, 1.0)):
            for layer in range(1, R1 + 1):
                x = R1 - layer if low else layer - 1
                rim[x] = jnp.full((rows1, size_z1), fill, F32)
                rim[x, R1:top1] = message[at]
                at += 1
                for distance in range(1, reach_of(layer) + 1):
                    for row in (R1 - distance, top1 + distance - 1):
                        rim[x, row : row + 1] = message[
                            loose // ROWS, loose % ROWS : loose % ROWS + 1
                        ]
                        loose += 1

    def stacked(low, which, high):
        whole = [(low, x) for x in range(R1)]
        whole += [(window_one.at[which], x) for x in range(tile_x1)]
        whole += [(high, x) for x in range(R1)]
        return Planes(0, whole)

    forcing1 = stacked(mixed_low, 0, mixed_high)
    kappa1 = stacked(kappa_low, 2, kappa_high)
    plane_setup(kappa1, cx1, cy1, cz1, w1, None, 0.25, 1, planes1 - 1)
    row = iota((rows1, size_z1), 0)
    for mixed, rim, low in ((mixed_low, first_low, True), (mixed_high, first_high, False)):
        for layer in range(1, R1 + 1):
            x = R1 - layer if low else layer - 1
            if layer == R1:
                rim[x] = mixed[x]
            else:
                reach = reach_of(layer) - 1
                inside = (row >= R1 - reach) & (row < top1 + reach)
                at = x if low else R1 + tile_x1 + x
                rim[x] = jnp.where(inside, w1[at] * mixed[x], mixed[x])
    start1 = stacked(first_low, 1, first_high)
    plane_sweep(start1, v_one, forcing1, cx1, cy1, cz1, w1, 1, planes1 - 1)

    solved = solve_whole(forcing2, levels, exact)
    solved = solved.reshape(sizes[0] * sizes[1], LANES)

    whole_x1, whole_y1 = 2 * sizes[0], 2 * sizes[1]
    start_x = lax.axis_index("tx") * tile_x1 + (whole_x1 - R1)
    start_y = lax.axis_index("ty") * tile_y1 + (whole_y1 - R1)
    row = iota((planes1 * rows1, 1), 0)
    at_x = mod(div(row, rows1) + start_x, whole_x1)
    at_y = mod(mod(row, rows1) + start_y, whole_y1)
    target = div(at_x, 2) * sizes[1] + div(at_y, 2)
    left = ones_where(iota((planes1 * rows1, sizes[0] * sizes[1]), 1) == target)
    shape = (LANES, size_z1)
    right = ones_where(iota(shape, 0) == div(iota(shape, 1), 2))
    raised = times_right(times_left(left, solved), right)
    for x in range(1, planes1 - 1):
        one_a[x] = v_one[x] + raised[x * rows1 : (x + 1) * rows1]
    plane_sweep(one_a, one_b, forcing1, cx1, cy1, cz1, w1, 2, planes1 - 2)
    plane_sweep(one_b, one_a, forcing1, cx1, cy1, cz1, w1, 3, planes1 - 3)

    planes, rows, size_z = zero_a.shape
    v_zero, forcing0 = kept(v_zero, RX - 1), kept(forcing0, RX - 1)
    cx, cy, cz, weight = kept(cx, RX - 2), kept(cy, RX - 1), kept(cz, RX - 1), kept(weight, RX - 1)
    first, last = R1 - 1, planes1 - R1 + 1
    stack = jnp.concatenate([one_a[x] for x in range(first, last)], 0)
    count = last - first
    shape = (count * rows, count * rows1)
    out_row, in_row = iota((count * rows, 1), 0), iota(shape, 1)
    target = div(out_row, rows) * rows1 + div(mod(out_row, rows) + (2 * R1 - RY), 2)
    left = ones_where(in_row == target)
    shape = (size_z1, size_z)
    right = ones_where(iota(shape, 0) == div(iota(shape, 1), 2))
    raised = times_right(times_left(left, stack), right)
    chunks = size_z // LANES
    top = rows - RY
    for x in range(RX - 1, planes - RX + 1):
        zero_b[x] = v_zero[x]
    for rim_x in (RX - 2, planes - RX + 1):
        zero_b[rim_x] = jnp.zeros((rows, size_z), F32)
    for x in range(planes - 2 * RX):
        at = 3 * tile_x1 * R1 // ROWS
        for chunk in range(chunks):
            lanes = slice(chunk * LANES, (chunk + 1) * LANES)
            zero_b[RX + x, RY - 2 : RY - 1, lanes] = row_low[at + chunk, x : x + 1]
            zero_b[RX + x, top + 1 : top + 2, lanes] = row_high[at + chunk, x : x + 1]
    for message, second, nearest in (
        (one_low, RX - 2, RX - 1), (one_high, planes - RX + 1, planes - RX)
    ):
        loose = 2 * R1 * ROWS + 2 * sum(2 * reach_of(layer) for layer in range(1, R1 + 1))
        for r in (RY - 1, top):
            for chunk in range(chunks):
                lanes = slice(chunk * LANES, (chunk + 1) * LANES)
                zero_b[nearest, r : r + 1, lanes] = message[
                    loose // ROWS, loose % ROWS : loose % ROWS + 1
                ]
                loose += 1
        at = -(-loose // ROWS)
        for chunk in range(chunks):
            lanes = slice(chunk * LANES, (chunk + 1) * LANES)
            for half in range((top - RY) // ROWS):
                zero_b[second, RY + half * ROWS : RY + (half + 1) * ROWS, lanes] = message[at]
                at += 1
    for x in range(RX - 2, planes - RX + 2):
        at = (x - RX + 2 * R1) // 2 - first
        zero_a[x] = zero_b[x] + raised[at * rows : (at + 1) * rows]
    plane_sweep(zero_a, zero_b, forcing0, cx, cy, cz, weight, RX - 1, planes - RX + 1)
    plane_sweep(zero_b, zero_a, forcing0, cx, cy, cz, weight, RX, planes - RX)
    for x in range(planes - 2 * RX):
        out[x] = zero_a[x + RX, RY:top]


VM = pl.BlockSpec(memory_space=pltpu.VMEM)
IN_PLACE = pl.BlockSpec(memory_space=pltpu.HBM)


def call(kernel, operands, outputs, scratch, spec=VM):
    def typed(output):
        return output if isinstance(output, jax.ShapeDtypeStruct) else jax.ShapeDtypeStruct(output, F32)

    return pl.pallas_call(
        kernel,
        in_specs=[spec] * len(operands),
        out_specs=[VM] * len(outputs),
        out_shape=[typed(output) for output in outputs],
        scratch_shapes=[pltpu.VMEM(s, F32) if isinstance(s, tuple) else s for s in scratch],
        compiler_params=pltpu.CompilerParams(vmem_limit_bytes=24 * 1024 * 1024),
    )(*operands)


def exchange(near, far, axis):
    count = lax.axis_size(axis)
    assert count % 2 == 0
    partner = [(i, i ^ 1) for i in range(count)]
    other = [(i, (i - 1 if i % 2 == 0 else i + 1) % count) for i in range(count)]
    from_far = lax.ppermute(far, axis, other)
    from_near = lax.ppermute(near, axis, partner)
    return from_near, from_far


def to_everyone(blocks):
    return lax.all_to_all(blocks, ("tx", "ty"), 0, 0)


def cycle(concentration, source, material):
    tile_x, tile_y, size_z = concentration.shape
    chunks = size_z // LANES
    counts = lax.axis_size("tx"), lax.axis_size("ty")
    everyone = counts[0] * counts[1]
    rows = tile_y + 2 * RY
    message = (tile_x + 1, ROWS, size_z)
    *inputs, near, far = call(
        edges,
        tuple(
            pltpu.with_memory_space_constraint(v, pltpu.HBM)
            for v in (concentration, source, material)
        ),
        tuple(jax.ShapeDtypeStruct(v.shape, v.dtype) for v in (concentration, source, material))
        + (message, message),
        (pltpu.SemaphoreType.DMA((3,)),),
        IN_PLACE,
    )
    from_near, from_far = exchange(near, far, "ty")
    message = (len(BASE_PLANES) + 1, tile_y, size_z)
    window, near, far = call(
        sides, (*inputs, from_near, from_far), ((3, tile_x, rows, size_z), message, message), ()
    )
    from_near, from_far = exchange(near, far, "tx")

    zero = (tile_x + 2 * RX, rows, size_z)
    inner = (tile_x + 2, rows, size_z)
    one_tile = (tile_x // 2, tile_y // 2, size_z // 2)
    two_tile = tuple(extent // 2 for extent in one_tile)
    grids = levels_of(counts, two_tile)
    (kappa_blocks,) = call(
        shrink,
        (window,),
        ((everyone, two_tile[1], LANES),),
        ((one_tile[0], rows, LANES), one_tile[1:]),
    )
    kappa_blocks = to_everyone(kappa_blocks)

    wide = -(-rows // (2 * ROWS)) * ROWS
    small = (one_tile[0] + 2 * RC, wide, one_tile[2])
    pairs1 = small[0] // 2
    short = pairs1 // 2 * (two_tile[1] + RC) // SHORT
    assert pairs1 // 2 * (two_tile[1] + RC) % SHORT == 0
    message = (3 * one_tile[0] * R1 // ROWS + chunks, ROWS, LANES)
    assert one_tile[2] == LANES and tile_x <= ROWS and one_tile[1] == ROWS
    v_zero, forcing0, cx, cy, cz, weight, level_one, blocks, near, far = call(
        fine_down,
        (window, from_near, from_far),
        (inner, inner, (tile_x + 3, rows, size_z), inner, inner, inner)
        + ((3,) + one_tile, (everyone, short, SHORT, LANES), message, message),
        (
            (6, rows, size_z),
            (4, rows, size_z),
            (8, rows, size_z),
            zero,
            zero,
            (chunks, max(small[0], tile_x), 2 * wide, LANES),
            (8, rows, size_z),
        )
        + (small,) * 9
        + ((pairs1, wide, one_tile[2]), (pairs1, ROWS, one_tile[2])),
    )
    row_near, row_far = exchange(near, far, "ty")
    blocks = to_everyone(blocks)
    rows1 = one_tile[1] + 2 * R1
    message = (middle_tiles(tile_y, chunks), ROWS, LANES)
    window_one, near, far = call(
        middle,
        (level_one, v_zero, row_near, row_far),
        ((3, one_tile[0], rows1, one_tile[2]), message, message),
        (),
    )
    one_near, one_far = exchange(near, far, "tx")
    lattice = grids[0].sizes[1], LANES
    prepared = call(
        functools.partial(prepare, counts, grids),
        (kappa_blocks, window_one),
        tuple((5, grid.sizes[0]) + lattice for grid in grids[:-1])
        + ((-(-grids[-1].cells // ROWS) * ROWS, LANES),),
        (),
    )
    one = (one_tile[0] + 2 * R1, rows1, one_tile[2])
    rim = (R1,) + one[1:]
    (updated,) = call(
        functools.partial(coarse_up, counts, grids),
        (blocks, window_one, one_near, one_far, row_near, row_far)
        + (v_zero, forcing0, cx, cy, cz, weight, *prepared),
        (concentration.shape,),
        (rim,) * 6 + (one,) * 7 + (zero, zero),
    )
    return updated


def solution(mesh):
    placed = (P("tx", "ty", None), P("tx", "ty", None), P("tx", "ty", None))
    return jax.shard_map(
        cycle, mesh=mesh, in_specs=placed, out_specs=P("tx", "ty", None), check_vma=False
    )
```

```python
import functools

import jax
import jax.numpy as jnp
from jax import lax
from jax.experimental import pallas as pl
from jax.experimental.pallas import tpu as pltpu
from jax.sharding import PartitionSpec as P


mass_rate = 0.001
relax_weight = 0.8
diffusivities = (0.15, 0.3, 0.5, 0.8, 1.2, 2.0, 3.2, 5.0)
LANES = 128
ROWS = 8
SHORT = 4
RX = 2
RY = 4
R1 = 4
RC = 2
F32 = jnp.float32
BF16 = jnp.bfloat16


def lookup(material):
    result = jnp.zeros(material.shape, F32)
    for slot_id, coeff_value in enumerate(diffusivities):
        result = jnp.where(material == slot_id, F32(coeff_value), result)
    return result


class Planes:
    def __init__(self, first, planes):
        self.first = first
        self.planes = planes

    def __getitem__(self, x):
        ref, index = self.planes[x - self.first]
        return ref[index]

    def __setitem__(self, x, value):
        ref, index = self.planes[x - self.first]
        ref[index] = value


def kept(ref, first):
    return Planes(first, [(ref, x) for x in range(ref.shape[0])])


def is_even(axis):
    return lax.rem(lax.axis_index(axis), 2) == 0


def on_sides(axis, near, far, body):
    @pl.when(is_even(axis))
    def _():
        body(far, near)

    @pl.when(jnp.logical_not(is_even(axis)))
    def _():
        body(near, far)


class Picked:
    def __init__(self, flag, when_true, when_false):
        self.flag = flag
        self.when_true = when_true
        self.when_false = when_false

    def __getitem__(self, index):
        first, second = self.when_true[index], self.when_false[index]
        flag = jnp.where(self.flag, jnp.int32(1), jnp.int32(0))
        return jnp.where(jnp.full(first.shape, flag) == 1, first, second)


def by_side(axis, near, far):
    even = is_even(axis)
    return Picked(even, far, near), Picked(even, near, far)


def iota(shape, dim):
    return lax.broadcasted_iota(jnp.int32, shape, dim)


def div(a, b):
    return lax.div(a, jnp.full_like(a, b))


def mod(a, b):
    return lax.rem(a, jnp.full_like(a, b))


def ones_where(mask):
    return jnp.where(mask, F32(1.0), F32(0.0)).astype(BF16)


def three_terms(x):
    high = x.astype(BF16)
    rest = x - high.astype(F32)
    middle = rest.astype(BF16)
    low = (rest - middle.astype(F32)).astype(BF16)
    return high, middle, low


def times_right(x, selector):
    parts = [jnp.dot(part, selector, preferred_element_type=F32) for part in three_terms(x)]
    return parts[0] + (parts[1] + parts[2])


def times_left(selector, x):
    parts = [jnp.dot(selector, part, preferred_element_type=F32) for part in three_terms(x)]
    return parts[0] + (parts[1] + parts[2])


def back(v, axis, step=1):
    return pltpu.roll(v, step, axis)


def ahead(v, axis, step=1):
    return pltpu.roll(v, v.shape[axis] - step, axis)


def halve_lanes(fine, coarse, start=0):
    shape = (fine, coarse)
    return ones_where(div(iota(shape, 0), 2) + start == iota(shape, 1))


def plane_setup(kappa, cx, cy, cz, weight, diag, scale, first, last):
    half = 0.5 * scale
    for x in range(first - 1, last):
        cx[x] = half * (kappa[x] + kappa[x + 1])
    for x in range(first, last):
        k = kappa[x]
        y_part = half * (k + ahead(k, 0))
        z_part = half * (k + ahead(k, 1))
        cy[x] = y_part
        cz[x] = z_part
        d = mass_rate + cx[x] + cx[x - 1] + y_part + back(y_part, 0) + z_part + back(z_part, 1)
        weight[x] = relax_weight / d
        if diag is not None:
            diag[x] = d


def in_plane(here, cy, cz, x):
    y_part = cy[x]
    z_part = cz[x]
    total = y_part * ahead(here, 0) + back(y_part * here, 0)
    return total + (z_part * ahead(here, 1) + back(z_part * here, 1))


def neighbours(v, cx, cy, cz, x):
    return (cx[x] * v[x + 1] + cx[x - 1] * v[x - 1]) + in_plane(v[x], cy, cz, x)


def plane_sweep(v, out, forcing, cx, cy, cz, weight, first, last):
    for x in range(first, last):
        out[x] = (1.0 - relax_weight) * v[x] + weight[x] * (forcing[x] + neighbours(v, cx, cy, cz, x))


def edges(conc_in, source_in, material_in, conc, source, material, to_low, to_high, arrived):
    copies = [
        pltpu.make_async_copy(whence, whither, arrived.at[n])
        for n, (whence, whither) in enumerate(
            ((conc_in, conc), (source_in, source), (material_in, material))
        )
    ]
    for copy in copies:
        copy.start()
    for copy in copies:
        copy.wait()
    tile_x, tile_y, _ = conc.shape
    for to, low in ((to_low, True), (to_high, False)):
        for x in range(tile_x):
            rows = slice(0, 4) if low else slice(tile_y - 4, tile_y)
            near = slice(0, 3) if low else slice(1, 4)
            pair = slice(0, 2) if low else slice(2, 4)
            c = conc[x, rows]
            f = mass_rate * c + source[x, rows]
            k = lookup(material[x, rows])
            to[x, 0:3] = c[near]
            to[x, 3:5] = f[pair]
            to[x, 5:8] = k[near]
            to[tile_x, x : x + 1] = k[3:4] if low else k[0:1]


def sides(conc, source, material, k_tile, from_low, from_high, window, to_low, to_high, swept):
    tile_x, tile_y, size_z = conc.shape
    top = RY + tile_y
    for x in range(tile_x):
        c = conc[x]
        window[0, x, RY:top] = c
        window[1, x, RY:top] = mass_rate * c + source[x]
        window[2, x, RY:top] = lookup(material[x])
        window[0, x, 0:1] = jnp.zeros((1, size_z), F32)
        window[0, x, 1:4] = from_low[x, 0:3]
        window[0, x, top : top + 3] = from_high[x, 0:3]
        window[0, x, top + 3 :] = jnp.zeros((1, size_z), F32)
        window[1, x, 0:2] = jnp.zeros((2, size_z), F32)
        window[1, x, 2:4] = from_low[x, 3:5]
        window[1, x, top : top + 2] = from_high[x, 3:5]
        window[1, x, top + 2 :] = jnp.zeros((2, size_z), F32)
        window[2, x, 0:1] = from_low[tile_x, x : x + 1]
        window[2, x, 1:4] = from_low[x, 5:8]
        window[2, x, top : top + 3] = from_high[x, 5:8]
        window[2, x, top + 3 :] = from_high[tile_x, x : x + 1]
    per_plane = tile_y // ROWS
    for to, low in ((to_low, True), (to_high, False)):

        def plane(layer):
            return layer - 1 if low else tile_x - layer

        def send(at, values):
            for n in range(per_plane):
                to[at + n] = values(n)

        for n, (which, layer) in enumerate(BASE_PLANES):
            send(
                n * per_plane,
                lambda n: window[which, plane(layer), RY + n * ROWS : RY + (n + 1) * ROWS],
            )
        first_sweep(window, plane(2), swept)
        at = len(BASE_PLANES) * per_plane
        send(at, lambda n: swept[RY + n * ROWS : RY + (n + 1) * ROWS])
        loose = (at + per_plane) * ROWS
        for which, layer, reach in EXTRA_ROWS:
            for start in (RY - reach, top):
                to[loose // ROWS, loose % ROWS : loose % ROWS + reach] = window[
                    which, plane(layer), start : start + reach
                ]
                loose += reach
        at = -(-loose // ROWS)
        to[at, :, 0 : size_z // 2] = k_tile[1 if low else k_tile.shape[0] - 2]
        to[at, :, size_z // 2 :] = jnp.zeros((ROWS, size_z - size_z // 2), F32)


def first_sweep(window, x, out):
    c, f, k = window[0, x], window[1, x], window[2, x]
    next_part = 0.5 * (k + window[2, x + 1])
    last_part = 0.5 * (k + window[2, x - 1])
    y_part = 0.5 * (k + ahead(k, 0))
    z_part = 0.5 * (k + ahead(k, 1))
    d = mass_rate + next_part + last_part
    d = d + y_part + back(y_part, 0) + z_part + back(z_part, 1)
    total = next_part * window[0, x + 1] + last_part * window[0, x - 1]
    total = total + (y_part * ahead(c, 0) + back(y_part * c, 0))
    total = total + (z_part * ahead(c, 1) + back(z_part * c, 1))
    out[...] = (1.0 - relax_weight) * c + (relax_weight / d) * (f + total)


BASE_PLANES = ((0, 1), (0, 2), (1, 1), (2, 1), (2, 2))
EXTRA_ROWS = ((0, 1, 2), (0, 2, 1), (1, 1, 1), (2, 1, 2), (2, 2, 2))


def plane_tiles(tile_y):
    loose = sum(2 * reach for _, _, reach in EXTRA_ROWS)
    return (len(BASE_PLANES) + 1) * tile_y // ROWS + -(-loose // ROWS) + 1


def shrink(material, k_tile, blocks, paired, paired_one):
    tile_x, tile_y, size_z = material.shape
    tile_x1, tile_y1, size_z1 = tile_x // 2, tile_y // 2, size_z // 2
    k_one = None
    for chunk in range(size_z // LANES):
        lanes = slice(chunk * LANES, (chunk + 1) * LANES)
        for pair in range(tile_x1):
            paired[pair] = lookup(material[2 * pair, :, lanes]) + lookup(
                material[2 * pair + 1, :, lanes]
            )
        stack = [
            paired[pair, pl.ds(0, tile_y1, stride=2)] + paired[pair, pl.ds(1, tile_y1, stride=2)]
            for pair in range(tile_x1)
        ]
        part = times_right(
            jnp.concatenate(stack, 0), halve_lanes(LANES, size_z1, chunk * LANES // 2)
        )
        k_one = part if k_one is None else k_one + part
    k_one = 0.125 * k_one
    for x in range(tile_x1):
        k_tile[x] = k_one[x * tile_y1 : (x + 1) * tile_y1]
    assert tile_x1 // 2 * (size_z1 // 2) <= LANES
    block = None
    for pair in range(tile_x1 // 2):
        at = 2 * pair * tile_y1
        paired_one[...] = k_one[at : at + tile_y1] + k_one[at + tile_y1 : at + 2 * tile_y1]
        piece = (
            paired_one[pl.ds(0, tile_y1 // 2, stride=2)] + paired_one[pl.ds(1, tile_y1 // 2, stride=2)]
        )
        part = times_right(piece, halve_lanes(size_z1, LANES, pair * size_z1 // 2))
        block = part if block is None else block + part
    block = 0.125 * block
    for device in range(blocks.shape[0]):
        blocks[device] = block


def fine_down(
    window, from_low, from_high,
    v_zero, forcing_out, cx, cy, cz, weight, level_one, blocks_out, to_low, to_high,
    conc_rim, forcing_rim, kappa_rim, once, diag, paired, blocks, left,
    k_one, f_one, u_one, v_one, cx1, cy1, cz1, w1, d1, paired_one, packed,
):
    _, tile_x, rows, size_z = window.shape
    tile_y = rows - 2 * RY
    top = RY + tile_y
    planes = tile_x + 2 * RX
    rims = (conc_rim, forcing_rim, kappa_rim)
    depths = (2, 1, 2)
    for which, rim in enumerate(rims):
        fill = jnp.full((rows, size_z), 1.0 if which == 2 else 0.0, F32)
        for x in range(2 * depths[which]):
            rim[x] = fill

    def place(which, layer, low):
        return depths[which] - layer if low else depths[which] + layer - 1

    per_plane = tile_y // ROWS
    last_tile = plane_tiles(tile_y) - 1
    for message, low in ((from_low, True), (from_high, False)):
        for at, (which, layer) in enumerate(BASE_PLANES):
            for n in range(per_plane):
                start = RY + n * ROWS
                rims[which][place(which, layer, low), start : start + ROWS] = message[
                    at * per_plane + n
                ]
        rim_x = 0 if low else planes - 1
        once[rim_x] = jnp.zeros((rows, size_z), F32)
        at = len(BASE_PLANES) * per_plane
        for n in range(per_plane):
            start = RY + n * ROWS
            once[rim_x, start : start + ROWS] = message[at + n]
        loose = (at + per_plane) * ROWS
        for which, layer, reach in EXTRA_ROWS:
            for start in (RY - reach, top):
                rims[which][place(which, layer, low), start : start + reach] = message[
                    loose // ROWS, loose % ROWS : loose % ROWS + reach
                ]
                loose += reach

    def stacked(which):
        depth = depths[which]
        whole = [(rims[which], x) for x in range(depth)]
        whole += [(window.at[which], x) for x in range(tile_x)]
        whole += [(rims[which], depth + x) for x in range(depth)]
        return Planes(RX - depth, whole)

    conc, forcing, kappa = stacked(0), stacked(1), stacked(2)
    cx, cy, cz, weight = kept(cx, RX - 2), kept(cy, RX - 1), kept(cz, RX - 1), kept(weight, RX - 1)
    v_out = kept(v_zero, RX - 1)
    plane_setup(kappa, cx, cy, cz, weight, diag, 1.0, 1, planes - 1)
    plane_sweep(conc, once, forcing, cx, cy, cz, weight, 1, planes - 1)
    plane_sweep(once, v_out, forcing, cx, cy, cz, weight, 1, planes - 1)
    chunks = size_z // LANES
    size_z1 = size_z // 2
    to_half = [halve_lanes(LANES, size_z1, chunk * LANES // 2) for chunk in range(chunks)]
    tile_x1, tile_y1 = tile_x // 2, tile_y // 2

    def put(pair, total):
        for chunk in range(chunks):
            paired[chunk, pair, 0:rows] = total[:, chunk * LANES : (chunk + 1) * LANES]

    def narrowed(pairs, start, count):
        result = None
        for chunk in range(chunks):
            stack = [
                paired[chunk, pair, pl.ds(start, count, stride=2)]
                + paired[chunk, pair, pl.ds(start + 1, count, stride=2)]
                for pair in range(pairs)
            ]
            part = times_right(jnp.concatenate(stack, 0), to_half[chunk])
            result = part if result is None else result + part
        return 0.125 * result

    wide = paired.shape[2] // 2
    planes1 = tile_x1 + 2 * RC
    if 2 * wide > rows:
        for chunk in range(chunks):
            for pair in range(planes1 - 2):
                paired[chunk, pair, rows:] = jnp.ones((2 * wide - rows, LANES), F32)
    for pair in range(planes1 - 2):
        put(pair, kappa[2 * pair] + kappa[2 * pair + 1])
    coarse = narrowed(planes1 - 2, 0, wide)
    for pair in range(planes1 - 2):
        k_one[pair + 1] = coarse[pair * wide : (pair + 1) * wide]
    for message, x in ((from_low, 0), (from_high, planes1 - 1)):
        k_one[x] = jnp.ones((wide, size_z1), F32)
        k_one[x, RC : RC + tile_y1] = message[last_tile, :, 0:size_z1]
    plane_setup(k_one, cx1, cy1, cz1, w1, d1, 0.25, 1, planes1 - 1)

    for pair in range(tile_x1):
        total = None
        for x in (RX + 2 * pair, RX + 2 * pair + 1):
            part = forcing[x] + neighbours(v_out, cx, cy, cz, x) - diag[x] * v_out[x]
            total = part if total is None else total + part
        put(pair, total)
    forcing_one = narrowed(tile_x1, RY, tile_y1)

    low, high = RC, RC + tile_y1
    nothing = jnp.zeros((wide, size_z1), F32)
    for x in range(planes1):
        f_one[x] = nothing
        if x in (0, planes1 - 1):
            v_one[x] = nothing
    for x in (0, 1, planes1 - 2, planes1 - 1):
        u_one[x] = nothing
    for x in range(tile_x1):
        f = forcing_one[x * tile_y1 : (x + 1) * tile_y1]
        f_one[x + RC, low:high] = f
        u_one[x + RC] = w1[x + RC] * f_one[x + RC]
        level_one[0, x] = f
        level_one[1, x] = u_one[x + RC, low:high]
        level_one[2, x] = k_one[x + RC, low:high]
    plane_sweep(u_one, v_one, f_one, cx1, cy1, cz1, w1, 1, planes1 - 1)
    pairs1 = planes1 // 2
    for pair in range(pairs1):
        total = None
        for x in (2 * pair, 2 * pair + 1):
            if x == 0:
                part = cx1[0] * v_one[1]
            elif x == planes1 - 1:
                part = cx1[x - 1] * v_one[x - 1]
            else:
                part = f_one[x] + neighbours(v_one, cx1, cy1, cz1, x) - d1[x] * v_one[x]
            total = part if total is None else total + part
        paired_one[pair] = total
    for pair in range(pairs1):
        packed[pair] = (
            paired_one[pair, pl.ds(0, ROWS, stride=2)] + paired_one[pair, pl.ds(1, ROWS, stride=2)]
        )
    half_pairs = pairs1 // 2
    result = times_right(
        jnp.concatenate([packed[p] for p in range(half_pairs)], 0), halve_lanes(size_z1, size_z1)
    ) + times_right(
        jnp.concatenate([packed[half_pairs + p] for p in range(half_pairs)], 0),
        halve_lanes(size_z1, size_z1, size_z1 // 2),
    )
    used = tile_y1 // 2 + RC
    block = jnp.concatenate([result[p * ROWS : p * ROWS + used] for p in range(half_pairs)], 0)
    block = 0.125 * block
    for part in range(blocks.shape[1]):
        piece = block[part * SHORT : (part + 1) * SHORT]
        for device in range(blocks.shape[0]):
            blocks[device, part] = piece
    copy = pltpu.make_async_copy(blocks, blocks_out, left)
    copy.start()
    for x in range(RX - 1, planes - RX + 1):
        forcing_out[x - RX + 1] = forcing[x]

    for to, rows1, row0 in (
        (to_low, slice(0, R1), RY + 1),
        (to_high, slice(tile_y1 - R1, tile_y1), top - 2),
    ):
        for which in range(3):
            for x in range(tile_x1):
                flat_row = which * tile_x1 * R1 + x * R1
                to[flat_row // ROWS, flat_row % ROWS : flat_row % ROWS + R1] = level_one[
                    which, x, rows1
                ]
        start = 3 * tile_x1 * R1 // ROWS
        for x in range(tile_x):
            row = v_zero[x + 1, row0 : row0 + 1]
            for chunk in range(chunks):
                to[start + chunk, x : x + 1] = row[:, chunk * LANES : (chunk + 1) * LANES]
    copy.wait()


def reach_of(layer):
    return R1 + 1 - layer


def middle(level_one, v_zero, from_low, from_high, window, near, far):
    _, tile_x1, tile_y1, _ = level_one.shape
    planes, rows, size_z = v_zero.shape
    top1 = R1 + tile_y1
    for which in range(3):
        for x in range(tile_x1):
            flat_row = which * tile_x1 * R1 + x * R1
            at, sub = flat_row // ROWS, flat_row % ROWS
            window[which, x, R1:top1] = level_one[which, x]
            window[which, x, 0:R1] = from_low[at, sub : sub + R1]
            window[which, x, top1:] = from_high[at, sub : sub + R1]
    chunks = size_z // LANES
    top = rows - RY

    def pack(to_low, to_high):
        for to, low in ((to_low, True), (to_high, False)):
            at = 0
            for which in (0, 2):
                for layer in range(1, R1 + 1):
                    x = layer - 1 if low else tile_x1 - layer
                    outer = 1 if which == 0 and layer == R1 else which
                    to[at] = window[outer, x, R1:top1]
                    at += 1
            loose = at * ROWS
            for which in (0, 2):
                for layer in range(1, R1 + 1):
                    x = layer - 1 if low else tile_x1 - layer
                    outer = 1 if which == 0 else which
                    for distance in range(1, reach_of(layer) + 1):
                        source = outer if distance == reach_of(layer) else which
                        for row in (R1 - distance, top1 + distance - 1):
                            to[loose // ROWS, loose % ROWS : loose % ROWS + 1] = window[
                                source, x, row : row + 1
                            ]
                            loose += 1
            second, first = (2, 1) if low else (planes - 3, planes - 2)
            for row in (RY - 1, top):
                for chunk in range(chunks):
                    lanes = slice(chunk * LANES, (chunk + 1) * LANES)
                    to[loose // ROWS, loose % ROWS : loose % ROWS + 1] = v_zero[first, row : row + 1, lanes]
                    loose += 1
            at = -(-loose // ROWS)
            for chunk in range(chunks):
                lanes = slice(chunk * LANES, (chunk + 1) * LANES)
                for half in range((top - RY) // ROWS):
                    to[at] = v_zero[second, RY + half * ROWS : RY + (half + 1) * ROWS, lanes]
                    at += 1

    on_sides("tx", near, far, pack)


def middle_tiles(tile_y, chunks):
    loose = 2 * sum(2 * reach_of(layer) for layer in range(1, R1 + 1)) + 2 * chunks
    return 2 * R1 + -(-loose // ROWS) + chunks * tile_y // ROWS


class Grid:
    def __init__(self, sizes, strides, scales, rows, lanes):
        self.sizes = sizes
        self.strides = strides
        self.scales = scales
        self.rows = rows
        self.lanes = lanes
        self.ratios = tuple(2 if extent % 2 == 0 else 1 for extent in sizes)
        self.cells = sizes[0] * sizes[1] * sizes[2]
        self.exact = self.cells <= 64 or self.ratios == (1, 1, 1)

    def coarser(self):
        sizes = tuple(extent // ratio for extent, ratio in zip(self.sizes, self.ratios))
        scales = tuple(s / (ratio * ratio) for s, ratio in zip(self.scales, self.ratios))
        strides = tuple(s * ratio for s, ratio in zip(self.strides, self.ratios[1:]))
        return Grid(sizes, strides, scales, self.rows, self.lanes)


def next_plane(v):
    return v if v.shape[0] == 1 else jnp.concatenate([v[1:], v[:1]], 0)


def last_plane(v):
    return v if v.shape[0] == 1 else jnp.concatenate([v[-1:], v[:-1]], 0)


def restrict_whole(v, grid):
    if grid.ratios[0] == 2:
        v = jnp.concatenate(
            [v[2 * x : 2 * x + 1] + v[2 * x + 1 : 2 * x + 2] for x in range(grid.sizes[0] // 2)], 0
        )
    for axis in (1, 2):
        if grid.ratios[axis] == 2:
            step = grid.strides[axis - 1]
            even = mod(div(iota(v.shape, axis), step), 2) == 0
            v = v + jnp.where(even, ahead(v, axis, step), back(v, axis, step))
    return (1.0 / (grid.ratios[0] * grid.ratios[1] * grid.ratios[2])) * v


def prolong_whole(v, grid):
    if grid.ratios[0] == 1:
        return v
    return jnp.concatenate([v[x // 2 : x // 2 + 1] for x in range(grid.sizes[0])], 0)


def whole_operator(kappa, grid):
    half_x, half_y, half_z = (0.5 * s for s in grid.scales)
    step_y, step_z = grid.strides
    cx = half_x * (kappa + next_plane(kappa))
    cy = half_y * (kappa + ahead(kappa, 1, step_y))
    cz = half_z * (kappa + ahead(kappa, 2, step_z))
    diag = mass_rate + cx + last_plane(cx)
    diag = diag + (cy + back(cy, 1, step_y)) + (cz + back(cz, 2, step_z))
    return cx, cy, cz, diag, relax_weight / diag


def whole_neighbours(v, operator, grid):
    cx, cy, cz = operator[:3]
    step_y, step_z = grid.strides
    total = cx * next_plane(v) + last_plane(cx * v)
    total = total + (cy * ahead(v, 1, step_y) + back(cy * v, 1, step_y))
    return total + (cz * ahead(v, 2, step_z) + back(cz * v, 2, step_z))


def whole_sweep(v, forcing, operator, grid):
    return (1.0 - relax_weight) * v + operator[4] * (forcing + whole_neighbours(v, operator, grid))


class ExactSolve:
    def __init__(self, grid, kappa=None, inverse=None):
        size_x, size_y, size_z = grid.sizes
        self.grid = grid
        self.across = across = size_x * size_y
        _, step_z = grid.strides
        self.period = period = size_z * step_z
        cells = grid.cells
        padded = -(-cells // ROWS) * ROWS
        assert across <= step_z and 2 * period <= grid.lanes
        shape = (padded, grid.lanes)
        i, j = iota(shape, 0), iota(shape, 1)
        self.i, self.j = i, j
        if kappa is None:
            self.inverse = inverse
            return

        def places_of_row(n):
            sub = mod(n, across)
            return div(sub, size_y), mod(sub, size_y), div(n, across)

        def places_of_lane(n):
            n = mod(n, period)
            sub = mod(n, step_z)
            return div(sub, size_y), mod(sub, size_y), div(n, step_z)

        at_i, at_j = places_of_row(i), places_of_lane(j)
        live = (mod(j, step_z) < across) & (i < cells)
        same = (at_i[0] == at_j[0]) & (at_i[1] == at_j[1]) & (at_i[2] == at_j[2]) & live
        left = j < period
        factor = jnp.zeros(shape, F32)
        for d in range(3):
            equal = [at_i[other] == at_j[other] for other in range(3) if other != d]
            for step in (1, grid.sizes[d] - 1):
                hit = mod(at_i[d] + step, grid.sizes[d]) == at_j[d]
                factor = factor + jnp.where(
                    hit & equal[0] & equal[1], F32(0.5 * grid.scales[d]), F32(0.0)
                )
        k_row = self.as_row(kappa)
        k_column = jnp.sum(jnp.where(same & left, k_row, 0.0), axis=1, keepdims=True)
        coupled = jnp.where(live & left, factor * (k_column + k_row), 0.0)
        diag = mass_rate + jnp.sum(coupled, axis=1, keepdims=True)
        matrix = jnp.where(same & left, diag - coupled, -coupled)
        matrix = jnp.where(left, matrix, jnp.where(same, F32(1.0), F32(0.0)))
        for n in range(cells):
            lane = (n // across) * step_z + n % across
            pivot_row = matrix[n : n + 1] / matrix[n : n + 1, lane : lane + 1]
            column = matrix[:, lane : lane + 1]
            matrix = jnp.where(i == n, pivot_row, matrix - column * pivot_row)
        self.inverse = jnp.where((j >= period) & (j < 2 * period) & live, matrix, 0.0)

    def as_row(self, v):
        grid = self.grid
        size_x, size_y, _ = grid.sizes
        step_y, step_z = grid.strides
        sub = mod(iota((1, grid.lanes), 1), step_z)
        result = jnp.zeros((1, grid.lanes), F32)
        for x in range(size_x):
            for y in range(size_y):
                row = v[x, y * step_y : y * step_y + 1]
                result = jnp.where(sub == x * size_y + y, row, result)
        return result

    def solve(self, forcing):
        grid = self.grid
        size_x, size_y, _ = grid.sizes
        step_y, step_z = grid.strides
        solved = jnp.sum(self.inverse * self.as_row(forcing), axis=1, keepdims=True)
        at_z = div(mod(self.j, self.period), step_z)
        spread = jnp.where(div(self.i, self.across) == at_z, solved, 0.0)
        planes = []
        for x in range(size_x):
            rows = []
            for y in range(size_y):
                mine = mod(self.i, self.across) == x * size_y + y
                row = jnp.sum(jnp.where(mine, spread, 0.0), axis=0, keepdims=True)
                rows.append(jnp.broadcast_to(row, (step_y, grid.lanes)))
            planes.append(jnp.concatenate(rows, 0)[None])
        return jnp.concatenate(planes, 0)


def levels_of(counts, tile_sizes):
    sizes = tuple(count * extent for count, extent in zip(counts, tile_sizes)) + tile_sizes[2:]
    grid = Grid(sizes, (1, 1), (0.0625, 0.0625, 0.0625), sizes[1], LANES)
    grids = [grid]
    while not grid.exact:
        grid = grid.coarser()
        grids.append(grid)
    return grids


class Operator:
    def __init__(self, ref):
        self.ref = ref

    def __getitem__(self, part):
        if isinstance(part, slice):
            return [self.ref[p] for p in range(*part.indices(5))]
        return self.ref[part]


def prepare(counts, grids, blocks, _, *outputs):
    count_x, count_y = counts
    planes, rows, _ = grids[0].sizes
    half_x, half_y = planes // count_x, rows // count_y
    size_z2 = grids[0].sizes[2]
    assert half_x * size_z2 == LANES and half_x == 2 and ROWS % half_y == 0
    share = ROWS // half_y
    kappa = [[None] * (rows // ROWS) for _ in range(planes)]
    lane = iota((ROWS, LANES), 1)
    for tx in range(count_x):
        for group in range(rows // ROWS):
            pieces = [blocks[tx * count_y + group * share + n] for n in range(share)]
            piece = jnp.concatenate(pieces, 0)
            turned = pltpu.roll(piece, size_z2, 1)
            for p in range(half_x):
                mine = (lane < size_z2) == (p == 0)
                kappa[tx * half_x + p][group] = jnp.where(mine, piece, turned)
    kappa = jnp.concatenate([jnp.concatenate(groups, 0)[None] for groups in kappa], 0)
    kappas = [kappa]
    for grid in grids[:-1]:
        kappas.append(restrict_whole(kappas[-1], grid))
    outputs[-1][...] = ExactSolve(grids[-1], kappas[-1]).inverse
    for number, grid in enumerate(grids[:-1]):
        for part, value in enumerate(whole_operator(kappas[number], grid)):
            outputs[number][part] = value


def solve_whole(forcing, levels, exact):
    if not levels:
        return exact.solve(forcing)
    grid, operator = levels[0]
    v = operator[4] * forcing
    v = whole_sweep(v, forcing, operator, grid)
    residual = forcing + whole_neighbours(v, operator, grid) - operator[3] * v
    v = v + prolong_whole(solve_whole(restrict_whole(residual, grid), levels[1:], exact), grid)
    for _ in range(2):
        v = whole_sweep(v, forcing, operator, grid)
    return v


def assemble(blocks, count_x, count_y, half_x, half_y, size_z2):
    rows = count_y * half_y
    groups = rows // ROWS
    planes = count_x * half_x
    assert rows % ROWS == 0
    used = half_y + RC
    sub = iota((ROWS, LANES), 0)
    lane = iota((ROWS, LANES), 1)
    nothing = jnp.zeros((ROWS, LANES), F32)
    forcing = [[nothing] * groups for _ in range(planes)]
    half_pairs = (half_x + RC) // 2
    ring = RC // 2
    for tx in range(count_x):
        for ty in range(count_y):
            for p in range(half_pairs):
                tile, base = p * used // SHORT, p * used % SHORT
                assert base + used <= 2 * SHORT == ROWS
                source = tx * count_y + ty
                piece = jnp.concatenate([blocks[source, tile], blocks[source, tile + 1]], 0)
                start = (ty * half_y - ring) % rows
                group, offset = start // ROWS, start % ROWS
                shift = (offset - base) % ROWS
                piece = pltpu.roll(piece, shift, 0) if shift else piece
                turned = pltpu.roll(piece, size_z2, 1)
                for half in range(2):
                    moved = jnp.where((lane < size_z2) == (half == 0), piece, turned)
                    x = (tx * half_x - ring + half * half_pairs + p) % planes
                    at = group
                    mine = (sub >= offset) & (sub < offset + used)
                    forcing[x][at] = forcing[x][at] + jnp.where(mine, moved, 0.0)
                    if offset + used > ROWS:
                        at = (group + 1) % groups
                        mine = sub < offset + used - ROWS
                        forcing[x][at] = forcing[x][at] + jnp.where(mine, moved, 0.0)
    return jnp.concatenate([jnp.concatenate(groups, 0)[None] for groups in forcing], 0)


def coarse_up(
    counts, grids, blocks, window_one, one_near, one_far, row_low, row_high,
    v_zero, forcing0, cx, cy, cz, weight, *rest,
):
    prepared, rest = rest[: len(grids)], rest[len(grids) :]
    (
        out, mixed_low, mixed_high, kappa_low, kappa_high, first_low, first_high,
        v_one, cx1, cy1, cz1, w1, one_a, one_b, zero_a, zero_b,
    ) = rest
    count_x, count_y = counts
    one_low, one_high = by_side("tx", one_near, one_far)
    _, tile_x1, rows1, size_z1 = window_one.shape
    tile_y1 = rows1 - 2 * R1
    top1 = R1 + tile_y1
    half_x, half_y, size_z2 = tile_x1 // 2, tile_y1 // 2, size_z1 // 2
    sizes = grids[0].sizes
    forcing2 = assemble(blocks, count_x, count_y, half_x, half_y, size_z2)
    levels = [
        (grid, Operator(prepared[number])) for number, grid in enumerate(grids[:-1])
    ]
    exact = ExactSolve(grids[-1], inverse=prepared[-1][...])

    planes1 = tile_x1 + 2 * R1
    for message, mixed, kappa_rim, low in (
        (one_low, mixed_low, kappa_low, True), (one_high, mixed_high, kappa_high, False)
    ):
        at, loose = 0, 2 * R1 * ROWS
        for rim, fill in ((mixed, 0.0), (kappa_rim, 1.0)):
            for layer in range(1, R1 + 1):
                x = R1 - layer if low else layer - 1
                rim[x] = jnp.full((rows1, size_z1), fill, F32)
                rim[x, R1:top1] = message[at]
                at += 1
                for distance in range(1, reach_of(layer) + 1):
                    for row in (R1 - distance, top1 + distance - 1):
                        rim[x, row : row + 1] = message[
                            loose // ROWS, loose % ROWS : loose % ROWS + 1
                        ]
                        loose += 1

    def stacked(low, which, high):
        whole = [(low, x) for x in range(R1)]
        whole += [(window_one.at[which], x) for x in range(tile_x1)]
        whole += [(high, x) for x in range(R1)]
        return Planes(0, whole)

    forcing1 = stacked(mixed_low, 0, mixed_high)
    kappa1 = stacked(kappa_low, 2, kappa_high)
    plane_setup(kappa1, cx1, cy1, cz1, w1, None, 0.25, 1, planes1 - 1)
    row = iota((rows1, size_z1), 0)
    for mixed, rim, low in ((mixed_low, first_low, True), (mixed_high, first_high, False)):
        for layer in range(1, R1 + 1):
            x = R1 - layer if low else layer - 1
            if layer == R1:
                rim[x] = mixed[x]
            else:
                reach = reach_of(layer) - 1
                inside = (row >= R1 - reach) & (row < top1 + reach)
                at = x if low else R1 + tile_x1 + x
                rim[x] = jnp.where(inside, w1[at] * mixed[x], mixed[x])
    start1 = stacked(first_low, 1, first_high)
    plane_sweep(start1, v_one, forcing1, cx1, cy1, cz1, w1, 1, planes1 - 1)

    solved = solve_whole(forcing2, levels, exact)
    solved = solved.reshape(sizes[0] * sizes[1], LANES)

    whole_x1, whole_y1 = 2 * sizes[0], 2 * sizes[1]
    start_x = lax.axis_index("tx") * tile_x1 + (whole_x1 - R1)
    start_y = lax.axis_index("ty") * tile_y1 + (whole_y1 - R1)
    row = iota((planes1 * rows1, 1), 0)
    at_x = mod(div(row, rows1) + start_x, whole_x1)
    at_y = mod(mod(row, rows1) + start_y, whole_y1)
    target = div(at_x, 2) * sizes[1] + div(at_y, 2)
    left = ones_where(iota((planes1 * rows1, sizes[0] * sizes[1]), 1) == target)
    shape = (LANES, size_z1)
    right = ones_where(iota(shape, 0) == div(iota(shape, 1), 2))
    raised = times_right(times_left(left, solved), right)
    for x in range(1, planes1 - 1):
        one_a[x] = v_one[x] + raised[x * rows1 : (x + 1) * rows1]
    plane_sweep(one_a, one_b, forcing1, cx1, cy1, cz1, w1, 2, planes1 - 2)
    plane_sweep(one_b, one_a, forcing1, cx1, cy1, cz1, w1, 3, planes1 - 3)

    planes, rows, size_z = zero_a.shape
    v_zero, forcing0 = kept(v_zero, RX - 1), kept(forcing0, RX - 1)
    cx, cy, cz, weight = kept(cx, RX - 2), kept(cy, RX - 1), kept(cz, RX - 1), kept(weight, RX - 1)
    first, last = R1 - 1, planes1 - R1 + 1
    stack = jnp.concatenate([one_a[x] for x in range(first, last)], 0)
    count = last - first
    shape = (count * rows, count * rows1)
    out_row, in_row = iota((count * rows, 1), 0), iota(shape, 1)
    target = div(out_row, rows) * rows1 + div(mod(out_row, rows) + (2 * R1 - RY), 2)
    left = ones_where(in_row == target)
    shape = (size_z1, size_z)
    right = ones_where(iota(shape, 0) == div(iota(shape, 1), 2))
    raised = times_right(times_left(left, stack), right)
    chunks = size_z // LANES
    top = rows - RY
    for x in range(RX - 1, planes - RX + 1):
        zero_b[x] = v_zero[x]
    for rim_x in (RX - 2, planes - RX + 1):
        zero_b[rim_x] = jnp.zeros((rows, size_z), F32)
    for x in range(planes - 2 * RX):
        at = 3 * tile_x1 * R1 // ROWS
        for chunk in range(chunks):
            lanes = slice(chunk * LANES, (chunk + 1) * LANES)
            zero_b[RX + x, RY - 2 : RY - 1, lanes] = row_low[at + chunk, x : x + 1]
            zero_b[RX + x, top + 1 : top + 2, lanes] = row_high[at + chunk, x : x + 1]
    for message, second, nearest in (
        (one_low, RX - 2, RX - 1), (one_high, planes - RX + 1, planes - RX)
    ):
        loose = 2 * R1 * ROWS + 2 * sum(2 * reach_of(layer) for layer in range(1, R1 + 1))
        for r in (RY - 1, top):
            for chunk in range(chunks):
                lanes = slice(chunk * LANES, (chunk + 1) * LANES)
                zero_b[nearest, r : r + 1, lanes] = message[
                    loose // ROWS, loose % ROWS : loose % ROWS + 1
                ]
                loose += 1
        at = -(-loose // ROWS)
        for chunk in range(chunks):
            lanes = slice(chunk * LANES, (chunk + 1) * LANES)
            for half in range((top - RY) // ROWS):
                zero_b[second, RY + half * ROWS : RY + (half + 1) * ROWS, lanes] = message[at]
                at += 1
    for x in range(RX - 2, planes - RX + 2):
        at = (x - RX + 2 * R1) // 2 - first
        zero_a[x] = zero_b[x] + raised[at * rows : (at + 1) * rows]
    plane_sweep(zero_a, zero_b, forcing0, cx, cy, cz, weight, RX - 1, planes - RX + 1)
    plane_sweep(zero_b, zero_a, forcing0, cx, cy, cz, weight, RX, planes - RX)
    for x in range(planes - 2 * RX):
        out[x] = zero_a[x + RX, RY:top]


VM = pl.BlockSpec(memory_space=pltpu.VMEM)
IN_PLACE = pl.BlockSpec(memory_space=pltpu.HBM)


def call(kernel, operands, outputs, scratch, spec=VM, in_hbm=()):
    def typed(output):
        return output if isinstance(output, jax.ShapeDtypeStruct) else jax.ShapeDtypeStruct(output, F32)

    return pl.pallas_call(
        kernel,
        in_specs=[spec] * len(operands),
        out_specs=[IN_PLACE if n in in_hbm else VM for n in range(len(outputs))],
        out_shape=[typed(output) for output in outputs],
        scratch_shapes=[pltpu.VMEM(s, F32) if isinstance(s, tuple) else s for s in scratch],
        compiler_params=pltpu.CompilerParams(vmem_limit_bytes=24 * 1024 * 1024),
    )(*operands)


def shift_both(to_low, to_high, axis):
    count = lax.axis_size(axis)
    from_low = lax.ppermute(to_high, axis, [(i, (i + 1) % count) for i in range(count)])
    from_high = lax.ppermute(to_low, axis, [((i + 1) % count, i) for i in range(count)])
    return from_low, from_high


def swap_both(near, far, axis):
    count = lax.axis_size(axis)
    assert count % 2 == 0
    partner = [(i, i ^ 1) for i in range(count)]
    other = [(i, (i - 1 if i % 2 == 0 else i + 1) % count) for i in range(count)]
    from_far = lax.ppermute(far, axis, other)
    from_near = lax.ppermute(near, axis, partner)
    return from_near, from_far


def to_everyone(blocks):
    return lax.all_to_all(blocks, ("tx", "ty"), 0, 0)


def cycle(concentration, source, material):
    tile_x, tile_y, size_z = concentration.shape
    chunks = size_z // LANES
    counts = lax.axis_size("tx"), lax.axis_size("ty")
    everyone = counts[0] * counts[1]
    rows = tile_y + 2 * RY
    message = (tile_x + 1, ROWS, size_z)
    *inputs, to_low, to_high = call(
        edges,
        tuple(
            pltpu.with_memory_space_constraint(v, pltpu.HBM)
            for v in (concentration, source, material)
        ),
        tuple(jax.ShapeDtypeStruct(v.shape, v.dtype) for v in (concentration, source, material))
        + (message, message),
        (pltpu.SemaphoreType.DMA((3,)),),
        IN_PLACE,
    )
    from_low, from_high = shift_both(to_low, to_high, "ty")
    zero = (tile_x + 2 * RX, rows, size_z)
    inner = (tile_x + 2, rows, size_z)
    one_tile = (tile_x // 2, tile_y // 2, size_z // 2)
    two_tile = tuple(extent // 2 for extent in one_tile)
    grids = levels_of(counts, two_tile)
    k_tile, kappa_blocks = call(
        shrink,
        inputs[2:],
        (one_tile, (everyone, two_tile[1], LANES)),
        ((one_tile[0], tile_y, LANES), one_tile[1:]),
    )
    message = (plane_tiles(tile_y), ROWS, size_z)
    window, to_low, to_high = call(
        sides,
        (*inputs, k_tile, from_low, from_high),
        ((3, tile_x, rows, size_z), message, message),
        ((rows, size_z),),
    )
    from_low, from_high = shift_both(to_low, to_high, "tx")
    kappa_blocks = to_everyone(kappa_blocks)

    wide = -(-rows // (2 * ROWS)) * ROWS
    small = (one_tile[0] + 2 * RC, wide, one_tile[2])
    pairs1 = small[0] // 2
    short = pairs1 // 2 * (two_tile[1] + RC) // SHORT
    assert pairs1 // 2 * (two_tile[1] + RC) % SHORT == 0
    message = (3 * one_tile[0] * R1 // ROWS + chunks, ROWS, LANES)
    assert one_tile[2] == LANES and tile_x <= ROWS and one_tile[1] == ROWS
    v_zero, forcing0, cx, cy, cz, weight, level_one, blocks, to_low, to_high = call(
        fine_down,
        (window, from_low, from_high),
        (inner, inner, (tile_x + 3, rows, size_z), inner, inner, inner)
        + ((3,) + one_tile, (everyone, short, SHORT, LANES), message, message),
        (
            (4, rows, size_z),
            (2, rows, size_z),
            (4, rows, size_z),
            zero,
            zero,
            (chunks, max(small[0], tile_x), 2 * wide, LANES),
            (everyone, short, SHORT, LANES),
            pltpu.SemaphoreType.DMA,
        )
        + (small,) * 9
        + ((pairs1, wide, one_tile[2]), (pairs1, ROWS, one_tile[2])),
        in_hbm=(7,),
    )
    row_low, row_high = shift_both(to_low, to_high, "ty")
    blocks = to_everyone(blocks)
    rows1 = one_tile[1] + 2 * R1
    message = (middle_tiles(tile_y, chunks), ROWS, LANES)
    window_one, near, far = call(
        middle,
        (level_one, v_zero, row_low, row_high),
        ((3, one_tile[0], rows1, one_tile[2]), message, message),
        (),
    )
    one_near, one_far = swap_both(near, far, "tx")
    lattice = grids[0].sizes[1], LANES
    prepared = call(
        functools.partial(prepare, counts, grids),
        (kappa_blocks, window_one),
        tuple((5, grid.sizes[0]) + lattice for grid in grids[:-1])
        + ((-(-grids[-1].cells // ROWS) * ROWS, LANES),),
        (),
    )
    one = (one_tile[0] + 2 * R1, rows1, one_tile[2])
    rim = (R1,) + one[1:]
    (updated,) = call(
        functools.partial(coarse_up, counts, grids),
        (blocks, window_one, one_near, one_far, row_low, row_high)
        + (v_zero, forcing0, cx, cy, cz, weight, *prepared),
        (concentration.shape,),
        (rim,) * 6 + (one,) * 7 + (zero, zero),
    )
    return updated


def solution(mesh):
    placed = (P("tx", "ty", None), P("tx", "ty", None), P("tx", "ty", None))
    return jax.shard_map(
        cycle, mesh=mesh, in_specs=placed, out_specs=P("tx", "ty", None), check_vma=False
    )
```

```python
import functools

import jax
import jax.numpy as jnp
from jax import lax
from jax.experimental import pallas as pl
from jax.experimental.pallas import tpu as pltpu
from jax.sharding import PartitionSpec as P


mass_rate = 0.001
relax_weight = 0.8
diffusivities = (0.15, 0.3, 0.5, 0.8, 1.2, 2.0, 3.2, 5.0)
LANES = 128
ROWS = 8
SHORT = 4
RX = 2
RY = 4
R1 = 4
RC = 2
F32 = jnp.float32
BF16 = jnp.bfloat16


def lookup(material):
    result = jnp.zeros(material.shape, F32)
    for slot_id, coeff_value in enumerate(diffusivities):
        result = jnp.where(material == slot_id, F32(coeff_value), result)
    return result


class Planes:
    def __init__(self, first, planes):
        self.first = first
        self.planes = planes

    def __getitem__(self, x):
        ref, index = self.planes[x - self.first]
        return ref[index]

    def __setitem__(self, x, value):
        ref, index = self.planes[x - self.first]
        ref[index] = value


def kept(ref, first):
    return Planes(first, [(ref, x) for x in range(ref.shape[0])])


def is_even(axis):
    return lax.rem(lax.axis_index(axis), 2) == 0


def on_sides(axis, near, far, body):
    @pl.when(is_even(axis))
    def _():
        body(far, near)

    @pl.when(jnp.logical_not(is_even(axis)))
    def _():
        body(near, far)


class Picked:
    def __init__(self, flag, when_true, when_false):
        self.flag = flag
        self.when_true = when_true
        self.when_false = when_false

    def __getitem__(self, index):
        first, second = self.when_true[index], self.when_false[index]
        flag = jnp.where(self.flag, jnp.int32(1), jnp.int32(0))
        return jnp.where(jnp.full(first.shape, flag) == 1, first, second)


def by_side(axis, near, far):
    even = is_even(axis)
    return Picked(even, far, near), Picked(even, near, far)


def iota(shape, dim):
    return lax.broadcasted_iota(jnp.int32, shape, dim)


def div(a, b):
    return lax.div(a, jnp.full_like(a, b))


def mod(a, b):
    return lax.rem(a, jnp.full_like(a, b))


def ones_where(mask):
    return jnp.where(mask, F32(1.0), F32(0.0)).astype(BF16)


def three_terms(x):
    high = x.astype(BF16)
    rest = x - high.astype(F32)
    middle = rest.astype(BF16)
    low = (rest - middle.astype(F32)).astype(BF16)
    return high, middle, low


def times_right(x, selector):
    parts = [jnp.dot(part, selector, preferred_element_type=F32) for part in three_terms(x)]
    return parts[0] + (parts[1] + parts[2])


def back(v, axis, step=1):
    return pltpu.roll(v, step, axis)


def ahead(v, axis, step=1):
    return pltpu.roll(v, v.shape[axis] - step, axis)


def halve_lanes(fine, coarse, start=0):
    shape = (fine, coarse)
    return ones_where(div(iota(shape, 0), 2) + start == iota(shape, 1))


def plane_setup(kappa, cx, cy, cz, weight, diag, scale, first, last):
    half = 0.5 * scale
    for x in range(first - 1, last):
        cx[x] = half * (kappa[x] + kappa[x + 1])
    for x in range(first, last):
        k = kappa[x]
        y_part = half * (k + ahead(k, 0))
        z_part = half * (k + ahead(k, 1))
        cy[x] = y_part
        cz[x] = z_part
        d = mass_rate + cx[x] + cx[x - 1] + y_part + back(y_part, 0) + z_part + back(z_part, 1)
        weight[x] = relax_weight / d
        if diag is not None:
            diag[x] = d


def in_plane(here, cy, cz, x):
    y_part = cy[x]
    z_part = cz[x]
    total = y_part * ahead(here, 0) + back(y_part * here, 0)
    return total + (z_part * ahead(here, 1) + back(z_part * here, 1))


def neighbours(v, cx, cy, cz, x):
    return (cx[x] * v[x + 1] + cx[x - 1] * v[x - 1]) + in_plane(v[x], cy, cz, x)


def plane_sweep(v, out, forcing, cx, cy, cz, weight, first, last):
    for x in range(first, last):
        out[x] = (1.0 - relax_weight) * v[x] + weight[x] * (forcing[x] + neighbours(v, cx, cy, cz, x))


def edges(conc_in, source_in, material_in, conc, source, material, to_low, to_high, arrived):
    copies = [
        pltpu.make_async_copy(whence, whither, arrived.at[n])
        for n, (whence, whither) in enumerate(
            ((conc_in, conc), (source_in, source), (material_in, material))
        )
    ]
    for copy in copies:
        copy.start()
    for copy in copies:
        copy.wait()
    tile_x, tile_y, _ = conc.shape
    for to, low in ((to_low, True), (to_high, False)):
        for x in range(tile_x):
            rows = slice(0, 4) if low else slice(tile_y - 4, tile_y)
            near = slice(0, 3) if low else slice(1, 4)
            pair = slice(0, 2) if low else slice(2, 4)
            c = conc[x, rows]
            f = mass_rate * c + source[x, rows]
            k = lookup(material[x, rows])
            to[x, 0:3] = c[near]
            to[x, 3:5] = f[pair]
            to[x, 5:8] = k[near]
            to[tile_x, x : x + 1] = k[3:4] if low else k[0:1]


def sides(conc, source, material, k_tile, from_low, from_high, window, to_low, to_high, swept):
    tile_x, tile_y, size_z = conc.shape
    top = RY + tile_y
    for x in range(tile_x):
        c = conc[x]
        window[0, x, RY:top] = c
        window[1, x, RY:top] = mass_rate * c + source[x]
        window[2, x, RY:top] = lookup(material[x])
        window[0, x, 0:1] = jnp.zeros((1, size_z), F32)
        window[0, x, 1:4] = from_low[x, 0:3]
        window[0, x, top : top + 3] = from_high[x, 0:3]
        window[0, x, top + 3 :] = jnp.zeros((1, size_z), F32)
        window[1, x, 0:2] = jnp.zeros((2, size_z), F32)
        window[1, x, 2:4] = from_low[x, 3:5]
        window[1, x, top : top + 2] = from_high[x, 3:5]
        window[1, x, top + 2 :] = jnp.zeros((2, size_z), F32)
        window[2, x, 0:1] = from_low[tile_x, x : x + 1]
        window[2, x, 1:4] = from_low[x, 5:8]
        window[2, x, top : top + 3] = from_high[x, 5:8]
        window[2, x, top + 3 :] = from_high[tile_x, x : x + 1]
    per_plane = tile_y // ROWS
    for to, low in ((to_low, True), (to_high, False)):

        def plane(layer):
            return layer - 1 if low else tile_x - layer

        def send(at, values):
            for n in range(per_plane):
                to[at + n] = values(n)

        for n, (which, layer) in enumerate(BASE_PLANES):
            send(
                n * per_plane,
                lambda n: window[which, plane(layer), RY + n * ROWS : RY + (n + 1) * ROWS],
            )
        first_sweep(window, plane(2), swept)
        at = len(BASE_PLANES) * per_plane
        send(at, lambda n: swept[RY + n * ROWS : RY + (n + 1) * ROWS])
        loose = (at + per_plane) * ROWS
        for which, layer, reach in EXTRA_ROWS:
            for start in (RY - reach, top):
                to[loose // ROWS, loose % ROWS : loose % ROWS + reach] = window[
                    which, plane(layer), start : start + reach
                ]
                loose += reach
        at = -(-loose // ROWS)
        to[at, :, 0 : size_z // 2] = k_tile[1 if low else k_tile.shape[0] - 2]
        to[at, :, size_z // 2 :] = jnp.zeros((ROWS, size_z - size_z // 2), F32)


def first_sweep(window, x, out):
    c, f, k = window[0, x], window[1, x], window[2, x]
    next_part = 0.5 * (k + window[2, x + 1])
    last_part = 0.5 * (k + window[2, x - 1])
    y_part = 0.5 * (k + ahead(k, 0))
    z_part = 0.5 * (k + ahead(k, 1))
    d = mass_rate + next_part + last_part
    d = d + y_part + back(y_part, 0) + z_part + back(z_part, 1)
    total = next_part * window[0, x + 1] + last_part * window[0, x - 1]
    total = total + (y_part * ahead(c, 0) + back(y_part * c, 0))
    total = total + (z_part * ahead(c, 1) + back(z_part * c, 1))
    out[...] = (1.0 - relax_weight) * c + (relax_weight / d) * (f + total)


BASE_PLANES = ((0, 1), (0, 2), (1, 1), (2, 1), (2, 2))
EXTRA_ROWS = ((0, 1, 2), (0, 2, 1), (1, 1, 1), (2, 1, 2), (2, 2, 2))


def plane_tiles(tile_y):
    loose = sum(2 * reach for _, _, reach in EXTRA_ROWS)
    return (len(BASE_PLANES) + 1) * tile_y // ROWS + -(-loose // ROWS) + 1


def shrink(material, k_tile, k_two, halves, halves_one, paired, paired_one):
    tile_x, tile_y, size_z = material.shape
    tile_x1, tile_y1, size_z1 = tile_x // 2, tile_y // 2, size_z // 2
    k_one = None
    for chunk in range(size_z // LANES):
        lanes = slice(chunk * LANES, (chunk + 1) * LANES)
        for pair in range(tile_x1):
            paired[pair] = lookup(material[2 * pair, :, lanes]) + lookup(
                material[2 * pair + 1, :, lanes]
            )
        stack = [
            paired[pair, pl.ds(0, tile_y1, stride=2)] + paired[pair, pl.ds(1, tile_y1, stride=2)]
            for pair in range(tile_x1)
        ]
        part = times_right(
            jnp.concatenate(stack, 0), halve_lanes(LANES, size_z1, chunk * LANES // 2)
        )
        k_one = part if k_one is None else k_one + part
    k_one = 0.125 * k_one
    for x in range(tile_x1):
        k_tile[x] = k_one[x * tile_y1 : (x + 1) * tile_y1]
    assert tile_x1 // 2 * (size_z1 // 2) <= LANES
    block = None
    for pair in range(tile_x1 // 2):
        at = 2 * pair * tile_y1
        paired_one[...] = k_one[at : at + tile_y1] + k_one[at + tile_y1 : at + 2 * tile_y1]
        piece = (
            paired_one[pl.ds(0, tile_y1 // 2, stride=2)] + paired_one[pl.ds(1, tile_y1 // 2, stride=2)]
        )
        part = times_right(piece, halve_lanes(size_z1, LANES, pair * size_z1 // 2))
        block = part if block is None else block + part
    block = 0.125 * block
    k_two[...] = block
    for chunk in range(size_z // LANES):
        halves[chunk] = halve_lanes(LANES, size_z1, chunk * LANES // 2)
    for half in range(2):
        halves_one[half] = halve_lanes(size_z1, size_z1, half * size_z1 // 2)


def fine_down(
    window, k_two, halves, halves_one, from_low, from_high,
    v_zero, forcing_out, cx, cy, cz, weight, level_one, blocks_out, to_low, to_high,
    conc_rim, forcing_rim, kappa_rim, once, diag, paired, blocks, left,
    k_one, f_one, u_one, v_one, cx1, cy1, cz1, w1, d1, paired_one, packed,
):
    _, tile_x, rows, size_z = window.shape
    tile_y = rows - 2 * RY
    top = RY + tile_y
    planes = tile_x + 2 * RX
    rims = (conc_rim, forcing_rim, kappa_rim)
    depths = (2, 1, 2)
    for which, rim in enumerate(rims):
        fill = jnp.full((rows, size_z), 1.0 if which == 2 else 0.0, F32)
        for x in range(2 * depths[which]):
            rim[x] = fill

    def place(which, layer, low):
        return depths[which] - layer if low else depths[which] + layer - 1

    per_plane = tile_y // ROWS
    last_tile = plane_tiles(tile_y) - 1
    for message, low in ((from_low, True), (from_high, False)):
        for at, (which, layer) in enumerate(BASE_PLANES):
            for n in range(per_plane):
                start = RY + n * ROWS
                rims[which][place(which, layer, low), start : start + ROWS] = message[
                    at * per_plane + n
                ]
        rim_x = 0 if low else planes - 1
        once[rim_x] = jnp.zeros((rows, size_z), F32)
        at = len(BASE_PLANES) * per_plane
        for n in range(per_plane):
            start = RY + n * ROWS
            once[rim_x, start : start + ROWS] = message[at + n]
        loose = (at + per_plane) * ROWS
        for which, layer, reach in EXTRA_ROWS:
            for start in (RY - reach, top):
                rims[which][place(which, layer, low), start : start + reach] = message[
                    loose // ROWS, loose % ROWS : loose % ROWS + reach
                ]
                loose += reach

    def stacked(which):
        depth = depths[which]
        whole = [(rims[which], x) for x in range(depth)]
        whole += [(window.at[which], x) for x in range(tile_x)]
        whole += [(rims[which], depth + x) for x in range(depth)]
        return Planes(RX - depth, whole)

    conc, forcing, kappa = stacked(0), stacked(1), stacked(2)
    cx, cy, cz, weight = kept(cx, RX - 2), kept(cy, RX - 1), kept(cz, RX - 1), kept(weight, RX - 1)
    v_out = kept(v_zero, RX - 1)
    plane_setup(kappa, cx, cy, cz, weight, diag, 1.0, 1, planes - 1)
    plane_sweep(conc, once, forcing, cx, cy, cz, weight, 1, planes - 1)
    plane_sweep(once, v_out, forcing, cx, cy, cz, weight, 1, planes - 1)
    chunks = size_z // LANES
    size_z1 = size_z // 2
    to_half = [halves[chunk] for chunk in range(chunks)]
    tile_x1, tile_y1 = tile_x // 2, tile_y // 2

    def put(pair, total):
        for chunk in range(chunks):
            paired[chunk, pair, 0:rows] = total[:, chunk * LANES : (chunk + 1) * LANES]

    def narrowed(pairs, start, count):
        result = None
        for chunk in range(chunks):
            stack = [
                paired[chunk, pair, pl.ds(start, count, stride=2)]
                + paired[chunk, pair, pl.ds(start + 1, count, stride=2)]
                for pair in range(pairs)
            ]
            part = times_right(jnp.concatenate(stack, 0), to_half[chunk])
            result = part if result is None else result + part
        return 0.125 * result

    wide = paired.shape[2] // 2
    planes1 = tile_x1 + 2 * RC
    if 2 * wide > rows:
        for chunk in range(chunks):
            for pair in range(planes1 - 2):
                paired[chunk, pair, rows:] = jnp.ones((2 * wide - rows, LANES), F32)
    for pair in range(planes1 - 2):
        put(pair, kappa[2 * pair] + kappa[2 * pair + 1])
    coarse = narrowed(planes1 - 2, 0, wide)
    for pair in range(planes1 - 2):
        k_one[pair + 1] = coarse[pair * wide : (pair + 1) * wide]
    for message, x in ((from_low, 0), (from_high, planes1 - 1)):
        k_one[x] = jnp.ones((wide, size_z1), F32)
        k_one[x, RC : RC + tile_y1] = message[last_tile, :, 0:size_z1]
    plane_setup(k_one, cx1, cy1, cz1, w1, d1, 0.25, 1, planes1 - 1)

    for pair in range(tile_x1):
        total = None
        for x in (RX + 2 * pair, RX + 2 * pair + 1):
            part = forcing[x] + neighbours(v_out, cx, cy, cz, x) - diag[x] * v_out[x]
            total = part if total is None else total + part
        put(pair, total)
    forcing_one = narrowed(tile_x1, RY, tile_y1)

    low, high = RC, RC + tile_y1
    nothing = jnp.zeros((wide, size_z1), F32)
    for x in range(planes1):
        f_one[x] = nothing
        if x in (0, planes1 - 1):
            v_one[x] = nothing
    for x in (0, 1, planes1 - 2, planes1 - 1):
        u_one[x] = nothing
    for x in range(tile_x1):
        f = forcing_one[x * tile_y1 : (x + 1) * tile_y1]
        f_one[x + RC, low:high] = f
        u_one[x + RC] = w1[x + RC] * f_one[x + RC]
        level_one[0, x] = f
        level_one[1, x] = u_one[x + RC, low:high]
        level_one[2, x] = k_one[x + RC, low:high]
    plane_sweep(u_one, v_one, f_one, cx1, cy1, cz1, w1, 1, planes1 - 1)
    pairs1 = planes1 // 2
    for pair in range(pairs1):
        total = None
        for x in (2 * pair, 2 * pair + 1):
            if x == 0:
                part = cx1[0] * v_one[1]
            elif x == planes1 - 1:
                part = cx1[x - 1] * v_one[x - 1]
            else:
                part = f_one[x] + neighbours(v_one, cx1, cy1, cz1, x) - d1[x] * v_one[x]
            total = part if total is None else total + part
        paired_one[pair] = total
    for pair in range(pairs1):
        packed[pair] = (
            paired_one[pair, pl.ds(0, ROWS, stride=2)] + paired_one[pair, pl.ds(1, ROWS, stride=2)]
        )
    half_pairs = pairs1 // 2
    result = times_right(
        jnp.concatenate([packed[p] for p in range(half_pairs)], 0), halves_one[0]
    ) + times_right(
        jnp.concatenate([packed[half_pairs + p] for p in range(half_pairs)], 0), halves_one[1]
    )
    used = tile_y1 // 2 + RC
    block = jnp.concatenate([result[p * ROWS : p * ROWS + used] for p in range(half_pairs)], 0)
    block = 0.125 * block
    k_block = k_two[...]
    for device in range(blocks.shape[0]):
        blocks[device, blocks.shape[1] - 1] = k_block
    for part in range(blocks.shape[1] - 1):
        piece = block[part * SHORT : (part + 1) * SHORT]
        for device in range(blocks.shape[0]):
            blocks[device, part] = piece
    copy = pltpu.make_async_copy(blocks, blocks_out, left)
    copy.start()
    for x in range(RX - 1, planes - RX + 1):
        forcing_out[x - RX + 1] = forcing[x]

    for to, rows1, row0 in (
        (to_low, slice(0, R1), RY + 1),
        (to_high, slice(tile_y1 - R1, tile_y1), top - 2),
    ):
        for which in range(3):
            for x in range(tile_x1):
                flat_row = which * tile_x1 * R1 + x * R1
                to[flat_row // ROWS, flat_row % ROWS : flat_row % ROWS + R1] = level_one[
                    which, x, rows1
                ]
        start = 3 * tile_x1 * R1 // ROWS
        for x in range(tile_x):
            row = v_zero[x + 1, row0 : row0 + 1]
            for chunk in range(chunks):
                to[start + chunk, x : x + 1] = row[:, chunk * LANES : (chunk + 1) * LANES]
    copy.wait()


def reach_of(layer):
    return R1 + 1 - layer


def middle(level_one, v_zero, from_low, from_high, window, near, far):
    _, tile_x1, tile_y1, _ = level_one.shape
    planes, rows, size_z = v_zero.shape
    top1 = R1 + tile_y1
    for which in range(3):
        for x in range(tile_x1):
            flat_row = which * tile_x1 * R1 + x * R1
            at, sub = flat_row // ROWS, flat_row % ROWS
            window[which, x, R1:top1] = level_one[which, x]
            window[which, x, 0:R1] = from_low[at, sub : sub + R1]
            window[which, x, top1:] = from_high[at, sub : sub + R1]
    chunks = size_z // LANES
    top = rows - RY

    def pack(to_low, to_high):
        for to, low in ((to_low, True), (to_high, False)):
            at = 0
            for which in (0, 2):
                for layer in range(1, R1 + 1):
                    x = layer - 1 if low else tile_x1 - layer
                    outer = 1 if which == 0 and layer == R1 else which
                    to[at] = window[outer, x, R1:top1]
                    at += 1
            loose = at * ROWS
            for which in (0, 2):
                for layer in range(1, R1 + 1):
                    x = layer - 1 if low else tile_x1 - layer
                    outer = 1 if which == 0 else which
                    for distance in range(1, reach_of(layer) + 1):
                        source = outer if distance == reach_of(layer) else which
                        for row in (R1 - distance, top1 + distance - 1):
                            to[loose // ROWS, loose % ROWS : loose % ROWS + 1] = window[
                                source, x, row : row + 1
                            ]
                            loose += 1
            second, first = (2, 1) if low else (planes - 3, planes - 2)
            for row in (RY - 1, top):
                for chunk in range(chunks):
                    lanes = slice(chunk * LANES, (chunk + 1) * LANES)
                    to[loose // ROWS, loose % ROWS : loose % ROWS + 1] = v_zero[first, row : row + 1, lanes]
                    loose += 1
            at = -(-loose // ROWS)
            for chunk in range(chunks):
                lanes = slice(chunk * LANES, (chunk + 1) * LANES)
                for half in range((top - RY) // ROWS):
                    to[at] = v_zero[second, RY + half * ROWS : RY + (half + 1) * ROWS, lanes]
                    at += 1

    on_sides("tx", near, far, pack)


def middle_tiles(tile_y, chunks):
    loose = 2 * sum(2 * reach_of(layer) for layer in range(1, R1 + 1)) + 2 * chunks
    return 2 * R1 + -(-loose // ROWS) + chunks * tile_y // ROWS


class Grid:
    def __init__(self, sizes, strides, scales, rows, lanes):
        self.sizes = sizes
        self.strides = strides
        self.scales = scales
        self.rows = rows
        self.lanes = lanes
        self.ratios = tuple(2 if extent % 2 == 0 else 1 for extent in sizes)
        self.cells = sizes[0] * sizes[1] * sizes[2]
        self.exact = self.cells <= 64 or self.ratios == (1, 1, 1)

    def coarser(self):
        sizes = tuple(extent // ratio for extent, ratio in zip(self.sizes, self.ratios))
        scales = tuple(s / (ratio * ratio) for s, ratio in zip(self.scales, self.ratios))
        strides = tuple(s * ratio for s, ratio in zip(self.strides, self.ratios[1:]))
        return Grid(sizes, strides, scales, self.rows, self.lanes)


def next_plane(v):
    return v if v.shape[0] == 1 else jnp.concatenate([v[1:], v[:1]], 0)


def last_plane(v):
    return v if v.shape[0] == 1 else jnp.concatenate([v[-1:], v[:-1]], 0)


def restrict_whole(v, grid):
    if grid.ratios[0] == 2:
        v = jnp.concatenate(
            [v[2 * x : 2 * x + 1] + v[2 * x + 1 : 2 * x + 2] for x in range(grid.sizes[0] // 2)], 0
        )
    for axis in (1, 2):
        if grid.ratios[axis] == 2:
            step = grid.strides[axis - 1]
            even = mod(div(iota(v.shape, axis), step), 2) == 0
            v = v + jnp.where(even, ahead(v, axis, step), back(v, axis, step))
    return (1.0 / (grid.ratios[0] * grid.ratios[1] * grid.ratios[2])) * v


def prolong_whole(v, grid):
    if grid.ratios[0] == 1:
        return v
    return jnp.concatenate([v[x // 2 : x // 2 + 1] for x in range(grid.sizes[0])], 0)


def whole_operator(kappa, grid):
    half_x, half_y, half_z = (0.5 * s for s in grid.scales)
    step_y, step_z = grid.strides
    cx = half_x * (kappa + next_plane(kappa))
    cy = half_y * (kappa + ahead(kappa, 1, step_y))
    cz = half_z * (kappa + ahead(kappa, 2, step_z))
    diag = mass_rate + cx + last_plane(cx)
    diag = diag + (cy + back(cy, 1, step_y)) + (cz + back(cz, 2, step_z))
    return cx, cy, cz, diag, relax_weight / diag


def whole_neighbours(v, operator, grid):
    cx, cy, cz = operator[:3]
    step_y, step_z = grid.strides
    total = cx * next_plane(v) + last_plane(cx * v)
    total = total + (cy * ahead(v, 1, step_y) + back(cy * v, 1, step_y))
    return total + (cz * ahead(v, 2, step_z) + back(cz * v, 2, step_z))


def whole_sweep(v, forcing, operator, grid):
    return (1.0 - relax_weight) * v + operator[4] * (forcing + whole_neighbours(v, operator, grid))


class ExactSolve:
    def __init__(self, grid, kappa=None, inverse=None):
        size_x, size_y, size_z = grid.sizes
        self.grid = grid
        self.across = across = size_x * size_y
        _, step_z = grid.strides
        self.period = period = size_z * step_z
        cells = grid.cells
        padded = -(-cells // ROWS) * ROWS
        assert across <= step_z and 2 * period <= grid.lanes
        shape = (padded, grid.lanes)
        i, j = iota(shape, 0), iota(shape, 1)
        self.i, self.j = i, j
        if kappa is None:
            self.inverse = inverse
            return

        def places_of_row(n):
            sub = mod(n, across)
            return div(sub, size_y), mod(sub, size_y), div(n, across)

        def places_of_lane(n):
            n = mod(n, period)
            sub = mod(n, step_z)
            return div(sub, size_y), mod(sub, size_y), div(n, step_z)

        at_i, at_j = places_of_row(i), places_of_lane(j)
        live = (mod(j, step_z) < across) & (i < cells)
        same = (at_i[0] == at_j[0]) & (at_i[1] == at_j[1]) & (at_i[2] == at_j[2]) & live
        left = j < period
        factor = jnp.zeros(shape, F32)
        for d in range(3):
            equal = [at_i[other] == at_j[other] for other in range(3) if other != d]
            for step in (1, grid.sizes[d] - 1):
                hit = mod(at_i[d] + step, grid.sizes[d]) == at_j[d]
                factor = factor + jnp.where(
                    hit & equal[0] & equal[1], F32(0.5 * grid.scales[d]), F32(0.0)
                )
        k_row = self.as_row(kappa)
        k_column = jnp.sum(jnp.where(same & left, k_row, 0.0), axis=1, keepdims=True)
        coupled = jnp.where(live & left, factor * (k_column + k_row), 0.0)
        diag = mass_rate + jnp.sum(coupled, axis=1, keepdims=True)
        matrix = jnp.where(same & left, diag - coupled, -coupled)
        matrix = jnp.where(left, matrix, jnp.where(same, F32(1.0), F32(0.0)))
        for n in range(cells):
            lane = (n // across) * step_z + n % across
            pivot_row = matrix[n : n + 1] / matrix[n : n + 1, lane : lane + 1]
            column = matrix[:, lane : lane + 1]
            matrix = jnp.where(i == n, pivot_row, matrix - column * pivot_row)
        self.inverse = jnp.where((j >= period) & (j < 2 * period) & live, matrix, 0.0)

    def as_row(self, v):
        grid = self.grid
        size_x, size_y, _ = grid.sizes
        step_y, step_z = grid.strides
        sub = mod(iota((1, grid.lanes), 1), step_z)
        result = jnp.zeros((1, grid.lanes), F32)
        for x in range(size_x):
            for y in range(size_y):
                row = v[x, y * step_y : y * step_y + 1]
                result = jnp.where(sub == x * size_y + y, row, result)
        return result

    def solve(self, forcing):
        grid = self.grid
        size_x, size_y, _ = grid.sizes
        step_y, step_z = grid.strides
        solved = jnp.sum(self.inverse * self.as_row(forcing), axis=1, keepdims=True)
        at_z = div(mod(self.j, self.period), step_z)
        spread = jnp.where(div(self.i, self.across) == at_z, solved, 0.0)
        planes = []
        for x in range(size_x):
            rows = []
            for y in range(size_y):
                mine = mod(self.i, self.across) == x * size_y + y
                row = jnp.sum(jnp.where(mine, spread, 0.0), axis=0, keepdims=True)
                rows.append(jnp.broadcast_to(row, (step_y, grid.lanes)))
            planes.append(jnp.concatenate(rows, 0)[None])
        return jnp.concatenate(planes, 0)


def levels_of(counts, tile_sizes):
    sizes = tuple(count * extent for count, extent in zip(counts, tile_sizes)) + tile_sizes[2:]
    grid = Grid(sizes, (1, 1), (0.0625, 0.0625, 0.0625), sizes[1], LANES)
    grids = [grid]
    while not grid.exact:
        grid = grid.coarser()
        grids.append(grid)
    return grids


def kappa_of(blocks, counts, grid):
    count_x, count_y = counts
    planes, rows, size_z2 = grid.sizes
    half_x, half_y = planes // count_x, rows // count_y
    assert half_x * size_z2 == LANES and half_x == 2 and ROWS % half_y == 0 and half_y == SHORT
    share = ROWS // half_y
    kappa = [[None] * (rows // ROWS) for _ in range(planes)]
    lane = iota((ROWS, LANES), 1)
    at = blocks.shape[1] - 1
    for tx in range(count_x):
        for group in range(rows // ROWS):
            pieces = [blocks[tx * count_y + group * share + n, at] for n in range(share)]
            piece = jnp.concatenate(pieces, 0)
            turned = pltpu.roll(piece, size_z2, 1)
            for p in range(half_x):
                mine = (lane < size_z2) == (p == 0)
                kappa[tx * half_x + p][group] = jnp.where(mine, piece, turned)
    return jnp.concatenate([jnp.concatenate(groups, 0)[None] for groups in kappa], 0)


def prepare(kappa, grids):
    kappas = [kappa]
    for grid in grids[:-1]:
        kappas.append(restrict_whole(kappas[-1], grid))
    exact = ExactSolve(grids[-1], kappas[-1])
    return [(grid, whole_operator(k, grid)) for grid, k in zip(grids[:-1], kappas)], exact


def selectors(sizes, planes1, tile_x1, tile_y1, rows, _, left_one, right_one, left_zero, right_zero):
    rows1 = tile_y1 + 2 * R1
    whole_x1, whole_y1 = 2 * sizes[0], 2 * sizes[1]
    start_x = lax.axis_index("tx") * tile_x1 + (whole_x1 - R1)
    start_y = lax.axis_index("ty") * tile_y1 + (whole_y1 - R1)
    row = iota((planes1 * rows1, 1), 0)
    at_x = mod(div(row, rows1) + start_x, whole_x1)
    at_y = mod(mod(row, rows1) + start_y, whole_y1)
    target = div(at_x, 2) * sizes[1] + div(at_y, 2)
    left_one[...] = ones_where(iota(left_one.shape, 1) == target)
    shape = right_one.shape
    right_one[...] = ones_where(iota(shape, 0) == div(iota(shape, 1), 2))
    row = iota((left_zero.shape[0], 1), 0)
    target = div(row, rows) * rows1 + div(mod(row, rows) + (2 * R1 - RY), 2)
    left_zero[...] = ones_where(iota(left_zero.shape, 1) == target)
    shape = right_zero.shape
    right_zero[...] = ones_where(iota(shape, 0) == div(iota(shape, 1), 2))


def raise_level(left, right, v):
    def terms(x):
        high = x.astype(BF16)
        return high, (x - high.astype(F32)).astype(BF16)

    high, low = terms(v)
    picked = jnp.dot(left, high, preferred_element_type=F32)
    picked_low = jnp.dot(left, low, preferred_element_type=F32)
    return jnp.dot(picked.astype(BF16), right, preferred_element_type=F32) + jnp.dot(
        picked_low.astype(BF16), right, preferred_element_type=F32
    )


def solve_whole(forcing, levels, exact):
    if not levels:
        return exact.solve(forcing)
    grid, operator = levels[0]
    v = operator[4] * forcing
    v = whole_sweep(v, forcing, operator, grid)
    residual = forcing + whole_neighbours(v, operator, grid) - operator[3] * v
    v = v + prolong_whole(solve_whole(restrict_whole(residual, grid), levels[1:], exact), grid)
    for _ in range(2):
        v = whole_sweep(v, forcing, operator, grid)
    return v


def assemble(blocks, count_x, count_y, half_x, half_y, size_z2):
    rows = count_y * half_y
    groups = rows // ROWS
    planes = count_x * half_x
    assert rows % ROWS == 0
    used = half_y + RC
    sub = iota((ROWS, LANES), 0)
    lane = iota((ROWS, LANES), 1)
    nothing = jnp.zeros((ROWS, LANES), F32)
    forcing = [[nothing] * groups for _ in range(planes)]
    half_pairs = (half_x + RC) // 2
    ring = RC // 2
    for tx in range(count_x):
        for ty in range(count_y):
            for p in range(half_pairs):
                tile, base = p * used // SHORT, p * used % SHORT
                assert base + used <= 2 * SHORT == ROWS
                source = tx * count_y + ty
                piece = jnp.concatenate([blocks[source, tile], blocks[source, tile + 1]], 0)
                start = (ty * half_y - ring) % rows
                group, offset = start // ROWS, start % ROWS
                shift = (offset - base) % ROWS
                piece = pltpu.roll(piece, shift, 0) if shift else piece
                turned = pltpu.roll(piece, size_z2, 1)
                for half in range(2):
                    moved = jnp.where((lane < size_z2) == (half == 0), piece, turned)
                    x = (tx * half_x - ring + half * half_pairs + p) % planes
                    at = group
                    mine = (sub >= offset) & (sub < offset + used)
                    forcing[x][at] = forcing[x][at] + jnp.where(mine, moved, 0.0)
                    if offset + used > ROWS:
                        at = (group + 1) % groups
                        mine = sub < offset + used - ROWS
                        forcing[x][at] = forcing[x][at] + jnp.where(mine, moved, 0.0)
    return jnp.concatenate([jnp.concatenate(groups, 0)[None] for groups in forcing], 0)


def coarse_up(
    counts, grids, blocks, window_one, one_near, one_far, row_low, row_high,
    v_zero, forcing0, cx, cy, cz, weight, left_one, right_one, left_zero, right_zero, *rest,
):
    (
        out, mixed_low, mixed_high, kappa_low, kappa_high, first_low, first_high,
        v_one, cx1, cy1, cz1, w1, one_a, one_b, zero_a, zero_b,
    ) = rest
    count_x, count_y = counts
    one_low, one_high = by_side("tx", one_near, one_far)
    _, tile_x1, rows1, size_z1 = window_one.shape
    tile_y1 = rows1 - 2 * R1
    top1 = R1 + tile_y1
    half_x, half_y, size_z2 = tile_x1 // 2, tile_y1 // 2, size_z1 // 2
    sizes = grids[0].sizes
    forcing2 = assemble(blocks, count_x, count_y, half_x, half_y, size_z2)
    levels, exact = prepare(kappa_of(blocks, counts, grids[0]), grids)

    planes1 = tile_x1 + 2 * R1
    for message, mixed, kappa_rim, low in (
        (one_low, mixed_low, kappa_low, True), (one_high, mixed_high, kappa_high, False)
    ):
        at, loose = 0, 2 * R1 * ROWS
        for rim, fill in ((mixed, 0.0), (kappa_rim, 1.0)):
            for layer in range(1, R1 + 1):
                x = R1 - layer if low else layer - 1
                rim[x] = jnp.full((rows1, size_z1), fill, F32)
                rim[x, R1:top1] = message[at]
                at += 1
                for distance in range(1, reach_of(layer) + 1):
                    for row in (R1 - distance, top1 + distance - 1):
                        rim[x, row : row + 1] = message[
                            loose // ROWS, loose % ROWS : loose % ROWS + 1
                        ]
                        loose += 1

    def stacked(low, which, high):
        whole = [(low, x) for x in range(R1)]
        whole += [(window_one.at[which], x) for x in range(tile_x1)]
        whole += [(high, x) for x in range(R1)]
        return Planes(0, whole)

    forcing1 = stacked(mixed_low, 0, mixed_high)
    kappa1 = stacked(kappa_low, 2, kappa_high)
    plane_setup(kappa1, cx1, cy1, cz1, w1, None, 0.25, 1, planes1 - 1)
    row = iota((rows1, size_z1), 0)
    for mixed, rim, low in ((mixed_low, first_low, True), (mixed_high, first_high, False)):
        for layer in range(1, R1 + 1):
            x = R1 - layer if low else layer - 1
            if layer == R1:
                rim[x] = mixed[x]
            else:
                reach = reach_of(layer) - 1
                inside = (row >= R1 - reach) & (row < top1 + reach)
                at = x if low else R1 + tile_x1 + x
                rim[x] = jnp.where(inside, w1[at] * mixed[x], mixed[x])
    start1 = stacked(first_low, 1, first_high)
    plane_sweep(start1, v_one, forcing1, cx1, cy1, cz1, w1, 1, planes1 - 1)

    solved = solve_whole(forcing2, levels, exact)
    solved = solved.reshape(sizes[0] * sizes[1], LANES)

    raised = raise_level(left_one[...], right_one[...], solved)
    for x in range(1, planes1 - 1):
        one_a[x] = v_one[x] + raised[x * rows1 : (x + 1) * rows1]
    plane_sweep(one_a, one_b, forcing1, cx1, cy1, cz1, w1, 2, planes1 - 2)
    plane_sweep(one_b, one_a, forcing1, cx1, cy1, cz1, w1, 3, planes1 - 3)

    planes, rows, size_z = zero_a.shape
    v_zero, forcing0 = kept(v_zero, RX - 1), kept(forcing0, RX - 1)
    cx, cy, cz, weight = kept(cx, RX - 2), kept(cy, RX - 1), kept(cz, RX - 1), kept(weight, RX - 1)
    first, last = R1 - 1, planes1 - R1 + 1
    stack = jnp.concatenate([one_a[x] for x in range(first, last)], 0)
    raised = raise_level(left_zero[...], right_zero[...], stack)
    chunks = size_z // LANES
    top = rows - RY
    for x in range(RX - 1, planes - RX + 1):
        zero_b[x] = v_zero[x]
    for rim_x in (RX - 2, planes - RX + 1):
        zero_b[rim_x] = jnp.zeros((rows, size_z), F32)
    for x in range(planes - 2 * RX):
        at = 3 * tile_x1 * R1 // ROWS
        for chunk in range(chunks):
            lanes = slice(chunk * LANES, (chunk + 1) * LANES)
            zero_b[RX + x, RY - 2 : RY - 1, lanes] = row_low[at + chunk, x : x + 1]
            zero_b[RX + x, top + 1 : top + 2, lanes] = row_high[at + chunk, x : x + 1]
    for message, second, nearest in (
        (one_low, RX - 2, RX - 1), (one_high, planes - RX + 1, planes - RX)
    ):
        loose = 2 * R1 * ROWS + 2 * sum(2 * reach_of(layer) for layer in range(1, R1 + 1))
        for r in (RY - 1, top):
            for chunk in range(chunks):
                lanes = slice(chunk * LANES, (chunk + 1) * LANES)
                zero_b[nearest, r : r + 1, lanes] = message[
                    loose // ROWS, loose % ROWS : loose % ROWS + 1
                ]
                loose += 1
        at = -(-loose // ROWS)
        for chunk in range(chunks):
            lanes = slice(chunk * LANES, (chunk + 1) * LANES)
            for half in range((top - RY) // ROWS):
                zero_b[second, RY + half * ROWS : RY + (half + 1) * ROWS, lanes] = message[at]
                at += 1
    for x in range(RX - 2, planes - RX + 2):
        at = (x - RX + 2 * R1) // 2 - first
        zero_a[x] = zero_b[x] + raised[at * rows : (at + 1) * rows]
    plane_sweep(zero_a, zero_b, forcing0, cx, cy, cz, weight, RX - 1, planes - RX + 1)
    plane_sweep(zero_b, zero_a, forcing0, cx, cy, cz, weight, RX, planes - RX)
    for x in range(planes - 2 * RX):
        out[x] = zero_a[x + RX, RY:top]


VM = pl.BlockSpec(memory_space=pltpu.VMEM)
IN_PLACE = pl.BlockSpec(memory_space=pltpu.HBM)


def call(kernel, operands, outputs, scratch, spec=VM, in_hbm=()):
    def typed(output):
        return output if isinstance(output, jax.ShapeDtypeStruct) else jax.ShapeDtypeStruct(output, F32)

    return pl.pallas_call(
        kernel,
        in_specs=[spec] * len(operands),
        out_specs=[IN_PLACE if n in in_hbm else VM for n in range(len(outputs))],
        out_shape=[typed(output) for output in outputs],
        scratch_shapes=[pltpu.VMEM(s, F32) if isinstance(s, tuple) else s for s in scratch],
        compiler_params=pltpu.CompilerParams(vmem_limit_bytes=24 * 1024 * 1024),
    )(*operands)


def shift_both(to_low, to_high, axis):
    count = lax.axis_size(axis)
    from_low = lax.ppermute(to_high, axis, [(i, (i + 1) % count) for i in range(count)])
    from_high = lax.ppermute(to_low, axis, [((i + 1) % count, i) for i in range(count)])
    return from_low, from_high


def swap_both(near, far, axis):
    count = lax.axis_size(axis)
    assert count % 2 == 0
    partner = [(i, i ^ 1) for i in range(count)]
    other = [(i, (i - 1 if i % 2 == 0 else i + 1) % count) for i in range(count)]
    from_far = lax.ppermute(far, axis, other)
    from_near = lax.ppermute(near, axis, partner)
    return from_near, from_far


def to_everyone(blocks):
    return lax.all_to_all(blocks, ("tx", "ty"), 0, 0)


def cycle(concentration, source, material):
    tile_x, tile_y, size_z = concentration.shape
    chunks = size_z // LANES
    counts = lax.axis_size("tx"), lax.axis_size("ty")
    everyone = counts[0] * counts[1]
    rows = tile_y + 2 * RY
    message = (tile_x + 1, ROWS, size_z)
    *inputs, to_low, to_high = call(
        edges,
        tuple(
            pltpu.with_memory_space_constraint(v, pltpu.HBM)
            for v in (concentration, source, material)
        ),
        tuple(jax.ShapeDtypeStruct(v.shape, v.dtype) for v in (concentration, source, material))
        + (message, message),
        (pltpu.SemaphoreType.DMA((3,)),),
        IN_PLACE,
    )
    from_low, from_high = shift_both(to_low, to_high, "ty")
    zero = (tile_x + 2 * RX, rows, size_z)
    inner = (tile_x + 2, rows, size_z)
    one_tile = (tile_x // 2, tile_y // 2, size_z // 2)
    two_tile = tuple(extent // 2 for extent in one_tile)
    grids = levels_of(counts, two_tile)

    def bits(*shape):
        return jax.ShapeDtypeStruct(shape, BF16)

    k_tile, k_two, halves, halves_one = call(
        shrink,
        inputs[2:],
        (
            one_tile,
            (two_tile[1], LANES),
            bits(chunks, LANES, one_tile[2]),
            bits(2, one_tile[2], one_tile[2]),
        ),
        ((one_tile[0], tile_y, LANES), one_tile[1:]),
    )
    message = (plane_tiles(tile_y), ROWS, size_z)
    window, to_low, to_high = call(
        sides,
        (*inputs, k_tile, from_low, from_high),
        ((3, tile_x, rows, size_z), message, message),
        ((rows, size_z),),
    )
    from_low, from_high = shift_both(to_low, to_high, "tx")
    wide = -(-rows // (2 * ROWS)) * ROWS
    small = (one_tile[0] + 2 * RC, wide, one_tile[2])
    pairs1 = small[0] // 2
    short = pairs1 // 2 * (two_tile[1] + RC) // SHORT + 1
    assert pairs1 // 2 * (two_tile[1] + RC) % SHORT == 0
    message = (3 * one_tile[0] * R1 // ROWS + chunks, ROWS, LANES)
    assert one_tile[2] == LANES and tile_x <= ROWS and one_tile[1] == ROWS
    v_zero, forcing0, cx, cy, cz, weight, level_one, blocks, to_low, to_high = call(
        fine_down,
        (window, k_two, halves, halves_one, from_low, from_high),
        (inner, inner, (tile_x + 3, rows, size_z), inner, inner, inner)
        + ((3,) + one_tile, (everyone, short, SHORT, LANES), message, message),
        (
            (4, rows, size_z),
            (2, rows, size_z),
            (4, rows, size_z),
            zero,
            zero,
            (chunks, max(small[0], tile_x), 2 * wide, LANES),
            (everyone, short, SHORT, LANES),
            pltpu.SemaphoreType.DMA,
        )
        + (small,) * 9
        + ((pairs1, wide, one_tile[2]), (pairs1, ROWS, one_tile[2])),
        in_hbm=(7,),
    )
    row_low, row_high = shift_both(to_low, to_high, "ty")
    blocks = to_everyone(blocks)
    rows1 = one_tile[1] + 2 * R1
    message = (middle_tiles(tile_y, chunks), ROWS, LANES)
    window_one, near, far = call(
        middle,
        (level_one, v_zero, row_low, row_high),
        ((3, one_tile[0], rows1, one_tile[2]), message, message),
        (),
    )
    one_near, one_far = swap_both(near, far, "tx")
    one = (one_tile[0] + 2 * R1, rows1, one_tile[2])
    seen = one[0] - 2 * (R1 - 1)
    chosen = call(
        functools.partial(selectors, grids[0].sizes, one[0], one_tile[0], one_tile[1], rows),
        (window_one,),
        (
            bits(one[0] * rows1, grids[0].sizes[0] * grids[0].sizes[1]),
            bits(LANES, one_tile[2]),
            bits(seen * rows, seen * rows1),
            bits(one_tile[2], size_z),
        ),
        (),
    )
    rim = (R1,) + one[1:]
    (updated,) = call(
        functools.partial(coarse_up, counts, grids),
        (blocks, window_one, one_near, one_far, row_low, row_high)
        + (v_zero, forcing0, cx, cy, cz, weight, *chosen),
        (concentration.shape,),
        (rim,) * 6 + (one,) * 7 + (zero, zero),
    )
    return updated


def solution(mesh):
    placed = (P("tx", "ty", None), P("tx", "ty", None), P("tx", "ty", None))
    return jax.shard_map(
        cycle, mesh=mesh, in_specs=placed, out_specs=P("tx", "ty", None), check_vma=False
    )
```

```python
import functools

import jax
import jax.numpy as jnp
from jax import lax
from jax.experimental import pallas as pl
from jax.experimental.pallas import tpu as pltpu
from jax.sharding import PartitionSpec as P


mass_rate = 0.001
relax_weight = 0.8
diffusivities = (0.15, 0.3, 0.5, 0.8, 1.2, 2.0, 3.2, 5.0)
LANES = 128
ROWS = 8
SHORT = 4
RX = 2
RY = 4
R1 = 4
RC = 2
F32 = jnp.float32
BF16 = jnp.bfloat16


def lookup(material):
    result = jnp.zeros(material.shape, F32)
    for slot_id, coeff_value in enumerate(diffusivities):
        result = jnp.where(material == slot_id, F32(coeff_value), result)
    return result


class Planes:
    def __init__(self, first, planes):
        self.first = first
        self.planes = planes

    def __getitem__(self, x):
        ref, index = self.planes[x - self.first]
        return ref[index]

    def __setitem__(self, x, value):
        ref, index = self.planes[x - self.first]
        ref[index] = value


def kept(ref, first):
    return Planes(first, [(ref, x) for x in range(ref.shape[0])])


def is_even(axis):
    return lax.rem(lax.axis_index(axis), 2) == 0


def on_sides(axis, near, far, body):
    @pl.when(is_even(axis))
    def _():
        body(far, near)

    @pl.when(jnp.logical_not(is_even(axis)))
    def _():
        body(near, far)


class Picked:
    def __init__(self, flag, when_true, when_false):
        self.flag = flag
        self.when_true = when_true
        self.when_false = when_false

    def __getitem__(self, index):
        first, second = self.when_true[index], self.when_false[index]
        flag = jnp.where(self.flag, jnp.int32(1), jnp.int32(0))
        return jnp.where(jnp.full(first.shape, flag) == 1, first, second)


def by_side(axis, near, far):
    even = is_even(axis)
    return Picked(even, far, near), Picked(even, near, far)


def iota(shape, dim):
    return lax.broadcasted_iota(jnp.int32, shape, dim)


def div(a, b):
    return lax.div(a, jnp.full_like(a, b))


def mod(a, b):
    return lax.rem(a, jnp.full_like(a, b))


def ones_where(mask):
    return jnp.where(mask, F32(1.0), F32(0.0)).astype(BF16)


def three_terms(x):
    high = x.astype(BF16)
    rest = x - high.astype(F32)
    middle = rest.astype(BF16)
    low = (rest - middle.astype(F32)).astype(BF16)
    return high, middle, low


def times_right(x, selector):
    parts = [jnp.dot(part, selector, preferred_element_type=F32) for part in three_terms(x)]
    return parts[0] + (parts[1] + parts[2])


def back(v, axis, step=1):
    return pltpu.roll(v, step, axis)


def ahead(v, axis, step=1):
    return pltpu.roll(v, v.shape[axis] - step, axis)


def halve_lanes(fine, coarse, start=0):
    shape = (fine, coarse)
    return ones_where(div(iota(shape, 0), 2) + start == iota(shape, 1))


def plane_setup(kappa, cx, cy, cz, weight, diag, scale, first, last):
    half = 0.5 * scale
    for x in range(first - 1, last):
        cx[x] = half * (kappa[x] + kappa[x + 1])
    for x in range(first, last):
        k = kappa[x]
        y_part = half * (k + ahead(k, 0))
        z_part = half * (k + ahead(k, 1))
        cy[x] = y_part
        cz[x] = z_part
        d = mass_rate + cx[x] + cx[x - 1] + y_part + back(y_part, 0) + z_part + back(z_part, 1)
        weight[x] = relax_weight / d
        if diag is not None:
            diag[x] = d


def in_plane(here, cy, cz, x):
    y_part = cy[x]
    z_part = cz[x]
    total = y_part * ahead(here, 0) + back(y_part * here, 0)
    return total + (z_part * ahead(here, 1) + back(z_part * here, 1))


def neighbours(v, cx, cy, cz, x):
    return (cx[x] * v[x + 1] + cx[x - 1] * v[x - 1]) + in_plane(v[x], cy, cz, x)


def plane_sweep(v, out, forcing, cx, cy, cz, weight, first, last):
    for x in range(first, last):
        out[x] = (1.0 - relax_weight) * v[x] + weight[x] * (forcing[x] + neighbours(v, cx, cy, cz, x))


def edges(conc_in, source_in, material_in, conc, source, material, to_low, to_high, arrived):
    copies = [
        pltpu.make_async_copy(whence, whither, arrived.at[n])
        for n, (whence, whither) in enumerate(
            ((conc_in, conc), (source_in, source), (material_in, material))
        )
    ]
    for copy in copies:
        copy.start()
    for copy in copies:
        copy.wait()
    tile_x, tile_y, _ = conc.shape
    for to, low in ((to_low, True), (to_high, False)):
        for x in range(tile_x):
            rows = slice(0, 4) if low else slice(tile_y - 4, tile_y)
            near = slice(0, 3) if low else slice(1, 4)
            pair = slice(0, 2) if low else slice(2, 4)
            c = conc[x, rows]
            f = mass_rate * c + source[x, rows]
            k = lookup(material[x, rows])
            to[x, 0:3] = c[near]
            to[x, 3:5] = f[pair]
            to[x, 5:8] = k[near]
            to[tile_x, x : x + 1] = k[3:4] if low else k[0:1]


def sides(conc, source, material, k_tile, from_low, from_high, window, to_low, to_high, swept):
    tile_x, tile_y, size_z = conc.shape
    top = RY + tile_y
    for x in range(tile_x):
        c = conc[x]
        window[0, x, RY:top] = c
        window[1, x, RY:top] = mass_rate * c + source[x]
        window[2, x, RY:top] = lookup(material[x])
        window[0, x, 0:1] = jnp.zeros((1, size_z), F32)
        window[0, x, 1:4] = from_low[x, 0:3]
        window[0, x, top : top + 3] = from_high[x, 0:3]
        window[0, x, top + 3 :] = jnp.zeros((1, size_z), F32)
        window[1, x, 0:2] = jnp.zeros((2, size_z), F32)
        window[1, x, 2:4] = from_low[x, 3:5]
        window[1, x, top : top + 2] = from_high[x, 3:5]
        window[1, x, top + 2 :] = jnp.zeros((2, size_z), F32)
        window[2, x, 0:1] = from_low[tile_x, x : x + 1]
        window[2, x, 1:4] = from_low[x, 5:8]
        window[2, x, top : top + 3] = from_high[x, 5:8]
        window[2, x, top + 3 :] = from_high[tile_x, x : x + 1]
    per_plane = tile_y // ROWS
    for to, low in ((to_low, True), (to_high, False)):

        def plane(layer):
            return layer - 1 if low else tile_x - layer

        def send(at, values):
            for n in range(per_plane):
                to[at + n] = values(n)

        for n, (which, layer) in enumerate(BASE_PLANES):
            send(
                n * per_plane,
                lambda n: window[which, plane(layer), RY + n * ROWS : RY + (n + 1) * ROWS],
            )
        first_sweep(window, plane(2), swept)
        at = len(BASE_PLANES) * per_plane
        send(at, lambda n: swept[RY + n * ROWS : RY + (n + 1) * ROWS])
        loose = (at + per_plane) * ROWS
        for which, layer, reach in EXTRA_ROWS:
            for start in (RY - reach, top):
                to[loose // ROWS, loose % ROWS : loose % ROWS + reach] = window[
                    which, plane(layer), start : start + reach
                ]
                loose += reach
        at = -(-loose // ROWS)
        to[at, :, 0 : size_z // 2] = k_tile[1 if low else k_tile.shape[0] - 2]
        to[at, :, size_z // 2 :] = jnp.zeros((ROWS, size_z - size_z // 2), F32)


def first_sweep(window, x, out):
    c, f, k = window[0, x], window[1, x], window[2, x]
    next_part = 0.5 * (k + window[2, x + 1])
    last_part = 0.5 * (k + window[2, x - 1])
    y_part = 0.5 * (k + ahead(k, 0))
    z_part = 0.5 * (k + ahead(k, 1))
    d = mass_rate + next_part + last_part
    d = d + y_part + back(y_part, 0) + z_part + back(z_part, 1)
    total = next_part * window[0, x + 1] + last_part * window[0, x - 1]
    total = total + (y_part * ahead(c, 0) + back(y_part * c, 0))
    total = total + (z_part * ahead(c, 1) + back(z_part * c, 1))
    out[...] = (1.0 - relax_weight) * c + (relax_weight / d) * (f + total)


BASE_PLANES = ((0, 1), (0, 2), (1, 1), (2, 1), (2, 2))
EXTRA_ROWS = ((0, 1, 2), (0, 2, 1), (1, 1, 1), (2, 1, 2), (2, 2, 2))


def plane_tiles(tile_y):
    loose = sum(2 * reach for _, _, reach in EXTRA_ROWS)
    return (len(BASE_PLANES) + 1) * tile_y // ROWS + -(-loose // ROWS) + 1


def shrink(material, k_tile, blocks, halves, halves_one, paired, paired_one):
    tile_x, tile_y, size_z = material.shape
    tile_x1, tile_y1, size_z1 = tile_x // 2, tile_y // 2, size_z // 2
    k_one = None
    for chunk in range(size_z // LANES):
        lanes = slice(chunk * LANES, (chunk + 1) * LANES)
        for pair in range(tile_x1):
            paired[pair] = lookup(material[2 * pair, :, lanes]) + lookup(
                material[2 * pair + 1, :, lanes]
            )
        stack = [
            paired[pair, pl.ds(0, tile_y1, stride=2)] + paired[pair, pl.ds(1, tile_y1, stride=2)]
            for pair in range(tile_x1)
        ]
        part = times_right(
            jnp.concatenate(stack, 0), halve_lanes(LANES, size_z1, chunk * LANES // 2)
        )
        k_one = part if k_one is None else k_one + part
    k_one = 0.125 * k_one
    for x in range(tile_x1):
        k_tile[x] = k_one[x * tile_y1 : (x + 1) * tile_y1]
    assert tile_x1 // 2 * (size_z1 // 2) <= LANES
    block = None
    for pair in range(tile_x1 // 2):
        at = 2 * pair * tile_y1
        paired_one[...] = k_one[at : at + tile_y1] + k_one[at + tile_y1 : at + 2 * tile_y1]
        piece = (
            paired_one[pl.ds(0, tile_y1 // 2, stride=2)] + paired_one[pl.ds(1, tile_y1 // 2, stride=2)]
        )
        part = times_right(piece, halve_lanes(size_z1, LANES, pair * size_z1 // 2))
        block = part if block is None else block + part
    block = 0.125 * block
    for device in range(blocks.shape[0]):
        blocks[device] = block
    for chunk in range(size_z // LANES):
        halves[chunk] = halve_lanes(LANES, size_z1, chunk * LANES // 2)
    for half in range(2):
        halves_one[half] = halve_lanes(size_z1, size_z1, half * size_z1 // 2)


def fine_down(
    window, halves, halves_one, from_low, from_high,
    v_zero, forcing_out, cx, cy, cz, weight, level_one, blocks_out, to_low, to_high,
    conc_rim, forcing_rim, kappa_rim, once, diag, paired, blocks, left,
    k_one, f_one, u_one, v_one, cx1, cy1, cz1, w1, d1, paired_one, packed,
):
    _, tile_x, rows, size_z = window.shape
    tile_y = rows - 2 * RY
    top = RY + tile_y
    planes = tile_x + 2 * RX
    rims = (conc_rim, forcing_rim, kappa_rim)
    depths = (2, 1, 2)
    for which, rim in enumerate(rims):
        fill = jnp.full((rows, size_z), 1.0 if which == 2 else 0.0, F32)
        for x in range(2 * depths[which]):
            rim[x] = fill

    def place(which, layer, low):
        return depths[which] - layer if low else depths[which] + layer - 1

    per_plane = tile_y // ROWS
    last_tile = plane_tiles(tile_y) - 1
    for message, low in ((from_low, True), (from_high, False)):
        for at, (which, layer) in enumerate(BASE_PLANES):
            for n in range(per_plane):
                start = RY + n * ROWS
                rims[which][place(which, layer, low), start : start + ROWS] = message[
                    at * per_plane + n
                ]
        rim_x = 0 if low else planes - 1
        once[rim_x] = jnp.zeros((rows, size_z), F32)
        at = len(BASE_PLANES) * per_plane
        for n in range(per_plane):
            start = RY + n * ROWS
            once[rim_x, start : start + ROWS] = message[at + n]
        loose = (at + per_plane) * ROWS
        for which, layer, reach in EXTRA_ROWS:
            for start in (RY - reach, top):
                rims[which][place(which, layer, low), start : start + reach] = message[
                    loose // ROWS, loose % ROWS : loose % ROWS + reach
                ]
                loose += reach

    def stacked(which):
        depth = depths[which]
        whole = [(rims[which], x) for x in range(depth)]
        whole += [(window.at[which], x) for x in range(tile_x)]
        whole += [(rims[which], depth + x) for x in range(depth)]
        return Planes(RX - depth, whole)

    conc, forcing, kappa = stacked(0), stacked(1), stacked(2)
    cx, cy, cz, weight = kept(cx, RX - 2), kept(cy, RX - 1), kept(cz, RX - 1), kept(weight, RX - 1)
    v_out = kept(v_zero, RX - 1)
    plane_setup(kappa, cx, cy, cz, weight, diag, 1.0, 1, planes - 1)
    plane_sweep(conc, once, forcing, cx, cy, cz, weight, 1, planes - 1)
    plane_sweep(once, v_out, forcing, cx, cy, cz, weight, 1, planes - 1)
    chunks = size_z // LANES
    size_z1 = size_z // 2
    to_half = [halves[chunk] for chunk in range(chunks)]
    tile_x1, tile_y1 = tile_x // 2, tile_y // 2

    def put(pair, total):
        for chunk in range(chunks):
            paired[chunk, pair, 0:rows] = total[:, chunk * LANES : (chunk + 1) * LANES]

    def narrowed(pairs, start, count):
        result = None
        for chunk in range(chunks):
            stack = [
                paired[chunk, pair, pl.ds(start, count, stride=2)]
                + paired[chunk, pair, pl.ds(start + 1, count, stride=2)]
                for pair in range(pairs)
            ]
            part = times_right(jnp.concatenate(stack, 0), to_half[chunk])
            result = part if result is None else result + part
        return 0.125 * result

    wide = paired.shape[2] // 2
    planes1 = tile_x1 + 2 * RC
    if 2 * wide > rows:
        for chunk in range(chunks):
            for pair in range(planes1 - 2):
                paired[chunk, pair, rows:] = jnp.ones((2 * wide - rows, LANES), F32)
    for pair in range(planes1 - 2):
        put(pair, kappa[2 * pair] + kappa[2 * pair + 1])
    coarse = narrowed(planes1 - 2, 0, wide)
    for pair in range(planes1 - 2):
        k_one[pair + 1] = coarse[pair * wide : (pair + 1) * wide]
    for message, x in ((from_low, 0), (from_high, planes1 - 1)):
        k_one[x] = jnp.ones((wide, size_z1), F32)
        k_one[x, RC : RC + tile_y1] = message[last_tile, :, 0:size_z1]
    plane_setup(k_one, cx1, cy1, cz1, w1, d1, 0.25, 1, planes1 - 1)

    for pair in range(tile_x1):
        total = None
        for x in (RX + 2 * pair, RX + 2 * pair + 1):
            part = forcing[x] + neighbours(v_out, cx, cy, cz, x) - diag[x] * v_out[x]
            total = part if total is None else total + part
        put(pair, total)
    forcing_one = narrowed(tile_x1, RY, tile_y1)

    low, high = RC, RC + tile_y1
    nothing = jnp.zeros((wide, size_z1), F32)
    for x in range(planes1):
        f_one[x] = nothing
        if x in (0, planes1 - 1):
            v_one[x] = nothing
    for x in (0, 1, planes1 - 2, planes1 - 1):
        u_one[x] = nothing
    for x in range(tile_x1):
        f = forcing_one[x * tile_y1 : (x + 1) * tile_y1]
        f_one[x + RC, low:high] = f
        u_one[x + RC] = w1[x + RC] * f_one[x + RC]
        level_one[0, x] = f
        level_one[1, x] = u_one[x + RC, low:high]
        level_one[2, x] = k_one[x + RC, low:high]
    plane_sweep(u_one, v_one, f_one, cx1, cy1, cz1, w1, 1, planes1 - 1)
    pairs1 = planes1 // 2
    for pair in range(pairs1):
        total = None
        for x in (2 * pair, 2 * pair + 1):
            if x == 0:
                part = cx1[0] * v_one[1]
            elif x == planes1 - 1:
                part = cx1[x - 1] * v_one[x - 1]
            else:
                part = f_one[x] + neighbours(v_one, cx1, cy1, cz1, x) - d1[x] * v_one[x]
            total = part if total is None else total + part
        paired_one[pair] = total
    for pair in range(pairs1):
        packed[pair] = (
            paired_one[pair, pl.ds(0, ROWS, stride=2)] + paired_one[pair, pl.ds(1, ROWS, stride=2)]
        )
    half_pairs = pairs1 // 2
    result = times_right(
        jnp.concatenate([packed[p] for p in range(half_pairs)], 0), halves_one[0]
    ) + times_right(
        jnp.concatenate([packed[half_pairs + p] for p in range(half_pairs)], 0), halves_one[1]
    )
    used = tile_y1 // 2 + RC
    block = jnp.concatenate([result[p * ROWS : p * ROWS + used] for p in range(half_pairs)], 0)
    block = 0.125 * block
    for part in range(blocks.shape[1]):
        piece = block[part * SHORT : (part + 1) * SHORT]
        for device in range(blocks.shape[0]):
            blocks[device, part] = piece
    copy = pltpu.make_async_copy(blocks, blocks_out, left)
    copy.start()
    for x in range(RX - 1, planes - RX + 1):
        forcing_out[x - RX + 1] = forcing[x]

    for to, rows1, row0 in (
        (to_low, slice(0, R1), RY + 1),
        (to_high, slice(tile_y1 - R1, tile_y1), top - 2),
    ):
        for which in range(3):
            for x in range(tile_x1):
                flat_row = which * tile_x1 * R1 + x * R1
                to[flat_row // ROWS, flat_row % ROWS : flat_row % ROWS + R1] = level_one[
                    which, x, rows1
                ]
        start = 3 * tile_x1 * R1 // ROWS
        for x in range(tile_x):
            row = v_zero[x + 1, row0 : row0 + 1]
            for chunk in range(chunks):
                to[start + chunk, x : x + 1] = row[:, chunk * LANES : (chunk + 1) * LANES]
    copy.wait()


def reach_of(layer):
    return R1 + 1 - layer


def middle(level_one, v_zero, from_low, from_high, window, near, far):
    _, tile_x1, tile_y1, _ = level_one.shape
    planes, rows, size_z = v_zero.shape
    top1 = R1 + tile_y1
    for which in range(3):
        for x in range(tile_x1):
            flat_row = which * tile_x1 * R1 + x * R1
            at, sub = flat_row // ROWS, flat_row % ROWS
            window[which, x, R1:top1] = level_one[which, x]
            window[which, x, 0:R1] = from_low[at, sub : sub + R1]
            window[which, x, top1:] = from_high[at, sub : sub + R1]
    chunks = size_z // LANES
    top = rows - RY

    def pack(to_low, to_high):
        for to, low in ((to_low, True), (to_high, False)):
            at = 0
            for which in (0, 2):
                for layer in range(1, R1 + 1):
                    x = layer - 1 if low else tile_x1 - layer
                    outer = 1 if which == 0 and layer == R1 else which
                    to[at] = window[outer, x, R1:top1]
                    at += 1
            loose = at * ROWS
            for which in (0, 2):
                for layer in range(1, R1 + 1):
                    x = layer - 1 if low else tile_x1 - layer
                    outer = 1 if which == 0 else which
                    for distance in range(1, reach_of(layer) + 1):
                        source = outer if distance == reach_of(layer) else which
                        for row in (R1 - distance, top1 + distance - 1):
                            to[loose // ROWS, loose % ROWS : loose % ROWS + 1] = window[
                                source, x, row : row + 1
                            ]
                            loose += 1
            second, first = (2, 1) if low else (planes - 3, planes - 2)
            for row in (RY - 1, top):
                for chunk in range(chunks):
                    lanes = slice(chunk * LANES, (chunk + 1) * LANES)
                    to[loose // ROWS, loose % ROWS : loose % ROWS + 1] = v_zero[first, row : row + 1, lanes]
                    loose += 1
            at = -(-loose // ROWS)
            for chunk in range(chunks):
                lanes = slice(chunk * LANES, (chunk + 1) * LANES)
                for half in range((top - RY) // ROWS):
                    to[at] = v_zero[second, RY + half * ROWS : RY + (half + 1) * ROWS, lanes]
                    at += 1

    on_sides("tx", near, far, pack)


def middle_tiles(tile_y, chunks):
    loose = 2 * sum(2 * reach_of(layer) for layer in range(1, R1 + 1)) + 2 * chunks
    return 2 * R1 + -(-loose // ROWS) + chunks * tile_y // ROWS


class Grid:
    def __init__(self, sizes, strides, scales, rows, lanes):
        self.sizes = sizes
        self.strides = strides
        self.scales = scales
        self.rows = rows
        self.lanes = lanes
        self.ratios = tuple(2 if extent % 2 == 0 else 1 for extent in sizes)
        self.cells = sizes[0] * sizes[1] * sizes[2]
        self.exact = self.cells <= 64 or self.ratios == (1, 1, 1)

    def coarser(self):
        sizes = tuple(extent // ratio for extent, ratio in zip(self.sizes, self.ratios))
        scales = tuple(s / (ratio * ratio) for s, ratio in zip(self.scales, self.ratios))
        strides = tuple(s * ratio for s, ratio in zip(self.strides, self.ratios[1:]))
        return Grid(sizes, strides, scales, self.rows, self.lanes)


def swapped(v):
    return pltpu.roll(v, v.shape[-1] // 2, v.ndim - 1)


def along_z(v, step):
    lanes = v.shape[2]
    half = lanes // 2
    lane = mod(iota(v.shape, 2), half)
    if step > 0:
        mine = lane < half - step
        return jnp.where(mine, pltpu.roll(v, lanes - step, 2), pltpu.roll(v, half - step, 2))
    mine = lane >= -step
    return jnp.where(mine, pltpu.roll(v, -step, 2), pltpu.roll(v, half - step, 2))


def next_plane(v):
    return jnp.concatenate([v[1:], swapped(v[:1])], 0) if v.shape[0] > 1 else swapped(v)


def last_plane(v):
    return jnp.concatenate([swapped(v[-1:]), v[:-1]], 0) if v.shape[0] > 1 else swapped(v)


def restrict_whole(v, grid):
    assert grid.ratios == (2, 2, 2) and v.shape[0] % 2 == 0
    v = jnp.concatenate(
        [v[2 * x : 2 * x + 1] + v[2 * x + 1 : 2 * x + 2] for x in range(v.shape[0] // 2)], 0
    )
    step_y, step_z = grid.strides
    even = mod(div(iota(v.shape, 1), step_y), 2) == 0
    v = v + jnp.where(even, ahead(v, 1, step_y), back(v, 1, step_y))
    even = mod(div(iota(v.shape, 2), step_z), 2) == 0
    v = v + jnp.where(even, ahead(v, 2, step_z), back(v, 2, step_z))
    return 0.125 * v


def prolong_whole(v, grid):
    return jnp.concatenate([v[x // 2 : x // 2 + 1] for x in range(grid.sizes[0] // 2)], 0)


def whole_operator(kappa, grid):
    half_x, half_y, half_z = (0.5 * s for s in grid.scales)
    step_y, step_z = grid.strides
    cx = half_x * (kappa + next_plane(kappa))
    cy = half_y * (kappa + ahead(kappa, 1, step_y))
    cz = half_z * (kappa + along_z(kappa, step_z))
    diag = mass_rate + cx + last_plane(cx)
    diag = diag + (cy + back(cy, 1, step_y)) + (cz + along_z(cz, -step_z))
    return cx, cy, cz, diag, relax_weight / diag


def whole_neighbours(v, operator, grid):
    cx, cy, cz = operator[:3]
    step_y, step_z = grid.strides
    total = cx * next_plane(v) + last_plane(cx * v)
    total = total + (cy * ahead(v, 1, step_y) + back(cy * v, 1, step_y))
    return total + (cz * along_z(v, step_z) + along_z(cz * v, -step_z))


def whole_sweep(v, forcing, operator, grid):
    return (1.0 - relax_weight) * v + operator[4] * (forcing + whole_neighbours(v, operator, grid))


def doubled(planes):
    first, second = planes
    return jnp.where(iota(first.shape, first.ndim - 1) < first.shape[-1] // 2, first, second)


class ExactSolve:
    def __init__(self, grid, kappa=None, inverse=None):
        size_x, size_y, size_z = grid.sizes
        self.grid = grid
        self.across = across = size_x * size_y
        _, step_z = grid.strides
        self.period = period = size_z * step_z
        cells = grid.cells
        padded = -(-cells // ROWS) * ROWS
        assert across <= step_z and 2 * period <= grid.lanes
        shape = (padded, grid.lanes)
        i, j = iota(shape, 0), iota(shape, 1)
        self.i, self.j = i, j
        if kappa is None:
            self.inverse = inverse
            return

        def places_of_row(n):
            sub = mod(n, across)
            return div(sub, size_y), mod(sub, size_y), div(n, across)

        def places_of_lane(n):
            n = mod(n, period)
            sub = mod(n, step_z)
            return div(sub, size_y), mod(sub, size_y), div(n, step_z)

        at_i, at_j = places_of_row(i), places_of_lane(j)
        live = (mod(j, step_z) < across) & (i < cells)
        same = (at_i[0] == at_j[0]) & (at_i[1] == at_j[1]) & (at_i[2] == at_j[2]) & live
        left = j < period
        factor = jnp.zeros(shape, F32)
        for d in range(3):
            equal = [at_i[other] == at_j[other] for other in range(3) if other != d]
            for step in (1, grid.sizes[d] - 1):
                hit = mod(at_i[d] + step, grid.sizes[d]) == at_j[d]
                factor = factor + jnp.where(
                    hit & equal[0] & equal[1], F32(0.5 * grid.scales[d]), F32(0.0)
                )
        k_row = self.as_row(kappa)
        k_column = jnp.sum(jnp.where(same & left, k_row, 0.0), axis=1, keepdims=True)
        coupled = jnp.where(live & left, factor * (k_column + k_row), 0.0)
        diag = mass_rate + jnp.sum(coupled, axis=1, keepdims=True)
        matrix = jnp.where(same & left, diag - coupled, -coupled)
        matrix = jnp.where(left, matrix, jnp.where(same, F32(1.0), F32(0.0)))
        for n in range(cells):
            lane = (n // across) * step_z + n % across
            pivot_row = matrix[n : n + 1] / matrix[n : n + 1, lane : lane + 1]
            column = matrix[:, lane : lane + 1]
            matrix = jnp.where(i == n, pivot_row, matrix - column * pivot_row)
        self.inverse = jnp.where((j >= period) & (j < 2 * period) & live, matrix, 0.0)

    def as_row(self, v):
        grid = self.grid
        size_x, size_y, _ = grid.sizes
        step_y, step_z = grid.strides
        assert size_x == 2
        turned = swapped(v)
        planes = [doubled((v[0], turned[0])), doubled((turned[0], v[0]))]
        sub = mod(iota((1, grid.lanes), 1), step_z)
        result = jnp.zeros((1, grid.lanes), F32)
        for x in range(size_x):
            for y in range(size_y):
                row = planes[x][y * step_y : y * step_y + 1]
                result = jnp.where(sub == x * size_y + y, row, result)
        return result

    def solve(self, forcing):
        grid = self.grid
        size_x, size_y, _ = grid.sizes
        step_y, step_z = grid.strides
        solved = jnp.sum(self.inverse * self.as_row(forcing), axis=1, keepdims=True)
        at_z = div(mod(self.j, self.period), step_z)
        spread = jnp.where(div(self.i, self.across) == at_z, solved, 0.0)
        planes = []
        for x in range(size_x):
            rows = []
            for y in range(size_y):
                mine = mod(self.i, self.across) == x * size_y + y
                row = jnp.sum(jnp.where(mine, spread, 0.0), axis=0, keepdims=True)
                rows.append(jnp.broadcast_to(row, (step_y, grid.lanes)))
            planes.append(jnp.concatenate(rows, 0))
        return doubled(planes)[None]


def levels_of(counts, tile_sizes):
    sizes = tuple(count * extent for count, extent in zip(counts, tile_sizes)) + tile_sizes[2:]
    grid = Grid(sizes, (1, 1), (0.0625, 0.0625, 0.0625), sizes[1], LANES)
    grids = [grid]
    while not grid.exact:
        grid = grid.coarser()
        grids.append(grid)
    return grids


class Operator:
    def __init__(self, ref):
        self.ref = ref

    def __getitem__(self, part):
        if isinstance(part, slice):
            return [self.ref[p] for p in range(*part.indices(5))]
        return self.ref[part]


def prepare(counts, grids, blocks, _, *outputs):
    count_x, count_y = counts
    planes, rows, size_z2 = grids[0].sizes
    half_x, half_y = planes // count_x, rows // count_y
    assert 2 * size_z2 == LANES and half_x == 2 and half_y == SHORT and planes % 2 == 0
    share = ROWS // half_y
    pairs = planes // 2
    kappa = [[None] * (rows // ROWS) for _ in range(pairs)]
    lower = iota((ROWS, LANES), 1) < size_z2
    for tx in range(count_x):
        for group in range(rows // ROWS):
            piece = jnp.concatenate(
                [blocks[tx * count_y + group * share + n] for n in range(share)], 0
            )
            turned = swapped(piece)
            for p in range(half_x):
                x = tx * half_x + p
                value = piece if x // pairs == p else turned
                if x >= pairs:
                    value = jnp.where(lower, kappa[x % pairs][group], value)
                kappa[x % pairs][group] = value
    kappas = [jnp.concatenate([jnp.concatenate(groups, 0)[None] for groups in kappa], 0)]
    for grid in grids[:-1]:
        kappas.append(restrict_whole(kappas[-1], grid))
    outputs[-1][...] = ExactSolve(grids[-1], kappas[-1]).inverse
    for number, grid in enumerate(grids[:-1]):
        for part, value in enumerate(whole_operator(kappas[number], grid)):
            outputs[number][part] = value


def selectors(sizes, planes1, tile_x1, tile_y1, rows, _, left_one, right_one, left_zero, right_zero):
    rows1 = tile_y1 + 2 * R1
    whole_x1, whole_y1 = 2 * sizes[0], 2 * sizes[1]
    start_x = lax.axis_index("tx") * tile_x1 + (whole_x1 - R1)
    start_y = lax.axis_index("ty") * tile_y1 + (whole_y1 - R1)
    row = iota((planes1 * rows1, 1), 0)
    at_x = mod(div(row, rows1) + start_x, whole_x1)
    at_y = mod(mod(row, rows1) + start_y, whole_y1)
    target = div(at_x, 2) * sizes[1] + div(at_y, 2)
    left_one[...] = ones_where(iota(left_one.shape, 1) == target)
    shape = right_one.shape
    right_one[...] = ones_where(iota(shape, 0) == div(iota(shape, 1), 2))
    row = iota((left_zero.shape[0], 1), 0)
    target = div(row, rows) * rows1 + div(mod(row, rows) + (2 * R1 - RY), 2)
    left_zero[...] = ones_where(iota(left_zero.shape, 1) == target)
    shape = right_zero.shape
    right_zero[...] = ones_where(iota(shape, 0) == div(iota(shape, 1), 2))


def raise_level(left, right, v):
    def terms(x):
        high = x.astype(BF16)
        return high, (x - high.astype(F32)).astype(BF16)

    high, low = terms(v)
    picked = jnp.dot(left, high, preferred_element_type=F32)
    picked_low = jnp.dot(left, low, preferred_element_type=F32)
    return jnp.dot(picked.astype(BF16), right, preferred_element_type=F32) + jnp.dot(
        picked_low.astype(BF16), right, preferred_element_type=F32
    )


def solve_whole(forcing, levels, exact):
    if not levels:
        return exact.solve(forcing)
    grid, operator = levels[0]
    v = operator[4] * forcing
    v = whole_sweep(v, forcing, operator, grid)
    residual = forcing + whole_neighbours(v, operator, grid) - operator[3] * v
    v = v + prolong_whole(solve_whole(restrict_whole(residual, grid), levels[1:], exact), grid)
    for _ in range(2):
        v = whole_sweep(v, forcing, operator, grid)
    return v


def assemble(blocks, count_x, count_y, half_x, half_y, size_z2):
    rows = count_y * half_y
    groups = rows // ROWS
    planes = count_x * half_x
    assert rows % ROWS == 0
    used = half_y + RC
    sub = iota((ROWS, LANES), 0)
    lane = iota((ROWS, LANES), 1)
    nothing = jnp.zeros((ROWS, LANES), F32)
    pairs = planes // 2
    forcing = [[nothing] * groups for _ in range(pairs)]
    half_pairs = (half_x + RC) // 2
    ring = RC // 2
    for tx in range(count_x):
        for ty in range(count_y):
            for p in range(half_pairs):
                tile, base = p * used // SHORT, p * used % SHORT
                assert base + used <= 2 * SHORT == ROWS
                source = tx * count_y + ty
                piece = jnp.concatenate([blocks[source, tile], blocks[source, tile + 1]], 0)
                start = (ty * half_y - ring) % rows
                group, offset = start // ROWS, start % ROWS
                shift = (offset - base) % ROWS
                piece = pltpu.roll(piece, shift, 0) if shift else piece
                for half in range(2):
                    x = (tx * half_x - ring + half * half_pairs + p) % planes
                    moved = piece if x // pairs == half else swapped(piece)
                    here = (lane < size_z2) == (x < pairs)
                    at = group
                    mine = here & (sub >= offset) & (sub < offset + used)
                    forcing[x % pairs][at] = forcing[x % pairs][at] + jnp.where(mine, moved, 0.0)
                    if offset + used > ROWS:
                        at = (group + 1) % groups
                        mine = here & (sub < offset + used - ROWS)
                        forcing[x % pairs][at] = forcing[x % pairs][at] + jnp.where(mine, moved, 0.0)
    return jnp.concatenate([jnp.concatenate(groups, 0)[None] for groups in forcing], 0)


def coarse_up(
    counts, grids, blocks, window_one, one_near, one_far, row_low, row_high,
    v_zero, forcing0, cx, cy, cz, weight, left_one, right_one, left_zero, right_zero, *rest,
):
    prepared, rest = rest[: len(grids)], rest[len(grids) :]
    (
        out, mixed_low, mixed_high, kappa_low, kappa_high, first_low, first_high,
        v_one, cx1, cy1, cz1, w1, one_a, one_b, zero_a, zero_b,
    ) = rest
    count_x, count_y = counts
    one_low, one_high = by_side("tx", one_near, one_far)
    _, tile_x1, rows1, size_z1 = window_one.shape
    tile_y1 = rows1 - 2 * R1
    top1 = R1 + tile_y1
    half_x, half_y, size_z2 = tile_x1 // 2, tile_y1 // 2, size_z1 // 2
    sizes = grids[0].sizes
    forcing2 = assemble(blocks, count_x, count_y, half_x, half_y, size_z2)
    levels = [(grid, Operator(prepared[number])) for number, grid in enumerate(grids[:-1])]
    exact = ExactSolve(grids[-1], inverse=prepared[-1][...])

    planes1 = tile_x1 + 2 * R1
    for message, mixed, kappa_rim, low in (
        (one_low, mixed_low, kappa_low, True), (one_high, mixed_high, kappa_high, False)
    ):
        at, loose = 0, 2 * R1 * ROWS
        for rim, fill in ((mixed, 0.0), (kappa_rim, 1.0)):
            for layer in range(1, R1 + 1):
                x = R1 - layer if low else layer - 1
                rim[x] = jnp.full((rows1, size_z1), fill, F32)
                rim[x, R1:top1] = message[at]
                at += 1
                for distance in range(1, reach_of(layer) + 1):
                    for row in (R1 - distance, top1 + distance - 1):
                        rim[x, row : row + 1] = message[
                            loose // ROWS, loose % ROWS : loose % ROWS + 1
                        ]
                        loose += 1

    def stacked(low, which, high):
        whole = [(low, x) for x in range(R1)]
        whole += [(window_one.at[which], x) for x in range(tile_x1)]
        whole += [(high, x) for x in range(R1)]
        return Planes(0, whole)

    forcing1 = stacked(mixed_low, 0, mixed_high)
    kappa1 = stacked(kappa_low, 2, kappa_high)
    plane_setup(kappa1, cx1, cy1, cz1, w1, None, 0.25, 1, planes1 - 1)
    row = iota((rows1, size_z1), 0)
    for mixed, rim, low in ((mixed_low, first_low, True), (mixed_high, first_high, False)):
        for layer in range(1, R1 + 1):
            x = R1 - layer if low else layer - 1
            if layer == R1:
                rim[x] = mixed[x]
            else:
                reach = reach_of(layer) - 1
                inside = (row >= R1 - reach) & (row < top1 + reach)
                at = x if low else R1 + tile_x1 + x
                rim[x] = jnp.where(inside, w1[at] * mixed[x], mixed[x])
    start1 = stacked(first_low, 1, first_high)
    plane_sweep(start1, v_one, forcing1, cx1, cy1, cz1, w1, 1, planes1 - 1)

    solved = solve_whole(forcing2, levels, exact)
    solved = jnp.concatenate([solved, swapped(solved)], 0).reshape(sizes[0] * sizes[1], LANES)

    raised = raise_level(left_one[...], right_one[...], solved)
    for x in range(1, planes1 - 1):
        one_a[x] = v_one[x] + raised[x * rows1 : (x + 1) * rows1]
    plane_sweep(one_a, one_b, forcing1, cx1, cy1, cz1, w1, 2, planes1 - 2)
    plane_sweep(one_b, one_a, forcing1, cx1, cy1, cz1, w1, 3, planes1 - 3)

    planes, rows, size_z = zero_a.shape
    v_zero, forcing0 = kept(v_zero, RX - 1), kept(forcing0, RX - 1)
    cx, cy, cz, weight = kept(cx, RX - 2), kept(cy, RX - 1), kept(cz, RX - 1), kept(weight, RX - 1)
    first, last = R1 - 1, planes1 - R1 + 1
    stack = jnp.concatenate([one_a[x] for x in range(first, last)], 0)
    raised = raise_level(left_zero[...], right_zero[...], stack)
    chunks = size_z // LANES
    top = rows - RY
    for x in range(RX - 1, planes - RX + 1):
        zero_b[x] = v_zero[x]
    for rim_x in (RX - 2, planes - RX + 1):
        zero_b[rim_x] = jnp.zeros((rows, size_z), F32)
    for x in range(planes - 2 * RX):
        at = 3 * tile_x1 * R1 // ROWS
        for chunk in range(chunks):
            lanes = slice(chunk * LANES, (chunk + 1) * LANES)
            zero_b[RX + x, RY - 2 : RY - 1, lanes] = row_low[at + chunk, x : x + 1]
            zero_b[RX + x, top + 1 : top + 2, lanes] = row_high[at + chunk, x : x + 1]
    for message, second, nearest in (
        (one_low, RX - 2, RX - 1), (one_high, planes - RX + 1, planes - RX)
    ):
        loose = 2 * R1 * ROWS + 2 * sum(2 * reach_of(layer) for layer in range(1, R1 + 1))
        for r in (RY - 1, top):
            for chunk in range(chunks):
                lanes = slice(chunk * LANES, (chunk + 1) * LANES)
                zero_b[nearest, r : r + 1, lanes] = message[
                    loose // ROWS, loose % ROWS : loose % ROWS + 1
                ]
                loose += 1
        at = -(-loose // ROWS)
        for chunk in range(chunks):
            lanes = slice(chunk * LANES, (chunk + 1) * LANES)
            for half in range((top - RY) // ROWS):
                zero_b[second, RY + half * ROWS : RY + (half + 1) * ROWS, lanes] = message[at]
                at += 1
    for x in range(RX - 2, planes - RX + 2):
        at = (x - RX + 2 * R1) // 2 - first
        zero_a[x] = zero_b[x] + raised[at * rows : (at + 1) * rows]
    plane_sweep(zero_a, zero_b, forcing0, cx, cy, cz, weight, RX - 1, planes - RX + 1)
    plane_sweep(zero_b, zero_a, forcing0, cx, cy, cz, weight, RX, planes - RX)
    for x in range(planes - 2 * RX):
        out[x] = zero_a[x + RX, RY:top]


VM = pl.BlockSpec(memory_space=pltpu.VMEM)
IN_PLACE = pl.BlockSpec(memory_space=pltpu.HBM)


def call(kernel, operands, outputs, scratch, spec=VM, in_hbm=()):
    def typed(output):
        return output if isinstance(output, jax.ShapeDtypeStruct) else jax.ShapeDtypeStruct(output, F32)

    return pl.pallas_call(
        kernel,
        in_specs=[spec] * len(operands),
        out_specs=[IN_PLACE if n in in_hbm else VM for n in range(len(outputs))],
        out_shape=[typed(output) for output in outputs],
        scratch_shapes=[pltpu.VMEM(s, F32) if isinstance(s, tuple) else s for s in scratch],
        compiler_params=pltpu.CompilerParams(vmem_limit_bytes=24 * 1024 * 1024),
    )(*operands)


def shift_both(to_low, to_high, axis):
    count = lax.axis_size(axis)
    from_low = lax.ppermute(to_high, axis, [(i, (i + 1) % count) for i in range(count)])
    from_high = lax.ppermute(to_low, axis, [((i + 1) % count, i) for i in range(count)])
    return from_low, from_high


def swap_both(near, far, axis):
    count = lax.axis_size(axis)
    assert count % 2 == 0
    partner = [(i, i ^ 1) for i in range(count)]
    other = [(i, (i - 1 if i % 2 == 0 else i + 1) % count) for i in range(count)]
    from_far = lax.ppermute(far, axis, other)
    from_near = lax.ppermute(near, axis, partner)
    return from_near, from_far


def to_everyone(blocks):
    return lax.all_to_all(blocks, ("tx", "ty"), 0, 0)


def cycle(concentration, source, material):
    tile_x, tile_y, size_z = concentration.shape
    chunks = size_z // LANES
    counts = lax.axis_size("tx"), lax.axis_size("ty")
    everyone = counts[0] * counts[1]
    rows = tile_y + 2 * RY
    message = (tile_x + 1, ROWS, size_z)
    *inputs, to_low, to_high = call(
        edges,
        tuple(
            pltpu.with_memory_space_constraint(v, pltpu.HBM)
            for v in (concentration, source, material)
        ),
        tuple(jax.ShapeDtypeStruct(v.shape, v.dtype) for v in (concentration, source, material))
        + (message, message),
        (pltpu.SemaphoreType.DMA((3,)),),
        IN_PLACE,
    )
    from_low, from_high = shift_both(to_low, to_high, "ty")
    zero = (tile_x + 2 * RX, rows, size_z)
    inner = (tile_x + 2, rows, size_z)
    one_tile = (tile_x // 2, tile_y // 2, size_z // 2)
    two_tile = tuple(extent // 2 for extent in one_tile)
    grids = levels_of(counts, two_tile)

    def bits(*shape):
        return jax.ShapeDtypeStruct(shape, BF16)

    k_tile, kappa_blocks, halves, halves_one = call(
        shrink,
        inputs[2:],
        (
            one_tile,
            (everyone, two_tile[1], LANES),
            bits(chunks, LANES, one_tile[2]),
            bits(2, one_tile[2], one_tile[2]),
        ),
        ((one_tile[0], tile_y, LANES), one_tile[1:]),
    )
    message = (plane_tiles(tile_y), ROWS, size_z)
    window, to_low, to_high = call(
        sides,
        (*inputs, k_tile, from_low, from_high),
        ((3, tile_x, rows, size_z), message, message),
        ((rows, size_z),),
    )
    from_low, from_high = shift_both(to_low, to_high, "tx")
    kappa_blocks = to_everyone(kappa_blocks)
    wide = -(-rows // (2 * ROWS)) * ROWS
    small = (one_tile[0] + 2 * RC, wide, one_tile[2])
    pairs1 = small[0] // 2
    short = pairs1 // 2 * (two_tile[1] + RC) // SHORT
    assert pairs1 // 2 * (two_tile[1] + RC) % SHORT == 0
    message = (3 * one_tile[0] * R1 // ROWS + chunks, ROWS, LANES)
    assert one_tile[2] == LANES and tile_x <= ROWS and one_tile[1] == ROWS
    v_zero, forcing0, cx, cy, cz, weight, level_one, blocks, to_low, to_high = call(
        fine_down,
        (window, halves, halves_one, from_low, from_high),
        (inner, inner, (tile_x + 3, rows, size_z), inner, inner, inner)
        + ((3,) + one_tile, (everyone, short, SHORT, LANES), message, message),
        (
            (4, rows, size_z),
            (2, rows, size_z),
            (4, rows, size_z),
            zero,
            zero,
            (chunks, max(small[0], tile_x), 2 * wide, LANES),
            (everyone, short, SHORT, LANES),
            pltpu.SemaphoreType.DMA,
        )
        + (small,) * 9
        + ((pairs1, wide, one_tile[2]), (pairs1, ROWS, one_tile[2])),
        in_hbm=(7,),
    )
    row_low, row_high = shift_both(to_low, to_high, "ty")
    blocks = to_everyone(blocks)
    rows1 = one_tile[1] + 2 * R1
    message = (middle_tiles(tile_y, chunks), ROWS, LANES)
    window_one, near, far = call(
        middle,
        (level_one, v_zero, row_low, row_high),
        ((3, one_tile[0], rows1, one_tile[2]), message, message),
        (),
    )
    one_near, one_far = swap_both(near, far, "tx")
    one = (one_tile[0] + 2 * R1, rows1, one_tile[2])
    seen = one[0] - 2 * (R1 - 1)
    chosen = call(
        functools.partial(selectors, grids[0].sizes, one[0], one_tile[0], one_tile[1], rows),
        (window_one,),
        (
            bits(one[0] * rows1, grids[0].sizes[0] * grids[0].sizes[1]),
            bits(LANES, one_tile[2]),
            bits(seen * rows, seen * rows1),
            bits(one_tile[2], size_z),
        ),
        (),
    )
    lattice = grids[0].sizes[1], LANES
    prepared = call(
        functools.partial(prepare, counts, grids),
        (kappa_blocks, window_one),
        tuple((5, grid.sizes[0] // 2) + lattice for grid in grids[:-1])
        + ((-(-grids[-1].cells // ROWS) * ROWS, LANES),),
        (),
    )
    rim = (R1,) + one[1:]
    (updated,) = call(
        functools.partial(coarse_up, counts, grids),
        (blocks, window_one, one_near, one_far, row_low, row_high)
        + (v_zero, forcing0, cx, cy, cz, weight, *chosen, *prepared),
        (concentration.shape,),
        (rim,) * 6 + (one,) * 7 + (zero, zero),
    )
    return updated


def solution(mesh):
    placed = (P("tx", "ty", None), P("tx", "ty", None), P("tx", "ty", None))
    return jax.shard_map(
        cycle, mesh=mesh, in_specs=placed, out_specs=P("tx", "ty", None), check_vma=False
    )
```

```python
import functools

import jax
import jax.numpy as jnp
from jax import lax
from jax.experimental import pallas as pl
from jax.experimental.pallas import tpu as pltpu
from jax.sharding import PartitionSpec as P


mass_rate = 0.001
relax_weight = 0.8
diffusivities = (0.15, 0.3, 0.5, 0.8, 1.2, 2.0, 3.2, 5.0)
LANES = 128
ROWS = 8
SHORT = 4
RX = 2
RY = 4
R1 = 4
RC = 2
F32 = jnp.float32
BF16 = jnp.bfloat16


def lookup(material):
    result = jnp.zeros(material.shape, F32)
    for slot_id, coeff_value in enumerate(diffusivities):
        result = jnp.where(material == slot_id, F32(coeff_value), result)
    return result


class Planes:
    def __init__(self, first, planes):
        self.first = first
        self.planes = planes

    def __getitem__(self, x):
        ref, index = self.planes[x - self.first]
        return ref[index]

    def __setitem__(self, x, value):
        ref, index = self.planes[x - self.first]
        ref[index] = value


def kept(ref, first):
    return Planes(first, [(ref, x) for x in range(ref.shape[0])])


def is_even(axis):
    return lax.rem(lax.axis_index(axis), 2) == 0


def on_sides(axis, near, far, body):
    @pl.when(is_even(axis))
    def _():
        body(far, near)

    @pl.when(jnp.logical_not(is_even(axis)))
    def _():
        body(near, far)


class Picked:
    def __init__(self, flag, when_true, when_false):
        self.flag = flag
        self.when_true = when_true
        self.when_false = when_false

    def __getitem__(self, index):
        first, second = self.when_true[index], self.when_false[index]
        flag = jnp.where(self.flag, jnp.int32(1), jnp.int32(0))
        return jnp.where(jnp.full(first.shape, flag) == 1, first, second)


def by_side(axis, near, far):
    even = is_even(axis)
    return Picked(even, far, near), Picked(even, near, far)


def iota(shape, dim):
    return lax.broadcasted_iota(jnp.int32, shape, dim)


def div(a, b):
    return lax.div(a, jnp.full_like(a, b))


def mod(a, b):
    return lax.rem(a, jnp.full_like(a, b))


def ones_where(mask):
    return jnp.where(mask, F32(1.0), F32(0.0)).astype(BF16)


def three_terms(x):
    high = x.astype(BF16)
    rest = x - high.astype(F32)
    middle = rest.astype(BF16)
    low = (rest - middle.astype(F32)).astype(BF16)
    return high, middle, low


def times_right(x, selector):
    parts = [jnp.dot(part, selector, preferred_element_type=F32) for part in three_terms(x)]
    return parts[0] + (parts[1] + parts[2])


def back(v, axis, step=1):
    return pltpu.roll(v, step, axis)


def ahead(v, axis, step=1):
    return pltpu.roll(v, v.shape[axis] - step, axis)


def halve_lanes(fine, coarse, start=0):
    shape = (fine, coarse)
    return ones_where(div(iota(shape, 0), 2) + start == iota(shape, 1))


def plane_setup(kappa, cx, cy, cz, weight, diag, scale, first, last):
    half = 0.5 * scale
    for x in range(first - 1, last):
        cx[x] = half * (kappa[x] + kappa[x + 1])
    for x in range(first, last):
        k = kappa[x]
        y_part = half * (k + ahead(k, 0))
        z_part = half * (k + ahead(k, 1))
        cy[x] = y_part
        cz[x] = z_part
        d = mass_rate + cx[x] + cx[x - 1] + y_part + back(y_part, 0) + z_part + back(z_part, 1)
        weight[x] = relax_weight / d
        if diag is not None:
            diag[x] = d


def in_plane(here, cy, cz, x):
    y_part = cy[x]
    z_part = cz[x]
    total = y_part * ahead(here, 0) + back(y_part * here, 0)
    return total + (z_part * ahead(here, 1) + back(z_part * here, 1))


def neighbours(v, cx, cy, cz, x):
    return (cx[x] * v[x + 1] + cx[x - 1] * v[x - 1]) + in_plane(v[x], cy, cz, x)


def plane_sweep(v, out, forcing, cx, cy, cz, weight, first, last):
    for x in range(first, last):
        out[x] = (1.0 - relax_weight) * v[x] + weight[x] * (forcing[x] + neighbours(v, cx, cy, cz, x))


def edges(conc_in, source_in, material_in, conc, source, material, to_low, to_high, arrived):
    copies = [
        pltpu.make_async_copy(whence, whither, arrived.at[n])
        for n, (whence, whither) in enumerate(
            ((conc_in, conc), (source_in, source), (material_in, material))
        )
    ]
    for copy in copies:
        copy.start()
    for copy in copies:
        copy.wait()
    tile_x, tile_y, _ = conc.shape
    for to, low in ((to_low, True), (to_high, False)):
        for x in range(tile_x):
            rows = slice(0, 4) if low else slice(tile_y - 4, tile_y)
            near = slice(0, 3) if low else slice(1, 4)
            pair = slice(0, 2) if low else slice(2, 4)
            c = conc[x, rows]
            f = mass_rate * c + source[x, rows]
            k = lookup(material[x, rows])
            to[x, 0:3] = c[near]
            to[x, 3:5] = f[pair]
            to[x, 5:8] = k[near]
            to[tile_x, x : x + 1] = k[3:4] if low else k[0:1]


def sides(conc, source, material, k_tile, from_low, from_high, window, to_low, to_high, swept):
    tile_x, tile_y, size_z = conc.shape
    top = RY + tile_y
    for x in range(tile_x):
        c = conc[x]
        window[0, x, RY:top] = c
        window[1, x, RY:top] = mass_rate * c + source[x]
        window[2, x, RY:top] = lookup(material[x])
        window[0, x, 0:1] = jnp.zeros((1, size_z), F32)
        window[0, x, 1:4] = from_low[x, 0:3]
        window[0, x, top : top + 3] = from_high[x, 0:3]
        window[0, x, top + 3 :] = jnp.zeros((1, size_z), F32)
        window[1, x, 0:2] = jnp.zeros((2, size_z), F32)
        window[1, x, 2:4] = from_low[x, 3:5]
        window[1, x, top : top + 2] = from_high[x, 3:5]
        window[1, x, top + 2 :] = jnp.zeros((2, size_z), F32)
        window[2, x, 0:1] = from_low[tile_x, x : x + 1]
        window[2, x, 1:4] = from_low[x, 5:8]
        window[2, x, top : top + 3] = from_high[x, 5:8]
        window[2, x, top + 3 :] = from_high[tile_x, x : x + 1]
    per_plane = tile_y // ROWS
    for to, low in ((to_low, True), (to_high, False)):

        def plane(layer):
            return layer - 1 if low else tile_x - layer

        def send(at, values):
            for n in range(per_plane):
                to[at + n] = values(n)

        for n, (which, layer) in enumerate(BASE_PLANES):
            send(
                n * per_plane,
                lambda n: window[which, plane(layer), RY + n * ROWS : RY + (n + 1) * ROWS],
            )
        first_sweep(window, plane(2), swept)
        at = len(BASE_PLANES) * per_plane
        send(at, lambda n: swept[RY + n * ROWS : RY + (n + 1) * ROWS])
        loose = (at + per_plane) * ROWS
        for which, layer, reach in EXTRA_ROWS:
            for start in (RY - reach, top):
                to[loose // ROWS, loose % ROWS : loose % ROWS + reach] = window[
                    which, plane(layer), start : start + reach
                ]
                loose += reach
        at = -(-loose // ROWS)
        to[at, :, 0 : size_z // 2] = k_tile[1 if low else k_tile.shape[0] - 2]
        to[at, :, size_z // 2 :] = jnp.zeros((ROWS, size_z - size_z // 2), F32)


def first_sweep(window, x, out):
    c, f, k = window[0, x], window[1, x], window[2, x]
    next_part = 0.5 * (k + window[2, x + 1])
    last_part = 0.5 * (k + window[2, x - 1])
    y_part = 0.5 * (k + ahead(k, 0))
    z_part = 0.5 * (k + ahead(k, 1))
    d = mass_rate + next_part + last_part
    d = d + y_part + back(y_part, 0) + z_part + back(z_part, 1)
    total = next_part * window[0, x + 1] + last_part * window[0, x - 1]
    total = total + (y_part * ahead(c, 0) + back(y_part * c, 0))
    total = total + (z_part * ahead(c, 1) + back(z_part * c, 1))
    out[...] = (1.0 - relax_weight) * c + (relax_weight / d) * (f + total)


BASE_PLANES = ((0, 1), (0, 2), (1, 1), (2, 1), (2, 2))
EXTRA_ROWS = ((0, 1, 2), (0, 2, 1), (1, 1, 1), (2, 1, 2), (2, 2, 2))


def plane_tiles(tile_y):
    loose = sum(2 * reach for _, _, reach in EXTRA_ROWS)
    return (len(BASE_PLANES) + 1) * tile_y // ROWS + -(-loose // ROWS) + 1


def shrink(material, k_tile, blocks, halves, halves_one, paired, paired_one):
    tile_x, tile_y, size_z = material.shape
    tile_x1, tile_y1, size_z1 = tile_x // 2, tile_y // 2, size_z // 2
    k_one = None
    for chunk in range(size_z // LANES):
        lanes = slice(chunk * LANES, (chunk + 1) * LANES)
        for pair in range(tile_x1):
            paired[pair] = lookup(material[2 * pair, :, lanes]) + lookup(
                material[2 * pair + 1, :, lanes]
            )
        stack = [
            paired[pair, pl.ds(0, tile_y1, stride=2)] + paired[pair, pl.ds(1, tile_y1, stride=2)]
            for pair in range(tile_x1)
        ]
        part = times_right(
            jnp.concatenate(stack, 0), halve_lanes(LANES, size_z1, chunk * LANES // 2)
        )
        k_one = part if k_one is None else k_one + part
    k_one = 0.125 * k_one
    for x in range(tile_x1):
        k_tile[x] = k_one[x * tile_y1 : (x + 1) * tile_y1]
    assert tile_x1 // 2 * (size_z1 // 2) <= LANES
    block = None
    for pair in range(tile_x1 // 2):
        at = 2 * pair * tile_y1
        paired_one[...] = k_one[at : at + tile_y1] + k_one[at + tile_y1 : at + 2 * tile_y1]
        piece = (
            paired_one[pl.ds(0, tile_y1 // 2, stride=2)] + paired_one[pl.ds(1, tile_y1 // 2, stride=2)]
        )
        part = times_right(piece, halve_lanes(size_z1, LANES, pair * size_z1 // 2))
        block = part if block is None else block + part
    block = 0.125 * block
    for device in range(blocks.shape[0]):
        blocks[device] = block
    for chunk in range(size_z // LANES):
        halves[chunk] = halve_lanes(LANES, size_z1, chunk * LANES // 2)
    for half in range(2):
        halves_one[half] = halve_lanes(size_z1, size_z1, half * size_z1 // 2)


def fine_down(
    window, halves, halves_one, from_low, from_high,
    v_zero, forcing_out, cx, cy, cz, weight, level_one, blocks_out, to_low, to_high,
    conc_rim, forcing_rim, kappa_rim, once, diag, paired, blocks, left,
    k_one, f_one, u_one, v_one, cx1, cy1, cz1, w1, d1, paired_one, packed,
):
    _, tile_x, rows, size_z = window.shape
    tile_y = rows - 2 * RY
    top = RY + tile_y
    planes = tile_x + 2 * RX
    rims = (conc_rim, forcing_rim, kappa_rim)
    depths = (2, 1, 2)
    for which, rim in enumerate(rims):
        fill = jnp.full((rows, size_z), 1.0 if which == 2 else 0.0, F32)
        for x in range(2 * depths[which]):
            rim[x] = fill

    def place(which, layer, low):
        return depths[which] - layer if low else depths[which] + layer - 1

    per_plane = tile_y // ROWS
    last_tile = plane_tiles(tile_y) - 1
    for message, low in ((from_low, True), (from_high, False)):
        for at, (which, layer) in enumerate(BASE_PLANES):
            for n in range(per_plane):
                start = RY + n * ROWS
                rims[which][place(which, layer, low), start : start + ROWS] = message[
                    at * per_plane + n
                ]
        rim_x = 0 if low else planes - 1
        once[rim_x] = jnp.zeros((rows, size_z), F32)
        at = len(BASE_PLANES) * per_plane
        for n in range(per_plane):
            start = RY + n * ROWS
            once[rim_x, start : start + ROWS] = message[at + n]
        loose = (at + per_plane) * ROWS
        for which, layer, reach in EXTRA_ROWS:
            for start in (RY - reach, top):
                rims[which][place(which, layer, low), start : start + reach] = message[
                    loose // ROWS, loose % ROWS : loose % ROWS + reach
                ]
                loose += reach

    def stacked(which):
        depth = depths[which]
        whole = [(rims[which], x) for x in range(depth)]
        whole += [(window.at[which], x) for x in range(tile_x)]
        whole += [(rims[which], depth + x) for x in range(depth)]
        return Planes(RX - depth, whole)

    conc, forcing, kappa = stacked(0), stacked(1), stacked(2)
    cx, cy, cz, weight = kept(cx, RX - 2), kept(cy, RX - 1), kept(cz, RX - 1), kept(weight, RX - 1)
    v_out = kept(v_zero, RX - 1)
    plane_setup(kappa, cx, cy, cz, weight, diag, 1.0, 1, planes - 1)
    plane_sweep(conc, once, forcing, cx, cy, cz, weight, 1, planes - 1)
    plane_sweep(once, v_out, forcing, cx, cy, cz, weight, 1, planes - 1)
    chunks = size_z // LANES
    size_z1 = size_z // 2
    to_half = [halves[chunk] for chunk in range(chunks)]
    tile_x1, tile_y1 = tile_x // 2, tile_y // 2

    def put(pair, total):
        for chunk in range(chunks):
            paired[chunk, pair, 0:rows] = total[:, chunk * LANES : (chunk + 1) * LANES]

    def narrowed(pairs, start, count):
        result = None
        for chunk in range(chunks):
            stack = [
                paired[chunk, pair, pl.ds(start, count, stride=2)]
                + paired[chunk, pair, pl.ds(start + 1, count, stride=2)]
                for pair in range(pairs)
            ]
            part = times_right(jnp.concatenate(stack, 0), to_half[chunk])
            result = part if result is None else result + part
        return 0.125 * result

    wide = paired.shape[2] // 2
    planes1 = tile_x1 + 2 * RC
    if 2 * wide > rows:
        for chunk in range(chunks):
            for pair in range(planes1 - 2):
                paired[chunk, pair, rows:] = jnp.ones((2 * wide - rows, LANES), F32)
    for pair in range(planes1 - 2):
        put(pair, kappa[2 * pair] + kappa[2 * pair + 1])
    coarse = narrowed(planes1 - 2, 0, wide)
    for pair in range(planes1 - 2):
        k_one[pair + 1] = coarse[pair * wide : (pair + 1) * wide]
    for message, x in ((from_low, 0), (from_high, planes1 - 1)):
        k_one[x] = jnp.ones((wide, size_z1), F32)
        k_one[x, RC : RC + tile_y1] = message[last_tile, :, 0:size_z1]
    plane_setup(k_one, cx1, cy1, cz1, w1, d1, 0.25, 1, planes1 - 1)

    for pair in range(tile_x1):
        total = None
        for x in (RX + 2 * pair, RX + 2 * pair + 1):
            part = forcing[x] + neighbours(v_out, cx, cy, cz, x) - diag[x] * v_out[x]
            total = part if total is None else total + part
        put(pair, total)
    forcing_one = narrowed(tile_x1, RY, tile_y1)

    low, high = RC, RC + tile_y1
    nothing = jnp.zeros((wide, size_z1), F32)
    for x in range(planes1):
        f_one[x] = nothing
        if x in (0, planes1 - 1):
            v_one[x] = nothing
    for x in (0, 1, planes1 - 2, planes1 - 1):
        u_one[x] = nothing
    for x in range(tile_x1):
        f = forcing_one[x * tile_y1 : (x + 1) * tile_y1]
        f_one[x + RC, low:high] = f
        u_one[x + RC] = w1[x + RC] * f_one[x + RC]
        level_one[0, x] = f
        level_one[1, x] = u_one[x + RC, low:high]
        level_one[2, x] = k_one[x + RC, low:high]
    plane_sweep(u_one, v_one, f_one, cx1, cy1, cz1, w1, 1, planes1 - 1)
    pairs1 = planes1 // 2
    for pair in range(pairs1):
        total = None
        for x in (2 * pair, 2 * pair + 1):
            if x == 0:
                part = cx1[0] * v_one[1]
            elif x == planes1 - 1:
                part = cx1[x - 1] * v_one[x - 1]
            else:
                part = f_one[x] + neighbours(v_one, cx1, cy1, cz1, x) - d1[x] * v_one[x]
            total = part if total is None else total + part
        paired_one[pair] = total
    for pair in range(pairs1):
        packed[pair] = (
            paired_one[pair, pl.ds(0, ROWS, stride=2)] + paired_one[pair, pl.ds(1, ROWS, stride=2)]
        )
    half_pairs = pairs1 // 2
    result = times_right(
        jnp.concatenate([packed[p] for p in range(half_pairs)], 0), halves_one[0]
    ) + times_right(
        jnp.concatenate([packed[half_pairs + p] for p in range(half_pairs)], 0), halves_one[1]
    )
    used = tile_y1 // 2 + RC
    block = jnp.concatenate([result[p * ROWS : p * ROWS + used] for p in range(half_pairs)], 0)
    block = 0.125 * block
    for part in range(blocks.shape[1]):
        piece = block[part * SHORT : (part + 1) * SHORT]
        for device in range(blocks.shape[0]):
            blocks[device, part] = piece
    copy = pltpu.make_async_copy(blocks, blocks_out, left)
    copy.start()
    for x in range(RX - 1, planes - RX + 1):
        forcing_out[x - RX + 1] = forcing[x]

    for to, rows1, row0 in (
        (to_low, slice(0, R1), RY + 1),
        (to_high, slice(tile_y1 - R1, tile_y1), top - 2),
    ):
        for which in range(3):
            for x in range(tile_x1):
                flat_row = which * tile_x1 * R1 + x * R1
                to[flat_row // ROWS, flat_row % ROWS : flat_row % ROWS + R1] = level_one[
                    which, x, rows1
                ]
        start = 3 * tile_x1 * R1 // ROWS
        for x in range(tile_x):
            row = v_zero[x + 1, row0 : row0 + 1]
            for chunk in range(chunks):
                to[start + chunk, x : x + 1] = row[:, chunk * LANES : (chunk + 1) * LANES]
    copy.wait()


def reach_of(layer):
    return R1 + 1 - layer


def middle(level_one, v_zero, from_low, from_high, window, near, far):
    _, tile_x1, tile_y1, _ = level_one.shape
    planes, rows, size_z = v_zero.shape
    top1 = R1 + tile_y1
    for which in range(3):
        for x in range(tile_x1):
            flat_row = which * tile_x1 * R1 + x * R1
            at, sub = flat_row // ROWS, flat_row % ROWS
            window[which, x, R1:top1] = level_one[which, x]
            window[which, x, 0:R1] = from_low[at, sub : sub + R1]
            window[which, x, top1:] = from_high[at, sub : sub + R1]
    chunks = size_z // LANES
    top = rows - RY

    def pack(to_low, to_high):
        for to, low in ((to_low, True), (to_high, False)):
            at = 0
            for which in (0, 2):
                for layer in range(1, R1 + 1):
                    x = layer - 1 if low else tile_x1 - layer
                    outer = 1 if which == 0 and layer == R1 else which
                    to[at] = window[outer, x, R1:top1]
                    at += 1
            loose = at * ROWS
            for which in (0, 2):
                for layer in range(1, R1 + 1):
                    x = layer - 1 if low else tile_x1 - layer
                    outer = 1 if which == 0 else which
                    for distance in range(1, reach_of(layer) + 1):
                        source = outer if distance == reach_of(layer) else which
                        for row in (R1 - distance, top1 + distance - 1):
                            to[loose // ROWS, loose % ROWS : loose % ROWS + 1] = window[
                                source, x, row : row + 1
                            ]
                            loose += 1
            second, first = (2, 1) if low else (planes - 3, planes - 2)
            for row in (RY - 1, top):
                for chunk in range(chunks):
                    lanes = slice(chunk * LANES, (chunk + 1) * LANES)
                    to[loose // ROWS, loose % ROWS : loose % ROWS + 1] = v_zero[first, row : row + 1, lanes]
                    loose += 1
            at = -(-loose // ROWS)
            for chunk in range(chunks):
                lanes = slice(chunk * LANES, (chunk + 1) * LANES)
                for half in range((top - RY) // ROWS):
                    to[at] = v_zero[second, RY + half * ROWS : RY + (half + 1) * ROWS, lanes]
                    at += 1

    on_sides("tx", near, far, pack)


def middle_tiles(tile_y, chunks):
    loose = 2 * sum(2 * reach_of(layer) for layer in range(1, R1 + 1)) + 2 * chunks
    return 2 * R1 + -(-loose // ROWS) + chunks * tile_y // ROWS


class Grid:
    def __init__(self, sizes, strides, scales, rows, lanes):
        self.sizes = sizes
        self.strides = strides
        self.scales = scales
        self.rows = rows
        self.lanes = lanes
        self.ratios = tuple(2 if extent % 2 == 0 else 1 for extent in sizes)
        self.cells = sizes[0] * sizes[1] * sizes[2]
        self.exact = self.cells <= 64 or self.ratios == (1, 1, 1)

    def coarser(self):
        sizes = tuple(extent // ratio for extent, ratio in zip(self.sizes, self.ratios))
        scales = tuple(s / (ratio * ratio) for s, ratio in zip(self.scales, self.ratios))
        strides = tuple(s * ratio for s, ratio in zip(self.strides, self.ratios[1:]))
        return Grid(sizes, strides, scales, self.rows, self.lanes)


def next_plane(v):
    return v if v.shape[0] == 1 else jnp.concatenate([v[1:], v[:1]], 0)


def last_plane(v):
    return v if v.shape[0] == 1 else jnp.concatenate([v[-1:], v[:-1]], 0)


def restrict_whole(v, grid):
    if grid.ratios[0] == 2:
        v = jnp.concatenate(
            [v[2 * x : 2 * x + 1] + v[2 * x + 1 : 2 * x + 2] for x in range(grid.sizes[0] // 2)], 0
        )
    for axis in (1, 2):
        if grid.ratios[axis] == 2:
            step = grid.strides[axis - 1]
            even = mod(div(iota(v.shape, axis), step), 2) == 0
            v = v + jnp.where(even, ahead(v, axis, step), back(v, axis, step))
    return (1.0 / (grid.ratios[0] * grid.ratios[1] * grid.ratios[2])) * v


def prolong_whole(v, grid):
    if grid.ratios[0] == 1:
        return v
    return jnp.concatenate([v[x // 2 : x // 2 + 1] for x in range(grid.sizes[0])], 0)


def whole_operator(kappa, grid):
    half_x, half_y, half_z = (0.5 * s for s in grid.scales)
    step_y, step_z = grid.strides
    cx = half_x * (kappa + next_plane(kappa))
    cy = half_y * (kappa + ahead(kappa, 1, step_y))
    cz = half_z * (kappa + ahead(kappa, 2, step_z))
    diag = mass_rate + cx + last_plane(cx)
    diag = diag + (cy + back(cy, 1, step_y)) + (cz + back(cz, 2, step_z))
    return cx, cy, cz, diag, relax_weight / diag


def whole_neighbours(v, operator, grid):
    cx, cy, cz = operator[:3]
    step_y, step_z = grid.strides
    total = cx * next_plane(v) + last_plane(cx * v)
    total = total + (cy * ahead(v, 1, step_y) + back(cy * v, 1, step_y))
    return total + (cz * ahead(v, 2, step_z) + back(cz * v, 2, step_z))


def whole_sweep(v, forcing, operator, grid):
    return (1.0 - relax_weight) * v + operator[4] * (forcing + whole_neighbours(v, operator, grid))


class ExactSolve:
    def __init__(self, grid, kappa=None, inverse=None):
        size_x, size_y, size_z = grid.sizes
        self.grid = grid
        self.across = across = size_x * size_y
        _, step_z = grid.strides
        self.period = period = size_z * step_z
        cells = grid.cells
        padded = -(-cells // ROWS) * ROWS
        assert across <= step_z and 2 * period <= grid.lanes
        shape = (padded, grid.lanes)
        i, j = iota(shape, 0), iota(shape, 1)
        self.i, self.j = i, j
        if kappa is None:
            self.inverse = inverse
            return

        def places_of_row(n):
            sub = mod(n, across)
            return div(sub, size_y), mod(sub, size_y), div(n, across)

        def places_of_lane(n):
            n = mod(n, period)
            sub = mod(n, step_z)
            return div(sub, size_y), mod(sub, size_y), div(n, step_z)

        at_i, at_j = places_of_row(i), places_of_lane(j)
        live = (mod(j, step_z) < across) & (i < cells)
        same = (at_i[0] == at_j[0]) & (at_i[1] == at_j[1]) & (at_i[2] == at_j[2]) & live
        left = j < period
        factor = jnp.zeros(shape, F32)
        for d in range(3):
            equal = [at_i[other] == at_j[other] for other in range(3) if other != d]
            for step in (1, grid.sizes[d] - 1):
                hit = mod(at_i[d] + step, grid.sizes[d]) == at_j[d]
                factor = factor + jnp.where(
                    hit & equal[0] & equal[1], F32(0.5 * grid.scales[d]), F32(0.0)
                )
        k_row = self.as_row(kappa)
        k_column = jnp.sum(jnp.where(same & left, k_row, 0.0), axis=1, keepdims=True)
        coupled = jnp.where(live & left, factor * (k_column + k_row), 0.0)
        diag = mass_rate + jnp.sum(coupled, axis=1, keepdims=True)
        matrix = jnp.where(same & left, diag - coupled, -coupled)
        matrix = jnp.where(left, matrix, jnp.where(same, F32(1.0), F32(0.0)))
        for n in range(cells):
            lane = (n // across) * step_z + n % across
            pivot_row = matrix[n : n + 1] / matrix[n : n + 1, lane : lane + 1]
            column = matrix[:, lane : lane + 1]
            matrix = jnp.where(i == n, pivot_row, matrix - column * pivot_row)
        self.inverse = jnp.where((j >= period) & (j < 2 * period) & live, matrix, 0.0)

    def as_row(self, v):
        grid = self.grid
        size_x, size_y, _ = grid.sizes
        step_y, step_z = grid.strides
        sub = mod(iota((1, grid.lanes), 1), step_z)
        result = jnp.zeros((1, grid.lanes), F32)
        for x in range(size_x):
            for y in range(size_y):
                row = v[x, y * step_y : y * step_y + 1]
                result = jnp.where(sub == x * size_y + y, row, result)
        return result

    def solve(self, forcing):
        grid = self.grid
        size_x, size_y, _ = grid.sizes
        step_y, step_z = grid.strides
        solved = jnp.sum(self.inverse * self.as_row(forcing), axis=1, keepdims=True)
        at_z = div(mod(self.j, self.period), step_z)
        spread = jnp.where(div(self.i, self.across) == at_z, solved, 0.0)
        planes = []
        for x in range(size_x):
            rows = []
            for y in range(size_y):
                mine = mod(self.i, self.across) == x * size_y + y
                row = jnp.sum(jnp.where(mine, spread, 0.0), axis=0, keepdims=True)
                rows.append(jnp.broadcast_to(row, (step_y, grid.lanes)))
            planes.append(jnp.concatenate(rows, 0)[None])
        return jnp.concatenate(planes, 0)


def levels_of(counts, tile_sizes):
    sizes = tuple(count * extent for count, extent in zip(counts, tile_sizes)) + tile_sizes[2:]
    grid = Grid(sizes, (1, 1), (0.0625, 0.0625, 0.0625), sizes[1], LANES)
    grids = [grid]
    while not grid.exact:
        grid = grid.coarser()
        grids.append(grid)
    return grids


class Operator:
    def __init__(self, ref):
        self.ref = ref

    def __getitem__(self, part):
        if isinstance(part, slice):
            return [self.ref[p] for p in range(*part.indices(5))]
        return self.ref[part]


def kappa_of(blocks, counts, grid):
    count_x, count_y = counts
    planes, rows, size_z2 = grid.sizes
    half_x, half_y = planes // count_x, rows // count_y
    assert half_x * size_z2 == LANES and half_x == 2 and ROWS % half_y == 0 and half_y == SHORT
    share = ROWS // half_y
    kappa = [[None] * (rows // ROWS) for _ in range(planes)]
    lane = iota((ROWS, LANES), 1)
    for tx in range(count_x):
        for group in range(rows // ROWS):
            pieces = [blocks[tx * count_y + group * share + n] for n in range(share)]
            piece = jnp.concatenate(pieces, 0)
            turned = pltpu.roll(piece, size_z2, 1)
            for p in range(half_x):
                mine = (lane < size_z2) == (p == 0)
                kappa[tx * half_x + p][group] = jnp.where(mine, piece, turned)
    return jnp.concatenate([jnp.concatenate(groups, 0)[None] for groups in kappa], 0)


def prepare(counts, grids, blocks, _, *outputs):
    kappas = [kappa_of(blocks, counts, grids[0])]
    for grid in grids[:-1]:
        kappas.append(restrict_whole(kappas[-1], grid))
    outputs[-1][...] = ExactSolve(grids[-1], kappas[-1]).inverse
    for number, grid in enumerate(grids[:-1]):
        for part, value in enumerate(whole_operator(kappas[number], grid)):
            outputs[number][part] = value


def selectors(sizes, planes1, tile_x1, tile_y1, rows, _, left_one, right_one, left_zero, right_zero):
    rows1 = tile_y1 + 2 * R1
    whole_x1, whole_y1 = 2 * sizes[0], 2 * sizes[1]
    start_x = lax.axis_index("tx") * tile_x1 + (whole_x1 - R1)
    start_y = lax.axis_index("ty") * tile_y1 + (whole_y1 - R1)
    row = iota((planes1 * rows1, 1), 0)
    at_x = mod(div(row, rows1) + start_x, whole_x1)
    at_y = mod(mod(row, rows1) + start_y, whole_y1)
    target = div(at_x, 2) * sizes[1] + div(at_y, 2)
    left_one[...] = ones_where(iota(left_one.shape, 1) == target)
    shape = right_one.shape
    right_one[...] = ones_where(iota(shape, 0) == div(iota(shape, 1), 2))
    row = iota((left_zero.shape[0], 1), 0)
    target = div(row, rows) * rows1 + div(mod(row, rows) + (2 * R1 - RY), 2)
    left_zero[...] = ones_where(iota(left_zero.shape, 1) == target)
    shape = right_zero.shape
    right_zero[...] = ones_where(iota(shape, 0) == div(iota(shape, 1), 2))


def raise_level(left, right, v):
    def terms(x):
        high = x.astype(BF16)
        return high, (x - high.astype(F32)).astype(BF16)

    high, low = terms(v)
    picked = jnp.dot(left, high, preferred_element_type=F32)
    picked_low = jnp.dot(left, low, preferred_element_type=F32)
    return jnp.dot(picked.astype(BF16), right, preferred_element_type=F32) + jnp.dot(
        picked_low.astype(BF16), right, preferred_element_type=F32
    )


def solve_whole(forcing, levels, exact):
    if not levels:
        return exact.solve(forcing)
    grid, operator = levels[0]
    v = operator[4] * forcing
    v = whole_sweep(v, forcing, operator, grid)
    residual = forcing + whole_neighbours(v, operator, grid) - operator[3] * v
    v = v + prolong_whole(solve_whole(restrict_whole(residual, grid), levels[1:], exact), grid)
    for _ in range(2):
        v = whole_sweep(v, forcing, operator, grid)
    return v


def assemble(blocks, count_x, count_y, half_x, half_y, size_z2):
    rows = count_y * half_y
    groups = rows // ROWS
    planes = count_x * half_x
    assert rows % ROWS == 0
    used = half_y + RC
    sub = iota((ROWS, LANES), 0)
    lane = iota((ROWS, LANES), 1)
    nothing = jnp.zeros((ROWS, LANES), F32)
    forcing = [[nothing] * groups for _ in range(planes)]
    half_pairs = (half_x + RC) // 2
    ring = RC // 2
    for tx in range(count_x):
        for ty in range(count_y):
            for p in range(half_pairs):
                tile, base = p * used // SHORT, p * used % SHORT
                assert base + used <= 2 * SHORT == ROWS
                source = tx * count_y + ty
                piece = jnp.concatenate([blocks[source, tile], blocks[source, tile + 1]], 0)
                start = (ty * half_y - ring) % rows
                group, offset = start // ROWS, start % ROWS
                shift = (offset - base) % ROWS
                piece = pltpu.roll(piece, shift, 0) if shift else piece
                turned = pltpu.roll(piece, size_z2, 1)
                for half in range(2):
                    moved = jnp.where((lane < size_z2) == (half == 0), piece, turned)
                    x = (tx * half_x - ring + half * half_pairs + p) % planes
                    at = group
                    mine = (sub >= offset) & (sub < offset + used)
                    forcing[x][at] = forcing[x][at] + jnp.where(mine, moved, 0.0)
                    if offset + used > ROWS:
                        at = (group + 1) % groups
                        mine = sub < offset + used - ROWS
                        forcing[x][at] = forcing[x][at] + jnp.where(mine, moved, 0.0)
    return jnp.concatenate([jnp.concatenate(groups, 0)[None] for groups in forcing], 0)


def coarse_up(
    counts, grids, blocks, window_one, one_near, one_far, row_low, row_high,
    v_zero, forcing0, cx, cy, cz, weight, left_one, right_one, left_zero, right_zero, *rest,
):
    prepared, rest = rest[: len(grids)], rest[len(grids) :]
    (
        out, mixed_low, mixed_high, kappa_low, kappa_high, first_low, first_high,
        v_one, cx1, cy1, cz1, w1, one_a, one_b, zero_a, zero_b,
    ) = rest
    count_x, count_y = counts
    one_low, one_high = by_side("tx", one_near, one_far)
    _, tile_x1, rows1, size_z1 = window_one.shape
    tile_y1 = rows1 - 2 * R1
    top1 = R1 + tile_y1
    half_x, half_y, size_z2 = tile_x1 // 2, tile_y1 // 2, size_z1 // 2
    sizes = grids[0].sizes
    forcing2 = assemble(blocks, count_x, count_y, half_x, half_y, size_z2)
    levels = [(grid, Operator(prepared[number])) for number, grid in enumerate(grids[:-1])]
    exact = ExactSolve(grids[-1], inverse=prepared[-1][...])

    planes1 = tile_x1 + 2 * R1
    for message, mixed, kappa_rim, low in (
        (one_low, mixed_low, kappa_low, True), (one_high, mixed_high, kappa_high, False)
    ):
        at, loose = 0, 2 * R1 * ROWS
        for rim, fill in ((mixed, 0.0), (kappa_rim, 1.0)):
            for layer in range(1, R1 + 1):
                x = R1 - layer if low else layer - 1
                rim[x] = jnp.full((rows1, size_z1), fill, F32)
                rim[x, R1:top1] = message[at]
                at += 1
                for distance in range(1, reach_of(layer) + 1):
                    for row in (R1 - distance, top1 + distance - 1):
                        rim[x, row : row + 1] = message[
                            loose // ROWS, loose % ROWS : loose % ROWS + 1
                        ]
                        loose += 1

    def stacked(low, which, high):
        whole = [(low, x) for x in range(R1)]
        whole += [(window_one.at[which], x) for x in range(tile_x1)]
        whole += [(high, x) for x in range(R1)]
        return Planes(0, whole)

    forcing1 = stacked(mixed_low, 0, mixed_high)
    kappa1 = stacked(kappa_low, 2, kappa_high)
    plane_setup(kappa1, cx1, cy1, cz1, w1, None, 0.25, 1, planes1 - 1)
    row = iota((rows1, size_z1), 0)
    for mixed, rim, low in ((mixed_low, first_low, True), (mixed_high, first_high, False)):
        for layer in range(1, R1 + 1):
            x = R1 - layer if low else layer - 1
            if layer == R1:
                rim[x] = mixed[x]
            else:
                reach = reach_of(layer) - 1
                inside = (row >= R1 - reach) & (row < top1 + reach)
                at = x if low else R1 + tile_x1 + x
                rim[x] = jnp.where(inside, w1[at] * mixed[x], mixed[x])
    start1 = stacked(first_low, 1, first_high)
    plane_sweep(start1, v_one, forcing1, cx1, cy1, cz1, w1, 1, planes1 - 1)

    solved = solve_whole(forcing2, levels, exact)
    solved = solved.reshape(sizes[0] * sizes[1], LANES)

    raised = raise_level(left_one[...], right_one[...], solved)
    for x in range(1, planes1 - 1):
        one_a[x] = v_one[x] + raised[x * rows1 : (x + 1) * rows1]
    plane_sweep(one_a, one_b, forcing1, cx1, cy1, cz1, w1, 2, planes1 - 2)
    plane_sweep(one_b, one_a, forcing1, cx1, cy1, cz1, w1, 3, planes1 - 3)

    planes, rows, size_z = zero_a.shape
    v_zero, forcing0 = kept(v_zero, RX - 1), kept(forcing0, RX - 1)
    cx, cy, cz, weight = kept(cx, RX - 2), kept(cy, RX - 1), kept(cz, RX - 1), kept(weight, RX - 1)
    first, last = R1 - 1, planes1 - R1 + 1
    stack = jnp.concatenate([one_a[x] for x in range(first, last)], 0)
    raised = raise_level(left_zero[...], right_zero[...], stack)
    chunks = size_z // LANES
    top = rows - RY
    for x in range(RX - 1, planes - RX + 1):
        zero_b[x] = v_zero[x]
    for rim_x in (RX - 2, planes - RX + 1):
        zero_b[rim_x] = jnp.zeros((rows, size_z), F32)
    for x in range(planes - 2 * RX):
        at = 3 * tile_x1 * R1 // ROWS
        for chunk in range(chunks):
            lanes = slice(chunk * LANES, (chunk + 1) * LANES)
            zero_b[RX + x, RY - 2 : RY - 1, lanes] = row_low[at + chunk, x : x + 1]
            zero_b[RX + x, top + 1 : top + 2, lanes] = row_high[at + chunk, x : x + 1]
    for message, second, nearest in (
        (one_low, RX - 2, RX - 1), (one_high, planes - RX + 1, planes - RX)
    ):
        loose = 2 * R1 * ROWS + 2 * sum(2 * reach_of(layer) for layer in range(1, R1 + 1))
        for r in (RY - 1, top):
            for chunk in range(chunks):
                lanes = slice(chunk * LANES, (chunk + 1) * LANES)
                zero_b[nearest, r : r + 1, lanes] = message[
                    loose // ROWS, loose % ROWS : loose % ROWS + 1
                ]
                loose += 1
        at = -(-loose // ROWS)
        for chunk in range(chunks):
            lanes = slice(chunk * LANES, (chunk + 1) * LANES)
            for half in range((top - RY) // ROWS):
                zero_b[second, RY + half * ROWS : RY + (half + 1) * ROWS, lanes] = message[at]
                at += 1
    for x in range(RX - 2, planes - RX + 2):
        at = (x - RX + 2 * R1) // 2 - first
        zero_a[x] = zero_b[x] + raised[at * rows : (at + 1) * rows]
    plane_sweep(zero_a, zero_b, forcing0, cx, cy, cz, weight, RX - 1, planes - RX + 1)
    plane_sweep(zero_b, zero_a, forcing0, cx, cy, cz, weight, RX, planes - RX)
    for x in range(planes - 2 * RX):
        out[x] = zero_a[x + RX, RY:top]


VM = pl.BlockSpec(memory_space=pltpu.VMEM)
IN_PLACE = pl.BlockSpec(memory_space=pltpu.HBM)


def call(kernel, operands, outputs, scratch, spec=VM, in_hbm=()):
    def typed(output):
        return output if isinstance(output, jax.ShapeDtypeStruct) else jax.ShapeDtypeStruct(output, F32)

    return pl.pallas_call(
        kernel,
        in_specs=[spec] * len(operands),
        out_specs=[IN_PLACE if n in in_hbm else VM for n in range(len(outputs))],
        out_shape=[typed(output) for output in outputs],
        scratch_shapes=[pltpu.VMEM(s, F32) if isinstance(s, tuple) else s for s in scratch],
        compiler_params=pltpu.CompilerParams(vmem_limit_bytes=24 * 1024 * 1024),
    )(*operands)


def shift_both(to_low, to_high, axis):
    count = lax.axis_size(axis)
    from_low = lax.ppermute(to_high, axis, [(i, (i + 1) % count) for i in range(count)])
    from_high = lax.ppermute(to_low, axis, [((i + 1) % count, i) for i in range(count)])
    return from_low, from_high


def swap_both(near, far, axis):
    count = lax.axis_size(axis)
    assert count % 2 == 0
    partner = [(i, i ^ 1) for i in range(count)]
    other = [(i, (i - 1 if i % 2 == 0 else i + 1) % count) for i in range(count)]
    from_far = lax.ppermute(far, axis, other)
    from_near = lax.ppermute(near, axis, partner)
    return from_near, from_far


def to_everyone(blocks):
    return lax.all_to_all(blocks, ("tx", "ty"), 0, 0)


def cycle(concentration, source, material):
    tile_x, tile_y, size_z = concentration.shape
    chunks = size_z // LANES
    counts = lax.axis_size("tx"), lax.axis_size("ty")
    everyone = counts[0] * counts[1]
    rows = tile_y + 2 * RY
    message = (tile_x + 1, ROWS, size_z)
    *inputs, to_low, to_high = call(
        edges,
        tuple(
            pltpu.with_memory_space_constraint(v, pltpu.HBM)
            for v in (concentration, source, material)
        ),
        tuple(jax.ShapeDtypeStruct(v.shape, v.dtype) for v in (concentration, source, material))
        + (message, message),
        (pltpu.SemaphoreType.DMA((3,)),),
        IN_PLACE,
    )
    from_low, from_high = shift_both(to_low, to_high, "ty")
    zero = (tile_x + 2 * RX, rows, size_z)
    inner = (tile_x + 2, rows, size_z)
    one_tile = (tile_x // 2, tile_y // 2, size_z // 2)
    two_tile = tuple(extent // 2 for extent in one_tile)
    grids = levels_of(counts, two_tile)

    def bits(*shape):
        return jax.ShapeDtypeStruct(shape, BF16)

    k_tile, kappa_blocks, halves, halves_one = call(
        shrink,
        inputs[2:],
        (
            one_tile,
            (everyone, two_tile[1], LANES),
            bits(chunks, LANES, one_tile[2]),
            bits(2, one_tile[2], one_tile[2]),
        ),
        ((one_tile[0], tile_y, LANES), one_tile[1:]),
    )
    message = (plane_tiles(tile_y), ROWS, size_z)
    window, to_low, to_high = call(
        sides,
        (*inputs, k_tile, from_low, from_high),
        ((3, tile_x, rows, size_z), message, message),
        ((rows, size_z),),
    )
    from_low, from_high = shift_both(to_low, to_high, "tx")
    kappa_blocks = to_everyone(kappa_blocks)
    wide = -(-rows // (2 * ROWS)) * ROWS
    small = (one_tile[0] + 2 * RC, wide, one_tile[2])
    pairs1 = small[0] // 2
    short = pairs1 // 2 * (two_tile[1] + RC) // SHORT
    assert pairs1 // 2 * (two_tile[1] + RC) % SHORT == 0
    message = (3 * one_tile[0] * R1 // ROWS + chunks, ROWS, LANES)
    assert one_tile[2] == LANES and tile_x <= ROWS and one_tile[1] == ROWS
    v_zero, forcing0, cx, cy, cz, weight, level_one, blocks, to_low, to_high = call(
        fine_down,
        (window, halves, halves_one, from_low, from_high),
        (inner, inner, (tile_x + 3, rows, size_z), inner, inner, inner)
        + ((3,) + one_tile, (everyone, short, SHORT, LANES), message, message),
        (
            (4, rows, size_z),
            (2, rows, size_z),
            (4, rows, size_z),
            zero,
            zero,
            (chunks, max(small[0], tile_x), 2 * wide, LANES),
            (everyone, short, SHORT, LANES),
            pltpu.SemaphoreType.DMA,
        )
        + (small,) * 9
        + ((pairs1, wide, one_tile[2]), (pairs1, ROWS, one_tile[2])),
        in_hbm=(7,),
    )
    row_low, row_high = shift_both(to_low, to_high, "ty")
    blocks = to_everyone(blocks)
    rows1 = one_tile[1] + 2 * R1
    message = (middle_tiles(tile_y, chunks), ROWS, LANES)
    window_one, near, far = call(
        middle,
        (level_one, v_zero, row_low, row_high),
        ((3, one_tile[0], rows1, one_tile[2]), message, message),
        (),
    )
    one_near, one_far = swap_both(near, far, "tx")
    one = (one_tile[0] + 2 * R1, rows1, one_tile[2])
    seen = one[0] - 2 * (R1 - 1)
    chosen = call(
        functools.partial(selectors, grids[0].sizes, one[0], one_tile[0], one_tile[1], rows),
        (window_one,),
        (
            bits(one[0] * rows1, grids[0].sizes[0] * grids[0].sizes[1]),
            bits(LANES, one_tile[2]),
            bits(seen * rows, seen * rows1),
            bits(one_tile[2], size_z),
        ),
        (),
    )
    lattice = grids[0].sizes[1], LANES
    prepared = call(
        functools.partial(prepare, counts, grids),
        (kappa_blocks, window_one),
        tuple((5, grid.sizes[0]) + lattice for grid in grids[:-1])
        + ((-(-grids[-1].cells // ROWS) * ROWS, LANES),),
        (),
    )
    rim = (R1,) + one[1:]
    (updated,) = call(
        functools.partial(coarse_up, counts, grids),
        (blocks, window_one, one_near, one_far, row_low, row_high)
        + (v_zero, forcing0, cx, cy, cz, weight, *chosen, *prepared),
        (concentration.shape,),
        (rim,) * 6 + (one,) * 7 + (zero, zero),
    )
    return updated


def solution(mesh):
    placed = (P("tx", "ty", None), P("tx", "ty", None), P("tx", "ty", None))
    return jax.shard_map(
        cycle, mesh=mesh, in_specs=placed, out_specs=P("tx", "ty", None), check_vma=False
    )
```

```python
import functools

import jax
import jax.numpy as jnp
from jax import lax
from jax.experimental import pallas as pl
from jax.experimental.pallas import tpu as pltpu
from jax.sharding import PartitionSpec as P


mass_rate = 0.001
relax_weight = 0.8
diffusivities = (0.15, 0.3, 0.5, 0.8, 1.2, 2.0, 3.2, 5.0)
LANES = 128
ROWS = 8
SHORT = 4
RX = 2
RY = 4
R1 = 4
RC = 2
F32 = jnp.float32
BF16 = jnp.bfloat16


def lookup(material):
    result = jnp.zeros(material.shape, F32)
    for slot_id, coeff_value in enumerate(diffusivities):
        result = jnp.where(material == slot_id, F32(coeff_value), result)
    return result


class Planes:
    def __init__(self, first, planes):
        self.first = first
        self.planes = planes

    def __getitem__(self, x):
        ref, index = self.planes[x - self.first]
        return ref[index]

    def __setitem__(self, x, value):
        ref, index = self.planes[x - self.first]
        ref[index] = value


def kept(ref, first):
    return Planes(first, [(ref, x) for x in range(ref.shape[0])])


class Picked:
    def __init__(self, flag, when_true, when_false):
        self.flag = flag
        self.when_true = when_true
        self.when_false = when_false

    def __getitem__(self, index):
        first, second = self.when_true[index], self.when_false[index]
        flag = jnp.where(self.flag, jnp.int32(1), jnp.int32(0))
        return jnp.where(jnp.full(first.shape, flag) == 1, first, second)


def iota(shape, dim):
    return lax.broadcasted_iota(jnp.int32, shape, dim)


def div(a, b):
    return lax.div(a, jnp.full_like(a, b))


def mod(a, b):
    return lax.rem(a, jnp.full_like(a, b))


def ones_where(mask):
    return jnp.where(mask, F32(1.0), F32(0.0)).astype(BF16)


def three_terms(x):
    high = x.astype(BF16)
    rest = x - high.astype(F32)
    middle = rest.astype(BF16)
    low = (rest - middle.astype(F32)).astype(BF16)
    return high, middle, low


def times_right(x, selector):
    parts = [jnp.dot(part, selector, preferred_element_type=F32) for part in three_terms(x)]
    return parts[0] + (parts[1] + parts[2])


def back(v, axis, step=1):
    return pltpu.roll(v, step, axis)


def ahead(v, axis, step=1):
    return pltpu.roll(v, v.shape[axis] - step, axis)


def halve_lanes(fine, coarse, start=0):
    shape = (fine, coarse)
    return ones_where(div(iota(shape, 0), 2) + start == iota(shape, 1))


def plane_setup(kappa, cx, cy, cz, weight, diag, scale, first, last):
    half = 0.5 * scale
    for x in range(first - 1, last):
        cx[x] = half * (kappa[x] + kappa[x + 1])
    for x in range(first, last):
        k = kappa[x]
        y_part = half * (k + ahead(k, 0))
        z_part = half * (k + ahead(k, 1))
        cy[x] = y_part
        cz[x] = z_part
        d = mass_rate + cx[x] + cx[x - 1] + y_part + back(y_part, 0) + z_part + back(z_part, 1)
        weight[x] = relax_weight / d
        if diag is not None:
            diag[x] = d


def in_plane(here, cy, cz, x):
    y_part = cy[x]
    z_part = cz[x]
    total = y_part * ahead(here, 0) + back(y_part * here, 0)
    return total + (z_part * ahead(here, 1) + back(z_part * here, 1))


def neighbours(v, cx, cy, cz, x):
    return (cx[x] * v[x + 1] + cx[x - 1] * v[x - 1]) + in_plane(v[x], cy, cz, x)


def plane_sweep(v, out, forcing, cx, cy, cz, weight, first, last):
    for x in range(first, last):
        out[x] = (1.0 - relax_weight) * v[x] + weight[x] * (forcing[x] + neighbours(v, cx, cy, cz, x))


def edges(conc_in, source_in, material_in, conc, source, material, to_low, to_high, arrived):
    copies = [
        pltpu.make_async_copy(whence, whither, arrived.at[n])
        for n, (whence, whither) in enumerate(
            ((conc_in, conc), (source_in, source), (material_in, material))
        )
    ]
    for copy in copies:
        copy.start()
    for copy in copies:
        copy.wait()
    tile_x, tile_y, _ = conc.shape
    for to, low in ((to_low, True), (to_high, False)):
        for x in range(tile_x):
            rows = slice(0, 4) if low else slice(tile_y - 4, tile_y)
            near = slice(0, 3) if low else slice(1, 4)
            pair = slice(0, 2) if low else slice(2, 4)
            c = conc[x, rows]
            f = mass_rate * c + source[x, rows]
            k = lookup(material[x, rows])
            to[x, 0:3] = c[near]
            to[x, 3:5] = f[pair]
            to[x, 5:8] = k[near]
            to[tile_x, x : x + 1] = k[3:4] if low else k[0:1]


def sides(conc, source, material, k_tile, from_low, from_high, window, to_low, to_high, swept):
    tile_x, tile_y, size_z = conc.shape
    top = RY + tile_y
    for x in range(tile_x):
        c = conc[x]
        window[0, x, RY:top] = c
        window[1, x, RY:top] = mass_rate * c + source[x]
        window[2, x, RY:top] = lookup(material[x])
        window[0, x, 0:1] = jnp.zeros((1, size_z), F32)
        window[0, x, 1:4] = from_low[x, 0:3]
        window[0, x, top : top + 3] = from_high[x, 0:3]
        window[0, x, top + 3 :] = jnp.zeros((1, size_z), F32)
        window[1, x, 0:2] = jnp.zeros((2, size_z), F32)
        window[1, x, 2:4] = from_low[x, 3:5]
        window[1, x, top : top + 2] = from_high[x, 3:5]
        window[1, x, top + 2 :] = jnp.zeros((2, size_z), F32)
        window[2, x, 0:1] = from_low[tile_x, x : x + 1]
        window[2, x, 1:4] = from_low[x, 5:8]
        window[2, x, top : top + 3] = from_high[x, 5:8]
        window[2, x, top + 3 :] = from_high[tile_x, x : x + 1]
    per_plane = tile_y // ROWS
    for to, low in ((to_low, True), (to_high, False)):

        def plane(layer):
            return layer - 1 if low else tile_x - layer

        def send(at, values):
            for n in range(per_plane):
                to[at + n] = values(n)

        for n, (which, layer) in enumerate(BASE_PLANES):
            send(
                n * per_plane,
                lambda n: window[which, plane(layer), RY + n * ROWS : RY + (n + 1) * ROWS],
            )
        first_sweep(window, plane(2), swept)
        at = len(BASE_PLANES) * per_plane
        send(at, lambda n: swept[RY + n * ROWS : RY + (n + 1) * ROWS])
        loose = (at + per_plane) * ROWS
        for which, layer, reach in EXTRA_ROWS:
            for start in (RY - reach, top):
                to[loose // ROWS, loose % ROWS : loose % ROWS + reach] = window[
                    which, plane(layer), start : start + reach
                ]
                loose += reach
        at = -(-loose // ROWS)
        to[at, :, 0 : size_z // 2] = k_tile[1 if low else k_tile.shape[0] - 2]
        to[at, :, size_z // 2 :] = jnp.zeros((ROWS, size_z - size_z // 2), F32)


def first_sweep(window, x, out):
    c, f, k = window[0, x], window[1, x], window[2, x]
    next_part = 0.5 * (k + window[2, x + 1])
    last_part = 0.5 * (k + window[2, x - 1])
    y_part = 0.5 * (k + ahead(k, 0))
    z_part = 0.5 * (k + ahead(k, 1))
    d = mass_rate + next_part + last_part
    d = d + y_part + back(y_part, 0) + z_part + back(z_part, 1)
    total = next_part * window[0, x + 1] + last_part * window[0, x - 1]
    total = total + (y_part * ahead(c, 0) + back(y_part * c, 0))
    total = total + (z_part * ahead(c, 1) + back(z_part * c, 1))
    out[...] = (1.0 - relax_weight) * c + (relax_weight / d) * (f + total)


BASE_PLANES = ((0, 1), (0, 2), (1, 1), (2, 1), (2, 2))
EXTRA_ROWS = ((0, 1, 2), (0, 2, 1), (1, 1, 1), (2, 1, 2), (2, 2, 2))


def plane_tiles(tile_y):
    loose = sum(2 * reach for _, _, reach in EXTRA_ROWS)
    return (len(BASE_PLANES) + 1) * tile_y // ROWS + -(-loose // ROWS) + 1


def shrink(material, k_tile, blocks, halves, halves_one, twice_one, twice_zero, paired, paired_one):
    tile_x, tile_y, size_z = material.shape
    tile_x1, tile_y1, size_z1 = tile_x // 2, tile_y // 2, size_z // 2
    k_one = None
    for chunk in range(size_z // LANES):
        lanes = slice(chunk * LANES, (chunk + 1) * LANES)
        for pair in range(tile_x1):
            paired[pair] = lookup(material[2 * pair, :, lanes]) + lookup(
                material[2 * pair + 1, :, lanes]
            )
        stack = [
            paired[pair, pl.ds(0, tile_y1, stride=2)] + paired[pair, pl.ds(1, tile_y1, stride=2)]
            for pair in range(tile_x1)
        ]
        part = times_right(
            jnp.concatenate(stack, 0), halve_lanes(LANES, size_z1, chunk * LANES // 2)
        )
        k_one = part if k_one is None else k_one + part
    k_one = 0.125 * k_one
    for x in range(tile_x1):
        k_tile[x] = k_one[x * tile_y1 : (x + 1) * tile_y1]
    assert tile_x1 // 2 * (size_z1 // 2) <= LANES
    block = None
    for pair in range(tile_x1 // 2):
        at = 2 * pair * tile_y1
        paired_one[...] = k_one[at : at + tile_y1] + k_one[at + tile_y1 : at + 2 * tile_y1]
        piece = (
            paired_one[pl.ds(0, tile_y1 // 2, stride=2)] + paired_one[pl.ds(1, tile_y1 // 2, stride=2)]
        )
        part = times_right(piece, halve_lanes(size_z1, LANES, pair * size_z1 // 2))
        block = part if block is None else block + part
    block = 0.125 * block
    for device in range(blocks.shape[0]):
        blocks[device] = block
    for chunk in range(size_z // LANES):
        halves[chunk] = halve_lanes(LANES, size_z1, chunk * LANES // 2)
    for half in range(2):
        halves_one[half] = halve_lanes(size_z1, size_z1, half * size_z1 // 2)
    for twice in (twice_one, twice_zero):
        twice[...] = ones_where(iota(twice.shape, 0) == div(iota(twice.shape, 1), 2))


def fine_down(
    window, halves, halves_one, from_low, from_high,
    v_zero, forcing_out, cx, cy, cz, weight, level_one, blocks_out, to_low, to_high,
    conc_rim, forcing_rim, kappa_rim, once, diag, paired, blocks, left,
    k_one, f_one, u_one, v_one, cx1, cy1, cz1, w1, d1, paired_one, packed,
):
    _, tile_x, rows, size_z = window.shape
    tile_y = rows - 2 * RY
    top = RY + tile_y
    planes = tile_x + 2 * RX
    rims = (conc_rim, forcing_rim, kappa_rim)
    depths = (2, 1, 2)
    for which, rim in enumerate(rims):
        fill = jnp.full((rows, size_z), 1.0 if which == 2 else 0.0, F32)
        for x in range(2 * depths[which]):
            rim[x] = fill

    def place(which, layer, low):
        return depths[which] - layer if low else depths[which] + layer - 1

    per_plane = tile_y // ROWS
    last_tile = plane_tiles(tile_y) - 1
    for message, low in ((from_low, True), (from_high, False)):
        for at, (which, layer) in enumerate(BASE_PLANES):
            for n in range(per_plane):
                start = RY + n * ROWS
                rims[which][place(which, layer, low), start : start + ROWS] = message[
                    at * per_plane + n
                ]
        rim_x = 0 if low else planes - 1
        once[rim_x] = jnp.zeros((rows, size_z), F32)
        at = len(BASE_PLANES) * per_plane
        for n in range(per_plane):
            start = RY + n * ROWS
            once[rim_x, start : start + ROWS] = message[at + n]
        loose = (at + per_plane) * ROWS
        for which, layer, reach in EXTRA_ROWS:
            for start in (RY - reach, top):
                rims[which][place(which, layer, low), start : start + reach] = message[
                    loose // ROWS, loose % ROWS : loose % ROWS + reach
                ]
                loose += reach

    def stacked(which):
        depth = depths[which]
        whole = [(rims[which], x) for x in range(depth)]
        whole += [(window.at[which], x) for x in range(tile_x)]
        whole += [(rims[which], depth + x) for x in range(depth)]
        return Planes(RX - depth, whole)

    conc, forcing, kappa = stacked(0), stacked(1), stacked(2)
    cx, cy, cz, weight = kept(cx, RX - 2), kept(cy, RX - 1), kept(cz, RX - 1), kept(weight, RX - 1)
    v_out = kept(v_zero, RX - 1)
    plane_setup(kappa, cx, cy, cz, weight, diag, 1.0, 1, planes - 1)
    plane_sweep(conc, once, forcing, cx, cy, cz, weight, 1, planes - 1)
    plane_sweep(once, v_out, forcing, cx, cy, cz, weight, 1, planes - 1)
    chunks = size_z // LANES
    size_z1 = size_z // 2
    to_half = [halves[chunk] for chunk in range(chunks)]
    tile_x1, tile_y1 = tile_x // 2, tile_y // 2

    def put(pair, total):
        for chunk in range(chunks):
            paired[chunk, pair, 0:rows] = total[:, chunk * LANES : (chunk + 1) * LANES]

    def narrowed(pairs, start, count):
        result = None
        for chunk in range(chunks):
            stack = [
                paired[chunk, pair, pl.ds(start, count, stride=2)]
                + paired[chunk, pair, pl.ds(start + 1, count, stride=2)]
                for pair in range(pairs)
            ]
            part = times_right(jnp.concatenate(stack, 0), to_half[chunk])
            result = part if result is None else result + part
        return 0.125 * result

    wide = paired.shape[2] // 2
    planes1 = tile_x1 + 2 * RC
    if 2 * wide > rows:
        for chunk in range(chunks):
            for pair in range(planes1 - 2):
                paired[chunk, pair, rows:] = jnp.ones((2 * wide - rows, LANES), F32)
    for pair in range(planes1 - 2):
        put(pair, kappa[2 * pair] + kappa[2 * pair + 1])
    coarse = narrowed(planes1 - 2, 0, wide)
    for pair in range(planes1 - 2):
        k_one[pair + 1] = coarse[pair * wide : (pair + 1) * wide]
    for message, x in ((from_low, 0), (from_high, planes1 - 1)):
        k_one[x] = jnp.ones((wide, size_z1), F32)
        k_one[x, RC : RC + tile_y1] = message[last_tile, :, 0:size_z1]
    plane_setup(k_one, cx1, cy1, cz1, w1, d1, 0.25, 1, planes1 - 1)

    for pair in range(tile_x1):
        total = None
        for x in (RX + 2 * pair, RX + 2 * pair + 1):
            part = forcing[x] + neighbours(v_out, cx, cy, cz, x) - diag[x] * v_out[x]
            total = part if total is None else total + part
        put(pair, total)
    forcing_one = narrowed(tile_x1, RY, tile_y1)

    low, high = RC, RC + tile_y1
    nothing = jnp.zeros((wide, size_z1), F32)
    for x in range(planes1):
        f_one[x] = nothing
        if x in (0, planes1 - 1):
            v_one[x] = nothing
    for x in (0, 1, planes1 - 2, planes1 - 1):
        u_one[x] = nothing
    for x in range(tile_x1):
        f = forcing_one[x * tile_y1 : (x + 1) * tile_y1]
        f_one[x + RC, low:high] = f
        u_one[x + RC] = w1[x + RC] * f_one[x + RC]
        level_one[0, x] = f
        level_one[1, x] = u_one[x + RC, low:high]
        level_one[2, x] = k_one[x + RC, low:high]
    plane_sweep(u_one, v_one, f_one, cx1, cy1, cz1, w1, 1, planes1 - 1)
    pairs1 = planes1 // 2
    for pair in range(pairs1):
        total = None
        for x in (2 * pair, 2 * pair + 1):
            if x == 0:
                part = cx1[0] * v_one[1]
            elif x == planes1 - 1:
                part = cx1[x - 1] * v_one[x - 1]
            else:
                part = f_one[x] + neighbours(v_one, cx1, cy1, cz1, x) - d1[x] * v_one[x]
            total = part if total is None else total + part
        paired_one[pair] = total
    for pair in range(pairs1):
        packed[pair] = (
            paired_one[pair, pl.ds(0, ROWS, stride=2)] + paired_one[pair, pl.ds(1, ROWS, stride=2)]
        )
    half_pairs = pairs1 // 2
    result = times_right(
        jnp.concatenate([packed[p] for p in range(half_pairs)], 0), halves_one[0]
    ) + times_right(
        jnp.concatenate([packed[half_pairs + p] for p in range(half_pairs)], 0), halves_one[1]
    )
    used = tile_y1 // 2 + RC
    block = jnp.concatenate([result[p * ROWS : p * ROWS + used] for p in range(half_pairs)], 0)
    block = 0.125 * block
    for part in range(blocks.shape[1]):
        piece = block[part * SHORT : (part + 1) * SHORT]
        for device in range(blocks.shape[0]):
            blocks[device, part] = piece
    copy = pltpu.make_async_copy(blocks, blocks_out, left)
    copy.start()
    for x in range(RX - 1, planes - RX + 1):
        forcing_out[x - RX + 1] = forcing[x]

    for to, rows1, row0 in (
        (to_low, slice(0, R1), RY + 1),
        (to_high, slice(tile_y1 - R1, tile_y1), top - 2),
    ):
        for which in range(3):
            for x in range(tile_x1):
                flat_row = which * tile_x1 * R1 + x * R1
                to[flat_row // ROWS, flat_row % ROWS : flat_row % ROWS + R1] = level_one[
                    which, x, rows1
                ]
        start = 3 * tile_x1 * R1 // ROWS
        for x in range(tile_x):
            row = v_zero[x + 1, row0 : row0 + 1]
            for chunk in range(chunks):
                to[start + chunk, x : x + 1] = row[:, chunk * LANES : (chunk + 1) * LANES]
    copy.wait()


def reach_of(layer):
    return R1 + 1 - layer


def middle(level_one, v_zero, from_low, from_high, window, to_low, to_high):
    _, tile_x1, tile_y1, _ = level_one.shape
    planes, rows, size_z = v_zero.shape
    top1 = R1 + tile_y1
    for which in range(3):
        for x in range(tile_x1):
            flat_row = which * tile_x1 * R1 + x * R1
            at, sub = flat_row // ROWS, flat_row % ROWS
            window[which, x, R1:top1] = level_one[which, x]
            window[which, x, 0:R1] = from_low[at, sub : sub + R1]
            window[which, x, top1:] = from_high[at, sub : sub + R1]
    chunks = size_z // LANES
    top = rows - RY

    for to, low in ((to_low, True), (to_high, False)):
        at = 0
        for which in (0, 2):
            for layer in range(1, R1 + 1):
                x = layer - 1 if low else tile_x1 - layer
                outer = 1 if which == 0 and layer == R1 else which
                to[at] = window[outer, x, R1:top1]
                at += 1
        loose = at * ROWS
        for which in (0, 2):
            for layer in range(1, R1 + 1):
                x = layer - 1 if low else tile_x1 - layer
                outer = 1 if which == 0 else which
                for distance in range(1, reach_of(layer) + 1):
                    source = outer if distance == reach_of(layer) else which
                    for row in (R1 - distance, top1 + distance - 1):
                        to[loose // ROWS, loose % ROWS : loose % ROWS + 1] = window[
                            source, x, row : row + 1
                        ]
                        loose += 1
        second, first = (2, 1) if low else (planes - 3, planes - 2)
        for row in (RY - 1, top):
            for chunk in range(chunks):
                lanes = slice(chunk * LANES, (chunk + 1) * LANES)
                to[loose // ROWS, loose % ROWS : loose % ROWS + 1] = v_zero[first, row : row + 1, lanes]
                loose += 1
        at = -(-loose // ROWS)
        for chunk in range(chunks):
            lanes = slice(chunk * LANES, (chunk + 1) * LANES)
            for half in range((top - RY) // ROWS):
                to[at] = v_zero[second, RY + half * ROWS : RY + (half + 1) * ROWS, lanes]
                at += 1


def middle_tiles(tile_y, chunks):
    loose = 2 * sum(2 * reach_of(layer) for layer in range(1, R1 + 1)) + 2 * chunks
    return 2 * R1 + -(-loose // ROWS) + chunks * tile_y // ROWS


class Grid:
    def __init__(self, sizes, strides, scales, rows, lanes):
        self.sizes = sizes
        self.strides = strides
        self.scales = scales
        self.rows = rows
        self.lanes = lanes
        self.ratios = tuple(2 if extent % 2 == 0 else 1 for extent in sizes)
        self.cells = sizes[0] * sizes[1] * sizes[2]
        self.exact = self.cells <= 64 or self.ratios == (1, 1, 1)

    def coarser(self):
        sizes = tuple(extent // ratio for extent, ratio in zip(self.sizes, self.ratios))
        scales = tuple(s / (ratio * ratio) for s, ratio in zip(self.scales, self.ratios))
        strides = tuple(s * ratio for s, ratio in zip(self.strides, self.ratios[1:]))
        return Grid(sizes, strides, scales, self.rows, self.lanes)


def next_plane(v):
    return v if v.shape[0] == 1 else jnp.concatenate([v[1:], v[:1]], 0)


def last_plane(v):
    return v if v.shape[0] == 1 else jnp.concatenate([v[-1:], v[:-1]], 0)


def restrict_whole(v, grid):
    if grid.ratios[0] == 2:
        v = jnp.concatenate(
            [v[2 * x : 2 * x + 1] + v[2 * x + 1 : 2 * x + 2] for x in range(grid.sizes[0] // 2)], 0
        )
    for axis in (1, 2):
        if grid.ratios[axis] == 2:
            step = grid.strides[axis - 1]
            even = mod(div(iota(v.shape, axis), step), 2) == 0
            v = v + jnp.where(even, ahead(v, axis, step), back(v, axis, step))
    return (1.0 / (grid.ratios[0] * grid.ratios[1] * grid.ratios[2])) * v


def prolong_whole(v, grid):
    if grid.ratios[0] == 1:
        return v
    return jnp.concatenate([v[x // 2 : x // 2 + 1] for x in range(grid.sizes[0])], 0)


def whole_operator(kappa, grid):
    half_x, half_y, half_z = (0.5 * s for s in grid.scales)
    step_y, step_z = grid.strides
    cx = half_x * (kappa + next_plane(kappa))
    cy = half_y * (kappa + ahead(kappa, 1, step_y))
    cz = half_z * (kappa + ahead(kappa, 2, step_z))
    diag = mass_rate + cx + last_plane(cx)
    diag = diag + (cy + back(cy, 1, step_y)) + (cz + back(cz, 2, step_z))
    return cx, cy, cz, diag, relax_weight / diag


def whole_neighbours(v, operator, grid):
    cx, cy, cz = operator[:3]
    step_y, step_z = grid.strides
    total = cx * next_plane(v) + last_plane(cx * v)
    total = total + (cy * ahead(v, 1, step_y) + back(cy * v, 1, step_y))
    return total + (cz * ahead(v, 2, step_z) + back(cz * v, 2, step_z))


def whole_sweep(v, forcing, operator, grid):
    return (1.0 - relax_weight) * v + operator[4] * (forcing + whole_neighbours(v, operator, grid))


class ExactSolve:
    def __init__(self, grid, kappa=None, inverse=None):
        size_x, size_y, size_z = grid.sizes
        self.grid = grid
        self.across = across = size_x * size_y
        _, step_z = grid.strides
        self.period = period = size_z * step_z
        cells = grid.cells
        padded = -(-cells // ROWS) * ROWS
        assert across <= step_z and 2 * period <= grid.lanes
        shape = (padded, grid.lanes)
        i, j = iota(shape, 0), iota(shape, 1)
        self.i, self.j = i, j
        if kappa is None:
            self.inverse = inverse
            return

        def places_of_row(n):
            sub = mod(n, across)
            return div(sub, size_y), mod(sub, size_y), div(n, across)

        def places_of_lane(n):
            n = mod(n, period)
            sub = mod(n, step_z)
            return div(sub, size_y), mod(sub, size_y), div(n, step_z)

        at_i, at_j = places_of_row(i), places_of_lane(j)
        live = (mod(j, step_z) < across) & (i < cells)
        same = (at_i[0] == at_j[0]) & (at_i[1] == at_j[1]) & (at_i[2] == at_j[2]) & live
        left = j < period
        factor = jnp.zeros(shape, F32)
        for d in range(3):
            equal = [at_i[other] == at_j[other] for other in range(3) if other != d]
            for step in (1, grid.sizes[d] - 1):
                hit = mod(at_i[d] + step, grid.sizes[d]) == at_j[d]
                factor = factor + jnp.where(
                    hit & equal[0] & equal[1], F32(0.5 * grid.scales[d]), F32(0.0)
                )
        k_row = self.as_row(kappa)
        k_column = jnp.sum(jnp.where(same & left, k_row, 0.0), axis=1, keepdims=True)
        coupled = jnp.where(live & left, factor * (k_column + k_row), 0.0)
        diag = mass_rate + jnp.sum(coupled, axis=1, keepdims=True)
        matrix = jnp.where(same & left, diag - coupled, -coupled)
        matrix = jnp.where(left, matrix, jnp.where(same, F32(1.0), F32(0.0)))
        for n in range(cells):
            lane = (n // across) * step_z + n % across
            pivot_row = matrix[n : n + 1] / matrix[n : n + 1, lane : lane + 1]
            column = matrix[:, lane : lane + 1]
            matrix = jnp.where(i == n, pivot_row, matrix - column * pivot_row)
        self.inverse = jnp.where((j >= period) & (j < 2 * period) & live, matrix, 0.0)

    def as_row(self, v):
        grid = self.grid
        size_x, size_y, _ = grid.sizes
        step_y, step_z = grid.strides
        sub = mod(iota((1, grid.lanes), 1), step_z)
        result = jnp.zeros((1, grid.lanes), F32)
        for x in range(size_x):
            for y in range(size_y):
                row = v[x, y * step_y : y * step_y + 1]
                result = jnp.where(sub == x * size_y + y, row, result)
        return result

    def solve(self, forcing):
        grid = self.grid
        size_x, size_y, _ = grid.sizes
        step_y, step_z = grid.strides
        solved = jnp.sum(self.inverse * self.as_row(forcing), axis=1, keepdims=True)
        at_z = div(mod(self.j, self.period), step_z)
        spread = jnp.where(div(self.i, self.across) == at_z, solved, 0.0)
        planes = []
        for x in range(size_x):
            rows = []
            for y in range(size_y):
                mine = mod(self.i, self.across) == x * size_y + y
                row = jnp.sum(jnp.where(mine, spread, 0.0), axis=0, keepdims=True)
                rows.append(jnp.broadcast_to(row, (step_y, grid.lanes)))
            planes.append(jnp.concatenate(rows, 0)[None])
        return jnp.concatenate(planes, 0)


def levels_of(counts, tile_sizes):
    sizes = tuple(count * extent for count, extent in zip(counts, tile_sizes)) + tile_sizes[2:]
    grid = Grid(sizes, (1, 1), (0.0625, 0.0625, 0.0625), sizes[1], LANES)
    grids = [grid]
    while not grid.exact:
        grid = grid.coarser()
        grids.append(grid)
    return grids


class Operator:
    def __init__(self, ref):
        self.ref = ref

    def __getitem__(self, part):
        if isinstance(part, slice):
            return [self.ref[p] for p in range(*part.indices(5))]
        return self.ref[part]


def kappa_of(blocks, counts, grid):
    count_x, count_y = counts
    planes, rows, size_z2 = grid.sizes
    half_x, half_y = planes // count_x, rows // count_y
    assert half_x * size_z2 == LANES and half_x == 2 and ROWS % half_y == 0 and half_y == SHORT
    share = ROWS // half_y
    kappa = [[None] * (rows // ROWS) for _ in range(planes)]
    lane = iota((ROWS, LANES), 1)
    for tx in range(count_x):
        for group in range(rows // ROWS):
            pieces = [blocks[tx * count_y + group * share + n] for n in range(share)]
            piece = jnp.concatenate(pieces, 0)
            turned = pltpu.roll(piece, size_z2, 1)
            for p in range(half_x):
                mine = (lane < size_z2) == (p == 0)
                kappa[tx * half_x + p][group] = jnp.where(mine, piece, turned)
    return jnp.concatenate([jnp.concatenate(groups, 0)[None] for groups in kappa], 0)


def prepare(counts, grids, blocks, _, *outputs):
    kappas = [kappa_of(blocks, counts, grids[0])]
    for grid in grids[:-1]:
        kappas.append(restrict_whole(kappas[-1], grid))
    outputs[-1][...] = ExactSolve(grids[-1], kappas[-1]).inverse
    for number, grid in enumerate(grids[:-1]):
        for part, value in enumerate(whole_operator(kappas[number], grid)):
            outputs[number][part] = value


def spread_lanes(v, twice):
    high = v.astype(BF16)
    low = (v - high.astype(F32)).astype(BF16)
    return jnp.dot(high, twice, preferred_element_type=F32) + jnp.dot(
        low, twice, preferred_element_type=F32
    )


def solve_whole(forcing, levels, exact):
    if not levels:
        return exact.solve(forcing)
    grid, operator = levels[0]
    v = operator[4] * forcing
    v = whole_sweep(v, forcing, operator, grid)
    residual = forcing + whole_neighbours(v, operator, grid) - operator[3] * v
    v = v + prolong_whole(solve_whole(restrict_whole(residual, grid), levels[1:], exact), grid)
    for _ in range(2):
        v = whole_sweep(v, forcing, operator, grid)
    return v


def assemble(blocks, count_x, count_y, half_x, half_y, size_z2):
    rows = count_y * half_y
    groups = rows // ROWS
    planes = count_x * half_x
    assert rows % ROWS == 0
    used = half_y + RC
    sub = iota((ROWS, LANES), 0)
    lane = iota((ROWS, LANES), 1)
    nothing = jnp.zeros((ROWS, LANES), F32)
    forcing = [[nothing] * groups for _ in range(planes)]
    half_pairs = (half_x + RC) // 2
    ring = RC // 2
    for tx in range(count_x):
        for ty in range(count_y):
            for p in range(half_pairs):
                tile, base = p * used // SHORT, p * used % SHORT
                assert base + used <= 2 * SHORT == ROWS
                source = tx * count_y + ty
                piece = jnp.concatenate([blocks[source, tile], blocks[source, tile + 1]], 0)
                start = (ty * half_y - ring) % rows
                group, offset = start // ROWS, start % ROWS
                shift = (offset - base) % ROWS
                piece = pltpu.roll(piece, shift, 0) if shift else piece
                turned = pltpu.roll(piece, size_z2, 1)
                for half in range(2):
                    moved = jnp.where((lane < size_z2) == (half == 0), piece, turned)
                    x = (tx * half_x - ring + half * half_pairs + p) % planes
                    at = group
                    mine = (sub >= offset) & (sub < offset + used)
                    forcing[x][at] = forcing[x][at] + jnp.where(mine, moved, 0.0)
                    if offset + used > ROWS:
                        at = (group + 1) % groups
                        mine = sub < offset + used - ROWS
                        forcing[x][at] = forcing[x][at] + jnp.where(mine, moved, 0.0)
    return jnp.concatenate([jnp.concatenate(groups, 0)[None] for groups in forcing], 0)


def coarse_up(
    counts, grids, blocks, window_one, one_low, one_high, row_low, row_high,
    v_zero, forcing0, cx, cy, cz, weight, twice_one, twice_zero, *rest,
):
    prepared, rest = rest[: len(grids)], rest[len(grids) :]
    (
        out, mixed_low, mixed_high, kappa_low, kappa_high, first_low, first_high,
        v_one, cx1, cy1, cz1, w1, one_a, one_b, zero_a, zero_b, lattice, raised_one, raised_zero,
    ) = rest
    count_x, count_y = counts
    _, tile_x1, rows1, size_z1 = window_one.shape
    tile_y1 = rows1 - 2 * R1
    top1 = R1 + tile_y1
    half_x, half_y, size_z2 = tile_x1 // 2, tile_y1 // 2, size_z1 // 2
    sizes = grids[0].sizes
    forcing2 = assemble(blocks, count_x, count_y, half_x, half_y, size_z2)
    levels = [(grid, Operator(prepared[number])) for number, grid in enumerate(grids[:-1])]
    exact = ExactSolve(grids[-1], inverse=prepared[-1][...])

    planes1 = tile_x1 + 2 * R1
    for message, mixed, kappa_rim, low in (
        (one_low, mixed_low, kappa_low, True), (one_high, mixed_high, kappa_high, False)
    ):
        at, loose = 0, 2 * R1 * ROWS
        for rim, fill in ((mixed, 0.0), (kappa_rim, 1.0)):
            for layer in range(1, R1 + 1):
                x = R1 - layer if low else layer - 1
                rim[x] = jnp.full((rows1, size_z1), fill, F32)
                rim[x, R1:top1] = message[at]
                at += 1
                for distance in range(1, reach_of(layer) + 1):
                    for row in (R1 - distance, top1 + distance - 1):
                        rim[x, row : row + 1] = message[
                            loose // ROWS, loose % ROWS : loose % ROWS + 1
                        ]
                        loose += 1

    def stacked(low, which, high):
        whole = [(low, x) for x in range(R1)]
        whole += [(window_one.at[which], x) for x in range(tile_x1)]
        whole += [(high, x) for x in range(R1)]
        return Planes(0, whole)

    forcing1 = stacked(mixed_low, 0, mixed_high)
    kappa1 = stacked(kappa_low, 2, kappa_high)
    plane_setup(kappa1, cx1, cy1, cz1, w1, None, 0.25, 1, planes1 - 1)
    row = iota((rows1, size_z1), 0)
    for mixed, rim, low in ((mixed_low, first_low, True), (mixed_high, first_high, False)):
        for layer in range(1, R1 + 1):
            x = R1 - layer if low else layer - 1
            if layer == R1:
                rim[x] = mixed[x]
            else:
                reach = reach_of(layer) - 1
                inside = (row >= R1 - reach) & (row < top1 + reach)
                at = x if low else R1 + tile_x1 + x
                rim[x] = jnp.where(inside, w1[at] * mixed[x], mixed[x])
    start1 = stacked(first_low, 1, first_high)
    plane_sweep(start1, v_one, forcing1, cx1, cy1, cz1, w1, 1, planes1 - 1)

    solved = solve_whole(forcing2, levels, exact)
    lattice[:, 0 : sizes[1]] = solved
    wrap = rows1 // 2
    lattice[:, sizes[1] :] = solved[:, 0:wrap]
    start_x = lax.axis_index("tx") * half_x + (sizes[0] - R1 // 2)
    start_y = lax.rem(lax.axis_index("ty") * half_y + (sizes[1] - R1 // 2), sizes[1])
    pieces = [
        lattice[lax.rem(start_x + x, sizes[0]), pl.ds(start_y, wrap)] for x in range(planes1 // 2)
    ]
    wide = spread_lanes(jnp.concatenate(pieces, 0), twice_one[...])
    for x in range(planes1 // 2):
        for parity in range(2):
            raised_one[x, pl.ds(parity, wrap, stride=2)] = wide[x * wrap : (x + 1) * wrap]
    for x in range(1, planes1 - 1):
        one_a[x] = v_one[x] + raised_one[x // 2]
    plane_sweep(one_a, one_b, forcing1, cx1, cy1, cz1, w1, 2, planes1 - 2)
    plane_sweep(one_b, one_a, forcing1, cx1, cy1, cz1, w1, 3, planes1 - 3)

    planes, rows, size_z = zero_a.shape
    v_zero, forcing0 = kept(v_zero, RX - 1), kept(forcing0, RX - 1)
    cx, cy, cz, weight = kept(cx, RX - 2), kept(cy, RX - 1), kept(cz, RX - 1), kept(weight, RX - 1)
    first, last = R1 - 1, planes1 - R1 + 1
    stack = jnp.concatenate([one_a[x] for x in range(first, last)], 0)
    wide = spread_lanes(stack, twice_zero[...])
    chunks = size_z // LANES
    for x in range(last - first):
        for chunk in range(chunks):
            piece = wide[x * rows1 : (x + 1) * rows1, chunk * LANES : (chunk + 1) * LANES]
            for parity in range(2):
                raised_zero[chunk, x, pl.ds(parity, rows1, stride=2)] = piece
    top = rows - RY
    for x in range(RX - 1, planes - RX + 1):
        zero_b[x] = v_zero[x]
    for rim_x in (RX - 2, planes - RX + 1):
        zero_b[rim_x] = jnp.zeros((rows, size_z), F32)
    for x in range(planes - 2 * RX):
        at = 3 * tile_x1 * R1 // ROWS
        for chunk in range(chunks):
            lanes = slice(chunk * LANES, (chunk + 1) * LANES)
            zero_b[RX + x, RY - 2 : RY - 1, lanes] = row_low[at + chunk, x : x + 1]
            zero_b[RX + x, top + 1 : top + 2, lanes] = row_high[at + chunk, x : x + 1]
    for message, second, nearest in (
        (one_low, RX - 2, RX - 1), (one_high, planes - RX + 1, planes - RX)
    ):
        loose = 2 * R1 * ROWS + 2 * sum(2 * reach_of(layer) for layer in range(1, R1 + 1))
        for r in (RY - 1, top):
            for chunk in range(chunks):
                lanes = slice(chunk * LANES, (chunk + 1) * LANES)
                zero_b[nearest, r : r + 1, lanes] = message[
                    loose // ROWS, loose % ROWS : loose % ROWS + 1
                ]
                loose += 1
        at = -(-loose // ROWS)
        for chunk in range(chunks):
            lanes = slice(chunk * LANES, (chunk + 1) * LANES)
            for half in range((top - RY) // ROWS):
                zero_b[second, RY + half * ROWS : RY + (half + 1) * ROWS, lanes] = message[at]
                at += 1
    for x in range(RX - 2, planes - RX + 2):
        at = (x - RX + 2 * R1) // 2 - first
        for chunk in range(chunks):
            lanes = slice(chunk * LANES, (chunk + 1) * LANES)
            raised = raised_zero[chunk, at, 2 * R1 - RY : 2 * R1 - RY + rows]
            zero_a[x, :, lanes] = zero_b[x, :, lanes] + raised
    plane_sweep(zero_a, zero_b, forcing0, cx, cy, cz, weight, RX - 1, planes - RX + 1)
    plane_sweep(zero_b, zero_a, forcing0, cx, cy, cz, weight, RX, planes - RX)
    for x in range(planes - 2 * RX):
        out[x] = zero_a[x + RX, RY:top]


VM = pl.BlockSpec(memory_space=pltpu.VMEM)
IN_PLACE = pl.BlockSpec(memory_space=pltpu.HBM)


def call(kernel, operands, outputs, scratch, spec=VM, in_hbm=()):
    def typed(output):
        return output if isinstance(output, jax.ShapeDtypeStruct) else jax.ShapeDtypeStruct(output, F32)

    return pl.pallas_call(
        kernel,
        in_specs=[spec] * len(operands),
        out_specs=[IN_PLACE if n in in_hbm else VM for n in range(len(outputs))],
        out_shape=[typed(output) for output in outputs],
        scratch_shapes=[pltpu.VMEM(s, F32) if isinstance(s, tuple) else s for s in scratch],
        compiler_params=pltpu.CompilerParams(vmem_limit_bytes=24 * 1024 * 1024),
    )(*operands)


def shift_both(to_low, to_high, axis):
    count = lax.axis_size(axis)
    from_low = lax.ppermute(to_high, axis, [(i, (i + 1) % count) for i in range(count)])
    from_high = lax.ppermute(to_low, axis, [((i + 1) % count, i) for i in range(count)])
    return from_low, from_high


def to_everyone(blocks):
    return lax.all_to_all(blocks, ("tx", "ty"), 0, 0)


def cycle(concentration, source, material):
    tile_x, tile_y, size_z = concentration.shape
    chunks = size_z // LANES
    counts = lax.axis_size("tx"), lax.axis_size("ty")
    everyone = counts[0] * counts[1]
    rows = tile_y + 2 * RY
    message = (tile_x + 1, ROWS, size_z)
    *inputs, to_low, to_high = call(
        edges,
        tuple(
            pltpu.with_memory_space_constraint(v, pltpu.HBM)
            for v in (concentration, source, material)
        ),
        tuple(jax.ShapeDtypeStruct(v.shape, v.dtype) for v in (concentration, source, material))
        + (message, message),
        (pltpu.SemaphoreType.DMA((3,)),),
        IN_PLACE,
    )
    from_low, from_high = shift_both(to_low, to_high, "ty")
    zero = (tile_x + 2 * RX, rows, size_z)
    inner = (tile_x + 2, rows, size_z)
    one_tile = (tile_x // 2, tile_y // 2, size_z // 2)
    two_tile = tuple(extent // 2 for extent in one_tile)
    grids = levels_of(counts, two_tile)

    def bits(*shape):
        return jax.ShapeDtypeStruct(shape, BF16)

    k_tile, kappa_blocks, halves, halves_one, *twice = call(
        shrink,
        inputs[2:],
        (
            one_tile,
            (everyone, two_tile[1], LANES),
            bits(chunks, LANES, one_tile[2]),
            bits(2, one_tile[2], one_tile[2]),
            bits(LANES, one_tile[2]),
            bits(one_tile[2], size_z),
        ),
        ((one_tile[0], tile_y, LANES), one_tile[1:]),
    )
    message = (plane_tiles(tile_y), ROWS, size_z)
    window, to_low, to_high = call(
        sides,
        (*inputs, k_tile, from_low, from_high),
        ((3, tile_x, rows, size_z), message, message),
        ((rows, size_z),),
    )
    from_low, from_high = shift_both(to_low, to_high, "tx")
    kappa_blocks = to_everyone(kappa_blocks)
    wide = -(-rows // (2 * ROWS)) * ROWS
    small = (one_tile[0] + 2 * RC, wide, one_tile[2])
    pairs1 = small[0] // 2
    short = pairs1 // 2 * (two_tile[1] + RC) // SHORT
    assert pairs1 // 2 * (two_tile[1] + RC) % SHORT == 0
    message = (3 * one_tile[0] * R1 // ROWS + chunks, ROWS, LANES)
    assert one_tile[2] == LANES and tile_x <= ROWS and one_tile[1] == ROWS
    v_zero, forcing0, cx, cy, cz, weight, level_one, blocks, to_low, to_high = call(
        fine_down,
        (window, halves, halves_one, from_low, from_high),
        (inner, inner, (tile_x + 3, rows, size_z), inner, inner, inner)
        + ((3,) + one_tile, (everyone, short, SHORT, LANES), message, message),
        (
            (4, rows, size_z),
            (2, rows, size_z),
            (4, rows, size_z),
            zero,
            zero,
            (chunks, max(small[0], tile_x), 2 * wide, LANES),
            (everyone, short, SHORT, LANES),
            pltpu.SemaphoreType.DMA,
        )
        + (small,) * 9
        + ((pairs1, wide, one_tile[2]), (pairs1, ROWS, one_tile[2])),
        in_hbm=(7,),
    )
    row_low, row_high = shift_both(to_low, to_high, "ty")
    blocks = to_everyone(blocks)
    rows1 = one_tile[1] + 2 * R1
    message = (middle_tiles(tile_y, chunks), ROWS, LANES)
    window_one, to_low, to_high = call(
        middle,
        (level_one, v_zero, row_low, row_high),
        ((3, one_tile[0], rows1, one_tile[2]), message, message),
        (),
    )
    one_low, one_high = shift_both(to_low, to_high, "tx")
    one = (one_tile[0] + 2 * R1, rows1, one_tile[2])
    lattice = grids[0].sizes[1], LANES
    prepared = call(
        functools.partial(prepare, counts, grids),
        (kappa_blocks, window_one),
        tuple((5, grid.sizes[0]) + lattice for grid in grids[:-1])
        + ((-(-grids[-1].cells // ROWS) * ROWS, LANES),),
        (),
    )
    rim = (R1,) + one[1:]
    (updated,) = call(
        functools.partial(coarse_up, counts, grids),
        (blocks, window_one, one_low, one_high, row_low, row_high)
        + (v_zero, forcing0, cx, cy, cz, weight, *twice, *prepared),
        (concentration.shape,),
        (rim,) * 6
        + (one,) * 7
        + (zero, zero)
        + (
            (grids[0].sizes[0], grids[0].sizes[1] + rows1 // 2, LANES),
            (one[0] // 2, rows1, one[2]),
            (chunks, (one[0] - 2 * (R1 - 1)), 2 * rows1, LANES),
        ),
    )
    return updated


def solution(mesh):
    placed = (P("tx", "ty", None), P("tx", "ty", None), P("tx", "ty", None))
    return jax.shard_map(
        cycle, mesh=mesh, in_specs=placed, out_specs=P("tx", "ty", None), check_vma=False
    )
```

```python
import functools

import jax
import jax.numpy as jnp
from jax import lax
from jax.experimental import pallas as pl
from jax.experimental.pallas import tpu as pltpu
from jax.sharding import PartitionSpec as P


mass_rate = 0.001
relax_weight = 0.8
diffusivities = (0.15, 0.3, 0.5, 0.8, 1.2, 2.0, 3.2, 5.0)
LANES = 128
ROWS = 8
SHORT = 4
PIECES = 1
RX = 2
RY = 4
R1 = 4
RC = 2
F32 = jnp.float32
BF16 = jnp.bfloat16


def lookup(material):
    result = jnp.zeros(material.shape, F32)
    for slot_id, coeff_value in enumerate(diffusivities):
        result = jnp.where(material == slot_id, F32(coeff_value), result)
    return result


class Planes:
    def __init__(self, first, planes):
        self.first = first
        self.planes = planes

    def __getitem__(self, x):
        ref, index = self.planes[x - self.first]
        return ref[index]

    def __setitem__(self, x, value):
        ref, index = self.planes[x - self.first]
        ref[index] = value


def kept(ref, first):
    return Planes(first, [(ref, x) for x in range(ref.shape[0])])


class Picked:
    def __init__(self, flag, when_true, when_false):
        self.flag = flag
        self.when_true = when_true
        self.when_false = when_false

    def __getitem__(self, index):
        first, second = self.when_true[index], self.when_false[index]
        flag = jnp.where(self.flag, jnp.int32(1), jnp.int32(0))
        return jnp.where(jnp.full(first.shape, flag) == 1, first, second)


def iota(shape, dim):
    return lax.broadcasted_iota(jnp.int32, shape, dim)


def div(a, b):
    return lax.div(a, jnp.full_like(a, b))


def mod(a, b):
    return lax.rem(a, jnp.full_like(a, b))


def ones_where(mask):
    return jnp.where(mask, F32(1.0), F32(0.0)).astype(BF16)


def three_terms(x):
    high = x.astype(BF16)
    rest = x - high.astype(F32)
    middle = rest.astype(BF16)
    low = (rest - middle.astype(F32)).astype(BF16)
    return high, middle, low


def times_right(x, selector):
    parts = [jnp.dot(part, selector, preferred_element_type=F32) for part in three_terms(x)]
    return parts[0] + (parts[1] + parts[2])


def back(v, axis, step=1):
    return pltpu.roll(v, step, axis)


def ahead(v, axis, step=1):
    return pltpu.roll(v, v.shape[axis] - step, axis)


def halve_lanes(fine, coarse, start=0):
    shape = (fine, coarse)
    return ones_where(div(iota(shape, 0), 2) + start == iota(shape, 1))


def plane_setup(kappa, cx, cy, cz, weight, diag, scale, first, last):
    half = 0.5 * scale
    for x in range(first - 1, last):
        cx[x] = half * (kappa[x] + kappa[x + 1])
    for x in range(first, last):
        k = kappa[x]
        y_part = half * (k + ahead(k, 0))
        z_part = half * (k + ahead(k, 1))
        cy[x] = y_part
        cz[x] = z_part
        d = mass_rate + cx[x] + cx[x - 1] + y_part + back(y_part, 0) + z_part + back(z_part, 1)
        weight[x] = relax_weight / d
        if diag is not None:
            diag[x] = d


def in_plane(here, cy, cz, x):
    y_part = cy[x]
    z_part = cz[x]
    total = y_part * ahead(here, 0) + back(y_part * here, 0)
    return total + (z_part * ahead(here, 1) + back(z_part * here, 1))


def neighbours(v, cx, cy, cz, x):
    return (cx[x] * v[x + 1] + cx[x - 1] * v[x - 1]) + in_plane(v[x], cy, cz, x)


def plane_sweep(v, out, forcing, cx, cy, cz, weight, first, last):
    for x in range(first, last):
        out[x] = (1.0 - relax_weight) * v[x] + weight[x] * (forcing[x] + neighbours(v, cx, cy, cz, x))


def pieces_of(pairs, parts, semaphores):
    copies = []
    for n, (whence, whither) in enumerate(pairs):
        size = whence.shape[0] // parts
        assert size * parts == whence.shape[0]
        for part in range(parts):
            piece = pl.ds(part * size, size)
            copies.append(
                pltpu.make_async_copy(
                    whence.at[piece], whither.at[piece], semaphores.at[n * parts + part]
                )
            )
    return copies


def edges(conc_in, source_in, material_in, conc, source, material, to_low, to_high, arrived):
    copies = pieces_of(
        ((conc_in, conc), (source_in, source), (material_in, material)), conc.shape[0] // 2, arrived
    )
    for copy in copies:
        copy.start()
    for copy in copies:
        copy.wait()
    tile_x, tile_y, _ = conc.shape
    for to, low in ((to_low, True), (to_high, False)):
        for x in range(tile_x):
            rows = slice(0, 4) if low else slice(tile_y - 4, tile_y)
            near = slice(0, 3) if low else slice(1, 4)
            pair = slice(0, 2) if low else slice(2, 4)
            c = conc[x, rows]
            f = mass_rate * c + source[x, rows]
            k = lookup(material[x, rows])
            to[x, 0:3] = c[near]
            to[x, 3:5] = f[pair]
            to[x, 5:8] = k[near]
            to[tile_x, x : x + 1] = k[3:4] if low else k[0:1]


def sides(conc, source, material, k_tile, from_low, from_high, window, to_low, to_high, swept):
    tile_x, tile_y, size_z = conc.shape
    top = RY + tile_y
    for x in range(tile_x):
        c = conc[x]
        window[0, x, RY:top] = c
        window[1, x, RY:top] = mass_rate * c + source[x]
        window[2, x, RY:top] = lookup(material[x])
        window[0, x, 0:1] = jnp.zeros((1, size_z), F32)
        window[0, x, 1:4] = from_low[x, 0:3]
        window[0, x, top : top + 3] = from_high[x, 0:3]
        window[0, x, top + 3 :] = jnp.zeros((1, size_z), F32)
        window[1, x, 0:2] = jnp.zeros((2, size_z), F32)
        window[1, x, 2:4] = from_low[x, 3:5]
        window[1, x, top : top + 2] = from_high[x, 3:5]
        window[1, x, top + 2 :] = jnp.zeros((2, size_z), F32)
        window[2, x, 0:1] = from_low[tile_x, x : x + 1]
        window[2, x, 1:4] = from_low[x, 5:8]
        window[2, x, top : top + 3] = from_high[x, 5:8]
        window[2, x, top + 3 :] = from_high[tile_x, x : x + 1]
    per_plane = tile_y // ROWS
    for to, low in ((to_low, True), (to_high, False)):

        def plane(layer):
            return layer - 1 if low else tile_x - layer

        def send(at, values):
            for n in range(per_plane):
                to[at + n] = values(n)

        for n, (which, layer) in enumerate(BASE_PLANES):
            send(
                n * per_plane,
                lambda n: window[which, plane(layer), RY + n * ROWS : RY + (n + 1) * ROWS],
            )
        first_sweep(window, plane(2), swept)
        at = len(BASE_PLANES) * per_plane
        send(at, lambda n: swept[RY + n * ROWS : RY + (n + 1) * ROWS])
        loose = (at + per_plane) * ROWS
        for which, layer, reach in EXTRA_ROWS:
            for start in (RY - reach, top):
                to[loose // ROWS, loose % ROWS : loose % ROWS + reach] = window[
                    which, plane(layer), start : start + reach
                ]
                loose += reach
        at = -(-loose // ROWS)
        to[at, :, 0 : size_z // 2] = k_tile[1 if low else k_tile.shape[0] - 2]
        to[at, :, size_z // 2 :] = jnp.zeros((ROWS, size_z - size_z // 2), F32)


def first_sweep(window, x, out):
    c, f, k = window[0, x], window[1, x], window[2, x]
    next_part = 0.5 * (k + window[2, x + 1])
    last_part = 0.5 * (k + window[2, x - 1])
    y_part = 0.5 * (k + ahead(k, 0))
    z_part = 0.5 * (k + ahead(k, 1))
    d = mass_rate + next_part + last_part
    d = d + y_part + back(y_part, 0) + z_part + back(z_part, 1)
    total = next_part * window[0, x + 1] + last_part * window[0, x - 1]
    total = total + (y_part * ahead(c, 0) + back(y_part * c, 0))
    total = total + (z_part * ahead(c, 1) + back(z_part * c, 1))
    out[...] = (1.0 - relax_weight) * c + (relax_weight / d) * (f + total)


BASE_PLANES = ((0, 1), (0, 2), (1, 1), (2, 1), (2, 2))
EXTRA_ROWS = ((0, 1, 2), (0, 2, 1), (1, 1, 1), (2, 1, 2), (2, 2, 2))


def plane_tiles(tile_y):
    loose = sum(2 * reach for _, _, reach in EXTRA_ROWS)
    return (len(BASE_PLANES) + 1) * tile_y // ROWS + -(-loose // ROWS) + 1


def shrink(material, k_tile, blocks, halves, halves_one, twice_one, twice_zero, paired, paired_one):
    tile_x, tile_y, size_z = material.shape
    tile_x1, tile_y1, size_z1 = tile_x // 2, tile_y // 2, size_z // 2
    k_one = None
    for chunk in range(size_z // LANES):
        lanes = slice(chunk * LANES, (chunk + 1) * LANES)
        for pair in range(tile_x1):
            paired[pair] = lookup(material[2 * pair, :, lanes]) + lookup(
                material[2 * pair + 1, :, lanes]
            )
        stack = [
            paired[pair, pl.ds(0, tile_y1, stride=2)] + paired[pair, pl.ds(1, tile_y1, stride=2)]
            for pair in range(tile_x1)
        ]
        part = times_right(
            jnp.concatenate(stack, 0), halve_lanes(LANES, size_z1, chunk * LANES // 2)
        )
        k_one = part if k_one is None else k_one + part
    k_one = 0.125 * k_one
    for x in range(tile_x1):
        k_tile[x] = k_one[x * tile_y1 : (x + 1) * tile_y1]
    assert tile_x1 // 2 * (size_z1 // 2) <= LANES
    block = None
    for pair in range(tile_x1 // 2):
        at = 2 * pair * tile_y1
        paired_one[...] = k_one[at : at + tile_y1] + k_one[at + tile_y1 : at + 2 * tile_y1]
        piece = (
            paired_one[pl.ds(0, tile_y1 // 2, stride=2)] + paired_one[pl.ds(1, tile_y1 // 2, stride=2)]
        )
        part = times_right(piece, halve_lanes(size_z1, LANES, pair * size_z1 // 2))
        block = part if block is None else block + part
    block = 0.125 * block
    for device in range(blocks.shape[0]):
        blocks[device] = block
    for chunk in range(size_z // LANES):
        halves[chunk] = halve_lanes(LANES, size_z1, chunk * LANES // 2)
    for half in range(2):
        halves_one[half] = halve_lanes(size_z1, size_z1, half * size_z1 // 2)
    for twice in (twice_one, twice_zero):
        twice[...] = ones_where(iota(twice.shape, 0) == div(iota(twice.shape, 1), 2))


def fine_down(
    window, halves, halves_one, from_low, from_high,
    v_zero, forcing_out, cx, cy, cz, weight, level_one, blocks_out, to_low, to_high,
    conc_rim, forcing_rim, kappa_rim, once, diag, paired, blocks, left,
    k_one, f_one, u_one, v_one, cx1, cy1, cz1, w1, d1, paired_one, packed,
):
    _, tile_x, rows, size_z = window.shape
    tile_y = rows - 2 * RY
    top = RY + tile_y
    planes = tile_x + 2 * RX
    rims = (conc_rim, forcing_rim, kappa_rim)
    depths = (2, 1, 2)
    for which, rim in enumerate(rims):
        fill = jnp.full((rows, size_z), 1.0 if which == 2 else 0.0, F32)
        for x in range(2 * depths[which]):
            rim[x] = fill

    def place(which, layer, low):
        return depths[which] - layer if low else depths[which] + layer - 1

    per_plane = tile_y // ROWS
    last_tile = plane_tiles(tile_y) - 1
    for message, low in ((from_low, True), (from_high, False)):
        for at, (which, layer) in enumerate(BASE_PLANES):
            for n in range(per_plane):
                start = RY + n * ROWS
                rims[which][place(which, layer, low), start : start + ROWS] = message[
                    at * per_plane + n
                ]
        rim_x = 0 if low else planes - 1
        once[rim_x] = jnp.zeros((rows, size_z), F32)
        at = len(BASE_PLANES) * per_plane
        for n in range(per_plane):
            start = RY + n * ROWS
            once[rim_x, start : start + ROWS] = message[at + n]
        loose = (at + per_plane) * ROWS
        for which, layer, reach in EXTRA_ROWS:
            for start in (RY - reach, top):
                rims[which][place(which, layer, low), start : start + reach] = message[
                    loose // ROWS, loose % ROWS : loose % ROWS + reach
                ]
                loose += reach

    def stacked(which):
        depth = depths[which]
        whole = [(rims[which], x) for x in range(depth)]
        whole += [(window.at[which], x) for x in range(tile_x)]
        whole += [(rims[which], depth + x) for x in range(depth)]
        return Planes(RX - depth, whole)

    conc, forcing, kappa = stacked(0), stacked(1), stacked(2)
    cx, cy, cz, weight = kept(cx, RX - 2), kept(cy, RX - 1), kept(cz, RX - 1), kept(weight, RX - 1)
    v_out = kept(v_zero, RX - 1)
    plane_setup(kappa, cx, cy, cz, weight, diag, 1.0, 1, planes - 1)
    plane_sweep(conc, once, forcing, cx, cy, cz, weight, 1, planes - 1)
    plane_sweep(once, v_out, forcing, cx, cy, cz, weight, 1, planes - 1)
    chunks = size_z // LANES
    size_z1 = size_z // 2
    to_half = [halves[chunk] for chunk in range(chunks)]
    tile_x1, tile_y1 = tile_x // 2, tile_y // 2

    def put(pair, total):
        for chunk in range(chunks):
            paired[chunk, pair, 0:rows] = total[:, chunk * LANES : (chunk + 1) * LANES]

    def narrowed(pairs, start, count):
        result = None
        for chunk in range(chunks):
            stack = [
                paired[chunk, pair, pl.ds(start, count, stride=2)]
                + paired[chunk, pair, pl.ds(start + 1, count, stride=2)]
                for pair in range(pairs)
            ]
            part = times_right(jnp.concatenate(stack, 0), to_half[chunk])
            result = part if result is None else result + part
        return 0.125 * result

    wide = paired.shape[2] // 2
    planes1 = tile_x1 + 2 * RC
    if 2 * wide > rows:
        for chunk in range(chunks):
            for pair in range(planes1 - 2):
                paired[chunk, pair, rows:] = jnp.ones((2 * wide - rows, LANES), F32)
    for pair in range(planes1 - 2):
        put(pair, kappa[2 * pair] + kappa[2 * pair + 1])
    coarse = narrowed(planes1 - 2, 0, wide)
    for pair in range(planes1 - 2):
        k_one[pair + 1] = coarse[pair * wide : (pair + 1) * wide]
    for message, x in ((from_low, 0), (from_high, planes1 - 1)):
        k_one[x] = jnp.ones((wide, size_z1), F32)
        k_one[x, RC : RC + tile_y1] = message[last_tile, :, 0:size_z1]
    plane_setup(k_one, cx1, cy1, cz1, w1, d1, 0.25, 1, planes1 - 1)

    for pair in range(tile_x1):
        total = None
        for x in (RX + 2 * pair, RX + 2 * pair + 1):
            part = forcing[x] + neighbours(v_out, cx, cy, cz, x) - diag[x] * v_out[x]
            total = part if total is None else total + part
        put(pair, total)
    forcing_one = narrowed(tile_x1, RY, tile_y1)

    low, high = RC, RC + tile_y1
    nothing = jnp.zeros((wide, size_z1), F32)
    for x in range(planes1):
        f_one[x] = nothing
        if x in (0, planes1 - 1):
            v_one[x] = nothing
    for x in (0, 1, planes1 - 2, planes1 - 1):
        u_one[x] = nothing
    for x in range(tile_x1):
        f = forcing_one[x * tile_y1 : (x + 1) * tile_y1]
        f_one[x + RC, low:high] = f
        u_one[x + RC] = w1[x + RC] * f_one[x + RC]
        level_one[0, x] = f
        level_one[1, x] = u_one[x + RC, low:high]
        level_one[2, x] = k_one[x + RC, low:high]
    plane_sweep(u_one, v_one, f_one, cx1, cy1, cz1, w1, 1, planes1 - 1)
    pairs1 = planes1 // 2
    for pair in range(pairs1):
        total = None
        for x in (2 * pair, 2 * pair + 1):
            if x == 0:
                part = cx1[0] * v_one[1]
            elif x == planes1 - 1:
                part = cx1[x - 1] * v_one[x - 1]
            else:
                part = f_one[x] + neighbours(v_one, cx1, cy1, cz1, x) - d1[x] * v_one[x]
            total = part if total is None else total + part
        paired_one[pair] = total
    for pair in range(pairs1):
        packed[pair] = (
            paired_one[pair, pl.ds(0, ROWS, stride=2)] + paired_one[pair, pl.ds(1, ROWS, stride=2)]
        )
    half_pairs = pairs1 // 2
    result = times_right(
        jnp.concatenate([packed[p] for p in range(half_pairs)], 0), halves_one[0]
    ) + times_right(
        jnp.concatenate([packed[half_pairs + p] for p in range(half_pairs)], 0), halves_one[1]
    )
    used = tile_y1 // 2 + RC
    block = jnp.concatenate([result[p * ROWS : p * ROWS + used] for p in range(half_pairs)], 0)
    block = 0.125 * block
    for part in range(blocks.shape[1]):
        piece = block[part * SHORT : (part + 1) * SHORT]
        for device in range(blocks.shape[0]):
            blocks[device, part] = piece
    copies = pieces_of(((blocks, blocks_out),), left.shape[0], left)
    for copy in copies:
        copy.start()
    for x in range(RX - 1, planes - RX + 1):
        forcing_out[x - RX + 1] = forcing[x]

    for to, rows1, row0 in (
        (to_low, slice(0, R1), RY + 1),
        (to_high, slice(tile_y1 - R1, tile_y1), top - 2),
    ):
        for which in range(3):
            for x in range(tile_x1):
                flat_row = which * tile_x1 * R1 + x * R1
                to[flat_row // ROWS, flat_row % ROWS : flat_row % ROWS + R1] = level_one[
                    which, x, rows1
                ]
        start = 3 * tile_x1 * R1 // ROWS
        for x in range(tile_x):
            row = v_zero[x + 1, row0 : row0 + 1]
            for chunk in range(chunks):
                to[start + chunk, x : x + 1] = row[:, chunk * LANES : (chunk + 1) * LANES]
    for copy in copies:
        copy.wait()


def reach_of(layer):
    return R1 + 1 - layer


def middle(level_one, v_zero, from_low, from_high, window, to_low, to_high):
    _, tile_x1, tile_y1, _ = level_one.shape
    planes, rows, size_z = v_zero.shape
    top1 = R1 + tile_y1
    for which in range(3):
        for x in range(tile_x1):
            flat_row = which * tile_x1 * R1 + x * R1
            at, sub = flat_row // ROWS, flat_row % ROWS
            window[which, x, R1:top1] = level_one[which, x]
            window[which, x, 0:R1] = from_low[at, sub : sub + R1]
            window[which, x, top1:] = from_high[at, sub : sub + R1]
    chunks = size_z // LANES
    top = rows - RY

    for to, low in ((to_low, True), (to_high, False)):
        at = 0
        for which in (0, 2):
            for layer in range(1, R1 + 1):
                x = layer - 1 if low else tile_x1 - layer
                outer = 1 if which == 0 and layer == R1 else which
                to[at] = window[outer, x, R1:top1]
                at += 1
        loose = at * ROWS
        for which in (0, 2):
            for layer in range(1, R1 + 1):
                x = layer - 1 if low else tile_x1 - layer
                outer = 1 if which == 0 else which
                for distance in range(1, reach_of(layer) + 1):
                    source = outer if distance == reach_of(layer) else which
                    for row in (R1 - distance, top1 + distance - 1):
                        to[loose // ROWS, loose % ROWS : loose % ROWS + 1] = window[
                            source, x, row : row + 1
                        ]
                        loose += 1
        second, first = (2, 1) if low else (planes - 3, planes - 2)
        for row in (RY - 1, top):
            for chunk in range(chunks):
                lanes = slice(chunk * LANES, (chunk + 1) * LANES)
                to[loose // ROWS, loose % ROWS : loose % ROWS + 1] = v_zero[first, row : row + 1, lanes]
                loose += 1
        at = -(-loose // ROWS)
        for chunk in range(chunks):
            lanes = slice(chunk * LANES, (chunk + 1) * LANES)
            for half in range((top - RY) // ROWS):
                to[at] = v_zero[second, RY + half * ROWS : RY + (half + 1) * ROWS, lanes]
                at += 1


def middle_tiles(tile_y, chunks):
    loose = 2 * sum(2 * reach_of(layer) for layer in range(1, R1 + 1)) + 2 * chunks
    return 2 * R1 + -(-loose // ROWS) + chunks * tile_y // ROWS


class Grid:
    def __init__(self, sizes, strides, scales, rows, lanes):
        self.sizes = sizes
        self.strides = strides
        self.scales = scales
        self.rows = rows
        self.lanes = lanes
        self.ratios = tuple(2 if extent % 2 == 0 else 1 for extent in sizes)
        self.cells = sizes[0] * sizes[1] * sizes[2]
        self.exact = self.cells <= 64 or self.ratios == (1, 1, 1)

    def coarser(self):
        sizes = tuple(extent // ratio for extent, ratio in zip(self.sizes, self.ratios))
        scales = tuple(s / (ratio * ratio) for s, ratio in zip(self.scales, self.ratios))
        strides = tuple(s * ratio for s, ratio in zip(self.strides, self.ratios[1:]))
        return Grid(sizes, strides, scales, self.rows, self.lanes)


def next_plane(v):
    return v if v.shape[0] == 1 else jnp.concatenate([v[1:], v[:1]], 0)


def last_plane(v):
    return v if v.shape[0] == 1 else jnp.concatenate([v[-1:], v[:-1]], 0)


def restrict_whole(v, grid):
    if grid.ratios[0] == 2:
        v = jnp.concatenate(
            [v[2 * x : 2 * x + 1] + v[2 * x + 1 : 2 * x + 2] for x in range(grid.sizes[0] // 2)], 0
        )
    for axis in (1, 2):
        if grid.ratios[axis] == 2:
            step = grid.strides[axis - 1]
            even = mod(div(iota(v.shape, axis), step), 2) == 0
            v = v + jnp.where(even, ahead(v, axis, step), back(v, axis, step))
    return (1.0 / (grid.ratios[0] * grid.ratios[1] * grid.ratios[2])) * v


def prolong_whole(v, grid):
    if grid.ratios[0] == 1:
        return v
    return jnp.concatenate([v[x // 2 : x // 2 + 1] for x in range(grid.sizes[0])], 0)


def whole_operator(kappa, grid):
    half_x, half_y, half_z = (0.5 * s for s in grid.scales)
    step_y, step_z = grid.strides
    cx = half_x * (kappa + next_plane(kappa))
    cy = half_y * (kappa + ahead(kappa, 1, step_y))
    cz = half_z * (kappa + ahead(kappa, 2, step_z))
    diag = mass_rate + cx + last_plane(cx)
    diag = diag + (cy + back(cy, 1, step_y)) + (cz + back(cz, 2, step_z))
    return cx, cy, cz, diag, relax_weight / diag


def whole_neighbours(v, operator, grid):
    cx, cy, cz = operator[:3]
    step_y, step_z = grid.strides
    total = cx * next_plane(v) + last_plane(cx * v)
    total = total + (cy * ahead(v, 1, step_y) + back(cy * v, 1, step_y))
    return total + (cz * ahead(v, 2, step_z) + back(cz * v, 2, step_z))


def whole_sweep(v, forcing, operator, grid):
    return (1.0 - relax_weight) * v + operator[4] * (forcing + whole_neighbours(v, operator, grid))


class ExactSolve:
    def __init__(self, grid, kappa=None, inverse=None):
        size_x, size_y, size_z = grid.sizes
        self.grid = grid
        self.across = across = size_x * size_y
        _, step_z = grid.strides
        self.period = period = size_z * step_z
        cells = grid.cells
        padded = -(-cells // ROWS) * ROWS
        assert across <= step_z and 2 * period <= grid.lanes
        shape = (padded, grid.lanes)
        i, j = iota(shape, 0), iota(shape, 1)
        self.i, self.j = i, j
        if kappa is None:
            self.inverse = inverse
            return

        def places_of_row(n):
            sub = mod(n, across)
            return div(sub, size_y), mod(sub, size_y), div(n, across)

        def places_of_lane(n):
            n = mod(n, period)
            sub = mod(n, step_z)
            return div(sub, size_y), mod(sub, size_y), div(n, step_z)

        at_i, at_j = places_of_row(i), places_of_lane(j)
        live = (mod(j, step_z) < across) & (i < cells)
        same = (at_i[0] == at_j[0]) & (at_i[1] == at_j[1]) & (at_i[2] == at_j[2]) & live
        left = j < period
        factor = jnp.zeros(shape, F32)
        for d in range(3):
            equal = [at_i[other] == at_j[other] for other in range(3) if other != d]
            for step in (1, grid.sizes[d] - 1):
                hit = mod(at_i[d] + step, grid.sizes[d]) == at_j[d]
                factor = factor + jnp.where(
                    hit & equal[0] & equal[1], F32(0.5 * grid.scales[d]), F32(0.0)
                )
        k_row = self.as_row(kappa)
        k_column = jnp.sum(jnp.where(same & left, k_row, 0.0), axis=1, keepdims=True)
        coupled = jnp.where(live & left, factor * (k_column + k_row), 0.0)
        diag = mass_rate + jnp.sum(coupled, axis=1, keepdims=True)
        matrix = jnp.where(same & left, diag - coupled, -coupled)
        matrix = jnp.where(left, matrix, jnp.where(same, F32(1.0), F32(0.0)))
        for n in range(cells):
            lane = (n // across) * step_z + n % across
            pivot_row = matrix[n : n + 1] / matrix[n : n + 1, lane : lane + 1]
            column = matrix[:, lane : lane + 1]
            matrix = jnp.where(i == n, pivot_row, matrix - column * pivot_row)
        self.inverse = jnp.where((j >= period) & (j < 2 * period) & live, matrix, 0.0)

    def as_row(self, v):
        grid = self.grid
        size_x, size_y, _ = grid.sizes
        step_y, step_z = grid.strides
        sub = mod(iota((1, grid.lanes), 1), step_z)
        result = jnp.zeros((1, grid.lanes), F32)
        for x in range(size_x):
            for y in range(size_y):
                row = v[x, y * step_y : y * step_y + 1]
                result = jnp.where(sub == x * size_y + y, row, result)
        return result

    def solve(self, forcing):
        grid = self.grid
        size_x, size_y, _ = grid.sizes
        step_y, step_z = grid.strides
        solved = jnp.sum(self.inverse * self.as_row(forcing), axis=1, keepdims=True)
        at_z = div(mod(self.j, self.period), step_z)
        spread = jnp.where(div(self.i, self.across) == at_z, solved, 0.0)
        planes = []
        for x in range(size_x):
            rows = []
            for y in range(size_y):
                mine = mod(self.i, self.across) == x * size_y + y
                row = jnp.sum(jnp.where(mine, spread, 0.0), axis=0, keepdims=True)
                rows.append(jnp.broadcast_to(row, (step_y, grid.lanes)))
            planes.append(jnp.concatenate(rows, 0)[None])
        return jnp.concatenate(planes, 0)


def levels_of(counts, tile_sizes):
    sizes = tuple(count * extent for count, extent in zip(counts, tile_sizes)) + tile_sizes[2:]
    grid = Grid(sizes, (1, 1), (0.0625, 0.0625, 0.0625), sizes[1], LANES)
    grids = [grid]
    while not grid.exact:
        grid = grid.coarser()
        grids.append(grid)
    return grids


class Operator:
    def __init__(self, ref):
        self.ref = ref

    def __getitem__(self, part):
        if isinstance(part, slice):
            return [self.ref[p] for p in range(*part.indices(5))]
        return self.ref[part]


def kappa_of(blocks, counts, grid):
    count_x, count_y = counts
    planes, rows, size_z2 = grid.sizes
    half_x, half_y = planes // count_x, rows // count_y
    assert half_x * size_z2 == LANES and half_x == 2 and ROWS % half_y == 0 and half_y == SHORT
    share = ROWS // half_y
    kappa = [[None] * (rows // ROWS) for _ in range(planes)]
    lane = iota((ROWS, LANES), 1)
    for tx in range(count_x):
        for group in range(rows // ROWS):
            pieces = [blocks[tx * count_y + group * share + n] for n in range(share)]
            piece = jnp.concatenate(pieces, 0)
            turned = pltpu.roll(piece, size_z2, 1)
            for p in range(half_x):
                mine = (lane < size_z2) == (p == 0)
                kappa[tx * half_x + p][group] = jnp.where(mine, piece, turned)
    return jnp.concatenate([jnp.concatenate(groups, 0)[None] for groups in kappa], 0)


def prepare(counts, grids, blocks, _, *outputs):
    kappas = [kappa_of(blocks, counts, grids[0])]
    for grid in grids[:-1]:
        kappas.append(restrict_whole(kappas[-1], grid))
    outputs[-1][...] = ExactSolve(grids[-1], kappas[-1]).inverse
    for number, grid in enumerate(grids[:-1]):
        for part, value in enumerate(whole_operator(kappas[number], grid)):
            outputs[number][part] = value


def spread_lanes(v, twice):
    high = v.astype(BF16)
    low = (v - high.astype(F32)).astype(BF16)
    return jnp.dot(high, twice, preferred_element_type=F32) + jnp.dot(
        low, twice, preferred_element_type=F32
    )


def solve_whole(forcing, levels, exact):
    if not levels:
        return exact.solve(forcing)
    grid, operator = levels[0]
    v = operator[4] * forcing
    v = whole_sweep(v, forcing, operator, grid)
    residual = forcing + whole_neighbours(v, operator, grid) - operator[3] * v
    v = v + prolong_whole(solve_whole(restrict_whole(residual, grid), levels[1:], exact), grid)
    for _ in range(2):
        v = whole_sweep(v, forcing, operator, grid)
    return v


def assemble(blocks, count_x, count_y, half_x, half_y, size_z2):
    rows = count_y * half_y
    groups = rows // ROWS
    planes = count_x * half_x
    assert rows % ROWS == 0
    used = half_y + RC
    sub = iota((ROWS, LANES), 0)
    lane = iota((ROWS, LANES), 1)
    nothing = jnp.zeros((ROWS, LANES), F32)
    forcing = [[nothing] * groups for _ in range(planes)]
    half_pairs = (half_x + RC) // 2
    ring = RC // 2
    for tx in range(count_x):
        for ty in range(count_y):
            for p in range(half_pairs):
                tile, base = p * used // SHORT, p * used % SHORT
                assert base + used <= 2 * SHORT == ROWS
                source = tx * count_y + ty
                piece = jnp.concatenate([blocks[source, tile], blocks[source, tile + 1]], 0)
                start = (ty * half_y - ring) % rows
                group, offset = start // ROWS, start % ROWS
                shift = (offset - base) % ROWS
                piece = pltpu.roll(piece, shift, 0) if shift else piece
                turned = pltpu.roll(piece, size_z2, 1)
                for half in range(2):
                    moved = jnp.where((lane < size_z2) == (half == 0), piece, turned)
                    x = (tx * half_x - ring + half * half_pairs + p) % planes
                    at = group
                    mine = (sub >= offset) & (sub < offset + used)
                    forcing[x][at] = forcing[x][at] + jnp.where(mine, moved, 0.0)
                    if offset + used > ROWS:
                        at = (group + 1) % groups
                        mine = sub < offset + used - ROWS
                        forcing[x][at] = forcing[x][at] + jnp.where(mine, moved, 0.0)
    return jnp.concatenate([jnp.concatenate(groups, 0)[None] for groups in forcing], 0)


def coarse_up(
    counts, grids, blocks, window_one, one_low, one_high, row_low, row_high,
    v_zero, forcing0, cx, cy, cz, weight, twice_one, twice_zero, *rest,
):
    prepared, rest = rest[: len(grids)], rest[len(grids) :]
    (
        out, mixed_low, mixed_high, kappa_low, kappa_high, first_low, first_high,
        v_one, cx1, cy1, cz1, w1, one_a, one_b, zero_a, zero_b, lattice, raised_one, raised_zero,
        finished, left,
    ) = rest
    count_x, count_y = counts
    _, tile_x1, rows1, size_z1 = window_one.shape
    tile_y1 = rows1 - 2 * R1
    top1 = R1 + tile_y1
    half_x, half_y, size_z2 = tile_x1 // 2, tile_y1 // 2, size_z1 // 2
    sizes = grids[0].sizes
    forcing2 = assemble(blocks, count_x, count_y, half_x, half_y, size_z2)
    levels = [(grid, Operator(prepared[number])) for number, grid in enumerate(grids[:-1])]
    exact = ExactSolve(grids[-1], inverse=prepared[-1][...])

    planes1 = tile_x1 + 2 * R1
    for message, mixed, kappa_rim, low in (
        (one_low, mixed_low, kappa_low, True), (one_high, mixed_high, kappa_high, False)
    ):
        at, loose = 0, 2 * R1 * ROWS
        for rim, fill in ((mixed, 0.0), (kappa_rim, 1.0)):
            for layer in range(1, R1 + 1):
                x = R1 - layer if low else layer - 1
                rim[x] = jnp.full((rows1, size_z1), fill, F32)
                rim[x, R1:top1] = message[at]
                at += 1
                for distance in range(1, reach_of(layer) + 1):
                    for row in (R1 - distance, top1 + distance - 1):
                        rim[x, row : row + 1] = message[
                            loose // ROWS, loose % ROWS : loose % ROWS + 1
                        ]
                        loose += 1

    def stacked(low, which, high):
        whole = [(low, x) for x in range(R1)]
        whole += [(window_one.at[which], x) for x in range(tile_x1)]
        whole += [(high, x) for x in range(R1)]
        return Planes(0, whole)

    forcing1 = stacked(mixed_low, 0, mixed_high)
    kappa1 = stacked(kappa_low, 2, kappa_high)
    plane_setup(kappa1, cx1, cy1, cz1, w1, None, 0.25, 1, planes1 - 1)
    row = iota((rows1, size_z1), 0)
    for mixed, rim, low in ((mixed_low, first_low, True), (mixed_high, first_high, False)):
        for layer in range(1, R1 + 1):
            x = R1 - layer if low else layer - 1
            if layer == R1:
                rim[x] = mixed[x]
            else:
                reach = reach_of(layer) - 1
                inside = (row >= R1 - reach) & (row < top1 + reach)
                at = x if low else R1 + tile_x1 + x
                rim[x] = jnp.where(inside, w1[at] * mixed[x], mixed[x])
    start1 = stacked(first_low, 1, first_high)
    plane_sweep(start1, v_one, forcing1, cx1, cy1, cz1, w1, 1, planes1 - 1)

    solved = solve_whole(forcing2, levels, exact)
    lattice[:, 0 : sizes[1]] = solved
    wrap = rows1 // 2
    lattice[:, sizes[1] :] = solved[:, 0:wrap]
    start_x = lax.axis_index("tx") * half_x + (sizes[0] - R1 // 2)
    start_y = lax.rem(lax.axis_index("ty") * half_y + (sizes[1] - R1 // 2), sizes[1])
    pieces = [
        lattice[lax.rem(start_x + x, sizes[0]), pl.ds(start_y, wrap)] for x in range(planes1 // 2)
    ]
    wide = spread_lanes(jnp.concatenate(pieces, 0), twice_one[...])
    for x in range(planes1 // 2):
        for parity in range(2):
            raised_one[x, pl.ds(parity, wrap, stride=2)] = wide[x * wrap : (x + 1) * wrap]
    for x in range(1, planes1 - 1):
        one_a[x] = v_one[x] + raised_one[x // 2]
    plane_sweep(one_a, one_b, forcing1, cx1, cy1, cz1, w1, 2, planes1 - 2)
    plane_sweep(one_b, one_a, forcing1, cx1, cy1, cz1, w1, 3, planes1 - 3)

    planes, rows, size_z = zero_a.shape
    v_zero, forcing0 = kept(v_zero, RX - 1), kept(forcing0, RX - 1)
    cx, cy, cz, weight = kept(cx, RX - 2), kept(cy, RX - 1), kept(cz, RX - 1), kept(weight, RX - 1)
    first, last = R1 - 1, planes1 - R1 + 1
    stack = jnp.concatenate([one_a[x] for x in range(first, last)], 0)
    wide = spread_lanes(stack, twice_zero[...])
    chunks = size_z // LANES
    for x in range(last - first):
        for chunk in range(chunks):
            piece = wide[x * rows1 : (x + 1) * rows1, chunk * LANES : (chunk + 1) * LANES]
            for parity in range(2):
                raised_zero[chunk, x, pl.ds(parity, rows1, stride=2)] = piece
    top = rows - RY
    for x in range(RX - 1, planes - RX + 1):
        zero_b[x] = v_zero[x]
    for rim_x in (RX - 2, planes - RX + 1):
        zero_b[rim_x] = jnp.zeros((rows, size_z), F32)
    for x in range(planes - 2 * RX):
        at = 3 * tile_x1 * R1 // ROWS
        for chunk in range(chunks):
            lanes = slice(chunk * LANES, (chunk + 1) * LANES)
            zero_b[RX + x, RY - 2 : RY - 1, lanes] = row_low[at + chunk, x : x + 1]
            zero_b[RX + x, top + 1 : top + 2, lanes] = row_high[at + chunk, x : x + 1]
    for message, second, nearest in (
        (one_low, RX - 2, RX - 1), (one_high, planes - RX + 1, planes - RX)
    ):
        loose = 2 * R1 * ROWS + 2 * sum(2 * reach_of(layer) for layer in range(1, R1 + 1))
        for r in (RY - 1, top):
            for chunk in range(chunks):
                lanes = slice(chunk * LANES, (chunk + 1) * LANES)
                zero_b[nearest, r : r + 1, lanes] = message[
                    loose // ROWS, loose % ROWS : loose % ROWS + 1
                ]
                loose += 1
        at = -(-loose // ROWS)
        for chunk in range(chunks):
            lanes = slice(chunk * LANES, (chunk + 1) * LANES)
            for half in range((top - RY) // ROWS):
                zero_b[second, RY + half * ROWS : RY + (half + 1) * ROWS, lanes] = message[at]
                at += 1
    for x in range(RX - 2, planes - RX + 2):
        at = (x - RX + 2 * R1) // 2 - first
        for chunk in range(chunks):
            lanes = slice(chunk * LANES, (chunk + 1) * LANES)
            raised = raised_zero[chunk, at, 2 * R1 - RY : 2 * R1 - RY + rows]
            zero_a[x, :, lanes] = zero_b[x, :, lanes] + raised
    plane_sweep(zero_a, zero_b, forcing0, cx, cy, cz, weight, RX - 1, planes - RX + 1)
    copies = pieces_of(((finished, out),), finished.shape[0], left)
    for x in range(planes - 2 * RX):
        plane_sweep(zero_b, zero_a, forcing0, cx, cy, cz, weight, x + RX, x + RX + 1)
        finished[x] = zero_a[x + RX, RY:top]
        copies[x].start()
    for copy in copies:
        copy.wait()


VM = pl.BlockSpec(memory_space=pltpu.VMEM)
IN_PLACE = pl.BlockSpec(memory_space=pltpu.HBM)


def call(kernel, operands, outputs, scratch, spec=VM, in_hbm=()):
    def typed(output):
        return output if isinstance(output, jax.ShapeDtypeStruct) else jax.ShapeDtypeStruct(output, F32)

    return pl.pallas_call(
        kernel,
        in_specs=[spec] * len(operands),
        out_specs=[IN_PLACE if n in in_hbm else VM for n in range(len(outputs))],
        out_shape=[typed(output) for output in outputs],
        scratch_shapes=[pltpu.VMEM(s, F32) if isinstance(s, tuple) else s for s in scratch],
        compiler_params=pltpu.CompilerParams(vmem_limit_bytes=24 * 1024 * 1024),
    )(*operands)


def shift_both(to_low, to_high, axis):
    count = lax.axis_size(axis)
    from_low = lax.ppermute(to_high, axis, [(i, (i + 1) % count) for i in range(count)])
    from_high = lax.ppermute(to_low, axis, [((i + 1) % count, i) for i in range(count)])
    return from_low, from_high


def to_everyone(blocks):
    return lax.all_to_all(blocks, ("tx", "ty"), 0, 0)


def cycle(concentration, source, material):
    tile_x, tile_y, size_z = concentration.shape
    chunks = size_z // LANES
    counts = lax.axis_size("tx"), lax.axis_size("ty")
    everyone = counts[0] * counts[1]
    rows = tile_y + 2 * RY
    message = (tile_x + 1, ROWS, size_z)
    *inputs, to_low, to_high = call(
        edges,
        tuple(
            pltpu.with_memory_space_constraint(v, pltpu.HBM)
            for v in (concentration, source, material)
        ),
        tuple(jax.ShapeDtypeStruct(v.shape, v.dtype) for v in (concentration, source, material))
        + (message, message),
        (pltpu.SemaphoreType.DMA((3 * (tile_x // 2),)),),
        IN_PLACE,
    )
    from_low, from_high = shift_both(to_low, to_high, "ty")
    zero = (tile_x + 2 * RX, rows, size_z)
    inner = (tile_x + 2, rows, size_z)
    one_tile = (tile_x // 2, tile_y // 2, size_z // 2)
    two_tile = tuple(extent // 2 for extent in one_tile)
    grids = levels_of(counts, two_tile)

    def bits(*shape):
        return jax.ShapeDtypeStruct(shape, BF16)

    k_tile, kappa_blocks, halves, halves_one, *twice = call(
        shrink,
        inputs[2:],
        (
            one_tile,
            (everyone, two_tile[1], LANES),
            bits(chunks, LANES, one_tile[2]),
            bits(2, one_tile[2], one_tile[2]),
            bits(LANES, one_tile[2]),
            bits(one_tile[2], size_z),
        ),
        ((one_tile[0], tile_y, LANES), one_tile[1:]),
    )
    message = (plane_tiles(tile_y), ROWS, size_z)
    window, to_low, to_high = call(
        sides,
        (*inputs, k_tile, from_low, from_high),
        ((3, tile_x, rows, size_z), message, message),
        ((rows, size_z),),
    )
    from_low, from_high = shift_both(to_low, to_high, "tx")
    kappa_blocks = to_everyone(kappa_blocks)
    wide = -(-rows // (2 * ROWS)) * ROWS
    small = (one_tile[0] + 2 * RC, wide, one_tile[2])
    pairs1 = small[0] // 2
    short = pairs1 // 2 * (two_tile[1] + RC) // SHORT
    assert pairs1 // 2 * (two_tile[1] + RC) % SHORT == 0
    message = (3 * one_tile[0] * R1 // ROWS + chunks, ROWS, LANES)
    assert one_tile[2] == LANES and tile_x <= ROWS and one_tile[1] == ROWS
    v_zero, forcing0, cx, cy, cz, weight, level_one, blocks, to_low, to_high = call(
        fine_down,
        (window, halves, halves_one, from_low, from_high),
        (inner, inner, (tile_x + 3, rows, size_z), inner, inner, inner)
        + ((3,) + one_tile, (everyone, short, SHORT, LANES), message, message),
        (
            (4, rows, size_z),
            (2, rows, size_z),
            (4, rows, size_z),
            zero,
            zero,
            (chunks, max(small[0], tile_x), 2 * wide, LANES),
            (everyone, short, SHORT, LANES),
            pltpu.SemaphoreType.DMA((PIECES,)),
        )
        + (small,) * 9
        + ((pairs1, wide, one_tile[2]), (pairs1, ROWS, one_tile[2])),
        in_hbm=(7,),
    )
    row_low, row_high = shift_both(to_low, to_high, "ty")
    blocks = to_everyone(blocks)
    rows1 = one_tile[1] + 2 * R1
    message = (middle_tiles(tile_y, chunks), ROWS, LANES)
    window_one, to_low, to_high = call(
        middle,
        (level_one, v_zero, row_low, row_high),
        ((3, one_tile[0], rows1, one_tile[2]), message, message),
        (),
    )
    one_low, one_high = shift_both(to_low, to_high, "tx")
    one = (one_tile[0] + 2 * R1, rows1, one_tile[2])
    lattice = grids[0].sizes[1], LANES
    prepared = call(
        functools.partial(prepare, counts, grids),
        (kappa_blocks, window_one),
        tuple((5, grid.sizes[0]) + lattice for grid in grids[:-1])
        + ((-(-grids[-1].cells // ROWS) * ROWS, LANES),),
        (),
    )
    rim = (R1,) + one[1:]
    (updated,) = call(
        functools.partial(coarse_up, counts, grids),
        (blocks, window_one, one_low, one_high, row_low, row_high)
        + (v_zero, forcing0, cx, cy, cz, weight, *twice, *prepared),
        (concentration.shape,),
        (rim,) * 6
        + (one,) * 7
        + (zero, zero)
        + (
            (grids[0].sizes[0], grids[0].sizes[1] + rows1 // 2, LANES),
            (one[0] // 2, rows1, one[2]),
            (chunks, (one[0] - 2 * (R1 - 1)), 2 * rows1, LANES),
            concentration.shape,
            pltpu.SemaphoreType.DMA((tile_x,)),
        ),
        in_hbm=(0,),
    )
    return updated


def solution(mesh):
    placed = (P("tx", "ty", None), P("tx", "ty", None), P("tx", "ty", None))
    return jax.shard_map(
        cycle, mesh=mesh, in_specs=placed, out_specs=P("tx", "ty", None), check_vma=False
    )
```

```python
import functools

import jax
import jax.numpy as jnp
from jax import lax
from jax.experimental import pallas as pl
from jax.experimental.pallas import tpu as pltpu
from jax.sharding import PartitionSpec as P


mass_rate = 0.001
relax_weight = 0.8
diffusivities = (0.15, 0.3, 0.5, 0.8, 1.2, 2.0, 3.2, 5.0)
LANES = 128
ROWS = 8
SHORT = 4
PIECES = 1
RX = 2
RY = 4
R1 = 4
RC = 2
F32 = jnp.float32
BF16 = jnp.bfloat16


def lookup(material):
    result = jnp.zeros(material.shape, F32)
    for slot_id, coeff_value in enumerate(diffusivities):
        result = jnp.where(material == slot_id, F32(coeff_value), result)
    return result


class Planes:
    def __init__(self, first, planes):
        self.first = first
        self.planes = planes

    def __getitem__(self, x):
        ref, index = self.planes[x - self.first]
        return ref[index]

    def __setitem__(self, x, value):
        ref, index = self.planes[x - self.first]
        ref[index] = value


def kept(ref, first):
    return Planes(first, [(ref, x) for x in range(ref.shape[0])])


class Picked:
    def __init__(self, flag, when_true, when_false):
        self.flag = flag
        self.when_true = when_true
        self.when_false = when_false

    def __getitem__(self, index):
        first, second = self.when_true[index], self.when_false[index]
        flag = jnp.where(self.flag, jnp.int32(1), jnp.int32(0))
        return jnp.where(jnp.full(first.shape, flag) == 1, first, second)


def iota(shape, dim):
    return lax.broadcasted_iota(jnp.int32, shape, dim)


def div(a, b):
    return lax.div(a, jnp.full_like(a, b))


def mod(a, b):
    return lax.rem(a, jnp.full_like(a, b))


def ones_where(mask):
    return jnp.where(mask, F32(1.0), F32(0.0)).astype(BF16)


def three_terms(x):
    high = x.astype(BF16)
    rest = x - high.astype(F32)
    middle = rest.astype(BF16)
    low = (rest - middle.astype(F32)).astype(BF16)
    return high, middle, low


def times_right(x, selector):
    parts = [jnp.dot(part, selector, preferred_element_type=F32) for part in three_terms(x)]
    return parts[0] + (parts[1] + parts[2])


def back(v, axis, step=1):
    return pltpu.roll(v, step, axis)


def ahead(v, axis, step=1):
    return pltpu.roll(v, v.shape[axis] - step, axis)


def halve_lanes(fine, coarse, start=0):
    shape = (fine, coarse)
    return ones_where(div(iota(shape, 0), 2) + start == iota(shape, 1))


def plane_setup(kappa, cx, cy, cz, weight, diag, scale, first, last):
    half = 0.5 * scale
    for x in range(first - 1, last):
        cx[x] = half * (kappa[x] + kappa[x + 1])
    for x in range(first, last):
        k = kappa[x]
        y_part = half * (k + ahead(k, 0))
        z_part = half * (k + ahead(k, 1))
        cy[x] = y_part
        cz[x] = z_part
        d = mass_rate + cx[x] + cx[x - 1] + y_part + back(y_part, 0) + z_part + back(z_part, 1)
        weight[x] = relax_weight / d
        if diag is not None:
            diag[x] = d


def in_plane(here, cy, cz, x):
    y_part = cy[x]
    z_part = cz[x]
    total = y_part * ahead(here, 0) + back(y_part * here, 0)
    return total + (z_part * ahead(here, 1) + back(z_part * here, 1))


def neighbours(v, cx, cy, cz, x):
    return (cx[x] * v[x + 1] + cx[x - 1] * v[x - 1]) + in_plane(v[x], cy, cz, x)


def plane_sweep(v, out, forcing, cx, cy, cz, weight, first, last):
    for x in range(first, last):
        out[x] = (1.0 - relax_weight) * v[x] + weight[x] * (forcing[x] + neighbours(v, cx, cy, cz, x))


def pieces_of(pairs, parts, semaphores):
    copies = []
    for n, (whence, whither) in enumerate(pairs):
        size = whence.shape[0] // parts
        assert size * parts == whence.shape[0]
        for part in range(parts):
            piece = pl.ds(part * size, size)
            copies.append(
                pltpu.make_async_copy(
                    whence.at[piece], whither.at[piece], semaphores.at[n * parts + part]
                )
            )
    return copies


def edges(conc_in, source_in, material_in, conc, source, material, to_low, to_high, arrived):
    copies = pieces_of(
        ((conc_in, conc), (source_in, source), (material_in, material)), conc.shape[0] // 2, arrived
    )
    for copy in copies:
        copy.start()
    for copy in copies:
        copy.wait()
    tile_x, tile_y, _ = conc.shape
    for to, low in ((to_low, True), (to_high, False)):
        for x in range(tile_x):
            rows = slice(0, 4) if low else slice(tile_y - 4, tile_y)
            near = slice(0, 3) if low else slice(1, 4)
            pair = slice(0, 2) if low else slice(2, 4)
            c = conc[x, rows]
            f = mass_rate * c + source[x, rows]
            k = lookup(material[x, rows])
            to[x, 0:3] = c[near]
            to[x, 3:5] = f[pair]
            to[x, 5:8] = k[near]
            to[tile_x, x : x + 1] = k[3:4] if low else k[0:1]


def sides(conc, source, material, k_tile, from_low, from_high, window, to_low, to_high, swept):
    tile_x, tile_y, size_z = conc.shape
    top = RY + tile_y
    for x in range(tile_x):
        c = conc[x]
        window[0, x, RY:top] = c
        window[1, x, RY:top] = mass_rate * c + source[x]
        window[2, x, RY:top] = lookup(material[x])
        window[0, x, 0:1] = jnp.zeros((1, size_z), F32)
        window[0, x, 1:4] = from_low[x, 0:3]
        window[0, x, top : top + 3] = from_high[x, 0:3]
        window[0, x, top + 3 :] = jnp.zeros((1, size_z), F32)
        window[1, x, 0:2] = jnp.zeros((2, size_z), F32)
        window[1, x, 2:4] = from_low[x, 3:5]
        window[1, x, top : top + 2] = from_high[x, 3:5]
        window[1, x, top + 2 :] = jnp.zeros((2, size_z), F32)
        window[2, x, 0:1] = from_low[tile_x, x : x + 1]
        window[2, x, 1:4] = from_low[x, 5:8]
        window[2, x, top : top + 3] = from_high[x, 5:8]
        window[2, x, top + 3 :] = from_high[tile_x, x : x + 1]
    per_plane = tile_y // ROWS
    for to, low in ((to_low, True), (to_high, False)):

        def plane(layer):
            return layer - 1 if low else tile_x - layer

        def send(at, values):
            for n in range(per_plane):
                to[at + n] = values(n)

        for n, (which, layer) in enumerate(BASE_PLANES):
            send(
                n * per_plane,
                lambda n: window[which, plane(layer), RY + n * ROWS : RY + (n + 1) * ROWS],
            )
        first_sweep(window, plane(2), swept)
        at = len(BASE_PLANES) * per_plane
        send(at, lambda n: swept[RY + n * ROWS : RY + (n + 1) * ROWS])
        loose = (at + per_plane) * ROWS
        for which, layer, reach in EXTRA_ROWS:
            for start in (RY - reach, top):
                to[loose // ROWS, loose % ROWS : loose % ROWS + reach] = window[
                    which, plane(layer), start : start + reach
                ]
                loose += reach
        at = -(-loose // ROWS)
        to[at, :, 0 : size_z // 2] = k_tile[1 if low else k_tile.shape[0] - 2]
        to[at, :, size_z // 2 :] = jnp.zeros((ROWS, size_z - size_z // 2), F32)


def first_sweep(window, x, out):
    c, f, k = window[0, x], window[1, x], window[2, x]
    next_part = 0.5 * (k + window[2, x + 1])
    last_part = 0.5 * (k + window[2, x - 1])
    y_part = 0.5 * (k + ahead(k, 0))
    z_part = 0.5 * (k + ahead(k, 1))
    d = mass_rate + next_part + last_part
    d = d + y_part + back(y_part, 0) + z_part + back(z_part, 1)
    total = next_part * window[0, x + 1] + last_part * window[0, x - 1]
    total = total + (y_part * ahead(c, 0) + back(y_part * c, 0))
    total = total + (z_part * ahead(c, 1) + back(z_part * c, 1))
    out[...] = (1.0 - relax_weight) * c + (relax_weight / d) * (f + total)


BASE_PLANES = ((0, 1), (0, 2), (1, 1), (2, 1), (2, 2))
EXTRA_ROWS = ((0, 1, 2), (0, 2, 1), (1, 1, 1), (2, 1, 2), (2, 2, 2))


def plane_tiles(tile_y):
    loose = sum(2 * reach for _, _, reach in EXTRA_ROWS)
    return (len(BASE_PLANES) + 1) * tile_y // ROWS + -(-loose // ROWS) + 1


def shrink(material, k_tile, blocks, halves, halves_one, twice_one, twice_zero, paired, paired_one):
    tile_x, tile_y, size_z = material.shape
    tile_x1, tile_y1, size_z1 = tile_x // 2, tile_y // 2, size_z // 2
    k_one = None
    for chunk in range(size_z // LANES):
        lanes = slice(chunk * LANES, (chunk + 1) * LANES)
        for pair in range(tile_x1):
            paired[pair] = lookup(material[2 * pair, :, lanes]) + lookup(
                material[2 * pair + 1, :, lanes]
            )
        stack = [
            paired[pair, pl.ds(0, tile_y1, stride=2)] + paired[pair, pl.ds(1, tile_y1, stride=2)]
            for pair in range(tile_x1)
        ]
        part = times_right(
            jnp.concatenate(stack, 0), halve_lanes(LANES, size_z1, chunk * LANES // 2)
        )
        k_one = part if k_one is None else k_one + part
    k_one = 0.125 * k_one
    for x in range(tile_x1):
        k_tile[x] = k_one[x * tile_y1 : (x + 1) * tile_y1]
    assert tile_x1 // 2 * (size_z1 // 2) <= LANES
    block = None
    for pair in range(tile_x1 // 2):
        at = 2 * pair * tile_y1
        paired_one[...] = k_one[at : at + tile_y1] + k_one[at + tile_y1 : at + 2 * tile_y1]
        piece = (
            paired_one[pl.ds(0, tile_y1 // 2, stride=2)] + paired_one[pl.ds(1, tile_y1 // 2, stride=2)]
        )
        part = times_right(piece, halve_lanes(size_z1, LANES, pair * size_z1 // 2))
        block = part if block is None else block + part
    block = 0.125 * block
    for device in range(blocks.shape[0]):
        blocks[device] = block
    for chunk in range(size_z // LANES):
        halves[chunk] = halve_lanes(LANES, size_z1, chunk * LANES // 2)
    for half in range(2):
        halves_one[half] = halve_lanes(size_z1, size_z1, half * size_z1 // 2)
    for twice in (twice_one, twice_zero):
        twice[...] = ones_where(iota(twice.shape, 0) == div(iota(twice.shape, 1), 2))


def fine_down(
    window, halves, halves_one, from_low, from_high,
    v_zero, forcing_out, cx, cy, cz, weight, level_one, blocks_out, to_low, to_high,
    conc_rim, forcing_rim, kappa_rim, once, diag, paired, blocks, left,
    k_one, f_one, u_one, v_one, cx1, cy1, cz1, w1, d1, paired_one, packed,
):
    _, tile_x, rows, size_z = window.shape
    tile_y = rows - 2 * RY
    top = RY + tile_y
    planes = tile_x + 2 * RX
    rims = (conc_rim, forcing_rim, kappa_rim)
    depths = (2, 1, 2)
    for which, rim in enumerate(rims):
        fill = jnp.full((rows, size_z), 1.0 if which == 2 else 0.0, F32)
        for x in range(2 * depths[which]):
            rim[x] = fill

    def place(which, layer, low):
        return depths[which] - layer if low else depths[which] + layer - 1

    per_plane = tile_y // ROWS
    last_tile = plane_tiles(tile_y) - 1
    for message, low in ((from_low, True), (from_high, False)):
        for at, (which, layer) in enumerate(BASE_PLANES):
            for n in range(per_plane):
                start = RY + n * ROWS
                rims[which][place(which, layer, low), start : start + ROWS] = message[
                    at * per_plane + n
                ]
        rim_x = 0 if low else planes - 1
        once[rim_x] = jnp.zeros((rows, size_z), F32)
        at = len(BASE_PLANES) * per_plane
        for n in range(per_plane):
            start = RY + n * ROWS
            once[rim_x, start : start + ROWS] = message[at + n]
        loose = (at + per_plane) * ROWS
        for which, layer, reach in EXTRA_ROWS:
            for start in (RY - reach, top):
                rims[which][place(which, layer, low), start : start + reach] = message[
                    loose // ROWS, loose % ROWS : loose % ROWS + reach
                ]
                loose += reach

    def stacked(which):
        depth = depths[which]
        whole = [(rims[which], x) for x in range(depth)]
        whole += [(window.at[which], x) for x in range(tile_x)]
        whole += [(rims[which], depth + x) for x in range(depth)]
        return Planes(RX - depth, whole)

    conc, forcing, kappa = stacked(0), stacked(1), stacked(2)
    cx, cy, cz, weight = kept(cx, RX - 2), kept(cy, RX - 1), kept(cz, RX - 1), kept(weight, RX - 1)
    v_out = kept(v_zero, RX - 1)
    plane_setup(kappa, cx, cy, cz, weight, diag, 1.0, 1, planes - 1)
    plane_sweep(conc, once, forcing, cx, cy, cz, weight, 1, planes - 1)
    plane_sweep(once, v_out, forcing, cx, cy, cz, weight, 1, planes - 1)
    chunks = size_z // LANES
    size_z1 = size_z // 2
    to_half = [halves[chunk] for chunk in range(chunks)]
    tile_x1, tile_y1 = tile_x // 2, tile_y // 2

    def put(pair, total):
        for chunk in range(chunks):
            paired[chunk, pair, 0:rows] = total[:, chunk * LANES : (chunk + 1) * LANES]

    def narrowed(pairs, start, count):
        result = None
        for chunk in range(chunks):
            stack = [
                paired[chunk, pair, pl.ds(start, count, stride=2)]
                + paired[chunk, pair, pl.ds(start + 1, count, stride=2)]
                for pair in range(pairs)
            ]
            part = times_right(jnp.concatenate(stack, 0), to_half[chunk])
            result = part if result is None else result + part
        return 0.125 * result

    wide = paired.shape[2] // 2
    planes1 = tile_x1 + 2 * RC
    if 2 * wide > rows:
        for chunk in range(chunks):
            for pair in range(planes1 - 2):
                paired[chunk, pair, rows:] = jnp.ones((2 * wide - rows, LANES), F32)
    for pair in range(planes1 - 2):
        put(pair, kappa[2 * pair] + kappa[2 * pair + 1])
    coarse = narrowed(planes1 - 2, 0, wide)
    for pair in range(planes1 - 2):
        k_one[pair + 1] = coarse[pair * wide : (pair + 1) * wide]
    for message, x in ((from_low, 0), (from_high, planes1 - 1)):
        k_one[x] = jnp.ones((wide, size_z1), F32)
        k_one[x, RC : RC + tile_y1] = message[last_tile, :, 0:size_z1]
    plane_setup(k_one, cx1, cy1, cz1, w1, d1, 0.25, 1, planes1 - 1)

    for pair in range(tile_x1):
        total = None
        for x in (RX + 2 * pair, RX + 2 * pair + 1):
            part = forcing[x] + neighbours(v_out, cx, cy, cz, x) - diag[x] * v_out[x]
            total = part if total is None else total + part
        put(pair, total)
    forcing_one = narrowed(tile_x1, RY, tile_y1)

    low, high = RC, RC + tile_y1
    nothing = jnp.zeros((wide, size_z1), F32)
    for x in range(planes1):
        f_one[x] = nothing
        if x in (0, planes1 - 1):
            v_one[x] = nothing
    for x in (0, 1, planes1 - 2, planes1 - 1):
        u_one[x] = nothing
    for x in range(tile_x1):
        f = forcing_one[x * tile_y1 : (x + 1) * tile_y1]
        f_one[x + RC, low:high] = f
        u_one[x + RC] = w1[x + RC] * f_one[x + RC]
        level_one[0, x] = f
        level_one[1, x] = u_one[x + RC, low:high]
        level_one[2, x] = k_one[x + RC, low:high]
    plane_sweep(u_one, v_one, f_one, cx1, cy1, cz1, w1, 1, planes1 - 1)
    pairs1 = planes1 // 2
    for pair in range(pairs1):
        total = None
        for x in (2 * pair, 2 * pair + 1):
            if x == 0:
                part = cx1[0] * v_one[1]
            elif x == planes1 - 1:
                part = cx1[x - 1] * v_one[x - 1]
            else:
                part = f_one[x] + neighbours(v_one, cx1, cy1, cz1, x) - d1[x] * v_one[x]
            total = part if total is None else total + part
        paired_one[pair] = total
    for pair in range(pairs1):
        packed[pair] = (
            paired_one[pair, pl.ds(0, ROWS, stride=2)] + paired_one[pair, pl.ds(1, ROWS, stride=2)]
        )
    half_pairs = pairs1 // 2
    result = times_right(
        jnp.concatenate([packed[p] for p in range(half_pairs)], 0), halves_one[0]
    ) + times_right(
        jnp.concatenate([packed[half_pairs + p] for p in range(half_pairs)], 0), halves_one[1]
    )
    used = tile_y1 // 2 + RC
    block = jnp.concatenate([result[p * ROWS : p * ROWS + used] for p in range(half_pairs)], 0)
    block = 0.125 * block
    for part in range(blocks.shape[1]):
        piece = block[part * SHORT : (part + 1) * SHORT]
        for device in range(blocks.shape[0]):
            blocks[device, part] = piece
    copies = pieces_of(((blocks, blocks_out),), left.shape[0], left)
    for copy in copies:
        copy.start()
    for x in range(RX - 1, planes - RX + 1):
        forcing_out[x - RX + 1] = forcing[x]

    for to, rows1, row0 in (
        (to_low, slice(0, R1), RY + 1),
        (to_high, slice(tile_y1 - R1, tile_y1), top - 2),
    ):
        for which in range(3):
            for x in range(tile_x1):
                flat_row = which * tile_x1 * R1 + x * R1
                to[flat_row // ROWS, flat_row % ROWS : flat_row % ROWS + R1] = level_one[
                    which, x, rows1
                ]
        start = 3 * tile_x1 * R1 // ROWS
        for x in range(tile_x):
            row = v_zero[x + 1, row0 : row0 + 1]
            for chunk in range(chunks):
                to[start + chunk, x : x + 1] = row[:, chunk * LANES : (chunk + 1) * LANES]
    for copy in copies:
        copy.wait()


def reach_of(layer):
    return R1 + 1 - layer


def middle(level_one, v_zero, from_low, from_high, window, to_low, to_high):
    _, tile_x1, tile_y1, _ = level_one.shape
    planes, rows, size_z = v_zero.shape
    top1 = R1 + tile_y1
    for which in range(3):
        for x in range(tile_x1):
            flat_row = which * tile_x1 * R1 + x * R1
            at, sub = flat_row // ROWS, flat_row % ROWS
            window[which, x, R1:top1] = level_one[which, x]
            window[which, x, 0:R1] = from_low[at, sub : sub + R1]
            window[which, x, top1:] = from_high[at, sub : sub + R1]
    chunks = size_z // LANES
    top = rows - RY

    for to, low in ((to_low, True), (to_high, False)):
        at = 0
        for which in (0, 2):
            for layer in range(1, R1 + 1):
                x = layer - 1 if low else tile_x1 - layer
                outer = 1 if which == 0 and layer == R1 else which
                to[at] = window[outer, x, R1:top1]
                at += 1
        loose = at * ROWS
        for which in (0, 2):
            for layer in range(1, R1 + 1):
                x = layer - 1 if low else tile_x1 - layer
                outer = 1 if which == 0 else which
                for distance in range(1, reach_of(layer) + 1):
                    source = outer if distance == reach_of(layer) else which
                    for row in (R1 - distance, top1 + distance - 1):
                        to[loose // ROWS, loose % ROWS : loose % ROWS + 1] = window[
                            source, x, row : row + 1
                        ]
                        loose += 1
        second, first = (2, 1) if low else (planes - 3, planes - 2)
        for row in (RY - 1, top):
            for chunk in range(chunks):
                lanes = slice(chunk * LANES, (chunk + 1) * LANES)
                to[loose // ROWS, loose % ROWS : loose % ROWS + 1] = v_zero[first, row : row + 1, lanes]
                loose += 1
        at = -(-loose // ROWS)
        for chunk in range(chunks):
            lanes = slice(chunk * LANES, (chunk + 1) * LANES)
            for half in range((top - RY) // ROWS):
                to[at] = v_zero[second, RY + half * ROWS : RY + (half + 1) * ROWS, lanes]
                at += 1


def middle_tiles(tile_y, chunks):
    loose = 2 * sum(2 * reach_of(layer) for layer in range(1, R1 + 1)) + 2 * chunks
    return 2 * R1 + -(-loose // ROWS) + chunks * tile_y // ROWS


class Grid:
    def __init__(self, sizes, strides, scales, rows, lanes):
        self.sizes = sizes
        self.strides = strides
        self.scales = scales
        self.rows = rows
        self.lanes = lanes
        self.ratios = tuple(2 if extent % 2 == 0 else 1 for extent in sizes)
        self.cells = sizes[0] * sizes[1] * sizes[2]
        self.exact = self.cells <= 64 or self.ratios == (1, 1, 1)

    def coarser(self):
        sizes = tuple(extent // ratio for extent, ratio in zip(self.sizes, self.ratios))
        scales = tuple(s / (ratio * ratio) for s, ratio in zip(self.scales, self.ratios))
        strides = tuple(s * ratio for s, ratio in zip(self.strides, self.ratios[1:]))
        return Grid(sizes, strides, scales, self.rows, self.lanes)


def next_plane(v):
    return v if v.shape[0] == 1 else jnp.concatenate([v[1:], v[:1]], 0)


def last_plane(v):
    return v if v.shape[0] == 1 else jnp.concatenate([v[-1:], v[:-1]], 0)


def restrict_whole(v, grid):
    if grid.ratios[0] == 2:
        v = jnp.concatenate(
            [v[2 * x : 2 * x + 1] + v[2 * x + 1 : 2 * x + 2] for x in range(grid.sizes[0] // 2)], 0
        )
    for axis in (1, 2):
        if grid.ratios[axis] == 2:
            step = grid.strides[axis - 1]
            even = mod(div(iota(v.shape, axis), step), 2) == 0
            v = v + jnp.where(even, ahead(v, axis, step), back(v, axis, step))
    return (1.0 / (grid.ratios[0] * grid.ratios[1] * grid.ratios[2])) * v


def prolong_whole(v, grid):
    if grid.ratios[0] == 1:
        return v
    return jnp.concatenate([v[x // 2 : x // 2 + 1] for x in range(grid.sizes[0])], 0)


def whole_operator(kappa, grid):
    half_x, half_y, half_z = (0.5 * s for s in grid.scales)
    step_y, step_z = grid.strides
    cx = half_x * (kappa + next_plane(kappa))
    cy = half_y * (kappa + ahead(kappa, 1, step_y))
    cz = half_z * (kappa + ahead(kappa, 2, step_z))
    diag = mass_rate + cx + last_plane(cx)
    diag = diag + (cy + back(cy, 1, step_y)) + (cz + back(cz, 2, step_z))
    return cx, cy, cz, diag, relax_weight / diag


def whole_neighbours(v, operator, grid):
    cx, cy, cz = operator[:3]
    step_y, step_z = grid.strides
    total = cx * next_plane(v) + last_plane(cx * v)
    total = total + (cy * ahead(v, 1, step_y) + back(cy * v, 1, step_y))
    return total + (cz * ahead(v, 2, step_z) + back(cz * v, 2, step_z))


def whole_sweep(v, forcing, operator, grid):
    return (1.0 - relax_weight) * v + operator[4] * (forcing + whole_neighbours(v, operator, grid))


class ExactSolve:
    def __init__(self, grid, kappa=None, inverse=None):
        size_x, size_y, size_z = grid.sizes
        self.grid = grid
        self.across = across = size_x * size_y
        _, step_z = grid.strides
        self.period = period = size_z * step_z
        cells = grid.cells
        padded = -(-cells // ROWS) * ROWS
        assert across <= step_z and 2 * period <= grid.lanes
        shape = (padded, grid.lanes)
        i, j = iota(shape, 0), iota(shape, 1)
        self.i, self.j = i, j
        if kappa is None:
            self.inverse = inverse
            return

        def places_of_row(n):
            sub = mod(n, across)
            return div(sub, size_y), mod(sub, size_y), div(n, across)

        def places_of_lane(n):
            n = mod(n, period)
            sub = mod(n, step_z)
            return div(sub, size_y), mod(sub, size_y), div(n, step_z)

        at_i, at_j = places_of_row(i), places_of_lane(j)
        live = (mod(j, step_z) < across) & (i < cells)
        same = (at_i[0] == at_j[0]) & (at_i[1] == at_j[1]) & (at_i[2] == at_j[2]) & live
        left = j < period
        factor = jnp.zeros(shape, F32)
        for d in range(3):
            equal = [at_i[other] == at_j[other] for other in range(3) if other != d]
            for step in (1, grid.sizes[d] - 1):
                hit = mod(at_i[d] + step, grid.sizes[d]) == at_j[d]
                factor = factor + jnp.where(
                    hit & equal[0] & equal[1], F32(0.5 * grid.scales[d]), F32(0.0)
                )
        k_row = self.as_row(kappa)
        k_column = jnp.sum(jnp.where(same & left, k_row, 0.0), axis=1, keepdims=True)
        coupled = jnp.where(live & left, factor * (k_column + k_row), 0.0)
        diag = mass_rate + jnp.sum(coupled, axis=1, keepdims=True)
        matrix = jnp.where(same & left, diag - coupled, -coupled)
        matrix = jnp.where(left, matrix, jnp.where(same, F32(1.0), F32(0.0)))
        for n in range(cells):
            lane = (n // across) * step_z + n % across
            pivot_row = matrix[n : n + 1] / matrix[n : n + 1, lane : lane + 1]
            column = matrix[:, lane : lane + 1]
            matrix = jnp.where(i == n, pivot_row, matrix - column * pivot_row)
        self.inverse = jnp.where((j >= period) & (j < 2 * period) & live, matrix, 0.0)

    def as_row(self, v):
        grid = self.grid
        size_x, size_y, _ = grid.sizes
        step_y, step_z = grid.strides
        sub = mod(iota((1, grid.lanes), 1), step_z)
        result = jnp.zeros((1, grid.lanes), F32)
        for x in range(size_x):
            for y in range(size_y):
                row = v[x, y * step_y : y * step_y + 1]
                result = jnp.where(sub == x * size_y + y, row, result)
        return result

    def solve(self, forcing):
        grid = self.grid
        size_x, size_y, _ = grid.sizes
        step_y, step_z = grid.strides
        solved = jnp.sum(self.inverse * self.as_row(forcing), axis=1, keepdims=True)
        at_z = div(mod(self.j, self.period), step_z)
        spread = jnp.where(div(self.i, self.across) == at_z, solved, 0.0)
        planes = []
        for x in range(size_x):
            rows = []
            for y in range(size_y):
                mine = mod(self.i, self.across) == x * size_y + y
                row = jnp.sum(jnp.where(mine, spread, 0.0), axis=0, keepdims=True)
                rows.append(jnp.broadcast_to(row, (step_y, grid.lanes)))
            planes.append(jnp.concatenate(rows, 0)[None])
        return jnp.concatenate(planes, 0)


def levels_of(counts, tile_sizes):
    sizes = tuple(count * extent for count, extent in zip(counts, tile_sizes)) + tile_sizes[2:]
    grid = Grid(sizes, (1, 1), (0.0625, 0.0625, 0.0625), sizes[1], LANES)
    grids = [grid]
    while not grid.exact:
        grid = grid.coarser()
        grids.append(grid)
    return grids


class Operator:
    def __init__(self, ref):
        self.ref = ref

    def __getitem__(self, part):
        if isinstance(part, slice):
            return [self.ref[p] for p in range(*part.indices(5))]
        return self.ref[part]


def kappa_of(blocks, counts, grid):
    count_x, count_y = counts
    planes, rows, size_z2 = grid.sizes
    half_x, half_y = planes // count_x, rows // count_y
    assert half_x * size_z2 == LANES and half_x == 2 and ROWS % half_y == 0 and half_y == SHORT
    share = ROWS // half_y
    kappa = [[None] * (rows // ROWS) for _ in range(planes)]
    lane = iota((ROWS, LANES), 1)
    for tx in range(count_x):
        for group in range(rows // ROWS):
            pieces = [blocks[tx * count_y + group * share + n] for n in range(share)]
            piece = jnp.concatenate(pieces, 0)
            turned = pltpu.roll(piece, size_z2, 1)
            for p in range(half_x):
                mine = (lane < size_z2) == (p == 0)
                kappa[tx * half_x + p][group] = jnp.where(mine, piece, turned)
    return jnp.concatenate([jnp.concatenate(groups, 0)[None] for groups in kappa], 0)


def prepare(counts, grids, blocks, _, *outputs):
    kappas = [kappa_of(blocks, counts, grids[0])]
    for grid in grids[:-1]:
        kappas.append(restrict_whole(kappas[-1], grid))
    outputs[-1][...] = ExactSolve(grids[-1], kappas[-1]).inverse
    for number, grid in enumerate(grids[:-1]):
        for part, value in enumerate(whole_operator(kappas[number], grid)):
            outputs[number][part] = value


def spread_lanes(v, twice):
    high = v.astype(BF16)
    low = (v - high.astype(F32)).astype(BF16)
    return jnp.dot(high, twice, preferred_element_type=F32) + jnp.dot(
        low, twice, preferred_element_type=F32
    )


def solve_whole(forcing, levels, exact):
    if not levels:
        return exact.solve(forcing)
    grid, operator = levels[0]
    v = operator[4] * forcing
    v = whole_sweep(v, forcing, operator, grid)
    residual = forcing + whole_neighbours(v, operator, grid) - operator[3] * v
    v = v + prolong_whole(solve_whole(restrict_whole(residual, grid), levels[1:], exact), grid)
    for _ in range(2):
        v = whole_sweep(v, forcing, operator, grid)
    return v


def assemble(blocks, count_x, count_y, half_x, half_y, size_z2):
    rows = count_y * half_y
    groups = rows // ROWS
    planes = count_x * half_x
    assert rows % ROWS == 0
    used = half_y + RC
    sub = iota((ROWS, LANES), 0)
    lane = iota((ROWS, LANES), 1)
    nothing = jnp.zeros((ROWS, LANES), F32)
    forcing = [[nothing] * groups for _ in range(planes)]
    half_pairs = (half_x + RC) // 2
    ring = RC // 2
    for tx in range(count_x):
        for ty in range(count_y):
            for p in range(half_pairs):
                tile, base = p * used // SHORT, p * used % SHORT
                assert base + used <= 2 * SHORT == ROWS
                source = tx * count_y + ty
                piece = jnp.concatenate([blocks[source, tile], blocks[source, tile + 1]], 0)
                start = (ty * half_y - ring) % rows
                group, offset = start // ROWS, start % ROWS
                shift = (offset - base) % ROWS
                piece = pltpu.roll(piece, shift, 0) if shift else piece
                turned = pltpu.roll(piece, size_z2, 1)
                for half in range(2):
                    moved = jnp.where((lane < size_z2) == (half == 0), piece, turned)
                    x = (tx * half_x - ring + half * half_pairs + p) % planes
                    at = group
                    mine = (sub >= offset) & (sub < offset + used)
                    forcing[x][at] = forcing[x][at] + jnp.where(mine, moved, 0.0)
                    if offset + used > ROWS:
                        at = (group + 1) % groups
                        mine = sub < offset + used - ROWS
                        forcing[x][at] = forcing[x][at] + jnp.where(mine, moved, 0.0)
    return jnp.concatenate([jnp.concatenate(groups, 0)[None] for groups in forcing], 0)


def coarse_up(
    counts, grids, blocks, window_one, one_low, one_high, row_low, row_high,
    v_zero, forcing0, cx, cy, cz, weight, twice_one, twice_zero, *rest,
):
    prepared, rest = rest[: len(grids)], rest[len(grids) :]
    (
        out, mixed_low, mixed_high, kappa_low, kappa_high, first_low, first_high,
        v_one, cx1, cy1, cz1, w1, one_a, one_b, zero_a, zero_b, lattice, raised_one, raised_zero,
        finished, left,
    ) = rest
    count_x, count_y = counts
    _, tile_x1, rows1, size_z1 = window_one.shape
    tile_y1 = rows1 - 2 * R1
    top1 = R1 + tile_y1
    half_x, half_y, size_z2 = tile_x1 // 2, tile_y1 // 2, size_z1 // 2
    sizes = grids[0].sizes
    forcing2 = assemble(blocks, count_x, count_y, half_x, half_y, size_z2)
    levels = [(grid, Operator(prepared[number])) for number, grid in enumerate(grids[:-1])]
    exact = ExactSolve(grids[-1], inverse=prepared[-1][...])

    planes1 = tile_x1 + 2 * R1
    for message, mixed, kappa_rim, low in (
        (one_low, mixed_low, kappa_low, True), (one_high, mixed_high, kappa_high, False)
    ):
        at, loose = 0, 2 * R1 * ROWS
        for rim, fill in ((mixed, 0.0), (kappa_rim, 1.0)):
            for layer in range(1, R1 + 1):
                x = R1 - layer if low else layer - 1
                rim[x] = jnp.full((rows1, size_z1), fill, F32)
                rim[x, R1:top1] = message[at]
                at += 1
                for distance in range(1, reach_of(layer) + 1):
                    for row in (R1 - distance, top1 + distance - 1):
                        rim[x, row : row + 1] = message[
                            loose // ROWS, loose % ROWS : loose % ROWS + 1
                        ]
                        loose += 1

    def stacked(low, which, high):
        whole = [(low, x) for x in range(R1)]
        whole += [(window_one.at[which], x) for x in range(tile_x1)]
        whole += [(high, x) for x in range(R1)]
        return Planes(0, whole)

    forcing1 = stacked(mixed_low, 0, mixed_high)
    kappa1 = stacked(kappa_low, 2, kappa_high)
    plane_setup(kappa1, cx1, cy1, cz1, w1, None, 0.25, 1, planes1 - 1)
    row = iota((rows1, size_z1), 0)
    for mixed, rim, low in ((mixed_low, first_low, True), (mixed_high, first_high, False)):
        for layer in range(1, R1 + 1):
            x = R1 - layer if low else layer - 1
            if layer == R1:
                rim[x] = mixed[x]
            else:
                reach = reach_of(layer) - 1
                inside = (row >= R1 - reach) & (row < top1 + reach)
                at = x if low else R1 + tile_x1 + x
                rim[x] = jnp.where(inside, w1[at] * mixed[x], mixed[x])
    start1 = stacked(first_low, 1, first_high)
    plane_sweep(start1, v_one, forcing1, cx1, cy1, cz1, w1, 1, planes1 - 1)

    solved = solve_whole(forcing2, levels, exact)
    lattice[:, 0 : sizes[1]] = solved
    wrap = rows1 // 2
    lattice[:, sizes[1] :] = solved[:, 0:wrap]
    start_x = lax.axis_index("tx") * half_x + (sizes[0] - R1 // 2)
    start_y = lax.rem(lax.axis_index("ty") * half_y + (sizes[1] - R1 // 2), sizes[1])
    pieces = [
        lattice[lax.rem(start_x + x, sizes[0]), pl.ds(start_y, wrap)] for x in range(planes1 // 2)
    ]
    wide = spread_lanes(jnp.concatenate(pieces, 0), twice_one[...])
    for x in range(planes1 // 2):
        for parity in range(2):
            raised_one[x, pl.ds(parity, wrap, stride=2)] = wide[x * wrap : (x + 1) * wrap]
    for x in range(1, planes1 - 1):
        one_a[x] = v_one[x] + raised_one[x // 2]
    plane_sweep(one_a, one_b, forcing1, cx1, cy1, cz1, w1, 2, planes1 - 2)
    plane_sweep(one_b, one_a, forcing1, cx1, cy1, cz1, w1, 3, planes1 - 3)

    planes, rows, size_z = zero_a.shape
    v_zero, forcing0 = kept(v_zero, RX - 1), kept(forcing0, RX - 1)
    cx, cy, cz, weight = kept(cx, RX - 2), kept(cy, RX - 1), kept(cz, RX - 1), kept(weight, RX - 1)
    first, last = R1 - 1, planes1 - R1 + 1
    stack = jnp.concatenate([one_a[x] for x in range(first, last)], 0)
    wide = spread_lanes(stack, twice_zero[...])
    chunks = size_z // LANES
    for x in range(last - first):
        for chunk in range(chunks):
            piece = wide[x * rows1 : (x + 1) * rows1, chunk * LANES : (chunk + 1) * LANES]
            for parity in range(2):
                raised_zero[chunk, x, pl.ds(parity, rows1, stride=2)] = piece
    top = rows - RY
    for x in range(RX - 1, planes - RX + 1):
        zero_b[x] = v_zero[x]
    for rim_x in (RX - 2, planes - RX + 1):
        zero_b[rim_x] = jnp.zeros((rows, size_z), F32)
    for x in range(planes - 2 * RX):
        at = 3 * tile_x1 * R1 // ROWS
        for chunk in range(chunks):
            lanes = slice(chunk * LANES, (chunk + 1) * LANES)
            zero_b[RX + x, RY - 2 : RY - 1, lanes] = row_low[at + chunk, x : x + 1]
            zero_b[RX + x, top + 1 : top + 2, lanes] = row_high[at + chunk, x : x + 1]
    for message, second, nearest in (
        (one_low, RX - 2, RX - 1), (one_high, planes - RX + 1, planes - RX)
    ):
        loose = 2 * R1 * ROWS + 2 * sum(2 * reach_of(layer) for layer in range(1, R1 + 1))
        for r in (RY - 1, top):
            for chunk in range(chunks):
                lanes = slice(chunk * LANES, (chunk + 1) * LANES)
                zero_b[nearest, r : r + 1, lanes] = message[
                    loose // ROWS, loose % ROWS : loose % ROWS + 1
                ]
                loose += 1
        at = -(-loose // ROWS)
        for chunk in range(chunks):
            lanes = slice(chunk * LANES, (chunk + 1) * LANES)
            for half in range((top - RY) // ROWS):
                zero_b[second, RY + half * ROWS : RY + (half + 1) * ROWS, lanes] = message[at]
                at += 1
    for x in range(RX - 2, planes - RX + 2):
        at = (x - RX + 2 * R1) // 2 - first
        for chunk in range(chunks):
            lanes = slice(chunk * LANES, (chunk + 1) * LANES)
            raised = raised_zero[chunk, at, 2 * R1 - RY : 2 * R1 - RY + rows]
            zero_a[x, :, lanes] = zero_b[x, :, lanes] + raised
    plane_sweep(zero_a, zero_b, forcing0, cx, cy, cz, weight, RX - 1, planes - RX + 1)
    copies = pieces_of(((finished, out),), finished.shape[0], left)
    for x in range(planes - 2 * RX):
        at = x + RX
        total = forcing0[at] + neighbours(zero_b, cx, cy, cz, at)
        swept = (1.0 - relax_weight) * zero_b[at] + weight[at] * total
        finished[x] = swept[RY:top]
        copies[x].start()
    for copy in copies:
        copy.wait()


VM = pl.BlockSpec(memory_space=pltpu.VMEM)
IN_PLACE = pl.BlockSpec(memory_space=pltpu.HBM)


def call(kernel, operands, outputs, scratch, spec=VM, in_hbm=()):
    def typed(output):
        return output if isinstance(output, jax.ShapeDtypeStruct) else jax.ShapeDtypeStruct(output, F32)

    return pl.pallas_call(
        kernel,
        in_specs=[spec] * len(operands),
        out_specs=[IN_PLACE if n in in_hbm else VM for n in range(len(outputs))],
        out_shape=[typed(output) for output in outputs],
        scratch_shapes=[pltpu.VMEM(s, F32) if isinstance(s, tuple) else s for s in scratch],
        compiler_params=pltpu.CompilerParams(vmem_limit_bytes=24 * 1024 * 1024),
    )(*operands)


def shift_both(to_low, to_high, axis):
    count = lax.axis_size(axis)
    from_low = lax.ppermute(to_high, axis, [(i, (i + 1) % count) for i in range(count)])
    from_high = lax.ppermute(to_low, axis, [((i + 1) % count, i) for i in range(count)])
    return from_low, from_high


def to_everyone(blocks):
    return lax.all_to_all(blocks, ("tx", "ty"), 0, 0)


def cycle(concentration, source, material):
    tile_x, tile_y, size_z = concentration.shape
    chunks = size_z // LANES
    counts = lax.axis_size("tx"), lax.axis_size("ty")
    everyone = counts[0] * counts[1]
    rows = tile_y + 2 * RY
    message = (tile_x + 1, ROWS, size_z)
    *inputs, to_low, to_high = call(
        edges,
        tuple(
            pltpu.with_memory_space_constraint(v, pltpu.HBM)
            for v in (concentration, source, material)
        ),
        tuple(jax.ShapeDtypeStruct(v.shape, v.dtype) for v in (concentration, source, material))
        + (message, message),
        (pltpu.SemaphoreType.DMA((3 * (tile_x // 2),)),),
        IN_PLACE,
    )
    from_low, from_high = shift_both(to_low, to_high, "ty")
    zero = (tile_x + 2 * RX, rows, size_z)
    inner = (tile_x + 2, rows, size_z)
    one_tile = (tile_x // 2, tile_y // 2, size_z // 2)
    two_tile = tuple(extent // 2 for extent in one_tile)
    grids = levels_of(counts, two_tile)

    def bits(*shape):
        return jax.ShapeDtypeStruct(shape, BF16)

    k_tile, kappa_blocks, halves, halves_one, *twice = call(
        shrink,
        inputs[2:],
        (
            one_tile,
            (everyone, two_tile[1], LANES),
            bits(chunks, LANES, one_tile[2]),
            bits(2, one_tile[2], one_tile[2]),
            bits(LANES, one_tile[2]),
            bits(one_tile[2], size_z),
        ),
        ((one_tile[0], tile_y, LANES), one_tile[1:]),
    )
    message = (plane_tiles(tile_y), ROWS, size_z)
    window, to_low, to_high = call(
        sides,
        (*inputs, k_tile, from_low, from_high),
        ((3, tile_x, rows, size_z), message, message),
        ((rows, size_z),),
    )
    from_low, from_high = shift_both(to_low, to_high, "tx")
    kappa_blocks = to_everyone(kappa_blocks)
    wide = -(-rows // (2 * ROWS)) * ROWS
    small = (one_tile[0] + 2 * RC, wide, one_tile[2])
    pairs1 = small[0] // 2
    short = pairs1 // 2 * (two_tile[1] + RC) // SHORT
    assert pairs1 // 2 * (two_tile[1] + RC) % SHORT == 0
    message = (3 * one_tile[0] * R1 // ROWS + chunks, ROWS, LANES)
    assert one_tile[2] == LANES and tile_x <= ROWS and one_tile[1] == ROWS
    v_zero, forcing0, cx, cy, cz, weight, level_one, blocks, to_low, to_high = call(
        fine_down,
        (window, halves, halves_one, from_low, from_high),
        (inner, inner, (tile_x + 3, rows, size_z), inner, inner, inner)
        + ((3,) + one_tile, (everyone, short, SHORT, LANES), message, message),
        (
            (4, rows, size_z),
            (2, rows, size_z),
            (4, rows, size_z),
            zero,
            zero,
            (chunks, max(small[0], tile_x), 2 * wide, LANES),
            (everyone, short, SHORT, LANES),
            pltpu.SemaphoreType.DMA((PIECES,)),
        )
        + (small,) * 9
        + ((pairs1, wide, one_tile[2]), (pairs1, ROWS, one_tile[2])),
        in_hbm=(7,),
    )
    row_low, row_high = shift_both(to_low, to_high, "ty")
    blocks = to_everyone(blocks)
    rows1 = one_tile[1] + 2 * R1
    message = (middle_tiles(tile_y, chunks), ROWS, LANES)
    window_one, to_low, to_high = call(
        middle,
        (level_one, v_zero, row_low, row_high),
        ((3, one_tile[0], rows1, one_tile[2]), message, message),
        (),
    )
    one_low, one_high = shift_both(to_low, to_high, "tx")
    one = (one_tile[0] + 2 * R1, rows1, one_tile[2])
    lattice = grids[0].sizes[1], LANES
    prepared = call(
        functools.partial(prepare, counts, grids),
        (kappa_blocks, window_one),
        tuple((5, grid.sizes[0]) + lattice for grid in grids[:-1])
        + ((-(-grids[-1].cells // ROWS) * ROWS, LANES),),
        (),
    )
    rim = (R1,) + one[1:]
    (updated,) = call(
        functools.partial(coarse_up, counts, grids),
        (blocks, window_one, one_low, one_high, row_low, row_high)
        + (v_zero, forcing0, cx, cy, cz, weight, *twice, *prepared),
        (concentration.shape,),
        (rim,) * 6
        + (one,) * 7
        + (zero, zero)
        + (
            (grids[0].sizes[0], grids[0].sizes[1] + rows1 // 2, LANES),
            (one[0] // 2, rows1, one[2]),
            (chunks, (one[0] - 2 * (R1 - 1)), 2 * rows1, LANES),
            concentration.shape,
            pltpu.SemaphoreType.DMA((tile_x,)),
        ),
        in_hbm=(0,),
    )
    return updated


def solution(mesh):
    placed = (P("tx", "ty", None), P("tx", "ty", None), P("tx", "ty", None))
    return jax.shard_map(
        cycle, mesh=mesh, in_specs=placed, out_specs=P("tx", "ty", None), check_vma=False
    )
```
